32 devices in a mesh: rows: 4 (over z), pos: 8 (over y, x, core).
Axes of the slice: x: 2, y: 2, z: 4, core: 2. Of those that a mesh axis runs over, the one named last changes fastest.
Arguments:
- tokens: bfloat16 [16, 2048, 768], P('rows', 'pos'), may hold values from -6 to 6
- segment_ids: int32 [16, 2048], P('rows', 'pos'), may hold values from 0 to 2, as said below
- group_sizes: int32 [16, 2], P('rows'), may hold values from 4 to 16, as said below
- prefix_lens: int32 [16, 2], P('rows'), may hold values from 1 to 768, as said below
- solution_lens: int32 [16, 2, 16], P('rows'), may hold values from 0 to 657, as said below
- padding_counts: int32 [16], P('rows'), may hold values from 0 to 128, as said below
- attn_gain: bfloat16 [768], replicated, may hold values from 0.5 to 1.5
- attn_shift: bfloat16 [768], replicated, may hold values from -1 to 1
- w_qkv: bfloat16 [768, 2304], replicated, may hold values from -0.21875 to 0.21875
- query_bias: bfloat16 [768], replicated, may hold values from -2.5 to 2.5
- value_bias: bfloat16 [768], replicated, may hold values from -1.5 to 1.5
- w_out: bfloat16 [768, 768], replicated, may hold values from -0.875 to 0.875
- out_bias: bfloat16 [768], replicated, may hold values from -1.5 to 1.5
- ffn_gain: bfloat16 [768], replicated, may hold values from 0.5 to 1.5
- ffn_shift: bfloat16 [768], replicated, may hold values from -1 to 1
- w_up: bfloat16 [768, 3072], replicated, may hold values from -0.21875 to 0.21875
- up_bias: bfloat16 [3072], replicated, may hold values from -2.5 to 2.5
- w_down: bfloat16 [3072, 768], replicated, may hold values from -0.109375 to 0.109375
- down_bias: bfloat16 [768], replicated, may hold values from -1.5 to 1.5
- cotangent: bfloat16 [16, 2048, 768], P('rows', 'pos'), may hold values from -6 to 6
Outputs:
- layer_out: bfloat16 [16, 2048, 768], P('rows', 'pos')
- tokens_grad: bfloat16 [16, 2048, 768], P('rows', 'pos')
- grad_attn_gain: float32 [768], replicated
- grad_attn_shift: float32 [768], replicated
- grad_w_qkv: float32 [768, 2304], replicated
- grad_query_bias: float32 [768], replicated
- grad_value_bias: float32 [768], replicated
- grad_w_out: float32 [768, 768], replicated
- grad_out_bias: float32 [768], replicated
- grad_ffn_gain: float32 [768], replicated
- grad_ffn_shift: float32 [768], replicated
- grad_w_up: float32 [768, 3072], replicated
- grad_up_bias: float32 [3072], replicated
- grad_w_down: float32 [3072, 768], replicated
- grad_down_bias: float32 [768], replicated
The draws below stay inside these ranges and needn't reach their ends.
Inputs may be any that keep to these rules, and one draw needn't show every extreme that they name: `group_sizes`: each group holds this many solutions. `solution_lens`: A group's solutions at index group_sizes or more have length 0, the others 1 or more. `prefix_lens`: each prefix has 1 or more positions. `segment_ids`: A row holds group 0 (its prefix, then its solutions in order), then group 1, then padding_counts padding positions marked 2; together exactly 2048 positions. `padding_counts`: the row's positions after both groups.
All inputs are finite; a program needn't handle non-finite values.
Results may differ from the reference program's by a relative error of at most 0.012.
Values may be sent and summed in bfloat16 or wider, within the bound.
No kernel may reach another device: no remote copies, remote signals or barrier semaphores. Data moves between devices by JAX's collectives and lax.ppermute only.
A program may use at most 448 MiB of HBM per device.

```python
import math
from functools import partial
import jax
import jax.numpy as jnp
from jax import lax

D = 768
HEADS = 12
HEAD_DIM = 64
FF = 3072
MOST_SOL = 16
ROWS = 16
ROW_LEN = 2048


def layout(key):
    base = jax.random.fold_in(key, 11)
    cut_key, size_key, prefix_key, weight_key, pad_key = jax.random.split(base, 5)
    quarter = ROW_LEN // 4
    pad_most = ROW_LEN // 16
    padding = jax.random.randint(pad_key, (ROWS,), 0, pad_most + 1)
    padding = padding.at[0].set(pad_most).at[1].set(0).at[2].set(0)
    upper_cut = 3 * quarter - padding + 1
    cuts = jax.random.randint(cut_key, (ROWS,), quarter, upper_cut)
    cuts = cuts.at[1].set(quarter).at[2].set(3 * quarter)
    regions = jnp.stack([cuts, ROW_LEN - padding - cuts], axis=1)
    sizes = jax.random.randint(size_key, (ROWS, 2), 4, 17)
    sizes = sizes.at[0, 0].set(16).at[0, 1].set(4).at[1, 1].set(4)
    fraction = jax.random.randint(prefix_key, (ROWS, 2), 0, 1025)
    fraction = fraction.at[1, 1].set(0).at[2, 0].set(1024)
    prefix = regions // 4 + regions // 4 * fraction // 1024
    room = regions - prefix
    slots = jnp.arange(MOST_SOL)
    inside = slots[None, None, :] < sizes[:, :, None]
    is_last = slots[None, None, :] == sizes[:, :, None] - 1
    weights = jax.random.randint(weight_key, (ROWS, 2, MOST_SOL), 1, 5)
    weights = weights.at[1, 1, 0].set(4).at[1, 1, 1].set(1).at[1, 1, 2].set(1)
    weights = jnp.where(is_last, 1, weights)
    weights = jnp.where(inside, weights, 0)
    spare = room - sizes
    shares = jnp.where(inside, weights * spare[:, :, None] // jnp.sum(weights, axis=-1, keepdims=True), 0)
    rest = spare - jnp.sum(shares, axis=-1)
    lens = jnp.where(inside, 1 + shares, 0) + jnp.where(is_last, rest[:, :, None], 0)
    totals = prefix + jnp.sum(lens, axis=-1)
    places = jnp.arange(ROW_LEN)[None, :]
    segments = jnp.where(places < totals[:, :1], 0, jnp.where(places < totals[:, :1] + totals[:, 1:], 1, 2))
    return (segments.astype(jnp.int32), sizes.astype(jnp.int32), prefix.astype(jnp.int32), lens.astype(jnp.int32), padding.astype(jnp.int32))


def draw_segment_ids(key, part):
    return layout(key)[0]


def draw_group_sizes(key, part):
    return layout(key)[1]


def draw_prefix_lens(key, part):
    return layout(key)[2]


def draw_solution_lens(key, part):
    return layout(key)[3]


def draw_padding_counts(key, part):
    return layout(key)[4]


def shard_levels(stream_key, extent, shards, low, high):
    factor_of, own = 1.0, jax.random.fold_in(stream_key, 6)
    for dim, shards_of in shards:
        draws = jnp.exp(jax.random.uniform(jax.random.fold_in(own, dim), (shards_of,), jnp.float32, low / len(shards), high / len(shards)))
        factor_of = factor_of * jnp.repeat(draws, extent[dim] // shards_of).reshape([-1 if axis == dim else 1 for axis in range(len(extent))])
    return factor_of


def centred(own_key, extent, width, most, cuts=(), kind=jnp.bfloat16):
    level = shard_levels(own_key, extent, cuts, -0.22, 0.18) if cuts else 1.0
    drawn = jax.random.normal(own_key, extent, jnp.float32) * width * level
    return jnp.minimum(jnp.maximum(drawn, -most), most).astype(kind)


def setup_inputs(seed: int = 0) -> dict:
    splits = jax.random.split(jax.random.key(seed), 21)
    tokens = centred(splits[0], (ROWS, ROW_LEN, D), 1.0, 6.0, ((0, 4), (1, 8)))
    segment_ids = draw_segment_ids(jax.random.fold_in(splits[20], 71), 0)
    group_sizes = draw_group_sizes(jax.random.fold_in(splits[20], 71), 0)
    prefix_lens = draw_prefix_lens(jax.random.fold_in(splits[20], 71), 0)
    solution_lens = draw_solution_lens(jax.random.fold_in(splits[20], 71), 0)
    padding_counts = draw_padding_counts(jax.random.fold_in(splits[20], 71), 0)
    attn_gain = jnp.clip(1.0 + 0.1 * jax.random.normal(splits[6], (D,), jnp.float32), 0.5, 1.5).astype(jnp.bfloat16)
    attn_shift = centred(splits[7], (D,), 0.2, 1.0)
    w_qkv = centred(splits[8], (D, 3 * D), D ** -0.5, 0.21875)
    query_bias = centred(splits[9], (D,), 0.5, 2.5)
    value_bias = centred(splits[10], (D,), 0.3, 1.5)
    w_out = centred(splits[11], (D, D), (D // 16) ** -0.5, 0.875)
    out_bias = centred(splits[12], (D,), 0.3, 1.5)
    ffn_gain = jnp.clip(1.0 + 0.1 * jax.random.normal(splits[13], (D,), jnp.float32), 0.5, 1.5).astype(jnp.bfloat16)
    ffn_shift = centred(splits[14], (D,), 0.2, 1.0)
    w_up = centred(splits[15], (D, FF), D ** -0.5, 0.21875)
    up_bias = centred(splits[16], (FF,), 0.5, 2.5)
    w_down = centred(splits[17], (FF, D), FF ** -0.5, 0.109375)
    down_bias = centred(splits[18], (D,), 0.3, 1.5)
    cotangent = centred(splits[19], (ROWS, ROW_LEN, D), 1.0, 6.0, ((0, 4), (1, 8)))
    return {"tokens": tokens, "segment_ids": segment_ids, "group_sizes": group_sizes, "prefix_lens": prefix_lens, "solution_lens": solution_lens, "padding_counts": padding_counts, "attn_gain": attn_gain, "attn_shift": attn_shift, "w_qkv": w_qkv, "query_bias": query_bias, "value_bias": value_bias, "w_out": w_out, "out_bias": out_bias, "ffn_gain": ffn_gain, "ffn_shift": ffn_shift, "w_up": w_up, "up_bias": up_bias, "w_down": w_down, "down_bias": down_bias, "cotangent": cotangent}


EPS = 1e-05
NEG = -1e+30
GELU_C = 0.7978845608028654

@jax.custom_vjp
def low(v):
    return lax.optimization_barrier(v.astype(jnp.bfloat16)).astype(jnp.float32)

@jax.custom_vjp
def low_back(v):
    return v

def low_keep(v):
    return (low(v), None)

def low_pass(kept, grad):
    return (grad,)

def back_keep(v):
    return (v, None)

def back_low(kept, grad):
    return (low(grad),)
low.defvjp(low_keep, low_pass)
low_back.defvjp(back_keep, back_low)

def layer_norm(values, gain, shift):
    center = values - lax.optimization_barrier(jnp.mean(values, axis=-1, keepdims=True))
    spread = lax.optimization_barrier(jnp.mean(center * center, axis=-1, keepdims=True))
    return center * lax.rsqrt(spread + EPS) * gain + shift

def gelu_tanh(values):
    return 0.5 * values * (1.0 + jnp.tanh(GELU_C * (values + 0.044715 * values * values * values)))

def highest(left, right):
    return jnp.dot(left, right, precision=lax.Precision.HIGHEST, preferred_element_type=jnp.float32)

def classes(places, segments, sizes_row, prefix_row, lens_row, padding_row, length):
    slots = jnp.arange(lens_row.shape[-1], dtype=jnp.int32)
    kept_lens = jnp.where(slots[None, None, :] < sizes_row[:, :, None], lens_row, 0)
    solution_ends = jnp.cumsum(kept_lens, axis=-1).astype(jnp.int32)
    totals = (prefix_row + solution_ends[:, :, -1]).astype(jnp.int32)
    starts = (jnp.cumsum(totals, axis=-1) - totals).astype(jnp.int32)
    groups = jnp.arange(sizes_row.shape[-1], dtype=jnp.int32)
    member = segments[:, :, None] == groups[None, None, :]
    group_start = lax.optimization_barrier(jnp.sum(jnp.where(member, starts[:, None, :], 0), axis=-1)).astype(jnp.int32)
    prefix_here = lax.optimization_barrier(jnp.sum(jnp.where(member, prefix_row[:, None, :], 0), axis=-1)).astype(jnp.int32)
    inside = places[None, :] - group_start - prefix_here
    passed = jnp.where(member[:, :, :, None], inside[:, :, None, None] >= solution_ends[:, None, :, :], False)
    passed_count = lax.optimization_barrier(jnp.sum(passed.astype(jnp.int32), axis=(2, 3))).astype(jnp.int32)
    branch = jnp.where(inside < 0, -1, passed_count).astype(jnp.int32)
    padded = places[None, :] >= length - padding_row[:, None]
    class_id = jnp.where(padded, -1, segments).astype(jnp.int32)
    branch = jnp.where(padded, -2, branch).astype(jnp.int32)
    return (class_id, branch)

def visible(query_class, query_branch, query_places, key_class, key_branch, key_places):
    same = query_class[:, :, None] == key_class[:, None, :]
    causal = key_places[None, None, :] <= query_places[None, :, None]
    shared = (key_branch[:, None, :] == -1) | (key_branch[:, None, :] == query_branch[:, :, None])
    return same & causal & shared

def head_block(allowed, triple):
    query_head, key_head, value_head = triple
    raw = highest(query_head, key_head.T) * (1.0 / math.sqrt(HEAD_DIM))
    scores = jnp.where(allowed, low_back(raw), NEG)
    top = lax.optimization_barrier(jnp.max(scores, axis=-1, keepdims=True))
    weights = jnp.exp(scores - top)
    probs = weights / lax.optimization_barrier(jnp.sum(weights, axis=-1, keepdims=True))
    return highest(low(probs), value_head)

def split_heads(values):
    return values.reshape(values.shape[0], HEADS, HEAD_DIM).transpose(1, 0, 2)

def row_forward(inputs, params, allowed):
    attn_gain, attn_shift, w_qkv, query_bias, value_bias, w_out, out_bias, ffn_gain, ffn_shift, w_up, up_bias, w_down, down_bias = params
    act_one = low(layer_norm(inputs, attn_gain, attn_shift))
    projected = highest(act_one, w_qkv)
    queries = low(low_back(projected[:, :D] + query_bias))
    keys = low(low_back(projected[:, D:2 * D]))
    values = low(low_back(projected[:, 2 * D:] + value_bias))
    heads_out = lax.map(jax.checkpoint(partial(head_block, allowed)), (split_heads(queries), split_heads(keys), split_heads(values)))
    mixed = low(low_back(heads_out.transpose(1, 0, 2).reshape(inputs.shape[0], D)))
    attn = low_back(highest(mixed, w_out) + out_bias)
    resid = inputs + attn
    act_two = low(layer_norm(resid, ffn_gain, ffn_shift))
    upper = low_back(highest(act_two, w_up) + up_bias)
    hidden = low(gelu_tanh(upper))
    return resid + (highest(hidden, w_down) + down_bias)

def reference(tokens, segment_ids, group_sizes, prefix_lens, solution_lens, padding_counts, attn_gain, attn_shift, w_qkv, query_bias, value_bias, w_out, out_bias, ffn_gain, ffn_shift, w_up, up_bias, w_down, down_bias, cotangent):
    params = tuple((element.astype(jnp.float32) for element in (attn_gain, attn_shift, w_qkv, query_bias, value_bias, w_out, out_bias, ffn_gain, ffn_shift, w_up, up_bias, w_down, down_bias)))
    places = jnp.arange(ROW_LEN, dtype=jnp.int32)

    def one_row(totals, row_data):
        inputs, cot_row, segment_row, size_row, prefix_row, len_row, padding_row = row_data
        class_id, branch = classes(places, segment_row[None], size_row[None], prefix_row[None], len_row[None], padding_row[None], ROW_LEN)
        allowed = visible(class_id, branch, places, class_id, branch, places)[0]

        def forward(values, weights):
            return row_forward(values, weights, allowed)
        output, pullback = jax.vjp(forward, inputs.astype(jnp.float32), params)
        input_grad, weight_grads = pullback(cot_row.astype(jnp.float32))
        totals = jax.tree.map(jnp.add, totals, weight_grads)
        return (totals, (output.astype(jnp.bfloat16), input_grad.astype(jnp.bfloat16)))
    zeros = tuple((jnp.zeros_like(element) for element in params))
    totals, (layer_out, tokens_grad) = lax.scan(one_row, zeros, (tokens, cotangent, segment_ids, group_sizes, prefix_lens, solution_lens, padding_counts))
    return (layer_out, tokens_grad, totals[0], totals[1], totals[2], totals[3], totals[4], totals[5], totals[6], totals[7], totals[8], totals[9], totals[10], totals[11], totals[12])
```

```python
import functools

import jax
import jax.numpy as jnp
from jax import lax
from jax.experimental import pallas as pl
from jax.experimental.pallas import tpu as pltpu
from jax.sharding import PartitionSpec as P

HEAD_DIM = 64
EPS = 1e-05
NEG = -1e30
GELU_C = 0.7978845608028654
F32 = jnp.float32
BF16 = jnp.bfloat16
NT = (((1,), (1,)), ((), ()))
TN = (((0,), (0,)), ((), ()))


def layer_norm(values, gain, shift):
    center = values - jnp.mean(values, axis=-1, keepdims=True)
    spread = jnp.mean(center * center, axis=-1, keepdims=True)
    return center * lax.rsqrt(spread + EPS) * gain + shift


def gelu_tanh(values):
    return 0.5 * values * (1.0 + jnp.tanh(GELU_C * (values + 0.044715 * values * values * values)))


def matmul(left, right, dims=(((1,), (0,)), ((), ()))):
    return lax.dot_general(left, right, dims, preferred_element_type=F32)


def head_pairs(heads):
    return [(h // 2, min(128, heads * HEAD_DIM - (h // 2) * 128)) for h in range(heads)]


def mask_bias(info_ref, key_start, size):
    prefix_start, prefix_end = info_ref[0, 0:1, :], info_ref[0, 1:2, :]
    own_start, query_place = info_ref[0, 2:3, :], info_ref[0, 3:4, :]
    key_place = key_start + lax.broadcasted_iota(jnp.int32, (size, size), 0)
    allowed = ((key_place >= prefix_start) & (key_place < prefix_end)) | (
        (key_place >= own_start) & (key_place <= query_place)
    )
    return jnp.where(allowed, 0.0, NEG).astype(F32)


def fill_padded(source_ref, target_ref, heads):
    for h, (pair, width) in enumerate(head_pairs(heads)):
        rows = source_ref[0, pair * 128 : pair * 128 + width, :]
        if width == 128:
            keep = (lax.broadcasted_iota(jnp.int32, rows.shape, 0) // HEAD_DIM) == (h % 2)
            rows = jnp.where(keep, rows, jnp.zeros_like(rows))
        target_ref[h, 0:width, :] = rows


def forward_kernel(
    heads, blocks, phys_ref, flag_ref, query_t_ref, key_ref, value_t_ref, info_ref,
    mixed_ref, out_t_ref, lse_ref, bias_sc, top_sc, total_sc, acc_sc, query_sc,
):
    size = query_t_ref.shape[2]
    i = pl.program_id(0)
    fill_padded(query_t_ref, query_sc, heads)
    top_sc[...] = jnp.full_like(top_sc, NEG)
    total_sc[...] = jnp.zeros_like(total_sc)
    acc_sc[...] = jnp.zeros_like(acc_sc)

    @pl.loop(0, i + 1)
    def _(j):
        @pl.when(flag_ref[i * blocks + j] > 0)
        def _():
            at = phys_ref[j]
            bias_sc[...] = mask_bias(info_ref, j * size, size)
            for h, (pair, width) in enumerate(head_pairs(heads)):
                rows = slice(h * HEAD_DIM, (h + 1) * HEAD_DIM)
                scores = (
                    matmul(key_ref[at, :, pair * 128 : pair * 128 + width], query_sc[h, 0:width, :])
                    + bias_sc[...]
                )
                old = top_sc[h]
                top = jnp.maximum(old, jnp.max(scores, axis=0, keepdims=True))
                shrink = jnp.exp(old - top)
                weights = jnp.exp(scores - top)
                total_sc[h] = shrink * total_sc[h] + jnp.sum(weights, axis=0, keepdims=True)
                top_sc[h] = top
                acc_sc[rows, :] = shrink * acc_sc[rows, :] + matmul(
                    value_t_ref[at, rows, :], weights.astype(BF16)
                )

    for h in range(heads):
        rows = slice(h * HEAD_DIM, (h + 1) * HEAD_DIM)
        out_t_ref[0, rows, :] = acc_sc[rows, :] / total_sc[h]
        lse_ref[0, h : h + 1, :] = top_sc[h] + jnp.log(total_sc[h])
    mixed_ref[0] = out_t_ref[0].T.astype(BF16)


def attention_forward(phys, flags, query_t, key, value_t, info, heads):
    blocks, width, size = query_t.shape
    lse_rows = -(-heads // 8) * 8
    whole = pl.Buffered(1)
    spec = pltpu.PrefetchScalarGridSpec(
        num_scalar_prefetch=2,
        grid=(blocks,),
        in_specs=[
            pl.BlockSpec((1, width, size), lambda i, p, f: (p[i], 0, 0)),
            pl.BlockSpec((blocks, size, width), lambda i, p, f: (0, 0, 0), pipeline_mode=whole),
            pl.BlockSpec((blocks, width, size), lambda i, p, f: (0, 0, 0), pipeline_mode=whole),
            pl.BlockSpec((1, 8, size), lambda i, p, f: (i, 0, 0)),
        ],
        out_specs=[
            pl.BlockSpec((1, size, width), lambda i, p, f: (p[i], 0, 0)),
            pl.BlockSpec((1, width, size), lambda i, p, f: (p[i], 0, 0)),
            pl.BlockSpec((1, lse_rows, size), lambda i, p, f: (p[i], 0, 0)),
        ],
        scratch_shapes=[
            pltpu.VMEM((size, size), F32),
            pltpu.VMEM((heads, 1, size), F32),
            pltpu.VMEM((heads, 1, size), F32),
            pltpu.VMEM((width, size), F32),
            pltpu.VMEM((heads, 128, size), BF16),
        ],
    )
    pairs = heads * blocks * (blocks + 1) // 2 * size * size
    return pl.pallas_call(
        functools.partial(forward_kernel, heads, blocks),
        grid_spec=spec,
        out_shape=(
            jax.ShapeDtypeStruct((blocks, size, width), BF16),
            jax.ShapeDtypeStruct((blocks, width, size), F32),
            jax.ShapeDtypeStruct((blocks, lse_rows, size), F32),
        ),
        compiler_params=pltpu.CompilerParams(
            dimension_semantics=("arbitrary",), vmem_limit_bytes=60 * 1024 * 1024
        ),
        cost_estimate=pl.CostEstimate(
            flops=pairs * 4 * 128, transcendentals=pairs, bytes_accessed=blocks * size * width * 16
        ),
        name="attention_forward",
    )(phys, flags, query_t, key, value_t, info)


def backward_kernel(
    heads, blocks, phys_ref, flag_ref, query_t_ref, grad_t_ref, out_t_ref, lse_ref, info_ref,
    key_ref, key_t_ref, value_ref, query_grad_ref, key_grad_ref, value_grad_ref,
    bias_sc, query_grad_sc, key_grad_sc, value_grad_sc, query_sc, grad_sc, delta_sc,
):
    size = query_t_ref.shape[2]
    i = pl.program_id(0)

    @pl.when(i == 0)
    def _():
        key_grad_sc[...] = jnp.zeros_like(key_grad_sc)
        value_grad_sc[...] = jnp.zeros_like(value_grad_sc)

    fill_padded(query_t_ref, query_sc, heads)
    fill_padded(grad_t_ref, grad_sc, heads)
    query_grad_sc[...] = jnp.zeros_like(query_grad_sc)
    for h in range(heads):
        rows = slice(h * HEAD_DIM, (h + 1) * HEAD_DIM)
        delta_sc[h] = jnp.sum(
            grad_t_ref[0, rows, :].astype(F32) * out_t_ref[0, rows, :], axis=0, keepdims=True
        )

    @pl.loop(0, i + 1)
    def _(j):
        @pl.when(flag_ref[i * blocks + j] > 0)
        def _():
            at = phys_ref[j]
            bias_sc[...] = mask_bias(info_ref, j * size, size)
            for h, (pair, width) in enumerate(head_pairs(heads)):
                rows = slice(h * HEAD_DIM, (h + 1) * HEAD_DIM)
                lanes = slice(pair * 128, pair * 128 + width)
                scores = matmul(key_ref[at, :, lanes], query_sc[h, 0:width, :]) + bias_sc[...]
                probs = jnp.exp(scores - lse_ref[0, h : h + 1, :])
                grad_probs = matmul(value_ref[at, :, lanes], grad_sc[h, 0:width, :])
                grad_scores = (probs * (grad_probs - delta_sc[h])).astype(BF16)
                query_grad_sc[rows, :] += matmul(key_t_ref[at, rows, :], grad_scores)
                value_grad_sc[at, rows, :] += matmul(
                    grad_t_ref[0, rows, :], probs.astype(BF16), NT
                )
                key_grad_sc[at, rows, :] += matmul(query_t_ref[0, rows, :], grad_scores, NT)

    query_grad_ref[0] = (query_grad_sc[...] * 0.125).T.astype(BF16)

    @pl.when(i == blocks - 1)
    def _():
        for block in range(blocks):
            key_grad_ref[block] = key_grad_sc[block].T.astype(BF16)
            value_grad_ref[block] = value_grad_sc[block].T.astype(BF16)


def attention_backward(phys, flags, query_t, grad_t, out_t, lse, info, key, key_t, value, heads):
    blocks, width, size = query_t.shape
    moving_t = pl.BlockSpec((1, width, size), lambda i, p, f: (p[i], 0, 0))
    moving = pl.BlockSpec((1, size, width), lambda i, p, f: (p[i], 0, 0))
    whole = pl.BlockSpec(
        (blocks, size, width), lambda i, p, f: (0, 0, 0), pipeline_mode=pl.Buffered(1)
    )
    whole_t = pl.BlockSpec(
        (blocks, width, size), lambda i, p, f: (0, 0, 0), pipeline_mode=pl.Buffered(1)
    )
    spec = pltpu.PrefetchScalarGridSpec(
        num_scalar_prefetch=2,
        grid=(blocks,),
        in_specs=[
            moving_t,
            moving_t,
            moving_t,
            pl.BlockSpec((1, lse.shape[1], size), lambda i, p, f: (p[i], 0, 0)),
            pl.BlockSpec((1, 8, size), lambda i, p, f: (i, 0, 0)),
            whole,
            whole_t,
            whole,
        ],
        out_specs=[moving, whole, whole],
        scratch_shapes=[
            pltpu.VMEM((size, size), F32),
            pltpu.VMEM((width, size), F32),
            pltpu.VMEM((blocks, width, size), F32),
            pltpu.VMEM((blocks, width, size), F32),
            pltpu.VMEM((heads, 128, size), BF16),
            pltpu.VMEM((heads, 128, size), BF16),
            pltpu.VMEM((heads, 1, size), F32),
        ],
    )
    out = jax.ShapeDtypeStruct((blocks, size, width), BF16)
    pairs = heads * blocks * (blocks + 1) // 2 * size * size
    return pl.pallas_call(
        functools.partial(backward_kernel, heads, blocks),
        grid_spec=spec,
        out_shape=(out, out, out),
        compiler_params=pltpu.CompilerParams(
            dimension_semantics=("arbitrary",), vmem_limit_bytes=60 * 1024 * 1024
        ),
        cost_estimate=pl.CostEstimate(
            flops=pairs * 10 * 128, transcendentals=pairs, bytes_accessed=blocks * size * width * 20
        ),
        name="attention_backward",
    )(phys, flags, query_t, grad_t, out_t, lse, info, key, key_t, value)


def row_layout(sizes, prefixes, lens, padding, length, size):
    slots = jnp.arange(lens.shape[-1], dtype=jnp.int32)
    kept = jnp.where(slots[None, :] < sizes[:, None], lens, 0)
    ends = jnp.cumsum(kept, axis=-1)
    totals = prefixes + ends[:, -1]
    starts = jnp.cumsum(totals) - totals
    places = jnp.arange(length, dtype=jnp.int32)
    padded = places >= length - padding
    prefix_start = jnp.broadcast_to(length - padding, (length,))
    prefix_end = prefix_start
    own_start = prefix_start
    for g in range(sizes.shape[0]):
        member = (places >= starts[g]) & (places < starts[g] + totals[g]) & ~padded
        body = starts[g] + prefixes[g]
        inside = places - body
        base = jnp.max(jnp.where(inside[:, None] >= ends[g][None, :], ends[g][None, :], 0), axis=-1)
        solution = inside >= 0
        prefix_start = jnp.where(member, starts[g], prefix_start)
        prefix_end = jnp.where(member, jnp.where(solution, body, starts[g]), prefix_end)
        own_start = jnp.where(member, jnp.where(solution, body + base, starts[g]), own_start)
    blocks = length // size
    low = jnp.arange(blocks, dtype=jnp.int32)[None, :] * size
    high = low + size
    need = (
        jnp.maximum(prefix_start[:, None], low) < jnp.minimum(prefix_end[:, None], high)
    ) | (jnp.maximum(own_start[:, None], low) < jnp.minimum(places[:, None] + 1, high))
    flags = jnp.any(need.reshape(blocks, size, blocks), axis=1).astype(jnp.int32).reshape(-1)
    zero = jnp.zeros_like(places)
    info = jnp.stack([prefix_start, prefix_end, own_start, places, zero, zero, zero, zero])
    info = info.astype(jnp.int32).reshape(8, blocks, size).transpose(1, 0, 2)
    return info, flags


def swap(values, axis, mask):
    count = lax.axis_size(axis)
    return lax.ppermute(values, axis, [(i, i ^ mask) for i in range(count)])


def bits(count):
    return [1 << b for b in range(count.bit_length() - 1)]


def take(values, index):
    return lax.dynamic_index_in_dim(values, index, 0, keepdims=False)


def halve(values, steps):
    for axis, mask, bit in steps:
        two = values.reshape(2, values.shape[0] // 2, *values.shape[1:])
        arrived = swap(take(two, 1 - bit), axis, mask)
        values = (take(two, bit).astype(F32) + arrived.astype(F32)).astype(values.dtype)
    return values


def double(values, steps):
    for axis, mask, bit in reversed(steps):
        arrived = swap(values, axis, mask)
        first = jnp.where(bit == 0, values, arrived)
        second = jnp.where(bit == 0, arrived, values)
        values = jnp.concatenate([first, second], axis=0)
    return values


def per_device(
    row_axis,
    tokens,
    segment_ids,
    group_sizes,
    prefix_lens,
    solution_lens,
    padding_counts,
    attn_gain,
    attn_shift,
    w_qkv,
    query_bias,
    value_bias,
    w_out,
    out_bias,
    ffn_gain,
    ffn_shift,
    w_up,
    up_bias,
    w_down,
    down_bias,
    cotangent,
):
    rows, size, model = tokens.shape
    devices = lax.axis_size("pos")
    parts = devices // rows
    blocks = devices
    heads = model // HEAD_DIM // parts
    width = heads * HEAD_DIM
    place = lax.axis_index("pos")
    owner, part = place // parts, place % parts

    def bring(values):
        return jnp.stack(
            [
                swap(take(values, owner ^ m), "pos", m * parts) if m else take(values, owner)
                for m in range(rows)
            ]
        )

    def give_back(values):
        out = jnp.zeros_like(values)
        for m in range(rows):
            slab = swap(values[m], "pos", m * parts) if m else values[m]
            out = lax.dynamic_update_index_in_dim(out, slab, owner ^ m, 0)
        return out

    info, flags = row_layout(
        take(group_sizes, owner),
        take(prefix_lens, owner),
        take(solution_lens, owner),
        take(padding_counts, owner),
        blocks * size,
        size,
    )
    order = jnp.arange(blocks, dtype=jnp.int32)
    phys = (((order % parts) ^ part) * rows + ((order // parts) ^ owner)).astype(jnp.int32)

    def my_columns(start):
        return lax.dynamic_slice_in_dim(w_qkv, start * model + part * width, width, 1)

    w_mine = jnp.concatenate([my_columns(0), my_columns(1), my_columns(2)], axis=1)
    bias_q = lax.dynamic_slice_in_dim(query_bias, part * width, width, 0).astype(F32)
    bias_v = lax.dynamic_slice_in_dim(value_bias, part * width, width, 0).astype(F32)
    w_out_parts = [take(w_out.reshape(parts, width, model), part ^ s) for s in range(parts)]

    mine = bring(tokens)
    row = jnp.concatenate([mine] + [swap(mine, "pos", s) for s in range(1, parts)], axis=0)
    act_one = layer_norm(
        row.reshape(-1, model).astype(F32), attn_gain.astype(F32), attn_shift.astype(F32)
    ).astype(BF16)
    projected = matmul(act_one, w_mine)
    query = ((projected[:, :width] + bias_q).astype(BF16) * 0.125).astype(BF16)
    key = projected[:, width : 2 * width].astype(BF16)
    value = (projected[:, 2 * width :] + bias_v).astype(BF16)

    def blocked(values):
        return values.reshape(blocks, size, width)

    def turned(values):
        return blocked(values).transpose(0, 2, 1)

    query_t, key_t = turned(query), turned(key)
    mixed_all, out_t, lse = attention_forward(
        phys, flags, query_t, blocked(key), turned(value), info, heads
    )
    own_cotangent = bring(cotangent).reshape(-1, model)
    mixed_parts = []
    for s in range(parts):
        piece = mixed_all[s * rows : (s + 1) * rows]
        mixed_parts.append((swap(piece, "pos", s) if s else piece).reshape(-1, width))

    inputs = mine.reshape(-1, model).astype(F32)
    attn = sum(matmul(m, w) for m, w in zip(mixed_parts, w_out_parts))
    resid = inputs + (attn + out_bias.astype(F32))
    normed_two, norm_two_pull = jax.vjp(
        layer_norm, resid, ffn_gain.astype(F32), ffn_shift.astype(F32)
    )
    act_two = normed_two.astype(BF16)
    upper = matmul(act_two, w_up) + up_bias.astype(F32)
    hidden_full, gelu_pull = jax.vjp(gelu_tanh, upper)
    hidden = hidden_full.astype(BF16)
    layer_out = (resid + (matmul(hidden, w_down) + down_bias.astype(F32))).astype(BF16)
    grad_out = own_cotangent.astype(F32)
    grad_w_down = matmul(hidden, own_cotangent, TN).astype(BF16)
    grad_down_bias = jnp.sum(grad_out, axis=0)
    (grad_upper_full,) = gelu_pull(matmul(own_cotangent, w_down, NT))
    grad_upper = grad_upper_full.astype(BF16)
    grad_w_up = matmul(act_two, grad_upper, TN).astype(BF16)
    grad_up_bias = jnp.sum(grad_upper.astype(F32), axis=0)
    grad_resid_norm, grad_ffn_gain, grad_ffn_shift = norm_two_pull(matmul(grad_upper, w_up, NT))
    grad_resid = grad_out + grad_resid_norm
    grad_attn = grad_resid.astype(BF16)
    stacked = jnp.stack(mixed_parts)
    mixed = jnp.concatenate([take(stacked, g ^ part) for g in range(parts)], axis=1)
    grad_w_out = matmul(mixed, grad_attn, TN).astype(BF16)
    grad_out_bias = jnp.sum(grad_attn.astype(F32), axis=0)
    grad_mixed = [matmul(grad_attn, w, NT).astype(BF16) for w in w_out_parts]
    grad_all = jnp.concatenate(
        [swap(g, "pos", s) if s else g for s, g in enumerate(grad_mixed)], axis=0
    )
    grad_q, grad_k, grad_v = attention_backward(
        phys, flags, query_t, turned(grad_all), out_t, lse, info,
        blocked(key), key_t, blocked(value), heads,
    )
    grad_project = jnp.concatenate([grad_q, grad_k, grad_v], axis=2).reshape(-1, 3 * width)
    grad_w_mine = matmul(act_one, grad_project, TN).astype(BF16)
    grad_query_mine = jnp.sum(grad_q.astype(F32), axis=(0, 1))
    grad_value_mine = jnp.sum(grad_v.astype(F32), axis=(0, 1))
    grad_act = matmul(grad_project, w_mine, NT)
    local = rows * size
    grad_act_own = grad_act[:local]
    for s in range(1, parts):
        sent = grad_act[s * local : (s + 1) * local].astype(BF16)
        grad_act_own = grad_act_own + swap(sent, "pos", s).astype(F32)
    _, norm_one_pull = jax.vjp(layer_norm, inputs, attn_gain.astype(F32), attn_shift.astype(F32))
    grad_input_norm, grad_attn_gain, grad_attn_shift = norm_one_pull(grad_act_own)
    tokens_grad = (grad_resid + grad_input_norm).astype(BF16)

    row_place = lax.axis_index(row_axis)
    row_steps = [(row_axis, m, (row_place // m) % 2) for m in bits(lax.axis_size(row_axis))]
    own_steps = [("pos", m * parts, (owner // m) % 2) for m in bits(rows)]
    part_steps = [("pos", m, (part // m) % 2) for m in bits(parts)]
    one_way = part_steps + own_steps + row_steps
    other_way = part_steps + own_steps[::-1] + row_steps

    def total(values, steps):
        return double(halve(values, steps), steps).astype(F32)

    sum_w_down = total(grad_w_down, one_way)
    sum_w_up = total(grad_w_up, other_way)
    sum_w_out = total(grad_w_out, one_way)
    steps = other_way[len(part_steps) :]
    summed_mine = double(halve(grad_w_mine, steps), steps)
    pieces = [summed_mine] + [swap(summed_mine, "pos", s) for s in range(1, parts)]
    pieces = jnp.stack(pieces).reshape(parts, model, 3, width)
    pieces = [take(pieces, g ^ part) for g in range(parts)]
    sum_w_qkv = jnp.stack(pieces, axis=2).reshape(model, 3 * model).astype(F32)

    def placed(values):
        return lax.dynamic_update_slice_in_dim(jnp.zeros((model,), F32), values, part * width, 0)

    small = jnp.concatenate(
        [
            grad_attn_gain,
            grad_attn_shift,
            placed(grad_query_mine),
            placed(grad_value_mine),
            grad_out_bias,
            grad_ffn_gain,
            grad_ffn_shift,
            grad_down_bias,
            grad_up_bias,
        ]
    )
    for axis, mask, _ in one_way:
        small = small + swap(small, axis, mask)
    vectors = small[: 8 * model].reshape(8, model)
    return (
        give_back(layer_out.reshape(rows, size, model)),
        give_back(tokens_grad.reshape(rows, size, model)),
        vectors[0],
        vectors[1],
        sum_w_qkv,
        vectors[2],
        vectors[3],
        sum_w_out,
        vectors[4],
        vectors[5],
        vectors[6],
        sum_w_up,
        small[8 * model :],
        sum_w_down,
        vectors[7],
    )


def solution(mesh):
    in_specs = (
        P("rows", "pos", None),
        P("rows", "pos"),
        P("rows", None),
        P("rows", None),
        P("rows", None, None),
        P("rows"),
        *([P()] * 13),
        P("rows", "pos", None),
    )
    out_specs = (P("rows", "pos", None), P("rows", "pos", None), *([P()] * 13))
    return jax.shard_map(
        functools.partial(per_device, "rows"),
        mesh=mesh,
        in_specs=in_specs,
        out_specs=out_specs,
        check_vma=False,
    )
```

```python
import functools

import jax
import jax.numpy as jnp
from jax import lax
from jax.experimental import pallas as pl
from jax.experimental.pallas import tpu as pltpu
from jax.sharding import PartitionSpec as P

HEAD_DIM = 64
EPS = 1e-05
NEG = -1e30
GELU_C = 0.7978845608028654
F32 = jnp.float32
BF16 = jnp.bfloat16
VMEM_LIMIT = 60 * 1024 * 1024
NT = (((1,), (1,)), ((), ()))
TN = (((0,), (0,)), ((), ()))


def layer_norm(values, gain, shift):
    center = values - jnp.mean(values, axis=-1, keepdims=True)
    spread = jnp.mean(center * center, axis=-1, keepdims=True)
    return center * lax.rsqrt(spread + EPS) * gain + shift


def gelu_tanh(values):
    return 0.5 * values * (1.0 + jnp.tanh(GELU_C * (values + 0.044715 * values * values * values)))


def matmul(left, right, dims=(((1,), (0,)), ((), ()))):
    return lax.dot_general(left, right, dims, preferred_element_type=F32)


def head_pairs(heads):
    return [(h // 2, min(128, heads * HEAD_DIM - (h // 2) * 128)) for h in range(heads)]


def mask_bias(info_ref, key_start, size):
    prefix_start, prefix_end = info_ref[0, 0:1, :], info_ref[0, 1:2, :]
    own_start, query_place = info_ref[0, 2:3, :], info_ref[0, 3:4, :]
    key_place = key_start + lax.broadcasted_iota(jnp.int32, (size, size), 0)
    allowed = ((key_place >= prefix_start) & (key_place < prefix_end)) | (
        (key_place >= own_start) & (key_place <= query_place)
    )
    return jnp.where(allowed, 0.0, NEG).astype(F32)


def fill_padded(source_ref, target_ref, heads):
    for h, (pair, width) in enumerate(head_pairs(heads)):
        rows = source_ref[0, pair * 128 : pair * 128 + width, :]
        if width == 128:
            keep = (lax.broadcasted_iota(jnp.int32, rows.shape, 0) // HEAD_DIM) == (h % 2)
            rows = jnp.where(keep, rows, jnp.zeros_like(rows))
        target_ref[h, 0:width, :] = rows


def forward_kernel(
    heads, blocks, phys_ref, flag_ref, query_t_ref, key_ref, value_t_ref, info_ref,
    mixed_ref, out_t_ref, lse_ref, bias_sc, top_sc, total_sc, acc_sc, query_sc,
):
    size = query_t_ref.shape[2]
    i = pl.program_id(0)
    fill_padded(query_t_ref, query_sc, heads)
    top_sc[...] = jnp.full_like(top_sc, NEG)
    total_sc[...] = jnp.zeros_like(total_sc)
    acc_sc[...] = jnp.zeros_like(acc_sc)

    @pl.loop(0, i + 1)
    def _(j):
        @pl.when(flag_ref[i * blocks + j] > 0)
        def _():
            at = phys_ref[j]
            bias_sc[...] = mask_bias(info_ref, j * size, size)
            for h, (pair, width) in enumerate(head_pairs(heads)):
                rows = slice(h * HEAD_DIM, (h + 1) * HEAD_DIM)
                scores = (
                    matmul(key_ref[at, :, pair * 128 : pair * 128 + width], query_sc[h, 0:width, :])
                    + bias_sc[...]
                )
                old = top_sc[h]
                top = jnp.maximum(old, jnp.max(scores, axis=0, keepdims=True))
                shrink = jnp.exp(old - top)
                weights = jnp.exp(scores - top)
                total_sc[h] = shrink * total_sc[h] + jnp.sum(weights, axis=0, keepdims=True)
                top_sc[h] = top
                acc_sc[rows, :] = shrink * acc_sc[rows, :] + matmul(
                    value_t_ref[at, rows, :], weights.astype(BF16)
                )

    for h in range(heads):
        rows = slice(h * HEAD_DIM, (h + 1) * HEAD_DIM)
        out_t_ref[0, rows, :] = acc_sc[rows, :] / total_sc[h]
        lse_ref[0, h : h + 1, :] = top_sc[h] + jnp.log(total_sc[h])
    mixed_ref[0] = out_t_ref[0].T.astype(BF16)


def attention_forward(phys, flags, query_t, key, value_t, info, heads):
    blocks, width, size = query_t.shape
    lse_rows = -(-heads // 8) * 8
    whole = pl.Buffered(1)
    spec = pltpu.PrefetchScalarGridSpec(
        num_scalar_prefetch=2,
        grid=(blocks,),
        in_specs=[
            pl.BlockSpec((1, width, size), lambda i, p, f: (p[i], 0, 0)),
            pl.BlockSpec((blocks, size, width), lambda i, p, f: (0, 0, 0), pipeline_mode=whole),
            pl.BlockSpec((blocks, width, size), lambda i, p, f: (0, 0, 0), pipeline_mode=whole),
            pl.BlockSpec((1, 8, size), lambda i, p, f: (i, 0, 0)),
        ],
        out_specs=[
            pl.BlockSpec((1, size, width), lambda i, p, f: (p[i], 0, 0)),
            pl.BlockSpec((1, width, size), lambda i, p, f: (p[i], 0, 0)),
            pl.BlockSpec((1, lse_rows, size), lambda i, p, f: (p[i], 0, 0)),
        ],
        scratch_shapes=[
            pltpu.VMEM((size, size), F32),
            pltpu.VMEM((heads, 1, size), F32),
            pltpu.VMEM((heads, 1, size), F32),
            pltpu.VMEM((width, size), F32),
            pltpu.VMEM((heads, 128, size), BF16),
        ],
    )
    pairs = heads * blocks * (blocks + 1) // 2 * size * size
    return pl.pallas_call(
        functools.partial(forward_kernel, heads, blocks),
        grid_spec=spec,
        out_shape=(
            jax.ShapeDtypeStruct((blocks, size, width), BF16),
            jax.ShapeDtypeStruct((blocks, width, size), F32),
            jax.ShapeDtypeStruct((blocks, lse_rows, size), F32),
        ),
        compiler_params=pltpu.CompilerParams(
            dimension_semantics=("arbitrary",), vmem_limit_bytes=VMEM_LIMIT
        ),
        cost_estimate=pl.CostEstimate(
            flops=pairs * 4 * 128, transcendentals=pairs, bytes_accessed=blocks * size * width * 16
        ),
        name="attention_forward",
    )(phys, flags, query_t, key, value_t, info)


def backward_kernel(
    heads, first, blocks, phys_ref, flag_ref, query_t_ref, grad_t_ref, out_t_ref, lse_ref, info_ref,
    key_ref, key_t_ref, value_ref, grads_ref,
    bias_sc, query_grad_sc, key_grad_sc, value_grad_sc, query_sc, grad_sc, delta_sc,
):
    size = query_t_ref.shape[2]
    span = heads * HEAD_DIM
    i = pl.program_id(0)

    @pl.when(i == 0)
    def _():
        key_grad_sc[...] = jnp.zeros_like(key_grad_sc)
        value_grad_sc[...] = jnp.zeros_like(value_grad_sc)

    fill_padded(query_t_ref, query_sc, heads)
    fill_padded(grad_t_ref, grad_sc, heads)
    query_grad_sc[...] = jnp.zeros_like(query_grad_sc)
    for h in range(heads):
        rows = slice(h * HEAD_DIM, (h + 1) * HEAD_DIM)
        delta_sc[h] = jnp.sum(
            grad_t_ref[0, rows, :].astype(F32) * out_t_ref[0, rows, :], axis=0, keepdims=True
        )

    @pl.loop(0, i + 1)
    def _(j):
        @pl.when(flag_ref[i * blocks + j] > 0)
        def _():
            at = phys_ref[j]
            bias_sc[...] = mask_bias(info_ref, j * size, size)
            for h, (pair, width) in enumerate(head_pairs(heads)):
                rows = slice(h * HEAD_DIM, (h + 1) * HEAD_DIM)
                lanes = slice(pair * 128, pair * 128 + width)
                scores = matmul(key_ref[at, :, lanes], query_sc[h, 0:width, :]) + bias_sc[...]
                probs = jnp.exp(scores - lse_ref[0, first + h : first + h + 1, :])
                grad_probs = matmul(value_ref[at, :, lanes], grad_sc[h, 0:width, :])
                grad_scores = (probs * (grad_probs - delta_sc[h])).astype(BF16)
                query_grad_sc[rows, :] += matmul(key_t_ref[at, rows, :], grad_scores)
                value_grad_sc[at, rows, :] += matmul(
                    grad_t_ref[0, rows, :], probs.astype(BF16), NT
                )
                key_grad_sc[at, rows, :] += matmul(query_t_ref[0, rows, :], grad_scores, NT)

    grads_ref[phys_ref[i], :, 0:span] = (query_grad_sc[...] * 0.125).T.astype(BF16)

    @pl.when(i == blocks - 1)
    def _():
        for block in range(blocks):
            grads_ref[block, :, span : 2 * span] = key_grad_sc[block].T.astype(BF16)
            grads_ref[block, :, 2 * span :] = value_grad_sc[block].T.astype(BF16)


def attention_backward(
    phys, flags, query_t, grad_t, out_t, lse, info, key, key_t, value, heads, first
):
    blocks, _, size = query_t.shape
    span = heads * HEAD_DIM
    c = first // heads
    moving_t = pl.BlockSpec((1, span, size), lambda i, p, f: (p[i], c, 0))
    whole = pl.BlockSpec(
        (blocks, size, span), lambda i, p, f: (0, 0, c), pipeline_mode=pl.Buffered(1)
    )
    whole_t = pl.BlockSpec(
        (blocks, span, size), lambda i, p, f: (0, c, 0), pipeline_mode=pl.Buffered(1)
    )
    spec = pltpu.PrefetchScalarGridSpec(
        num_scalar_prefetch=2,
        grid=(blocks,),
        in_specs=[
            moving_t,
            moving_t,
            moving_t,
            pl.BlockSpec((1, lse.shape[1], size), lambda i, p, f: (p[i], 0, 0)),
            pl.BlockSpec((1, 8, size), lambda i, p, f: (i, 0, 0)),
            whole,
            whole_t,
            whole,
        ],
        out_specs=pl.BlockSpec(
            (blocks, size, 3 * span), lambda i, p, f: (0, 0, 0), pipeline_mode=pl.Buffered(1)
        ),
        scratch_shapes=[
            pltpu.VMEM((size, size), F32),
            pltpu.VMEM((span, size), F32),
            pltpu.VMEM((blocks, span, size), F32),
            pltpu.VMEM((blocks, span, size), F32),
            pltpu.VMEM((heads, 128, size), BF16),
            pltpu.VMEM((heads, 128, size), BF16),
            pltpu.VMEM((heads, 1, size), F32),
        ],
    )
    pairs = heads * blocks * (blocks + 1) // 2 * size * size
    return pl.pallas_call(
        functools.partial(backward_kernel, heads, first, blocks),
        grid_spec=spec,
        out_shape=jax.ShapeDtypeStruct((blocks, size, 3 * span), BF16),
        compiler_params=pltpu.CompilerParams(
            dimension_semantics=("arbitrary",), vmem_limit_bytes=VMEM_LIMIT
        ),
        cost_estimate=pl.CostEstimate(
            flops=pairs * 10 * 128, transcendentals=pairs, bytes_accessed=blocks * size * span * 20
        ),
        name="attention_backward",
    )(phys, flags, query_t, grad_t, out_t, lse, info, key, key_t, value)


def project_kernel(
    width, x_ref, gain_ref, shift_ref, w_ref, bias_q_ref, bias_v_ref,
    act_ref, query_t_ref, key_ref, key_t_ref, value_ref, value_t_ref,
):
    act = layer_norm(x_ref[0].astype(F32), gain_ref[...], shift_ref[...]).astype(BF16)
    act_ref[0] = act
    query = (matmul(act, w_ref[:, :width]) + bias_q_ref[...]).astype(BF16).astype(F32) * 0.125
    query_t_ref[0] = query.T.astype(BF16)
    key = matmul(act, w_ref[:, width : 2 * width])
    key_ref[0] = key.astype(BF16)
    key_t_ref[0] = key.T.astype(BF16)
    value = matmul(act, w_ref[:, 2 * width :]) + bias_v_ref[...]
    value_ref[0] = value.astype(BF16)
    value_t_ref[0] = value.T.astype(BF16)


def project(x, gain, shift, weight, bias_q, bias_v):
    blocks, size, model = x.shape
    width = bias_q.shape[1]
    still = lambda i: (0, 0)
    step = lambda i: (i, 0, 0)
    straight, turned = (
        jax.ShapeDtypeStruct((blocks, size, width), BF16),
        jax.ShapeDtypeStruct((blocks, width, size), BF16),
    )
    wide, tall = pl.BlockSpec((1, size, width), step), pl.BlockSpec((1, width, size), step)
    return pl.pallas_call(
        functools.partial(project_kernel, width),
        grid=(blocks,),
        in_specs=[
            pl.BlockSpec((1, size, model), step),
            pl.BlockSpec((1, model), still),
            pl.BlockSpec((1, model), still),
            pl.BlockSpec(weight.shape, still, pipeline_mode=pl.Buffered(1)),
            pl.BlockSpec((1, width), still),
            pl.BlockSpec((1, width), still),
        ],
        out_specs=[pl.BlockSpec((1, size, model), step), tall, wide, tall, wide, tall],
        out_shape=(
            jax.ShapeDtypeStruct((blocks, size, model), BF16),
            turned, straight, turned, straight, turned,
        ),
        compiler_params=pltpu.CompilerParams(
            dimension_semantics=("arbitrary",), vmem_limit_bytes=VMEM_LIMIT
        ),
        cost_estimate=pl.CostEstimate(
            flops=2 * blocks * size * model * 3 * width,
            transcendentals=blocks * size,
            bytes_accessed=blocks * size * (4 * model + 10 * width),
        ),
        name="project",
    )(x, gain, shift, weight, bias_q, bias_v)


def feed_kernel(
    parts, pieces, *refs
):
    mixed_refs, refs = refs[:parts], refs[parts:]
    x_ref, cot_ref, refs = refs[0], refs[1], refs[2:]
    w_out_refs, refs = refs[:parts], refs[parts:]
    (w_up_ref, w_down_ref, out_bias_ref, gain_ref, shift_ref, up_bias_ref, down_bias_ref), refs = (
        refs[:7], refs[7:],
    )
    act_ref, hidden_ref, grad_upper_ref, layer_ref, grad_resid_ref, grad_attn_ref = refs[:6]
    refs = refs[6:]
    grad_mixed_refs, refs = refs[:parts], refs[parts:]
    sums_ref, up_sum_ref, cot_sc, layer_sc, back_sc = refs
    first = pl.program_id(0) == 0

    @pl.when(first)
    def _():
        sums_ref[...] = jnp.zeros_like(sums_ref)
        up_sum_ref[...] = jnp.zeros_like(up_sum_ref)

    attn = out_bias_ref[...]
    for mixed_ref, w_ref in zip(mixed_refs, w_out_refs):
        attn = attn + matmul(mixed_ref[0], w_ref[...])
    resid = x_ref[0].astype(F32) + attn
    center = resid - jnp.mean(resid, axis=-1, keepdims=True)
    root = lax.rsqrt(jnp.mean(center * center, axis=-1, keepdims=True) + EPS)
    normed = center * root
    gain = gain_ref[...]
    act_ref[0] = (normed * gain + shift_ref[...]).astype(BF16)
    layer_sc[...] = resid + down_bias_ref[...]
    back_sc[...] = jnp.zeros_like(back_sc)
    span = w_up_ref.shape[1] // pieces

    for c in range(pieces):
        lanes = slice(c * span, (c + 1) * span)
        upper = matmul(act_ref[0], w_up_ref[:, lanes]) + up_bias_ref[:, lanes]
        square = upper * upper
        bend = jnp.tanh(GELU_C * upper * (1.0 + 0.044715 * square))
        half = 0.5 * (1.0 + bend)
        hidden = (upper * half).astype(BF16)
        hidden_ref[0, :, lanes] = hidden
        slope = half + 0.5 * GELU_C * upper * (1.0 - bend * bend) * (1.0 + 0.134145 * square)
        grad_upper = (matmul(cot_ref[0], w_down_ref[lanes, :], NT) * slope).astype(BF16)
        grad_upper_ref[0, :, lanes] = grad_upper
        up_sum_ref[0:1, lanes] += jnp.sum(grad_upper.astype(F32), axis=0, keepdims=True)
        layer_sc[...] += matmul(hidden, w_down_ref[lanes, :])
        back_sc[...] += matmul(grad_upper, w_up_ref[:, lanes], NT)

    layer_ref[0] = layer_sc[...].astype(BF16)
    back = back_sc[...]
    scaled = back * gain
    grad_out = cot_ref[0].astype(F32)
    grad_resid = grad_out + root * (
        scaled
        - jnp.mean(scaled, axis=-1, keepdims=True)
        - normed * jnp.mean(scaled * normed, axis=-1, keepdims=True)
    )
    grad_resid_ref[0] = grad_resid
    grad_attn = grad_resid.astype(BF16)
    grad_attn_ref[0] = grad_attn
    for w_ref, grad_mixed_ref in zip(w_out_refs, grad_mixed_refs):
        grad_mixed_ref[0] = matmul(grad_attn, w_ref[...], NT).astype(BF16)
    sums_ref[0:1, :] += jnp.sum(grad_attn.astype(F32), axis=0, keepdims=True)
    sums_ref[1:2, :] += jnp.sum(back * normed, axis=0, keepdims=True)
    sums_ref[2:3, :] += jnp.sum(back, axis=0, keepdims=True)
    sums_ref[3:4, :] += jnp.sum(grad_out, axis=0, keepdims=True)


def feed(mixed, x, cotangent, w_out, part, w_up, w_down, vectors, up_bias):
    parts = len(mixed)
    rows, size, model = x.shape
    width = mixed[0].shape[2]
    wide = w_up.shape[1]
    still = lambda i, p: (0, 0)
    step = lambda i, p: (i, 0, 0)
    once = pl.Buffered(1)
    slab = pl.BlockSpec((1, size, model), step)
    head_slab = pl.BlockSpec((1, size, width), step)
    wide_slab = pl.BlockSpec((1, size, wide), step)
    vector = pl.BlockSpec((1, model), still)
    w_out_specs = [
        pl.BlockSpec((width, model), lambda i, p, s=s: (p[0] ^ s, 0), pipeline_mode=once)
        for s in range(parts)
    ]

    def body(p_ref, *refs):
        feed_kernel(parts, wide // model, *refs)

    shape = jax.ShapeDtypeStruct
    out = pl.pallas_call(
        body,
        grid_spec=pltpu.PrefetchScalarGridSpec(
            num_scalar_prefetch=1,
            grid=(rows,),
            in_specs=[head_slab] * parts
            + [slab, slab]
            + w_out_specs
            + [
                pl.BlockSpec(w_up.shape, still, pipeline_mode=once),
                pl.BlockSpec(w_down.shape, still, pipeline_mode=once),
                vector,
                vector,
                vector,
                pl.BlockSpec((1, wide), still),
                vector,
            ],
            out_specs=[slab, wide_slab, wide_slab, slab, slab, slab]
            + [head_slab] * parts
            + [pl.BlockSpec((8, model), still), pl.BlockSpec((8, wide), still)],
            scratch_shapes=[
                pltpu.VMEM((8, 128), F32),
                pltpu.VMEM((size, model), F32),
                pltpu.VMEM((size, model), F32),
            ],
        ),
        out_shape=[
            shape((rows, size, model), BF16),
            shape((rows, size, wide), BF16),
            shape((rows, size, wide), BF16),
            shape((rows, size, model), BF16),
            shape((rows, size, model), F32),
            shape((rows, size, model), BF16),
        ]
        + [shape((rows, size, width), BF16)] * parts
        + [shape((8, model), F32), shape((8, wide), F32)],
        compiler_params=pltpu.CompilerParams(
            dimension_semantics=("arbitrary",), vmem_limit_bytes=VMEM_LIMIT
        ),
        cost_estimate=pl.CostEstimate(
            flops=2 * rows * size * model * (4 * wide + 2 * model),
            transcendentals=rows * size * wide,
            bytes_accessed=rows * size * (4 * wide + 16 * model),
        ),
        name="feed",
    )(
        part.reshape(1), *mixed, x, cotangent, *([w_out] * parts), w_up, w_down,
        vectors["out_bias"], vectors["gain"], vectors["shift"], up_bias, vectors["down_bias"],
    )
    return out[:6], out[6 : 6 + parts], out[6 + parts], out[7 + parts]


def row_layout(sizes, prefixes, lens, padding, length, size):
    slots = jnp.arange(lens.shape[-1], dtype=jnp.int32)
    kept = jnp.where(slots[None, :] < sizes[:, None], lens, 0)
    ends = jnp.cumsum(kept, axis=-1)
    totals = prefixes + ends[:, -1]
    starts = jnp.cumsum(totals) - totals
    places = jnp.arange(length, dtype=jnp.int32)
    padded = places >= length - padding
    prefix_start = jnp.broadcast_to(length - padding, (length,))
    prefix_end = prefix_start
    own_start = prefix_start
    for g in range(sizes.shape[0]):
        member = (places >= starts[g]) & (places < starts[g] + totals[g]) & ~padded
        body = starts[g] + prefixes[g]
        inside = places - body
        base = jnp.max(jnp.where(inside[:, None] >= ends[g][None, :], ends[g][None, :], 0), axis=-1)
        solution = inside >= 0
        prefix_start = jnp.where(member, starts[g], prefix_start)
        prefix_end = jnp.where(member, jnp.where(solution, body, starts[g]), prefix_end)
        own_start = jnp.where(member, jnp.where(solution, body + base, starts[g]), own_start)
    blocks = length // size
    low = jnp.arange(blocks, dtype=jnp.int32)[None, :] * size
    high = low + size
    need = (
        jnp.maximum(prefix_start[:, None], low) < jnp.minimum(prefix_end[:, None], high)
    ) | (jnp.maximum(own_start[:, None], low) < jnp.minimum(places[:, None] + 1, high))
    flags = jnp.any(need.reshape(blocks, size, blocks), axis=1).astype(jnp.int32).reshape(-1)
    zero = jnp.zeros_like(places)
    info = jnp.stack([prefix_start, prefix_end, own_start, places, zero, zero, zero, zero])
    info = info.astype(jnp.int32).reshape(8, blocks, size).transpose(1, 0, 2)
    return info, flags


def swap(values, axis, mask):
    count = lax.axis_size(axis)
    return lax.ppermute(values, axis, [(i, i ^ mask) for i in range(count)])


def bits(count):
    return [1 << b for b in range(count.bit_length() - 1)]


def take(values, index):
    return lax.dynamic_index_in_dim(values, index, 0, keepdims=False)


def halve(values, steps):
    for axis, mask, bit in steps:
        two = values.reshape(2, values.shape[0] // 2, *values.shape[1:])
        arrived = swap(take(two, 1 - bit), axis, mask)
        values = (take(two, bit).astype(F32) + arrived.astype(F32)).astype(values.dtype)
    return values


def double(values, steps):
    for axis, mask, bit in reversed(steps):
        arrived = swap(values, axis, mask)
        first = jnp.where(bit == 0, values, arrived)
        second = jnp.where(bit == 0, arrived, values)
        values = jnp.concatenate([first, second], axis=0)
    return values


def per_device(
    row_axis,
    tokens,
    segment_ids,
    group_sizes,
    prefix_lens,
    solution_lens,
    padding_counts,
    attn_gain,
    attn_shift,
    w_qkv,
    query_bias,
    value_bias,
    w_out,
    out_bias,
    ffn_gain,
    ffn_shift,
    w_up,
    up_bias,
    w_down,
    down_bias,
    cotangent,
):
    rows, size, model = tokens.shape
    devices = lax.axis_size("pos")
    parts = devices // rows
    blocks = devices
    heads = model // HEAD_DIM // parts
    width = heads * HEAD_DIM
    place = lax.axis_index("pos")
    owner, part = place // parts, place % parts

    def bring(values):
        return jnp.stack(
            [
                swap(take(values, owner ^ m), "pos", m * parts) if m else take(values, owner)
                for m in range(rows)
            ]
        )

    def give_back(values):
        out = jnp.zeros_like(values)
        for m in range(rows):
            slab = swap(values[m], "pos", m * parts) if m else values[m]
            out = lax.dynamic_update_index_in_dim(out, slab, owner ^ m, 0)
        return out

    info, flags = row_layout(
        take(group_sizes, owner),
        take(prefix_lens, owner),
        take(solution_lens, owner),
        take(padding_counts, owner),
        blocks * size,
        size,
    )
    order = jnp.arange(blocks, dtype=jnp.int32)
    phys = (((order % parts) ^ part) * rows + ((order // parts) ^ owner)).astype(jnp.int32)

    def my_columns(start, first=0, count=None):
        begin = start * model + part * width + first
        return lax.dynamic_slice_in_dim(w_qkv, begin, count or width, 1)

    def as_row(vector):
        return vector.astype(F32).reshape(1, -1)

    group = 2 if heads % 2 == 0 else heads
    starts = list(range(0, heads, group))
    span = group * HEAD_DIM
    w_mine = jnp.concatenate([my_columns(n) for n in range(3)], axis=1)
    w_groups = [
        jnp.concatenate([my_columns(n, h * HEAD_DIM, span) for n in range(3)], axis=1)
        for h in starts
    ]
    bias_q = lax.dynamic_slice_in_dim(query_bias, part * width, width, 0)
    bias_v = lax.dynamic_slice_in_dim(value_bias, part * width, width, 0)

    mine = bring(tokens)
    row = jnp.concatenate([mine] + [swap(mine, "pos", s) for s in range(1, parts)], axis=0)
    cotangent, row = lax.optimization_barrier((cotangent, row))
    own_cotangent = bring(cotangent)
    act_one, query_t, key, key_t, value, value_t = project(
        row, as_row(attn_gain), as_row(attn_shift), w_mine, as_row(bias_q), as_row(bias_v)
    )
    mixed_all, out_t, lse = attention_forward(
        phys, flags, query_t, key, value_t, info, heads
    )
    mixed_parts = []
    for s in range(parts):
        piece = mixed_all[s * rows : (s + 1) * rows]
        mixed_parts.append(swap(piece, "pos", s) if s else piece)

    (act_two, hidden, grad_upper, layer_out, grad_resid, grad_attn), grad_mixed, sums, up_sum = feed(
        mixed_parts, mine, own_cotangent, w_out, part, w_up, w_down,
        {
            "out_bias": as_row(out_bias),
            "gain": as_row(ffn_gain),
            "shift": as_row(ffn_shift),
            "down_bias": as_row(down_bias),
        },
        as_row(up_bias),
    )
    grad_all = jnp.concatenate(
        [swap(g, "pos", s) if s else g for s, g in enumerate(grad_mixed)], axis=0
    )
    grad_t = grad_all.transpose(0, 2, 1)
    layer_home = give_back(layer_out)

    local = rows * size

    def flat(values):
        return values.reshape(-1, values.shape[-1])

    row_place = lax.axis_index(row_axis)
    row_steps = [(row_axis, m, (row_place // m) % 2) for m in bits(lax.axis_size(row_axis))]
    own_steps = [("pos", m * parts, (owner // m) % 2) for m in bits(rows)]
    part_steps = [("pos", m, (part // m) % 2) for m in bits(parts)]
    one_way = part_steps + own_steps + row_steps
    other_way = part_steps + own_steps[::-1] + row_steps

    grad_w_down = matmul(flat(hidden), flat(own_cotangent), TN).astype(BF16)
    share_down = halve(grad_w_down, one_way)
    stacked = jnp.stack(mixed_parts)
    mixed = jnp.concatenate([flat(take(stacked, g ^ part)) for g in range(parts)], axis=1)
    grad_w_up = jnp.concatenate(
        [
            matmul(flat(act_two), flat(grad_upper), TN).astype(BF16),
            matmul(mixed, flat(grad_attn), TN).astype(BF16),
        ],
        axis=1,
    )
    share_up = halve(grad_w_up, other_way)

    grads = [
        attention_backward(
            phys, flags, query_t, grad_t, out_t, lse, info, key, key_t, value, group, h
        )
        for h in starts
    ]
    sum_w_down = double(share_down, one_way).astype(F32)
    sum_up = double(share_up, other_way)
    sum_w_up, sum_w_out = sum_up[:, : w_up.shape[1]].astype(F32), sum_up[:, w_up.shape[1] :].astype(F32)

    grad_act = sum(matmul(flat(g), w, NT) for g, w in zip(grads, w_groups))
    grad_act_own = grad_act[:local]
    for s in range(1, parts):
        sent = grad_act[s * local : (s + 1) * local].astype(BF16)
        grad_act_own = grad_act_own + swap(sent, "pos", s).astype(F32)
    inputs = flat(mine).astype(F32)
    _, norm_one_pull = jax.vjp(layer_norm, inputs, attn_gain.astype(F32), attn_shift.astype(F32))
    grad_input_norm, grad_attn_gain, grad_attn_shift = norm_one_pull(grad_act_own)
    tokens_grad = (flat(grad_resid) + grad_input_norm).astype(BF16).reshape(rows, size, model)

    steps = other_way[len(part_steps) :]
    summed = []
    for batch in (grads[:-1], grads[-1:]):
        if batch:
            share = jnp.concatenate([matmul(flat(act_one), flat(g), TN).astype(BF16) for g in batch], axis=1)
            summed.append(double(halve(share, steps), steps))
    summed_mine = jnp.concatenate(summed, axis=1)
    pieces = [summed_mine] + [swap(summed_mine, "pos", s) for s in range(1, parts)]
    pieces = jnp.stack(pieces).reshape(parts, model, len(starts), 3, span)
    pieces = jnp.stack([take(pieces, g ^ part) for g in range(parts)], axis=3)
    sum_w_qkv = pieces.transpose(0, 2, 3, 1, 4).reshape(model, 3 * model).astype(F32)

    grad_query_mine = jnp.concatenate([jnp.sum(flat(g)[:, :span].astype(F32), axis=0) for g in grads])
    grad_value_mine = jnp.concatenate([jnp.sum(flat(g)[:, 2 * span :].astype(F32), axis=0) for g in grads])

    def placed(values):
        return lax.dynamic_update_slice_in_dim(jnp.zeros((model,), F32), values, part * width, 0)

    small = jnp.concatenate(
        [
            grad_attn_gain,
            grad_attn_shift,
            placed(grad_query_mine),
            placed(grad_value_mine),
            sums[:4].reshape(-1),
            up_sum[0],
        ]
    )
    for axis, mask, _ in one_way:
        small = small + swap(small, axis, mask)
    vectors = small[: 8 * model].reshape(8, model)
    return (
        layer_home,
        give_back(tokens_grad),
        vectors[0],
        vectors[1],
        sum_w_qkv,
        vectors[2],
        vectors[3],
        sum_w_out,
        vectors[4],
        vectors[5],
        vectors[6],
        sum_w_up,
        small[8 * model :],
        sum_w_down,
        vectors[7],
    )


def solution(mesh):
    in_specs = (
        P("rows", "pos", None),
        P("rows", "pos"),
        P("rows", None),
        P("rows", None),
        P("rows", None, None),
        P("rows"),
        *([P()] * 13),
        P("rows", "pos", None),
    )
    out_specs = (P("rows", "pos", None), P("rows", "pos", None), *([P()] * 13))
    return jax.shard_map(
        functools.partial(per_device, "rows"),
        mesh=mesh,
        in_specs=in_specs,
        out_specs=out_specs,
        check_vma=False,
    )
```

```python
import functools

import jax
import jax.numpy as jnp
from jax import lax
from jax.experimental import pallas as pl
from jax.experimental.pallas import tpu as pltpu
from jax.sharding import PartitionSpec as P

HEAD_DIM = 64
EPS = 1e-05
NEG = -1e30
GELU_C = 0.7978845608028654
F32 = jnp.float32
BF16 = jnp.bfloat16
VMEM_LIMIT = 60 * 1024 * 1024
NT = (((1,), (1,)), ((), ()))
TN = (((0,), (0,)), ((), ()))


def layer_norm(values, gain, shift):
    center = values - jnp.mean(values, axis=-1, keepdims=True)
    spread = jnp.mean(center * center, axis=-1, keepdims=True)
    return center * lax.rsqrt(spread + EPS) * gain + shift


def gelu_tanh(values):
    return 0.5 * values * (1.0 + jnp.tanh(GELU_C * (values + 0.044715 * values * values * values)))


def matmul(left, right, dims=(((1,), (0,)), ((), ()))):
    return lax.dot_general(left, right, dims, preferred_element_type=F32)


def head_pairs(heads):
    return [(h // 2, min(128, heads * HEAD_DIM - (h // 2) * 128)) for h in range(heads)]


def mask_bias(info_ref, key_start, size):
    prefix_start, prefix_end = info_ref[0, 0:1, :], info_ref[0, 1:2, :]
    own_start, query_place = info_ref[0, 2:3, :], info_ref[0, 3:4, :]
    key_place = key_start + lax.broadcasted_iota(jnp.int32, (size, size), 0)
    allowed = ((key_place >= prefix_start) & (key_place < prefix_end)) | (
        (key_place >= own_start) & (key_place <= query_place)
    )
    return jnp.where(allowed, 0.0, NEG).astype(F32)


def fill_padded(source_ref, target_ref, heads):
    for h, (pair, width) in enumerate(head_pairs(heads)):
        rows = source_ref[0, pair * 128 : pair * 128 + width, :]
        if width == 128:
            keep = (lax.broadcasted_iota(jnp.int32, rows.shape, 0) // HEAD_DIM) == (h % 2)
            rows = jnp.where(keep, rows, jnp.zeros_like(rows))
        target_ref[h, 0:width, :] = rows


def forward_kernel(
    heads, blocks, phys_ref, flag_ref, query_t_ref, key_ref, value_t_ref, info_ref,
    mixed_ref, out_t_ref, lse_ref, bias_sc, top_sc, total_sc, acc_sc, query_sc,
):
    size = query_t_ref.shape[2]
    i = pl.program_id(0)
    fill_padded(query_t_ref, query_sc, heads)
    top_sc[...] = jnp.full_like(top_sc, NEG)
    total_sc[...] = jnp.zeros_like(total_sc)
    acc_sc[...] = jnp.zeros_like(acc_sc)

    @pl.loop(0, i + 1)
    def _(j):
        @pl.when(flag_ref[i * blocks + j] > 0)
        def _():
            at = phys_ref[j]
            bias_sc[...] = mask_bias(info_ref, j * size, size)
            for h, (pair, width) in enumerate(head_pairs(heads)):
                rows = slice(h * HEAD_DIM, (h + 1) * HEAD_DIM)
                scores = (
                    matmul(key_ref[at, :, pair * 128 : pair * 128 + width], query_sc[h, 0:width, :])
                    + bias_sc[...]
                )
                old = top_sc[h]
                top = jnp.maximum(old, jnp.max(scores, axis=0, keepdims=True))
                shrink = jnp.exp(old - top)
                weights = jnp.exp(scores - top)
                total_sc[h] = shrink * total_sc[h] + jnp.sum(weights, axis=0, keepdims=True)
                top_sc[h] = top
                acc_sc[rows, :] = shrink * acc_sc[rows, :] + matmul(
                    value_t_ref[at, rows, :], weights.astype(BF16)
                )

    for h in range(heads):
        rows = slice(h * HEAD_DIM, (h + 1) * HEAD_DIM)
        out_t_ref[0, rows, :] = acc_sc[rows, :] / total_sc[h]
        lse_ref[0, h : h + 1, :] = top_sc[h] + jnp.log(total_sc[h])
    mixed_ref[0] = out_t_ref[0].T.astype(BF16)


def attention_forward(phys, flags, query_t, key, value_t, info, heads):
    blocks, width, size = query_t.shape
    lse_rows = -(-heads // 8) * 8
    whole = pl.Buffered(1)
    spec = pltpu.PrefetchScalarGridSpec(
        num_scalar_prefetch=2,
        grid=(blocks,),
        in_specs=[
            pl.BlockSpec((1, width, size), lambda i, p, f: (p[i], 0, 0)),
            pl.BlockSpec((blocks, size, width), lambda i, p, f: (0, 0, 0), pipeline_mode=whole),
            pl.BlockSpec((blocks, width, size), lambda i, p, f: (0, 0, 0), pipeline_mode=whole),
            pl.BlockSpec((1, 8, size), lambda i, p, f: (i, 0, 0)),
        ],
        out_specs=[
            pl.BlockSpec((1, size, width), lambda i, p, f: (p[i], 0, 0)),
            pl.BlockSpec((1, width, size), lambda i, p, f: (p[i], 0, 0)),
            pl.BlockSpec((1, lse_rows, size), lambda i, p, f: (p[i], 0, 0)),
        ],
        scratch_shapes=[
            pltpu.VMEM((size, size), F32),
            pltpu.VMEM((heads, 1, size), F32),
            pltpu.VMEM((heads, 1, size), F32),
            pltpu.VMEM((width, size), F32),
            pltpu.VMEM((heads, 128, size), BF16),
        ],
    )
    pairs = heads * blocks * (blocks + 1) // 2 * size * size
    return pl.pallas_call(
        functools.partial(forward_kernel, heads, blocks),
        grid_spec=spec,
        out_shape=(
            jax.ShapeDtypeStruct((blocks, size, width), BF16),
            jax.ShapeDtypeStruct((blocks, width, size), F32),
            jax.ShapeDtypeStruct((blocks, lse_rows, size), F32),
        ),
        compiler_params=pltpu.CompilerParams(
            dimension_semantics=("arbitrary",), vmem_limit_bytes=VMEM_LIMIT
        ),
        cost_estimate=pl.CostEstimate(
            flops=pairs * 4 * 128, transcendentals=pairs, bytes_accessed=blocks * size * width * 16
        ),
        name="attention_forward",
    )(phys, flags, query_t, key, value_t, info)


def backward_kernel(
    heads, first, blocks, phys_ref, flag_ref, query_t_ref, grad_t_ref, out_t_ref, lse_ref, info_ref,
    key_ref, key_t_ref, value_ref, grads_ref,
    bias_sc, query_grad_sc, key_grad_sc, value_grad_sc, query_sc, grad_sc, delta_sc,
):
    size = query_t_ref.shape[2]
    span = heads * HEAD_DIM
    i = pl.program_id(0)

    @pl.when(i == 0)
    def _():
        key_grad_sc[...] = jnp.zeros_like(key_grad_sc)
        value_grad_sc[...] = jnp.zeros_like(value_grad_sc)

    fill_padded(query_t_ref, query_sc, heads)
    fill_padded(grad_t_ref, grad_sc, heads)
    query_grad_sc[...] = jnp.zeros_like(query_grad_sc)
    for h in range(heads):
        rows = slice(h * HEAD_DIM, (h + 1) * HEAD_DIM)
        delta_sc[h] = jnp.sum(
            grad_t_ref[0, rows, :].astype(F32) * out_t_ref[0, rows, :], axis=0, keepdims=True
        )

    @pl.loop(0, i + 1)
    def _(j):
        @pl.when(flag_ref[i * blocks + j] > 0)
        def _():
            at = phys_ref[j]
            bias_sc[...] = mask_bias(info_ref, j * size, size)
            for h, (pair, width) in enumerate(head_pairs(heads)):
                rows = slice(h * HEAD_DIM, (h + 1) * HEAD_DIM)
                lanes = slice(pair * 128, pair * 128 + width)
                scores = matmul(key_ref[at, :, lanes], query_sc[h, 0:width, :]) + bias_sc[...]
                probs = jnp.exp(scores - lse_ref[0, first + h : first + h + 1, :])
                grad_probs = matmul(value_ref[at, :, lanes], grad_sc[h, 0:width, :])
                grad_scores = (probs * (grad_probs - delta_sc[h])).astype(BF16)
                query_grad_sc[rows, :] += matmul(key_t_ref[at, rows, :], grad_scores)
                value_grad_sc[at, rows, :] += matmul(
                    grad_t_ref[0, rows, :], probs.astype(BF16), NT
                )
                key_grad_sc[at, rows, :] += matmul(query_t_ref[0, rows, :], grad_scores, NT)

    grads_ref[phys_ref[i], :, 0:span] = (query_grad_sc[...] * 0.125).T.astype(BF16)

    @pl.when(i == blocks - 1)
    def _():
        for block in range(blocks):
            grads_ref[block, :, span : 2 * span] = key_grad_sc[block].T.astype(BF16)
            grads_ref[block, :, 2 * span :] = value_grad_sc[block].T.astype(BF16)


def attention_backward(
    phys, flags, query_t, grad_t, out_t, lse, info, key, key_t, value, heads, first
):
    blocks, _, size = query_t.shape
    span = heads * HEAD_DIM
    c = first // heads
    moving_t = pl.BlockSpec((1, span, size), lambda i, p, f: (p[i], c, 0))
    whole = pl.BlockSpec(
        (blocks, size, span), lambda i, p, f: (0, 0, c), pipeline_mode=pl.Buffered(1)
    )
    whole_t = pl.BlockSpec(
        (blocks, span, size), lambda i, p, f: (0, c, 0), pipeline_mode=pl.Buffered(1)
    )
    spec = pltpu.PrefetchScalarGridSpec(
        num_scalar_prefetch=2,
        grid=(blocks,),
        in_specs=[
            moving_t,
            moving_t,
            moving_t,
            pl.BlockSpec((1, lse.shape[1], size), lambda i, p, f: (p[i], 0, 0)),
            pl.BlockSpec((1, 8, size), lambda i, p, f: (i, 0, 0)),
            whole,
            whole_t,
            whole,
        ],
        out_specs=pl.BlockSpec(
            (blocks, size, 3 * span), lambda i, p, f: (0, 0, 0), pipeline_mode=pl.Buffered(1)
        ),
        scratch_shapes=[
            pltpu.VMEM((size, size), F32),
            pltpu.VMEM((span, size), F32),
            pltpu.VMEM((blocks, span, size), F32),
            pltpu.VMEM((blocks, span, size), F32),
            pltpu.VMEM((heads, 128, size), BF16),
            pltpu.VMEM((heads, 128, size), BF16),
            pltpu.VMEM((heads, 1, size), F32),
        ],
    )
    pairs = heads * blocks * (blocks + 1) // 2 * size * size
    return pl.pallas_call(
        functools.partial(backward_kernel, heads, first, blocks),
        grid_spec=spec,
        out_shape=jax.ShapeDtypeStruct((blocks, size, 3 * span), BF16),
        compiler_params=pltpu.CompilerParams(
            dimension_semantics=("arbitrary",), vmem_limit_bytes=VMEM_LIMIT
        ),
        cost_estimate=pl.CostEstimate(
            flops=pairs * 10 * 128, transcendentals=pairs, bytes_accessed=blocks * size * span * 20
        ),
        name="attention_backward",
    )(phys, flags, query_t, grad_t, out_t, lse, info, key, key_t, value)


def project_kernel(
    width, x_ref, gain_ref, shift_ref, w_ref, bias_q_ref, bias_v_ref,
    act_ref, query_t_ref, key_ref, key_t_ref, value_ref, value_t_ref,
):
    act = layer_norm(x_ref[0].astype(F32), gain_ref[...], shift_ref[...]).astype(BF16)
    act_ref[0] = act
    query = (matmul(act, w_ref[:, :width]) + bias_q_ref[...]).astype(BF16).astype(F32) * 0.125
    query_t_ref[0] = query.T.astype(BF16)
    key = matmul(act, w_ref[:, width : 2 * width])
    key_ref[0] = key.astype(BF16)
    key_t_ref[0] = key.T.astype(BF16)
    value = matmul(act, w_ref[:, 2 * width :]) + bias_v_ref[...]
    value_ref[0] = value.astype(BF16)
    value_t_ref[0] = value.T.astype(BF16)


def project(x, gain, shift, weight, bias_q, bias_v):
    blocks, size, model = x.shape
    width = bias_q.shape[1]
    still = lambda i: (0, 0)
    step = lambda i: (i, 0, 0)
    straight, turned = (
        jax.ShapeDtypeStruct((blocks, size, width), BF16),
        jax.ShapeDtypeStruct((blocks, width, size), BF16),
    )
    wide, tall = pl.BlockSpec((1, size, width), step), pl.BlockSpec((1, width, size), step)
    return pl.pallas_call(
        functools.partial(project_kernel, width),
        grid=(blocks,),
        in_specs=[
            pl.BlockSpec((1, size, model), step),
            pl.BlockSpec((1, model), still),
            pl.BlockSpec((1, model), still),
            pl.BlockSpec(weight.shape, still, pipeline_mode=pl.Buffered(1)),
            pl.BlockSpec((1, width), still),
            pl.BlockSpec((1, width), still),
        ],
        out_specs=[pl.BlockSpec((1, size, model), step), tall, wide, tall, wide, tall],
        out_shape=(
            jax.ShapeDtypeStruct((blocks, size, model), BF16),
            turned, straight, turned, straight, turned,
        ),
        compiler_params=pltpu.CompilerParams(
            dimension_semantics=("arbitrary",), vmem_limit_bytes=VMEM_LIMIT
        ),
        cost_estimate=pl.CostEstimate(
            flops=2 * blocks * size * model * 3 * width,
            transcendentals=blocks * size,
            bytes_accessed=blocks * size * (4 * model + 10 * width),
        ),
        name="project",
    )(x, gain, shift, weight, bias_q, bias_v)


def feed_kernel(
    parts, pieces, *refs
):
    mixed_refs, refs = refs[:parts], refs[parts:]
    x_ref, cot_ref, refs = refs[0], refs[1], refs[2:]
    w_out_refs, refs = refs[:parts], refs[parts:]
    (w_up_ref, w_down_ref, out_bias_ref, gain_ref, shift_ref, up_bias_ref, down_bias_ref), refs = (
        refs[:7], refs[7:],
    )
    act_ref, hidden_ref, grad_upper_ref, layer_ref, grad_resid_ref, grad_attn_ref = refs[:6]
    refs = refs[6:]
    grad_mixed_refs, refs = refs[:parts], refs[parts:]
    sums_ref, up_sum_ref, layer_sc, back_sc = refs
    first = pl.program_id(0) == 0

    @pl.when(first)
    def _():
        sums_ref[...] = jnp.zeros_like(sums_ref)
        up_sum_ref[...] = jnp.zeros_like(up_sum_ref)

    attn = out_bias_ref[...]
    for mixed_ref, w_ref in zip(mixed_refs, w_out_refs):
        attn = attn + matmul(mixed_ref[0], w_ref[...])
    resid = x_ref[0].astype(F32) + attn
    center = resid - jnp.mean(resid, axis=-1, keepdims=True)
    root = lax.rsqrt(jnp.mean(center * center, axis=-1, keepdims=True) + EPS)
    normed = center * root
    gain = gain_ref[...]
    act_ref[0] = (normed * gain + shift_ref[...]).astype(BF16)
    layer_sc[...] = resid + down_bias_ref[...]
    back_sc[...] = jnp.zeros_like(back_sc)
    span = w_up_ref.shape[1] // pieces

    for c in range(pieces):
        lanes = slice(c * span, (c + 1) * span)
        upper = matmul(act_ref[0], w_up_ref[:, lanes]) + up_bias_ref[:, lanes]
        square = upper * upper
        bend = jnp.tanh(GELU_C * upper * (1.0 + 0.044715 * square))
        half = 0.5 * (1.0 + bend)
        hidden = (upper * half).astype(BF16)
        hidden_ref[0, :, lanes] = hidden
        slope = half + 0.5 * GELU_C * upper * (1.0 - bend * bend) * (1.0 + 0.134145 * square)
        grad_upper = (matmul(cot_ref[0], w_down_ref[lanes, :], NT) * slope).astype(BF16)
        grad_upper_ref[0, :, lanes] = grad_upper
        up_sum_ref[0:1, lanes] += jnp.sum(grad_upper.astype(F32), axis=0, keepdims=True)
        layer_sc[...] += matmul(hidden, w_down_ref[lanes, :])
        back_sc[...] += matmul(grad_upper, w_up_ref[:, lanes], NT)

    layer_ref[0] = layer_sc[...].astype(BF16)
    back = back_sc[...]
    scaled = back * gain
    grad_out = cot_ref[0].astype(F32)
    grad_resid = grad_out + root * (
        scaled
        - jnp.mean(scaled, axis=-1, keepdims=True)
        - normed * jnp.mean(scaled * normed, axis=-1, keepdims=True)
    )
    grad_resid_ref[0] = grad_resid
    grad_attn = grad_resid.astype(BF16)
    grad_attn_ref[0] = grad_attn
    for w_ref, grad_mixed_ref in zip(w_out_refs, grad_mixed_refs):
        grad_mixed_ref[0] = matmul(grad_attn, w_ref[...], NT).astype(BF16)
    sums_ref[0:1, :] += jnp.sum(grad_attn.astype(F32), axis=0, keepdims=True)
    sums_ref[1:2, :] += jnp.sum(back * normed, axis=0, keepdims=True)
    sums_ref[2:3, :] += jnp.sum(back, axis=0, keepdims=True)
    sums_ref[3:4, :] += jnp.sum(grad_out, axis=0, keepdims=True)


def feed(mixed, x, cotangent, w_out, part, w_up, w_down, vectors, up_bias):
    parts = len(mixed)
    rows, size, model = x.shape
    width = mixed[0].shape[2]
    wide = w_up.shape[1]
    still = lambda i, p: (0, 0)
    step = lambda i, p: (i, 0, 0)
    once = pl.Buffered(1)
    slab = pl.BlockSpec((1, size, model), step)
    head_slab = pl.BlockSpec((1, size, width), step)
    wide_slab = pl.BlockSpec((1, size, wide), step)
    vector = pl.BlockSpec((1, model), still)
    w_out_specs = [
        pl.BlockSpec((width, model), lambda i, p, s=s: (p[0] ^ s, 0), pipeline_mode=once)
        for s in range(parts)
    ]

    def body(p_ref, *refs):
        feed_kernel(parts, wide // model, *refs)

    shape = jax.ShapeDtypeStruct
    out = pl.pallas_call(
        body,
        grid_spec=pltpu.PrefetchScalarGridSpec(
            num_scalar_prefetch=1,
            grid=(rows,),
            in_specs=[head_slab] * parts
            + [slab, slab]
            + w_out_specs
            + [
                pl.BlockSpec(w_up.shape, still, pipeline_mode=once),
                pl.BlockSpec(w_down.shape, still, pipeline_mode=once),
                vector,
                vector,
                vector,
                pl.BlockSpec((1, wide), still),
                vector,
            ],
            out_specs=[slab, wide_slab, wide_slab, slab, slab, slab]
            + [head_slab] * parts
            + [pl.BlockSpec((8, model), still), pl.BlockSpec((8, wide), still)],
            scratch_shapes=[
                pltpu.VMEM((size, model), F32),
                pltpu.VMEM((size, model), F32),
            ],
        ),
        out_shape=[
            shape((rows, size, model), BF16),
            shape((rows, size, wide), BF16),
            shape((rows, size, wide), BF16),
            shape((rows, size, model), BF16),
            shape((rows, size, model), F32),
            shape((rows, size, model), BF16),
        ]
        + [shape((rows, size, width), BF16)] * parts
        + [shape((8, model), F32), shape((8, wide), F32)],
        compiler_params=pltpu.CompilerParams(
            dimension_semantics=("arbitrary",), vmem_limit_bytes=VMEM_LIMIT
        ),
        cost_estimate=pl.CostEstimate(
            flops=2 * rows * size * model * (4 * wide + 2 * model),
            transcendentals=rows * size * wide,
            bytes_accessed=rows * size * (4 * wide + 16 * model),
        ),
        name="feed",
    )(
        part.reshape(1), *mixed, x, cotangent, *([w_out] * parts), w_up, w_down,
        vectors["out_bias"], vectors["gain"], vectors["shift"], up_bias, vectors["down_bias"],
    )
    return out[:6], out[6 : 6 + parts], out[6 + parts], out[7 + parts]


def join_kernel(splits, bit_ref, mine_ref, other_ref, *out_refs):
    mine = pl.program_id(0) == bit_ref[0]
    begin = 0
    for out_ref, count in zip(out_refs, splits):
        lanes = slice(begin, begin + count)
        out_ref[...] = jnp.where(mine, mine_ref[:, lanes], other_ref[:, lanes]).astype(F32)
        begin += count


def join(mine, other, bit, splits):
    count, columns = mine.shape
    tall = next(t for t in (192, 96, 48, count) if count % t == 0)
    steps = count // tall

    def mine_map(h, i, b):
        return jnp.where(h == b[0], i, jnp.where(h < b[0], 0, steps - 1)), 0

    def other_map(h, i, b):
        return jnp.where(h != b[0], i, jnp.where(h < 1 - b[0], 0, steps - 1)), 0

    return pl.pallas_call(
        functools.partial(join_kernel, splits),
        grid_spec=pltpu.PrefetchScalarGridSpec(
            num_scalar_prefetch=1,
            grid=(2, steps),
            in_specs=[
                pl.BlockSpec((tall, columns), mine_map),
                pl.BlockSpec((tall, columns), other_map),
            ],
            out_specs=[
                pl.BlockSpec((tall, n), lambda h, i, b: (h * steps + i, 0)) for n in splits
            ],
        ),
        out_shape=[jax.ShapeDtypeStruct((2 * count, n), F32) for n in splits],
        compiler_params=pltpu.CompilerParams(
            dimension_semantics=("arbitrary", "arbitrary"), vmem_limit_bytes=VMEM_LIMIT
        ),
        cost_estimate=pl.CostEstimate(
            flops=2 * count * columns, transcendentals=0, bytes_accessed=12 * count * columns
        ),
        name="join",
    )(bit.reshape(1), mine, other)


def spread_kernel(parts, spans, part_ref, *refs):
    out_ref, refs = refs[-1], refs[:-1]
    part = part_ref[0]
    begin = 0
    for which in range(3):
        for p in range(parts):
            for g, span in enumerate(spans):
                piece = None
                for s in range(parts):
                    here = refs[s * len(spans) + g][:, which * span : (which + 1) * span]
                    piece = here if piece is None else jnp.where((part ^ p) == s, here, piece)
                out_ref[:, begin : begin + span] = piece.astype(F32)
                begin += span


def spread(pieces, part, spans):
    parts = len(pieces)
    count = pieces[0][0].shape[0]
    tall = next(t for t in (192, 96, 48, count) if count % t == 0)
    flat = [p for piece in pieces for p in piece]
    columns = 3 * parts * sum(spans)
    return pl.pallas_call(
        functools.partial(spread_kernel, parts, spans),
        grid_spec=pltpu.PrefetchScalarGridSpec(
            num_scalar_prefetch=1,
            grid=(count // tall,),
            in_specs=[pl.BlockSpec((tall, p.shape[1]), lambda i, b: (i, 0)) for p in flat],
            out_specs=pl.BlockSpec((tall, columns), lambda i, b: (i, 0)),
        ),
        out_shape=jax.ShapeDtypeStruct((count, columns), F32),
        compiler_params=pltpu.CompilerParams(
            dimension_semantics=("arbitrary",), vmem_limit_bytes=VMEM_LIMIT
        ),
        cost_estimate=pl.CostEstimate(
            flops=count * columns, transcendentals=0, bytes_accessed=6 * count * columns
        ),
        name="spread",
    )(part.reshape(1), *flat)


def row_layout(sizes, prefixes, lens, padding, length, size):
    slots = jnp.arange(lens.shape[-1], dtype=jnp.int32)
    kept = jnp.where(slots[None, :] < sizes[:, None], lens, 0)
    ends = jnp.cumsum(kept, axis=-1)
    totals = prefixes + ends[:, -1]
    starts = jnp.cumsum(totals) - totals
    places = jnp.arange(length, dtype=jnp.int32)
    padded = places >= length - padding
    prefix_start = jnp.broadcast_to(length - padding, (length,))
    prefix_end = prefix_start
    own_start = prefix_start
    for g in range(sizes.shape[0]):
        member = (places >= starts[g]) & (places < starts[g] + totals[g]) & ~padded
        body = starts[g] + prefixes[g]
        inside = places - body
        base = jnp.max(jnp.where(inside[:, None] >= ends[g][None, :], ends[g][None, :], 0), axis=-1)
        solution = inside >= 0
        prefix_start = jnp.where(member, starts[g], prefix_start)
        prefix_end = jnp.where(member, jnp.where(solution, body, starts[g]), prefix_end)
        own_start = jnp.where(member, jnp.where(solution, body + base, starts[g]), own_start)
    blocks = length // size
    low = jnp.arange(blocks, dtype=jnp.int32)[None, :] * size
    high = low + size
    need = (
        jnp.maximum(prefix_start[:, None], low) < jnp.minimum(prefix_end[:, None], high)
    ) | (jnp.maximum(own_start[:, None], low) < jnp.minimum(places[:, None] + 1, high))
    flags = jnp.any(need.reshape(blocks, size, blocks), axis=1).astype(jnp.int32).reshape(-1)
    zero = jnp.zeros_like(places)
    info = jnp.stack([prefix_start, prefix_end, own_start, places, zero, zero, zero, zero])
    info = info.astype(jnp.int32).reshape(8, blocks, size).transpose(1, 0, 2)
    return info, flags


def swap(values, axis, mask):
    count = lax.axis_size(axis)
    return lax.ppermute(values, axis, [(i, i ^ mask) for i in range(count)])


def bits(count):
    return [1 << b for b in range(count.bit_length() - 1)]


def take(values, index):
    return lax.dynamic_index_in_dim(values, index, 0, keepdims=False)


def halve(values, steps):
    for axis, mask, bit in steps:
        two = values.reshape(2, values.shape[0] // 2, *values.shape[1:])
        arrived = swap(take(two, 1 - bit), axis, mask)
        values = (take(two, bit).astype(F32) + arrived.astype(F32)).astype(values.dtype)
    return values


def double(values, steps):
    for axis, mask, bit in reversed(steps):
        arrived = swap(values, axis, mask)
        first = jnp.where(bit == 0, values, arrived)
        second = jnp.where(bit == 0, arrived, values)
        values = jnp.concatenate([first, second], axis=0)
    return values


def per_device(
    row_axis,
    tokens,
    segment_ids,
    group_sizes,
    prefix_lens,
    solution_lens,
    padding_counts,
    attn_gain,
    attn_shift,
    w_qkv,
    query_bias,
    value_bias,
    w_out,
    out_bias,
    ffn_gain,
    ffn_shift,
    w_up,
    up_bias,
    w_down,
    down_bias,
    cotangent,
):
    rows, size, model = tokens.shape
    devices = lax.axis_size("pos")
    parts = devices // rows
    blocks = devices
    heads = model // HEAD_DIM // parts
    width = heads * HEAD_DIM
    place = lax.axis_index("pos")
    owner, part = place // parts, place % parts

    def bring(values):
        return jnp.stack(
            [
                swap(take(values, owner ^ m), "pos", m * parts) if m else take(values, owner)
                for m in range(rows)
            ]
        )

    def give_back(values):
        out = jnp.zeros_like(values)
        for m in range(rows):
            slab = swap(values[m], "pos", m * parts) if m else values[m]
            out = lax.dynamic_update_index_in_dim(out, slab, owner ^ m, 0)
        return out

    info, flags = row_layout(
        take(group_sizes, owner),
        take(prefix_lens, owner),
        take(solution_lens, owner),
        take(padding_counts, owner),
        blocks * size,
        size,
    )
    order = jnp.arange(blocks, dtype=jnp.int32)
    phys = (((order % parts) ^ part) * rows + ((order // parts) ^ owner)).astype(jnp.int32)

    def my_columns(start, first=0, count=None):
        begin = start * model + part * width + first
        return lax.dynamic_slice_in_dim(w_qkv, begin, count or width, 1)

    def as_row(vector):
        return vector.astype(F32).reshape(1, -1)

    groups = [(0, 4), (4, 2)] if heads == 6 else [(0, heads)]
    spans = [count * HEAD_DIM for _, count in groups]
    w_mine = jnp.concatenate([my_columns(n) for n in range(3)], axis=1)
    w_groups = [
        jnp.concatenate([my_columns(n, h * HEAD_DIM, c * HEAD_DIM) for n in range(3)], axis=1)
        for h, c in groups
    ]
    bias_q = lax.dynamic_slice_in_dim(query_bias, part * width, width, 0)
    bias_v = lax.dynamic_slice_in_dim(value_bias, part * width, width, 0)

    mine = bring(tokens)
    row = jnp.concatenate([mine] + [swap(mine, "pos", s) for s in range(1, parts)], axis=0)
    cotangent, row = lax.optimization_barrier((cotangent, row))
    own_cotangent = bring(cotangent)
    act_one, query_t, key, key_t, value, value_t = project(
        row, as_row(attn_gain), as_row(attn_shift), w_mine, as_row(bias_q), as_row(bias_v)
    )
    mixed_all, out_t, lse = attention_forward(
        phys, flags, query_t, key, value_t, info, heads
    )
    mixed_all, own_cotangent = lax.optimization_barrier((mixed_all, own_cotangent))
    mixed_parts = []
    for s in range(parts):
        piece = mixed_all[s * rows : (s + 1) * rows]
        mixed_parts.append(swap(piece, "pos", s) if s else piece)

    (act_two, hidden, grad_upper, layer_out, grad_resid, grad_attn), grad_mixed, sums, up_sum = feed(
        mixed_parts, mine, own_cotangent, w_out, part, w_up, w_down,
        {
            "out_bias": as_row(out_bias),
            "gain": as_row(ffn_gain),
            "shift": as_row(ffn_shift),
            "down_bias": as_row(down_bias),
        },
        as_row(up_bias),
    )
    grad_all = jnp.concatenate(
        [swap(g, "pos", s) if s else g for s, g in enumerate(grad_mixed)], axis=0
    )
    grad_t = grad_all.transpose(0, 2, 1)
    layer_home = give_back(layer_out)

    local = rows * size

    def flat(values):
        return values.reshape(-1, values.shape[-1])

    row_place = lax.axis_index(row_axis)
    row_steps = [(row_axis, m, (row_place // m) % 2) for m in bits(lax.axis_size(row_axis))]
    own_steps = [("pos", m * parts, (owner // m) % 2) for m in bits(rows)]
    part_steps = [("pos", m, (part // m) % 2) for m in bits(parts)]

    grad_w_down = matmul(flat(hidden), flat(own_cotangent), TN).astype(BF16)
    share_down = halve(grad_w_down, part_steps)
    stacked = jnp.stack(mixed_parts)
    mixed = jnp.concatenate([flat(take(stacked, g ^ part)) for g in range(parts)], axis=1)
    grad_w_up = jnp.concatenate(
        [
            matmul(flat(act_two), flat(grad_upper), TN).astype(BF16),
            matmul(mixed, flat(grad_attn), TN).astype(BF16),
        ],
        axis=1,
    )
    share_up = halve(grad_w_up, part_steps)
    rest_down, rest_up = own_steps + row_steps, own_steps[::-1] + row_steps

    grads = []
    stage = 0
    for h, count in groups:
        grad_t, share_down, share_up, grads, layer_home = lax.optimization_barrier(
            (grad_t, share_down, share_up, grads, layer_home)
        )
        grads = grads + [
            attention_backward(
                phys, flags, query_t, grad_t, out_t, lse, info, key, key_t, value, count, h
            )
        ]
        share_down = halve(share_down, rest_down[stage : stage + 1])
        share_up = halve(share_up, rest_up[stage : stage + 1])
        stage += 1
    share_down = double(halve(share_down, rest_down[stage:]), part_steps[1:] + rest_down)
    share_up = double(halve(share_up, rest_up[stage:]), part_steps[1:] + rest_up)
    axis, mask, bit = part_steps[0]
    (sum_w_down,) = join(share_down, swap(share_down, axis, mask), bit, (model,))
    sum_w_up, sum_w_out = join(
        share_up, swap(share_up, axis, mask), bit, (w_up.shape[1], model)
    )

    grad_act = sum(matmul(flat(g), w, NT) for g, w in zip(grads, w_groups))
    grad_act_own = grad_act[:local]
    for s in range(1, parts):
        sent = grad_act[s * local : (s + 1) * local].astype(BF16)
        grad_act_own = grad_act_own + swap(sent, "pos", s).astype(F32)
    inputs = flat(mine).astype(F32)
    _, norm_one_pull = jax.vjp(layer_norm, inputs, attn_gain.astype(F32), attn_shift.astype(F32))
    grad_input_norm, grad_attn_gain, grad_attn_shift = norm_one_pull(grad_act_own)
    tokens_grad = (flat(grad_resid) + grad_input_norm).astype(BF16).reshape(rows, size, model)

    summed = []
    for g in grads:
        share = matmul(flat(act_one), flat(g), TN).astype(BF16)
        summed.append(double(halve(share, rest_up), rest_up))
    pieces = [summed] + [[swap(g, "pos", s) for g in summed] for s in range(1, parts)]
    sum_w_qkv = spread(pieces, part, spans)

    def column_sums(which):
        return jnp.concatenate(
            [
                jnp.sum(flat(g)[:, which * n : (which + 1) * n].astype(F32), axis=0)
                for g, n in zip(grads, spans)
            ]
        )

    grad_query_mine, grad_value_mine = column_sums(0), column_sums(2)

    def placed(values):
        return lax.dynamic_update_slice_in_dim(jnp.zeros((model,), F32), values, part * width, 0)

    small = jnp.concatenate(
        [
            grad_attn_gain,
            grad_attn_shift,
            placed(grad_query_mine),
            placed(grad_value_mine),
            sums[:4].reshape(-1),
            up_sum[0],
        ]
    )
    for axis, mask, _ in part_steps + rest_down:
        small = small + swap(small, axis, mask)
    vectors = small[: 8 * model].reshape(8, model)
    return (
        layer_home,
        give_back(tokens_grad),
        vectors[0],
        vectors[1],
        sum_w_qkv,
        vectors[2],
        vectors[3],
        sum_w_out,
        vectors[4],
        vectors[5],
        vectors[6],
        sum_w_up,
        small[8 * model :],
        sum_w_down,
        vectors[7],
    )


def solution(mesh):
    in_specs = (
        P("rows", "pos", None),
        P("rows", "pos"),
        P("rows", None),
        P("rows", None),
        P("rows", None, None),
        P("rows"),
        *([P()] * 13),
        P("rows", "pos", None),
    )
    out_specs = (P("rows", "pos", None), P("rows", "pos", None), *([P()] * 13))
    return jax.shard_map(
        functools.partial(per_device, "rows"),
        mesh=mesh,
        in_specs=in_specs,
        out_specs=out_specs,
        check_vma=False,
    )
```

```python
import functools

import jax
import jax.numpy as jnp
from jax import lax
from jax.experimental import pallas as pl
from jax.experimental.pallas import tpu as pltpu
from jax.sharding import PartitionSpec as P

HEAD_DIM = 64
EPS = 1e-05
NEG = -1e30
GELU_C = 0.7978845608028654
F32 = jnp.float32
BF16 = jnp.bfloat16
VMEM_LIMIT = 60 * 1024 * 1024
NT = (((1,), (1,)), ((), ()))
TN = (((0,), (0,)), ((), ()))


def layer_norm(values, gain, shift):
    center = values - jnp.mean(values, axis=-1, keepdims=True)
    spread = jnp.mean(center * center, axis=-1, keepdims=True)
    return center * lax.rsqrt(spread + EPS) * gain + shift


def gelu_tanh(values):
    return 0.5 * values * (1.0 + jnp.tanh(GELU_C * (values + 0.044715 * values * values * values)))


def matmul(left, right, dims=(((1,), (0,)), ((), ()))):
    return lax.dot_general(left, right, dims, preferred_element_type=F32)


def head_pairs(heads):
    return [(h // 2, min(128, heads * HEAD_DIM - (h // 2) * 128)) for h in range(heads)]


def mask_bias(info_ref, key_start, size):
    prefix_start, prefix_end = info_ref[0, 0:1, :], info_ref[0, 1:2, :]
    own_start, query_place = info_ref[0, 2:3, :], info_ref[0, 3:4, :]
    key_place = key_start + lax.broadcasted_iota(jnp.int32, (size, size), 0)
    allowed = ((key_place >= prefix_start) & (key_place < prefix_end)) | (
        (key_place >= own_start) & (key_place <= query_place)
    )
    return jnp.where(allowed, 0.0, NEG).astype(F32)


def fill_padded(source_ref, target_ref, heads):
    for h, (pair, width) in enumerate(head_pairs(heads)):
        rows = source_ref[0, pair * 128 : pair * 128 + width, :]
        if width == 128:
            keep = (lax.broadcasted_iota(jnp.int32, rows.shape, 0) // HEAD_DIM) == (h % 2)
            rows = jnp.where(keep, rows, jnp.zeros_like(rows))
        target_ref[h, 0:width, :] = rows


def forward_kernel(
    heads, blocks, phys_ref, flag_ref, query_t_ref, key_ref, value_t_ref, info_ref,
    mixed_ref, out_t_ref, lse_ref, bias_sc, top_sc, total_sc, acc_sc, query_sc,
):
    size = query_t_ref.shape[2]
    i = pl.program_id(0)
    fill_padded(query_t_ref, query_sc, heads)
    top_sc[...] = jnp.full_like(top_sc, NEG)
    total_sc[...] = jnp.zeros_like(total_sc)
    acc_sc[...] = jnp.zeros_like(acc_sc)

    @pl.loop(0, i + 1)
    def _(j):
        @pl.when(flag_ref[i * blocks + j] > 0)
        def _():
            at = phys_ref[j]
            bias_sc[...] = mask_bias(info_ref, j * size, size)
            for h, (pair, width) in enumerate(head_pairs(heads)):
                rows = slice(h * HEAD_DIM, (h + 1) * HEAD_DIM)
                scores = (
                    matmul(key_ref[at, :, pair * 128 : pair * 128 + width], query_sc[h, 0:width, :])
                    + bias_sc[...]
                )
                old = top_sc[h]
                top = jnp.maximum(old, jnp.max(scores, axis=0, keepdims=True))
                shrink = jnp.exp(old - top)
                weights = jnp.exp(scores - top)
                total_sc[h] = shrink * total_sc[h] + jnp.sum(weights, axis=0, keepdims=True)
                top_sc[h] = top
                acc_sc[rows, :] = shrink * acc_sc[rows, :] + matmul(
                    value_t_ref[at, rows, :], weights.astype(BF16)
                )

    for h in range(heads):
        rows = slice(h * HEAD_DIM, (h + 1) * HEAD_DIM)
        out_t_ref[0, rows, :] = acc_sc[rows, :] / total_sc[h]
        lse_ref[0, h : h + 1, :] = top_sc[h] + jnp.log(total_sc[h])
    mixed_ref[0] = out_t_ref[0].T.astype(BF16)


def attention_forward(phys, flags, query_t, key, value_t, info, heads):
    blocks, width, size = query_t.shape
    lse_rows = -(-heads // 8) * 8
    whole = pl.Buffered(1)
    spec = pltpu.PrefetchScalarGridSpec(
        num_scalar_prefetch=2,
        grid=(blocks,),
        in_specs=[
            pl.BlockSpec((1, width, size), lambda i, p, f: (p[i], 0, 0)),
            pl.BlockSpec((blocks, size, width), lambda i, p, f: (0, 0, 0), pipeline_mode=whole),
            pl.BlockSpec((blocks, width, size), lambda i, p, f: (0, 0, 0), pipeline_mode=whole),
            pl.BlockSpec((1, 8, size), lambda i, p, f: (i, 0, 0)),
        ],
        out_specs=[
            pl.BlockSpec((1, size, width), lambda i, p, f: (p[i], 0, 0)),
            pl.BlockSpec((1, width, size), lambda i, p, f: (p[i], 0, 0)),
            pl.BlockSpec((1, lse_rows, size), lambda i, p, f: (p[i], 0, 0)),
        ],
        scratch_shapes=[
            pltpu.VMEM((size, size), F32),
            pltpu.VMEM((heads, 1, size), F32),
            pltpu.VMEM((heads, 1, size), F32),
            pltpu.VMEM((width, size), F32),
            pltpu.VMEM((heads, 128, size), BF16),
        ],
    )
    pairs = heads * blocks * (blocks + 1) // 2 * size * size
    return pl.pallas_call(
        functools.partial(forward_kernel, heads, blocks),
        grid_spec=spec,
        out_shape=(
            jax.ShapeDtypeStruct((blocks, size, width), BF16),
            jax.ShapeDtypeStruct((blocks, width, size), F32),
            jax.ShapeDtypeStruct((blocks, lse_rows, size), F32),
        ),
        compiler_params=pltpu.CompilerParams(
            dimension_semantics=("arbitrary",), vmem_limit_bytes=VMEM_LIMIT
        ),
        cost_estimate=pl.CostEstimate(
            flops=pairs * 4 * 128, transcendentals=pairs, bytes_accessed=blocks * size * width * 16
        ),
        name="attention_forward",
    )(phys, flags, query_t, key, value_t, info)


def backward_kernel(
    heads, first, blocks, phys_ref, flag_ref, query_t_ref, grad_t_ref, out_t_ref, lse_ref, info_ref,
    key_ref, key_t_ref, value_ref, grads_ref,
    bias_sc, query_grad_sc, key_grad_sc, value_grad_sc, query_sc, grad_sc, delta_sc,
):
    size = query_t_ref.shape[2]
    span = heads * HEAD_DIM
    i = pl.program_id(0)

    @pl.when(i == 0)
    def _():
        key_grad_sc[...] = jnp.zeros_like(key_grad_sc)
        value_grad_sc[...] = jnp.zeros_like(value_grad_sc)

    fill_padded(query_t_ref, query_sc, heads)
    fill_padded(grad_t_ref, grad_sc, heads)
    query_grad_sc[...] = jnp.zeros_like(query_grad_sc)
    for h in range(heads):
        rows = slice(h * HEAD_DIM, (h + 1) * HEAD_DIM)
        delta_sc[h] = jnp.sum(
            grad_t_ref[0, rows, :].astype(F32) * out_t_ref[0, rows, :], axis=0, keepdims=True
        )

    @pl.loop(0, i + 1)
    def _(j):
        @pl.when(flag_ref[i * blocks + j] > 0)
        def _():
            at = phys_ref[j]
            bias_sc[...] = mask_bias(info_ref, j * size, size)
            for h, (pair, width) in enumerate(head_pairs(heads)):
                rows = slice(h * HEAD_DIM, (h + 1) * HEAD_DIM)
                lanes = slice(pair * 128, pair * 128 + width)
                scores = matmul(key_ref[at, :, lanes], query_sc[h, 0:width, :]) + bias_sc[...]
                probs = jnp.exp(scores - lse_ref[0, first + h : first + h + 1, :])
                grad_probs = matmul(value_ref[at, :, lanes], grad_sc[h, 0:width, :])
                grad_scores = (probs * (grad_probs - delta_sc[h])).astype(BF16)
                query_grad_sc[rows, :] += matmul(key_t_ref[at, rows, :], grad_scores)
                value_grad_sc[at, rows, :] += matmul(
                    grad_t_ref[0, rows, :], probs.astype(BF16), NT
                )
                key_grad_sc[at, rows, :] += matmul(query_t_ref[0, rows, :], grad_scores, NT)

    grads_ref[phys_ref[i], :, 0:span] = (query_grad_sc[...] * 0.125).T.astype(BF16)

    @pl.when(i == blocks - 1)
    def _():
        for block in range(blocks):
            grads_ref[block, :, span : 2 * span] = key_grad_sc[block].T.astype(BF16)
            grads_ref[block, :, 2 * span :] = value_grad_sc[block].T.astype(BF16)


def attention_backward(
    phys, flags, query_t, grad_t, out_t, lse, info, key, key_t, value, heads, first
):
    blocks, _, size = query_t.shape
    span = heads * HEAD_DIM
    c = first // heads
    moving_t = pl.BlockSpec((1, span, size), lambda i, p, f: (p[i], c, 0))
    whole = pl.BlockSpec(
        (blocks, size, span), lambda i, p, f: (0, 0, c), pipeline_mode=pl.Buffered(1)
    )
    whole_t = pl.BlockSpec(
        (blocks, span, size), lambda i, p, f: (0, c, 0), pipeline_mode=pl.Buffered(1)
    )
    spec = pltpu.PrefetchScalarGridSpec(
        num_scalar_prefetch=2,
        grid=(blocks,),
        in_specs=[
            moving_t,
            moving_t,
            moving_t,
            pl.BlockSpec((1, lse.shape[1], size), lambda i, p, f: (p[i], 0, 0)),
            pl.BlockSpec((1, 8, size), lambda i, p, f: (i, 0, 0)),
            whole,
            whole_t,
            whole,
        ],
        out_specs=pl.BlockSpec(
            (blocks, size, 3 * span), lambda i, p, f: (0, 0, 0), pipeline_mode=pl.Buffered(1)
        ),
        scratch_shapes=[
            pltpu.VMEM((size, size), F32),
            pltpu.VMEM((span, size), F32),
            pltpu.VMEM((blocks, span, size), F32),
            pltpu.VMEM((blocks, span, size), F32),
            pltpu.VMEM((heads, 128, size), BF16),
            pltpu.VMEM((heads, 128, size), BF16),
            pltpu.VMEM((heads, 1, size), F32),
        ],
    )
    pairs = heads * blocks * (blocks + 1) // 2 * size * size
    return pl.pallas_call(
        functools.partial(backward_kernel, heads, first, blocks),
        grid_spec=spec,
        out_shape=jax.ShapeDtypeStruct((blocks, size, 3 * span), BF16),
        compiler_params=pltpu.CompilerParams(
            dimension_semantics=("arbitrary",), vmem_limit_bytes=VMEM_LIMIT
        ),
        cost_estimate=pl.CostEstimate(
            flops=pairs * 10 * 128, transcendentals=pairs, bytes_accessed=blocks * size * span * 20
        ),
        name="attention_backward",
    )(phys, flags, query_t, grad_t, out_t, lse, info, key, key_t, value)


def project_kernel(
    width, x_ref, gain_ref, shift_ref, w_ref, bias_q_ref, bias_v_ref,
    act_ref, query_t_ref, key_ref, key_t_ref, value_ref, value_t_ref,
):
    act = layer_norm(x_ref[0].astype(F32), gain_ref[...], shift_ref[...]).astype(BF16)
    act_ref[0] = act
    query = (matmul(act, w_ref[:, :width]) + bias_q_ref[...]).astype(BF16).astype(F32) * 0.125
    query_t_ref[0] = query.T.astype(BF16)
    key = matmul(act, w_ref[:, width : 2 * width])
    key_ref[0] = key.astype(BF16)
    key_t_ref[0] = key.T.astype(BF16)
    value = matmul(act, w_ref[:, 2 * width :]) + bias_v_ref[...]
    value_ref[0] = value.astype(BF16)
    value_t_ref[0] = value.T.astype(BF16)


def project(x, gain, shift, weight, bias_q, bias_v):
    blocks, size, model = x.shape
    width = bias_q.shape[1]
    still = lambda i: (0, 0)
    step = lambda i: (i, 0, 0)
    straight, turned = (
        jax.ShapeDtypeStruct((blocks, size, width), BF16),
        jax.ShapeDtypeStruct((blocks, width, size), BF16),
    )
    wide, tall = pl.BlockSpec((1, size, width), step), pl.BlockSpec((1, width, size), step)
    return pl.pallas_call(
        functools.partial(project_kernel, width),
        grid=(blocks,),
        in_specs=[
            pl.BlockSpec((1, size, model), step),
            pl.BlockSpec((1, model), still),
            pl.BlockSpec((1, model), still),
            pl.BlockSpec(weight.shape, still, pipeline_mode=pl.Buffered(1)),
            pl.BlockSpec((1, width), still),
            pl.BlockSpec((1, width), still),
        ],
        out_specs=[pl.BlockSpec((1, size, model), step), tall, wide, tall, wide, tall],
        out_shape=(
            jax.ShapeDtypeStruct((blocks, size, model), BF16),
            turned, straight, turned, straight, turned,
        ),
        compiler_params=pltpu.CompilerParams(
            dimension_semantics=("arbitrary",), vmem_limit_bytes=VMEM_LIMIT
        ),
        cost_estimate=pl.CostEstimate(
            flops=2 * blocks * size * model * 3 * width,
            transcendentals=blocks * size,
            bytes_accessed=blocks * size * (4 * model + 10 * width),
        ),
        name="project",
    )(x, gain, shift, weight, bias_q, bias_v)


def feed_kernel(
    parts, pieces, *refs
):
    mixed_refs, refs = refs[:parts], refs[parts:]
    x_ref, cot_ref, refs = refs[0], refs[1], refs[2:]
    w_out_refs, refs = refs[:parts], refs[parts:]
    (w_up_ref, w_down_ref, out_bias_ref, gain_ref, shift_ref, up_bias_ref, down_bias_ref), refs = (
        refs[:7], refs[7:],
    )
    act_ref, hidden_ref, grad_upper_ref, layer_ref, grad_resid_ref, grad_attn_ref = refs[:6]
    refs = refs[6:]
    grad_mixed_refs, refs = refs[:parts], refs[parts:]
    sums_ref, up_sum_ref, layer_sc, back_sc = refs
    first = pl.program_id(0) == 0

    @pl.when(first)
    def _():
        sums_ref[...] = jnp.zeros_like(sums_ref)
        up_sum_ref[...] = jnp.zeros_like(up_sum_ref)

    attn = out_bias_ref[...]
    for mixed_ref, w_ref in zip(mixed_refs, w_out_refs):
        attn = attn + matmul(mixed_ref[0], w_ref[...])
    resid = x_ref[0].astype(F32) + attn
    center = resid - jnp.mean(resid, axis=-1, keepdims=True)
    root = lax.rsqrt(jnp.mean(center * center, axis=-1, keepdims=True) + EPS)
    normed = center * root
    gain = gain_ref[...]
    act_ref[0] = (normed * gain + shift_ref[...]).astype(BF16)
    layer_sc[...] = resid + down_bias_ref[...]
    back_sc[...] = jnp.zeros_like(back_sc)
    span = w_up_ref.shape[1] // pieces

    for c in range(pieces):
        lanes = slice(c * span, (c + 1) * span)
        upper = matmul(act_ref[0], w_up_ref[:, lanes]) + up_bias_ref[:, lanes]
        square = upper * upper
        bend = jnp.tanh(GELU_C * upper * (1.0 + 0.044715 * square))
        half = 0.5 * (1.0 + bend)
        hidden = (upper * half).astype(BF16)
        hidden_ref[0, :, lanes] = hidden
        slope = half + 0.5 * GELU_C * upper * (1.0 - bend * bend) * (1.0 + 0.134145 * square)
        grad_upper = (matmul(cot_ref[0], w_down_ref[lanes, :], NT) * slope).astype(BF16)
        grad_upper_ref[0, :, lanes] = grad_upper
        up_sum_ref[0:1, lanes] += jnp.sum(grad_upper.astype(F32), axis=0, keepdims=True)
        layer_sc[...] += matmul(hidden, w_down_ref[lanes, :])
        back_sc[...] += matmul(grad_upper, w_up_ref[:, lanes], NT)

    layer_ref[0] = layer_sc[...].astype(BF16)
    back = back_sc[...]
    scaled = back * gain
    grad_out = cot_ref[0].astype(F32)
    grad_resid = grad_out + root * (
        scaled
        - jnp.mean(scaled, axis=-1, keepdims=True)
        - normed * jnp.mean(scaled * normed, axis=-1, keepdims=True)
    )
    grad_resid_ref[0] = grad_resid
    grad_attn = grad_resid.astype(BF16)
    grad_attn_ref[0] = grad_attn
    for w_ref, grad_mixed_ref in zip(w_out_refs, grad_mixed_refs):
        grad_mixed_ref[0] = matmul(grad_attn, w_ref[...], NT).astype(BF16)
    sums_ref[0:1, :] += jnp.sum(grad_attn.astype(F32), axis=0, keepdims=True)
    sums_ref[1:2, :] += jnp.sum(back * normed, axis=0, keepdims=True)
    sums_ref[2:3, :] += jnp.sum(back, axis=0, keepdims=True)
    sums_ref[3:4, :] += jnp.sum(grad_out, axis=0, keepdims=True)


def feed(mixed, x, cotangent, w_out, part, w_up, w_down, vectors, up_bias):
    parts = len(mixed)
    rows, size, model = x.shape
    width = mixed[0].shape[2]
    wide = w_up.shape[1]
    still = lambda i, p: (0, 0)
    step = lambda i, p: (i, 0, 0)
    once = pl.Buffered(1)
    slab = pl.BlockSpec((1, size, model), step)
    head_slab = pl.BlockSpec((1, size, width), step)
    wide_slab = pl.BlockSpec((1, size, wide), step)
    vector = pl.BlockSpec((1, model), still)
    w_out_specs = [
        pl.BlockSpec((width, model), lambda i, p, s=s: (p[0] ^ s, 0), pipeline_mode=once)
        for s in range(parts)
    ]

    def body(p_ref, *refs):
        feed_kernel(parts, wide // model, *refs)

    shape = jax.ShapeDtypeStruct
    out = pl.pallas_call(
        body,
        grid_spec=pltpu.PrefetchScalarGridSpec(
            num_scalar_prefetch=1,
            grid=(rows,),
            in_specs=[head_slab] * parts
            + [slab, slab]
            + w_out_specs
            + [
                pl.BlockSpec(w_up.shape, still, pipeline_mode=once),
                pl.BlockSpec(w_down.shape, still, pipeline_mode=once),
                vector,
                vector,
                vector,
                pl.BlockSpec((1, wide), still),
                vector,
            ],
            out_specs=[slab, wide_slab, wide_slab, slab, slab, slab]
            + [head_slab] * parts
            + [pl.BlockSpec((8, model), still), pl.BlockSpec((8, wide), still)],
            scratch_shapes=[
                pltpu.VMEM((size, model), F32),
                pltpu.VMEM((size, model), F32),
            ],
        ),
        out_shape=[
            shape((rows, size, model), BF16),
            shape((rows, size, wide), BF16),
            shape((rows, size, wide), BF16),
            shape((rows, size, model), BF16),
            shape((rows, size, model), F32),
            shape((rows, size, model), BF16),
        ]
        + [shape((rows, size, width), BF16)] * parts
        + [shape((8, model), F32), shape((8, wide), F32)],
        compiler_params=pltpu.CompilerParams(
            dimension_semantics=("arbitrary",), vmem_limit_bytes=VMEM_LIMIT
        ),
        cost_estimate=pl.CostEstimate(
            flops=2 * rows * size * model * (4 * wide + 2 * model),
            transcendentals=rows * size * wide,
            bytes_accessed=rows * size * (4 * wide + 16 * model),
        ),
        name="feed",
    )(
        part.reshape(1), *mixed, x, cotangent, *([w_out] * parts), w_up, w_down,
        vectors["out_bias"], vectors["gain"], vectors["shift"], up_bias, vectors["down_bias"],
    )
    return out[:6], out[6 : 6 + parts], out[6 + parts], out[7 + parts]


def join_kernel(sources, moves, bit_ref, *refs):
    mine_refs, other_refs, out_refs = refs[:sources], refs[sources : 2 * sources], refs[2 * sources :]
    mine = pl.program_id(0) == bit_ref[0]
    for source, begin, out, place, count in moves:
        lanes = slice(begin, begin + count)
        out_refs[out][:, place : place + count] = jnp.where(
            mine, mine_refs[source][:, lanes], other_refs[source][:, lanes]
        ).astype(F32)


def join(mine, other, bit, moves, widths):
    count = mine[0].shape[0]
    tall = next(t for t in (192, 96, 48, count) if count % t == 0)
    steps = count // tall

    def mine_map(h, i, b):
        return jnp.where(h == b[0], i, jnp.where(h < b[0], 0, steps - 1)), 0

    def other_map(h, i, b):
        return jnp.where(h != b[0], i, jnp.where(h < 1 - b[0], 0, steps - 1)), 0

    columns = sum(widths)
    return pl.pallas_call(
        functools.partial(join_kernel, len(mine), moves),
        grid_spec=pltpu.PrefetchScalarGridSpec(
            num_scalar_prefetch=1,
            grid=(2, steps),
            in_specs=[pl.BlockSpec((tall, m.shape[1]), mine_map) for m in mine]
            + [pl.BlockSpec((tall, m.shape[1]), other_map) for m in mine],
            out_specs=[
                pl.BlockSpec((tall, n), lambda h, i, b: (h * steps + i, 0)) for n in widths
            ],
        ),
        out_shape=[jax.ShapeDtypeStruct((2 * count, n), F32) for n in widths],
        compiler_params=pltpu.CompilerParams(
            dimension_semantics=("arbitrary", "arbitrary"), vmem_limit_bytes=VMEM_LIMIT
        ),
        cost_estimate=pl.CostEstimate(
            flops=2 * count * columns, transcendentals=0, bytes_accessed=12 * count * columns
        ),
        name="join",
    )(bit.reshape(1), *mine, *other)


def spread_kernel(parts, spans, part_ref, *refs):
    out_ref, refs = refs[-1], refs[:-1]
    part = part_ref[0]
    begin = 0
    for which in range(3):
        for p in range(parts):
            for g, span in enumerate(spans):
                piece = None
                for s in range(parts):
                    here = refs[s * len(spans) + g][:, which * span : (which + 1) * span]
                    piece = here if piece is None else jnp.where((part ^ p) == s, here, piece)
                out_ref[:, begin : begin + span] = piece.astype(F32)
                begin += span


def spread(pieces, part, spans):
    parts = len(pieces)
    count = pieces[0][0].shape[0]
    tall = next(t for t in (192, 96, 48, count) if count % t == 0)
    flat = [p for piece in pieces for p in piece]
    columns = 3 * parts * sum(spans)
    return pl.pallas_call(
        functools.partial(spread_kernel, parts, spans),
        grid_spec=pltpu.PrefetchScalarGridSpec(
            num_scalar_prefetch=1,
            grid=(count // tall,),
            in_specs=[pl.BlockSpec((tall, p.shape[1]), lambda i, b: (i, 0)) for p in flat],
            out_specs=pl.BlockSpec((tall, columns), lambda i, b: (i, 0)),
        ),
        out_shape=jax.ShapeDtypeStruct((count, columns), F32),
        compiler_params=pltpu.CompilerParams(
            dimension_semantics=("arbitrary",), vmem_limit_bytes=VMEM_LIMIT
        ),
        cost_estimate=pl.CostEstimate(
            flops=count * columns, transcendentals=0, bytes_accessed=6 * count * columns
        ),
        name="spread",
    )(part.reshape(1), *flat)


def row_layout(sizes, prefixes, lens, padding, length, size):
    slots = jnp.arange(lens.shape[-1], dtype=jnp.int32)
    kept = jnp.where(slots[None, :] < sizes[:, None], lens, 0)
    ends = jnp.cumsum(kept, axis=-1)
    totals = prefixes + ends[:, -1]
    starts = jnp.cumsum(totals) - totals
    places = jnp.arange(length, dtype=jnp.int32)
    padded = places >= length - padding
    prefix_start = jnp.broadcast_to(length - padding, (length,))
    prefix_end = prefix_start
    own_start = prefix_start
    for g in range(sizes.shape[0]):
        member = (places >= starts[g]) & (places < starts[g] + totals[g]) & ~padded
        body = starts[g] + prefixes[g]
        inside = places - body
        base = jnp.max(jnp.where(inside[:, None] >= ends[g][None, :], ends[g][None, :], 0), axis=-1)
        solution = inside >= 0
        prefix_start = jnp.where(member, starts[g], prefix_start)
        prefix_end = jnp.where(member, jnp.where(solution, body, starts[g]), prefix_end)
        own_start = jnp.where(member, jnp.where(solution, body + base, starts[g]), own_start)
    blocks = length // size
    low = jnp.arange(blocks, dtype=jnp.int32)[None, :] * size
    high = low + size
    need = (
        jnp.maximum(prefix_start[:, None], low) < jnp.minimum(prefix_end[:, None], high)
    ) | (jnp.maximum(own_start[:, None], low) < jnp.minimum(places[:, None] + 1, high))
    flags = jnp.any(need.reshape(blocks, size, blocks), axis=1).astype(jnp.int32).reshape(-1)
    zero = jnp.zeros_like(places)
    info = jnp.stack([prefix_start, prefix_end, own_start, places, zero, zero, zero, zero])
    info = info.astype(jnp.int32).reshape(8, blocks, size).transpose(1, 0, 2)
    return info, flags


def swap(values, axis, mask):
    count = lax.axis_size(axis)
    return lax.ppermute(values, axis, [(i, i ^ mask) for i in range(count)])


def bits(count):
    return [1 << b for b in range(count.bit_length() - 1)]


def take(values, index):
    return lax.dynamic_index_in_dim(values, index, 0, keepdims=False)


def halve(values, step):
    axis, mask, bit = step
    two = values.reshape(2, values.shape[0] // 2, *values.shape[1:])
    arrived = swap(take(two, 1 - bit), axis, mask)
    return (take(two, bit).astype(F32) + arrived.astype(F32)).astype(values.dtype)


def double(values, step):
    axis, mask, bit = step
    arrived = swap(values, axis, mask)
    first = jnp.where(bit == 0, values, arrived)
    second = jnp.where(bit == 0, arrived, values)
    return jnp.concatenate([first, second], axis=0)


class Chain:
    def __init__(self, values, down, up):
        self.values = values
        self.left = [(halve, step) for step in down] + [(double, step) for step in up]

    def advance(self):
        if self.left:
            move, step = self.left.pop(0)
            self.values = move(self.values, step)


def close(chains, *others):
    tied, others = lax.optimization_barrier(([c.values for c in chains], others))
    for chain, values in zip(chains, tied):
        chain.values = values
    return others


def per_device(
    row_axis,
    tokens,
    segment_ids,
    group_sizes,
    prefix_lens,
    solution_lens,
    padding_counts,
    attn_gain,
    attn_shift,
    w_qkv,
    query_bias,
    value_bias,
    w_out,
    out_bias,
    ffn_gain,
    ffn_shift,
    w_up,
    up_bias,
    w_down,
    down_bias,
    cotangent,
):
    rows, size, model = tokens.shape
    devices = lax.axis_size("pos")
    parts = devices // rows
    blocks = devices
    heads = model // HEAD_DIM // parts
    width = heads * HEAD_DIM
    place = lax.axis_index("pos")
    owner, part = place // parts, place % parts

    def bring(values):
        return jnp.stack(
            [
                swap(take(values, owner ^ m), "pos", m * parts) if m else take(values, owner)
                for m in range(rows)
            ]
        )

    def send_back(values, m):
        return swap(values[m], "pos", m * parts) if m else values[m]

    def arrange(slabs):
        out = jnp.zeros((rows, *slabs[0].shape), slabs[0].dtype)
        for m, slab in enumerate(slabs):
            out = lax.dynamic_update_index_in_dim(out, slab, owner ^ m, 0)
        return out

    info, flags = row_layout(
        take(group_sizes, owner),
        take(prefix_lens, owner),
        take(solution_lens, owner),
        take(padding_counts, owner),
        blocks * size,
        size,
    )
    order = jnp.arange(blocks, dtype=jnp.int32)
    phys = (((order % parts) ^ part) * rows + ((order // parts) ^ owner)).astype(jnp.int32)

    def my_columns(start, first=0, count=None):
        begin = start * model + part * width + first
        return lax.dynamic_slice_in_dim(w_qkv, begin, count or width, 1)

    def as_row(vector):
        return vector.astype(F32).reshape(1, -1)

    groups = [(0, 4), (4, 2)] if heads == 6 else [(0, heads)]
    spans = [count * HEAD_DIM for _, count in groups]
    w_mine = jnp.concatenate([my_columns(n) for n in range(3)], axis=1)
    w_groups = [
        jnp.concatenate([my_columns(n, h * HEAD_DIM, c * HEAD_DIM) for n in range(3)], axis=1)
        for h, c in groups
    ]
    bias_q = lax.dynamic_slice_in_dim(query_bias, part * width, width, 0)
    bias_v = lax.dynamic_slice_in_dim(value_bias, part * width, width, 0)

    mine = bring(tokens)
    row = jnp.concatenate([mine] + [swap(mine, "pos", s) for s in range(1, parts)], axis=0)
    cotangent, row = lax.optimization_barrier((cotangent, row))
    own_cotangent = bring(cotangent)
    act_one, query_t, key, key_t, value, value_t = project(
        row, as_row(attn_gain), as_row(attn_shift), w_mine, as_row(bias_q), as_row(bias_v)
    )
    mixed_all, out_t, lse = attention_forward(
        phys, flags, query_t, key, value_t, info, heads
    )
    mixed_all, own_cotangent = lax.optimization_barrier((mixed_all, own_cotangent))
    mixed_parts = []
    for s in range(parts):
        piece = mixed_all[s * rows : (s + 1) * rows]
        mixed_parts.append(swap(piece, "pos", s) if s else piece)

    (act_two, hidden, grad_upper, layer_out, grad_resid, grad_attn), grad_mixed, sums, up_sum = feed(
        mixed_parts, mine, own_cotangent, w_out, part, w_up, w_down,
        {
            "out_bias": as_row(out_bias),
            "gain": as_row(ffn_gain),
            "shift": as_row(ffn_shift),
            "down_bias": as_row(down_bias),
        },
        as_row(up_bias),
    )
    local = rows * size

    def flat(values):
        return values.reshape(-1, values.shape[-1])

    row_place = lax.axis_index(row_axis)
    row_steps = [(row_axis, m, (row_place // m) % 2) for m in bits(lax.axis_size(row_axis))]
    own_steps = [("pos", m * parts, (owner // m) % 2) for m in bits(rows)]
    part_steps = [("pos", m, (part // m) % 2) for m in bits(parts)]
    turning, last = own_steps + row_steps[:1], row_steps[1:]

    def order(turn):
        turn %= len(turning)
        return turning[turn:] + turning[:turn] + last

    def chain(values, turn, parted=True):
        down = order(turn)
        up = down[::-1] + (part_steps[:0:-1] if parted else [])
        return Chain(values, (part_steps if parted else []) + down, up)

    wide = w_up.shape[1]
    cut = wide * 2 // 3
    near = [m for m in range(1, rows) if m & (m - 1) == 0]
    far = [m for m in range(1, rows) if m & (m - 1)]

    received = [g if s == 0 else swap(g, "pos", s) for s, g in enumerate(grad_mixed)]
    layer_slabs = {m: send_back(layer_out, m) for m in [0] + near}
    down = chain(matmul(flat(hidden), flat(own_cotangent), TN).astype(BF16), 0)
    received, layer_slabs, layer_out, grad_upper = close(
        [down], received, layer_slabs, layer_out, grad_upper
    )
    down.advance()
    layer_slabs.update({m: send_back(layer_out, m) for m in far})
    stacked = jnp.stack(mixed_parts)
    mixed = jnp.concatenate([flat(take(stacked, g ^ part)) for g in range(parts)], axis=1)
    grad_up_flat = flat(grad_upper)
    up_one = chain(matmul(flat(act_two), grad_up_flat[:, :cut], TN).astype(BF16), 1)
    up_two = chain(
        jnp.concatenate(
            [
                matmul(flat(act_two), grad_up_flat[:, cut:], TN).astype(BF16),
                matmul(mixed, flat(grad_attn), TN).astype(BF16),
            ],
            axis=1,
        ),
        2,
    )
    chains = [down, up_one, up_two]
    received, layer_slabs = close(chains, received, layer_slabs)
    layer_home = arrange([layer_slabs[m] for m in range(rows)])
    up_one.advance()
    up_two.advance()
    for _ in part_steps[1:]:
        for c in chains:
            c.advance()
    grad_t = jnp.concatenate(received, axis=0).transpose(0, 2, 1)
    grad_t, layer_home = close(chains, grad_t, layer_home)

    grads, shares = [], []
    for h, count in groups:
        for c in chains + shares:
            c.advance()
        grad = attention_backward(
            phys, flags, query_t, grad_t, out_t, lse, info, key, key_t, value, count, h
        )
        grad, grad_t = close(chains + shares, grad, grad_t)
        grads.append(grad)
        shares.append(chain(matmul(flat(act_one), flat(grad), TN).astype(BF16), 0, False))
        if len(grads) < len(groups):
            (grad_t,) = close(chains + shares, grad_t)

    def column_sums(which):
        return jnp.concatenate(
            [
                jnp.sum(flat(g)[:, which * n : (which + 1) * n].astype(F32), axis=0)
                for g, n in zip(grads, spans)
            ]
        )

    def placed(values):
        return lax.dynamic_update_slice_in_dim(jnp.zeros((model,), F32), values, part * width, 0)

    for c in chains + shares:
        c.advance()
    grad_act = sum(matmul(flat(g), w, NT) for g, w in zip(grads, w_groups))
    grad_act_own = grad_act[:local]
    for s in range(1, parts):
        sent = grad_act[s * local : (s + 1) * local].astype(BF16)
        grad_act_own = grad_act_own + swap(sent, "pos", s).astype(F32)
    sums_q, sums_v = placed(column_sums(0)), placed(column_sums(2))
    grad_act_own, sums_q, sums_v = close(chains + shares, grad_act_own, sums_q, sums_v)

    for c in chains + shares:
        c.advance()
    inputs = flat(mine).astype(F32)
    _, norm_one_pull = jax.vjp(layer_norm, inputs, attn_gain.astype(F32), attn_shift.astype(F32))
    grad_input_norm, grad_attn_gain, grad_attn_shift = norm_one_pull(grad_act_own)
    tokens_grad = (flat(grad_resid) + grad_input_norm).astype(BF16).reshape(rows, size, model)
    small = jnp.concatenate(
        [
            grad_attn_gain,
            grad_attn_shift,
            sums_q,
            sums_v,
            sums[:4].reshape(-1),
            up_sum[0],
        ]
    )
    tokens_grad, small = close(chains + shares, tokens_grad, small)

    small_steps = part_steps + own_steps + row_steps
    token_slabs = {}
    waves = [[0] + near, far]
    while any(c.left for c in chains):
        for c in chains + shares:
            c.advance()
        if small_steps:
            axis, mask, _ = small_steps.pop(0)
            small = small + swap(small, axis, mask)
        if waves:
            token_slabs.update({m: send_back(tokens_grad, m) for m in waves.pop(0)})
        small, token_slabs, tokens_grad = close(chains + shares, small, token_slabs, tokens_grad)

    axis, mask, bit = part_steps[0]
    others = [swap(c.values, axis, mask) for c in chains]
    for c in shares:
        c.advance()
    for axis, mask, _ in small_steps:
        small = small + swap(small, axis, mask)
    others, small = close(chains + shares, others, small)
    (sum_w_down,) = join([down.values], others[:1], bit, ((0, 0, 0, 0, model),), (model,))
    sum_w_up, sum_w_out = join(
        [up_one.values, up_two.values],
        others[1:],
        bit,
        ((0, 0, 0, 0, cut), (1, 0, 0, cut, wide - cut), (1, wide - cut, 1, 0, model)),
        (wide, model),
    )
    tokens_home = arrange([token_slabs[m] for m in range(rows)])
    while any(c.left for c in shares):
        for c in shares:
            c.advance()
    summed = [c.values for c in shares]
    pieces = [summed] + [[swap(g, "pos", s) for g in summed] for s in range(1, parts)]
    sum_w_qkv = spread(pieces, part, spans)

    vectors = small[: 8 * model].reshape(8, model)
    return (
        layer_home,
        tokens_home,
        vectors[0],
        vectors[1],
        sum_w_qkv,
        vectors[2],
        vectors[3],
        sum_w_out,
        vectors[4],
        vectors[5],
        vectors[6],
        sum_w_up,
        small[8 * model :],
        sum_w_down,
        vectors[7],
    )


def solution(mesh):
    in_specs = (
        P("rows", "pos", None),
        P("rows", "pos"),
        P("rows", None),
        P("rows", None),
        P("rows", None, None),
        P("rows"),
        *([P()] * 13),
        P("rows", "pos", None),
    )
    out_specs = (P("rows", "pos", None), P("rows", "pos", None), *([P()] * 13))
    return jax.shard_map(
        functools.partial(per_device, "rows"),
        mesh=mesh,
        in_specs=in_specs,
        out_specs=out_specs,
        check_vma=False,
    )
```

```python
import functools

import jax
import jax.numpy as jnp
from jax import lax
from jax.experimental import pallas as pl
from jax.experimental.pallas import tpu as pltpu
from jax.sharding import Mesh, PartitionSpec as P

HEAD_DIM = 64
EPS = 1e-05
NEG = -1e30
GELU_C = 0.7978845608028654
F32 = jnp.float32
BF16 = jnp.bfloat16
VMEM_LIMIT = 60 * 1024 * 1024
NT = (((1,), (1,)), ((), ()))
TN = (((0,), (0,)), ((), ()))


def layer_norm(values, gain, shift):
    center = values - jnp.mean(values, axis=-1, keepdims=True)
    spread = jnp.mean(center * center, axis=-1, keepdims=True)
    return center * lax.rsqrt(spread + EPS) * gain + shift


def gelu_tanh(values):
    return 0.5 * values * (1.0 + jnp.tanh(GELU_C * (values + 0.044715 * values * values * values)))


def matmul(left, right, dims=(((1,), (0,)), ((), ()))):
    return lax.dot_general(left, right, dims, preferred_element_type=F32)


def head_pairs(heads):
    return [(h // 2, min(128, heads * HEAD_DIM - (h // 2) * 128)) for h in range(heads)]


def mask_bias(info_ref, key_start, size):
    prefix_start, prefix_end = info_ref[0, 0:1, :], info_ref[0, 1:2, :]
    own_start, query_place = info_ref[0, 2:3, :], info_ref[0, 3:4, :]
    key_place = key_start + lax.broadcasted_iota(jnp.int32, (size, size), 0)
    allowed = ((key_place >= prefix_start) & (key_place < prefix_end)) | (
        (key_place >= own_start) & (key_place <= query_place)
    )
    return jnp.where(allowed, 0.0, NEG).astype(F32)


def fill_padded(source_ref, target_ref, heads):
    for h, (pair, width) in enumerate(head_pairs(heads)):
        rows = source_ref[0, pair * 128 : pair * 128 + width, :]
        if width == 128:
            keep = (lax.broadcasted_iota(jnp.int32, rows.shape, 0) // HEAD_DIM) == (h % 2)
            rows = jnp.where(keep, rows, jnp.zeros_like(rows))
        target_ref[h, 0:width, :] = rows


def forward_kernel(
    heads, blocks, phys_ref, flag_ref, query_t_ref, key_ref, value_t_ref, info_ref,
    mixed_ref, out_t_ref, lse_ref, bias_sc, top_sc, total_sc, acc_sc, query_sc,
):
    size = query_t_ref.shape[2]
    i = pl.program_id(0)
    fill_padded(query_t_ref, query_sc, heads)
    top_sc[...] = jnp.full_like(top_sc, NEG)
    total_sc[...] = jnp.zeros_like(total_sc)
    acc_sc[...] = jnp.zeros_like(acc_sc)

    @pl.loop(0, i + 1)
    def _(j):
        @pl.when(flag_ref[i * blocks + j] > 0)
        def _():
            at = phys_ref[j]
            bias_sc[...] = mask_bias(info_ref, j * size, size)
            for h, (pair, width) in enumerate(head_pairs(heads)):
                rows = slice(h * HEAD_DIM, (h + 1) * HEAD_DIM)
                scores = (
                    matmul(key_ref[at, :, pair * 128 : pair * 128 + width], query_sc[h, 0:width, :])
                    + bias_sc[...]
                )
                old = top_sc[h]
                top = jnp.maximum(old, jnp.max(scores, axis=0, keepdims=True))
                shrink = jnp.exp(old - top)
                weights = jnp.exp(scores - top)
                total_sc[h] = shrink * total_sc[h] + jnp.sum(weights, axis=0, keepdims=True)
                top_sc[h] = top
                acc_sc[rows, :] = shrink * acc_sc[rows, :] + matmul(
                    value_t_ref[at, rows, :], weights.astype(BF16)
                )

    for h in range(heads):
        rows = slice(h * HEAD_DIM, (h + 1) * HEAD_DIM)
        out_t_ref[0, rows, :] = acc_sc[rows, :] / total_sc[h]
        lse_ref[0, h : h + 1, :] = top_sc[h] + jnp.log(total_sc[h])
    mixed_ref[0] = out_t_ref[0].T.astype(BF16)


def attention_forward(phys, flags, query_t, key, value_t, info, heads):
    blocks, width, size = query_t.shape
    lse_rows = -(-heads // 8) * 8
    whole = pl.Buffered(1)
    spec = pltpu.PrefetchScalarGridSpec(
        num_scalar_prefetch=2,
        grid=(blocks,),
        in_specs=[
            pl.BlockSpec((1, width, size), lambda i, p, f: (p[i], 0, 0)),
            pl.BlockSpec((blocks, size, width), lambda i, p, f: (0, 0, 0), pipeline_mode=whole),
            pl.BlockSpec((blocks, width, size), lambda i, p, f: (0, 0, 0), pipeline_mode=whole),
            pl.BlockSpec((1, 8, size), lambda i, p, f: (i, 0, 0)),
        ],
        out_specs=[
            pl.BlockSpec((1, size, width), lambda i, p, f: (p[i], 0, 0)),
            pl.BlockSpec((1, width, size), lambda i, p, f: (p[i], 0, 0)),
            pl.BlockSpec((1, lse_rows, size), lambda i, p, f: (p[i], 0, 0)),
        ],
        scratch_shapes=[
            pltpu.VMEM((size, size), F32),
            pltpu.VMEM((heads, 1, size), F32),
            pltpu.VMEM((heads, 1, size), F32),
            pltpu.VMEM((width, size), F32),
            pltpu.VMEM((heads, 128, size), BF16),
        ],
    )
    pairs = heads * blocks * (blocks + 1) // 2 * size * size
    return pl.pallas_call(
        functools.partial(forward_kernel, heads, blocks),
        grid_spec=spec,
        out_shape=(
            jax.ShapeDtypeStruct((blocks, size, width), BF16),
            jax.ShapeDtypeStruct((blocks, width, size), F32),
            jax.ShapeDtypeStruct((blocks, lse_rows, size), F32),
        ),
        compiler_params=pltpu.CompilerParams(
            dimension_semantics=("arbitrary",), vmem_limit_bytes=VMEM_LIMIT
        ),
        cost_estimate=pl.CostEstimate(
            flops=pairs * 4 * 128, transcendentals=pairs, bytes_accessed=blocks * size * width * 16
        ),
        name="attention_forward",
    )(phys, flags, query_t, key, value_t, info)


def backward_kernel(
    heads, first, blocks, phys_ref, flag_ref, query_t_ref, grad_t_ref, out_t_ref, lse_ref, info_ref,
    key_ref, key_t_ref, value_ref, grads_ref,
    bias_sc, query_grad_sc, key_grad_sc, value_grad_sc, query_sc, grad_sc, delta_sc,
):
    size = query_t_ref.shape[2]
    span = heads * HEAD_DIM
    i = pl.program_id(0)

    @pl.when(i == 0)
    def _():
        key_grad_sc[...] = jnp.zeros_like(key_grad_sc)
        value_grad_sc[...] = jnp.zeros_like(value_grad_sc)

    fill_padded(query_t_ref, query_sc, heads)
    fill_padded(grad_t_ref, grad_sc, heads)
    query_grad_sc[...] = jnp.zeros_like(query_grad_sc)
    for h in range(heads):
        rows = slice(h * HEAD_DIM, (h + 1) * HEAD_DIM)
        delta_sc[h] = jnp.sum(
            grad_t_ref[0, rows, :].astype(F32) * out_t_ref[0, rows, :], axis=0, keepdims=True
        )

    @pl.loop(0, i + 1)
    def _(j):
        @pl.when(flag_ref[i * blocks + j] > 0)
        def _():
            at = phys_ref[j]
            bias_sc[...] = mask_bias(info_ref, j * size, size)
            for h, (pair, width) in enumerate(head_pairs(heads)):
                rows = slice(h * HEAD_DIM, (h + 1) * HEAD_DIM)
                lanes = slice(pair * 128, pair * 128 + width)
                scores = matmul(key_ref[at, :, lanes], query_sc[h, 0:width, :]) + bias_sc[...]
                probs = jnp.exp(scores - lse_ref[0, first + h : first + h + 1, :])
                grad_probs = matmul(value_ref[at, :, lanes], grad_sc[h, 0:width, :])
                grad_scores = (probs * (grad_probs - delta_sc[h])).astype(BF16)
                query_grad_sc[rows, :] += matmul(key_t_ref[at, rows, :], grad_scores)
                value_grad_sc[at, rows, :] += matmul(
                    grad_t_ref[0, rows, :], probs.astype(BF16), NT
                )
                key_grad_sc[at, rows, :] += matmul(query_t_ref[0, rows, :], grad_scores, NT)

    grads_ref[phys_ref[i], :, 0:span] = (query_grad_sc[...] * 0.125).T.astype(BF16)

    @pl.when(i == blocks - 1)
    def _():
        for block in range(blocks):
            grads_ref[block, :, span : 2 * span] = key_grad_sc[block].T.astype(BF16)
            grads_ref[block, :, 2 * span :] = value_grad_sc[block].T.astype(BF16)


def attention_backward(
    phys, flags, query_t, grad_t, out_t, lse, info, key, key_t, value, heads, first
):
    blocks, _, size = query_t.shape
    span = heads * HEAD_DIM
    c = first // heads
    moving_t = pl.BlockSpec((1, span, size), lambda i, p, f: (p[i], c, 0))
    whole = pl.BlockSpec(
        (blocks, size, span), lambda i, p, f: (0, 0, c), pipeline_mode=pl.Buffered(1)
    )
    whole_t = pl.BlockSpec(
        (blocks, span, size), lambda i, p, f: (0, c, 0), pipeline_mode=pl.Buffered(1)
    )
    spec = pltpu.PrefetchScalarGridSpec(
        num_scalar_prefetch=2,
        grid=(blocks,),
        in_specs=[
            moving_t,
            moving_t,
            moving_t,
            pl.BlockSpec((1, lse.shape[1], size), lambda i, p, f: (p[i], 0, 0)),
            pl.BlockSpec((1, 8, size), lambda i, p, f: (i, 0, 0)),
            whole,
            whole_t,
            whole,
        ],
        out_specs=pl.BlockSpec(
            (blocks, size, 3 * span), lambda i, p, f: (0, 0, 0), pipeline_mode=pl.Buffered(1)
        ),
        scratch_shapes=[
            pltpu.VMEM((size, size), F32),
            pltpu.VMEM((span, size), F32),
            pltpu.VMEM((blocks, span, size), F32),
            pltpu.VMEM((blocks, span, size), F32),
            pltpu.VMEM((heads, 128, size), BF16),
            pltpu.VMEM((heads, 128, size), BF16),
            pltpu.VMEM((heads, 1, size), F32),
        ],
    )
    pairs = heads * blocks * (blocks + 1) // 2 * size * size
    return pl.pallas_call(
        functools.partial(backward_kernel, heads, first, blocks),
        grid_spec=spec,
        out_shape=jax.ShapeDtypeStruct((blocks, size, 3 * span), BF16),
        compiler_params=pltpu.CompilerParams(
            dimension_semantics=("arbitrary",), vmem_limit_bytes=VMEM_LIMIT
        ),
        cost_estimate=pl.CostEstimate(
            flops=pairs * 10 * 128, transcendentals=pairs, bytes_accessed=blocks * size * span * 20
        ),
        name="attention_backward",
    )(phys, flags, query_t, grad_t, out_t, lse, info, key, key_t, value)


def project_kernel(
    width, x_ref, gain_ref, shift_ref, w_ref, bias_q_ref, bias_v_ref,
    act_ref, query_t_ref, key_ref, key_t_ref, value_ref, value_t_ref,
):
    act = layer_norm(x_ref[0].astype(F32), gain_ref[...], shift_ref[...]).astype(BF16)
    act_ref[0] = act
    query = (matmul(act, w_ref[:, :width]) + bias_q_ref[...]).astype(BF16).astype(F32) * 0.125
    query_t_ref[0] = query.T.astype(BF16)
    key = matmul(act, w_ref[:, width : 2 * width])
    key_ref[0] = key.astype(BF16)
    key_t_ref[0] = key.T.astype(BF16)
    value = matmul(act, w_ref[:, 2 * width :]) + bias_v_ref[...]
    value_ref[0] = value.astype(BF16)
    value_t_ref[0] = value.T.astype(BF16)


def project(x, gain, shift, weight, bias_q, bias_v):
    blocks, size, model = x.shape
    width = bias_q.shape[1]
    still = lambda i: (0, 0)
    step = lambda i: (i, 0, 0)
    straight, turned = (
        jax.ShapeDtypeStruct((blocks, size, width), BF16),
        jax.ShapeDtypeStruct((blocks, width, size), BF16),
    )
    wide, tall = pl.BlockSpec((1, size, width), step), pl.BlockSpec((1, width, size), step)
    return pl.pallas_call(
        functools.partial(project_kernel, width),
        grid=(blocks,),
        in_specs=[
            pl.BlockSpec((1, size, model), step),
            pl.BlockSpec((1, model), still),
            pl.BlockSpec((1, model), still),
            pl.BlockSpec(weight.shape, still, pipeline_mode=pl.Buffered(1)),
            pl.BlockSpec((1, width), still),
            pl.BlockSpec((1, width), still),
        ],
        out_specs=[pl.BlockSpec((1, size, model), step), tall, wide, tall, wide, tall],
        out_shape=(
            jax.ShapeDtypeStruct((blocks, size, model), BF16),
            turned, straight, turned, straight, turned,
        ),
        compiler_params=pltpu.CompilerParams(
            dimension_semantics=("arbitrary",), vmem_limit_bytes=VMEM_LIMIT
        ),
        cost_estimate=pl.CostEstimate(
            flops=2 * blocks * size * model * 3 * width,
            transcendentals=blocks * size,
            bytes_accessed=blocks * size * (4 * model + 10 * width),
        ),
        name="project",
    )(x, gain, shift, weight, bias_q, bias_v)


def feed_kernel(
    parts, pieces, *refs
):
    mixed_refs, refs = refs[:parts], refs[parts:]
    x_ref, cot_ref, refs = refs[0], refs[1], refs[2:]
    w_out_refs, refs = refs[:parts], refs[parts:]
    (w_up_ref, w_down_ref, out_bias_ref, gain_ref, shift_ref, up_bias_ref, down_bias_ref), refs = (
        refs[:7], refs[7:],
    )
    act_ref, hidden_ref, grad_upper_ref, layer_ref, grad_resid_ref, grad_attn_ref = refs[:6]
    refs = refs[6:]
    grad_mixed_refs, refs = refs[:parts], refs[parts:]
    sums_ref, up_sum_ref, layer_sc, back_sc = refs
    first = pl.program_id(0) == 0

    @pl.when(first)
    def _():
        sums_ref[...] = jnp.zeros_like(sums_ref)
        up_sum_ref[...] = jnp.zeros_like(up_sum_ref)

    attn = out_bias_ref[...]
    for mixed_ref, w_ref in zip(mixed_refs, w_out_refs):
        attn = attn + matmul(mixed_ref[0], w_ref[...])
    resid = x_ref[0].astype(F32) + attn
    center = resid - jnp.mean(resid, axis=-1, keepdims=True)
    root = lax.rsqrt(jnp.mean(center * center, axis=-1, keepdims=True) + EPS)
    normed = center * root
    gain = gain_ref[...]
    act_ref[0] = (normed * gain + shift_ref[...]).astype(BF16)
    layer_sc[...] = resid + down_bias_ref[...]
    back_sc[...] = jnp.zeros_like(back_sc)
    span = w_up_ref.shape[1] // pieces

    for c in range(pieces):
        lanes = slice(c * span, (c + 1) * span)
        upper = matmul(act_ref[0], w_up_ref[:, lanes]) + up_bias_ref[:, lanes]
        square = upper * upper
        bend = jnp.tanh(GELU_C * upper * (1.0 + 0.044715 * square))
        half = 0.5 * (1.0 + bend)
        hidden = (upper * half).astype(BF16)
        hidden_ref[0, :, lanes] = hidden
        slope = half + 0.5 * GELU_C * upper * (1.0 - bend * bend) * (1.0 + 0.134145 * square)
        grad_upper = (matmul(cot_ref[0], w_down_ref[lanes, :], NT) * slope).astype(BF16)
        grad_upper_ref[0, :, lanes] = grad_upper
        up_sum_ref[0:1, lanes] += jnp.sum(grad_upper.astype(F32), axis=0, keepdims=True)
        layer_sc[...] += matmul(hidden, w_down_ref[lanes, :])
        back_sc[...] += matmul(grad_upper, w_up_ref[:, lanes], NT)

    layer_ref[0] = layer_sc[...].astype(BF16)
    back = back_sc[...]
    scaled = back * gain
    grad_out = cot_ref[0].astype(F32)
    grad_resid = grad_out + root * (
        scaled
        - jnp.mean(scaled, axis=-1, keepdims=True)
        - normed * jnp.mean(scaled * normed, axis=-1, keepdims=True)
    )
    grad_resid_ref[0] = grad_resid
    grad_attn = grad_resid.astype(BF16)
    grad_attn_ref[0] = grad_attn
    for w_ref, grad_mixed_ref in zip(w_out_refs, grad_mixed_refs):
        grad_mixed_ref[0] = matmul(grad_attn, w_ref[...], NT).astype(BF16)
    sums_ref[0:1, :] += jnp.sum(grad_attn.astype(F32), axis=0, keepdims=True)
    sums_ref[1:2, :] += jnp.sum(back * normed, axis=0, keepdims=True)
    sums_ref[2:3, :] += jnp.sum(back, axis=0, keepdims=True)
    sums_ref[3:4, :] += jnp.sum(grad_out, axis=0, keepdims=True)


def feed(mixed, x, cotangent, w_out, part, w_up, w_down, vectors, up_bias):
    parts = len(mixed)
    rows, size, model = x.shape
    width = mixed[0].shape[2]
    wide = w_up.shape[1]
    still = lambda i, p: (0, 0)
    step = lambda i, p: (i, 0, 0)
    once = pl.Buffered(1)
    slab = pl.BlockSpec((1, size, model), step)
    head_slab = pl.BlockSpec((1, size, width), step)
    wide_slab = pl.BlockSpec((1, size, wide), step)
    vector = pl.BlockSpec((1, model), still)
    w_out_specs = [
        pl.BlockSpec((width, model), lambda i, p, s=s: (p[0] ^ s, 0), pipeline_mode=once)
        for s in range(parts)
    ]

    def body(p_ref, *refs):
        feed_kernel(parts, wide // model, *refs)

    shape = jax.ShapeDtypeStruct
    out = pl.pallas_call(
        body,
        grid_spec=pltpu.PrefetchScalarGridSpec(
            num_scalar_prefetch=1,
            grid=(rows,),
            in_specs=[head_slab] * parts
            + [slab, slab]
            + w_out_specs
            + [
                pl.BlockSpec(w_up.shape, still, pipeline_mode=once),
                pl.BlockSpec(w_down.shape, still, pipeline_mode=once),
                vector,
                vector,
                vector,
                pl.BlockSpec((1, wide), still),
                vector,
            ],
            out_specs=[slab, wide_slab, wide_slab, slab, slab, slab]
            + [head_slab] * parts
            + [pl.BlockSpec((8, model), still), pl.BlockSpec((8, wide), still)],
            scratch_shapes=[
                pltpu.VMEM((size, model), F32),
                pltpu.VMEM((size, model), F32),
            ],
        ),
        out_shape=[
            shape((rows, size, model), BF16),
            shape((rows, size, wide), BF16),
            shape((rows, size, wide), BF16),
            shape((rows, size, model), BF16),
            shape((rows, size, model), F32),
            shape((rows, size, model), BF16),
        ]
        + [shape((rows, size, width), BF16)] * parts
        + [shape((8, model), F32), shape((8, wide), F32)],
        compiler_params=pltpu.CompilerParams(
            dimension_semantics=("arbitrary",), vmem_limit_bytes=VMEM_LIMIT
        ),
        cost_estimate=pl.CostEstimate(
            flops=2 * rows * size * model * (4 * wide + 2 * model),
            transcendentals=rows * size * wide,
            bytes_accessed=rows * size * (4 * wide + 16 * model),
        ),
        name="feed",
    )(
        part.reshape(1), *mixed, x, cotangent, *([w_out] * parts), w_up, w_down,
        vectors["out_bias"], vectors["gain"], vectors["shift"], up_bias, vectors["down_bias"],
    )
    return out[:6], out[6 : 6 + parts], out[6 + parts], out[7 + parts]


def join_kernel(sources, moves, bit_ref, *refs):
    mine_refs, other_refs, out_refs = refs[:sources], refs[sources : 2 * sources], refs[2 * sources :]
    mine = pl.program_id(0) == bit_ref[0]
    for source, begin, out, place, count in moves:
        lanes = slice(begin, begin + count)
        out_refs[out][:, place : place + count] = jnp.where(
            mine, mine_refs[source][:, lanes], other_refs[source][:, lanes]
        ).astype(F32)


def join(mine, other, bit, moves, widths):
    count = mine[0].shape[0]
    tall = next(t for t in (192, 96, 48, count) if count % t == 0)
    steps = count // tall

    def mine_map(h, i, b):
        return jnp.where(h == b[0], i, jnp.where(h < b[0], 0, steps - 1)), 0

    def other_map(h, i, b):
        return jnp.where(h != b[0], i, jnp.where(h < 1 - b[0], 0, steps - 1)), 0

    columns = sum(widths)
    return pl.pallas_call(
        functools.partial(join_kernel, len(mine), moves),
        grid_spec=pltpu.PrefetchScalarGridSpec(
            num_scalar_prefetch=1,
            grid=(2, steps),
            in_specs=[pl.BlockSpec((tall, m.shape[1]), mine_map) for m in mine]
            + [pl.BlockSpec((tall, m.shape[1]), other_map) for m in mine],
            out_specs=[
                pl.BlockSpec((tall, n), lambda h, i, b: (h * steps + i, 0)) for n in widths
            ],
        ),
        out_shape=[jax.ShapeDtypeStruct((2 * count, n), F32) for n in widths],
        compiler_params=pltpu.CompilerParams(
            dimension_semantics=("arbitrary", "arbitrary"), vmem_limit_bytes=VMEM_LIMIT
        ),
        cost_estimate=pl.CostEstimate(
            flops=2 * count * columns, transcendentals=0, bytes_accessed=12 * count * columns
        ),
        name="join",
    )(bit.reshape(1), *mine, *other)


def spread_kernel(parts, spans, part_ref, *refs):
    out_ref, refs = refs[-1], refs[:-1]
    part = part_ref[0]
    begin = 0
    for which in range(3):
        for p in range(parts):
            first = 0
            for span in spans:
                lanes = slice(first + which * span, first + (which + 1) * span)
                piece = None
                for s in range(parts):
                    here = refs[s][:, lanes]
                    piece = here if piece is None else jnp.where((part ^ p) == s, here, piece)
                out_ref[:, begin : begin + span] = piece.astype(F32)
                begin += span
                first += 3 * span


def spread(pieces, part, spans):
    parts = len(pieces)
    count = pieces[0].shape[0]
    tall = next(t for t in (192, 96, 48, count) if count % t == 0)
    columns = 3 * parts * sum(spans)
    return pl.pallas_call(
        functools.partial(spread_kernel, parts, spans),
        grid_spec=pltpu.PrefetchScalarGridSpec(
            num_scalar_prefetch=1,
            grid=(count // tall,),
            in_specs=[pl.BlockSpec((tall, p.shape[1]), lambda i, b: (i, 0)) for p in pieces],
            out_specs=pl.BlockSpec((tall, columns), lambda i, b: (i, 0)),
        ),
        out_shape=jax.ShapeDtypeStruct((count, columns), F32),
        compiler_params=pltpu.CompilerParams(
            dimension_semantics=("arbitrary",), vmem_limit_bytes=VMEM_LIMIT
        ),
        cost_estimate=pl.CostEstimate(
            flops=count * columns, transcendentals=0, bytes_accessed=6 * count * columns
        ),
        name="spread",
    )(part.reshape(1), *pieces)


def row_layout(sizes, prefixes, lens, padding, length, size):
    slots = jnp.arange(lens.shape[-1], dtype=jnp.int32)
    kept = jnp.where(slots[None, :] < sizes[:, None], lens, 0)
    ends = jnp.cumsum(kept, axis=-1)
    totals = prefixes + ends[:, -1]
    starts = jnp.cumsum(totals) - totals
    places = jnp.arange(length, dtype=jnp.int32)
    padded = places >= length - padding
    prefix_start = jnp.broadcast_to(length - padding, (length,))
    prefix_end = prefix_start
    own_start = prefix_start
    for g in range(sizes.shape[0]):
        member = (places >= starts[g]) & (places < starts[g] + totals[g]) & ~padded
        body = starts[g] + prefixes[g]
        inside = places - body
        base = jnp.max(jnp.where(inside[:, None] >= ends[g][None, :], ends[g][None, :], 0), axis=-1)
        solution = inside >= 0
        prefix_start = jnp.where(member, starts[g], prefix_start)
        prefix_end = jnp.where(member, jnp.where(solution, body, starts[g]), prefix_end)
        own_start = jnp.where(member, jnp.where(solution, body + base, starts[g]), own_start)
    blocks = length // size
    low = jnp.arange(blocks, dtype=jnp.int32)[None, :] * size
    high = low + size
    need = (
        jnp.maximum(prefix_start[:, None], low) < jnp.minimum(prefix_end[:, None], high)
    ) | (jnp.maximum(own_start[:, None], low) < jnp.minimum(places[:, None] + 1, high))
    flags = jnp.any(need.reshape(blocks, size, blocks), axis=1).astype(jnp.int32).reshape(-1)
    zero = jnp.zeros_like(places)
    info = jnp.stack([prefix_start, prefix_end, own_start, places, zero, zero, zero, zero])
    info = info.astype(jnp.int32).reshape(8, blocks, size).transpose(1, 0, 2)
    return info, flags


POS = ("own", "part")


def swap(values, axis, mask):
    count = lax.psum(1, axis)
    return lax.ppermute(values, axis, [(i, i ^ mask) for i in range(count)])


def bits(count):
    return [1 << b for b in range(count.bit_length() - 1)]


def take(values, index):
    return lax.dynamic_index_in_dim(values, index, 0, keepdims=False)


def halve(values, step):
    axis, mask, bit = step
    two = values.reshape(2, values.shape[0] // 2, *values.shape[1:])
    arrived = swap(take(two, 1 - bit), axis, mask)
    return (take(two, bit).astype(F32) + arrived.astype(F32)).astype(values.dtype)


def double(values, step):
    axis, mask, bit = step
    arrived = swap(values, axis, mask)
    first = jnp.where(bit == 0, values, arrived)
    second = jnp.where(bit == 0, arrived, values)
    return jnp.concatenate([first, second], axis=0)


def scatter(values, group):
    axis, stride, count, index = group
    pieces = values.reshape(count, values.shape[0] // count, *values.shape[1:])
    total = take(pieces, index).astype(F32)
    for m in range(1, count):
        total = total + swap(take(pieces, index ^ m), axis, m * stride).astype(F32)
    return total.astype(values.dtype)


def gather(values, group):
    axis, stride, count, index = group
    slabs = [values] + [swap(values, axis, m * stride) for m in range(1, count)]
    for b in bits(count):
        slabs = [jnp.where((index & b) == 0, slabs[j], slabs[j ^ b]) for j in range(count)]
    return jnp.concatenate(slabs, axis=0)


def close(*values):
    return lax.optimization_barrier(values)


def per_device(
    row_axis,
    tokens,
    segment_ids,
    group_sizes,
    prefix_lens,
    solution_lens,
    padding_counts,
    attn_gain,
    attn_shift,
    w_qkv,
    query_bias,
    value_bias,
    w_out,
    out_bias,
    ffn_gain,
    ffn_shift,
    w_up,
    up_bias,
    w_down,
    down_bias,
    cotangent,
):
    rows, size, model = tokens.shape
    devices = lax.psum(1, POS)
    parts = devices // rows
    blocks = devices
    heads = model // HEAD_DIM // parts
    width = heads * HEAD_DIM
    place = lax.axis_index(POS)
    owner, part = place // parts, place % parts

    def bring(values):
        return jnp.stack(
            [
                swap(take(values, owner ^ m), POS, m * parts) if m else take(values, owner)
                for m in range(rows)
            ]
        )

    def send_back(values, m):
        return swap(values[m], POS, m * parts) if m else values[m]

    def arrange(slabs):
        out = jnp.zeros((rows, *slabs[0].shape), slabs[0].dtype)
        for m, slab in enumerate(slabs):
            out = lax.dynamic_update_index_in_dim(out, slab, owner ^ m, 0)
        return out

    info, flags = row_layout(
        take(group_sizes, owner),
        take(prefix_lens, owner),
        take(solution_lens, owner),
        take(padding_counts, owner),
        blocks * size,
        size,
    )
    order = jnp.arange(blocks, dtype=jnp.int32)
    phys = (((order % parts) ^ part) * rows + ((order // parts) ^ owner)).astype(jnp.int32)

    def my_columns(start, first=0, count=None):
        begin = start * model + part * width + first
        return lax.dynamic_slice_in_dim(w_qkv, begin, count or width, 1)

    def as_row(vector):
        return vector.astype(F32).reshape(1, -1)

    groups = [(0, 4), (4, 2)] if heads == 6 else [(0, heads)]
    spans = [count * HEAD_DIM for _, count in groups]
    w_mine = jnp.concatenate([my_columns(n) for n in range(3)], axis=1)
    w_groups = [
        jnp.concatenate([my_columns(n, h * HEAD_DIM, c * HEAD_DIM) for n in range(3)], axis=1)
        for h, c in groups
    ]
    bias_q = lax.dynamic_slice_in_dim(query_bias, part * width, width, 0)
    bias_v = lax.dynamic_slice_in_dim(value_bias, part * width, width, 0)

    mine = bring(tokens)
    row = jnp.concatenate([mine] + [swap(mine, POS, s) for s in range(1, parts)], axis=0)
    cotangent, row = lax.optimization_barrier((cotangent, row))
    own_cotangent = bring(cotangent)
    act_one, query_t, key, key_t, value, value_t = project(
        row, as_row(attn_gain), as_row(attn_shift), w_mine, as_row(bias_q), as_row(bias_v)
    )
    mixed_all, out_t, lse = attention_forward(
        phys, flags, query_t, key, value_t, info, heads
    )
    mixed_all, own_cotangent = lax.optimization_barrier((mixed_all, own_cotangent))
    mixed_parts = []
    for s in range(parts):
        piece = mixed_all[s * rows : (s + 1) * rows]
        mixed_parts.append(swap(piece, POS, s) if s else piece)

    (act_two, hidden, grad_upper, layer_out, grad_resid, grad_attn), grad_mixed, sums, up_sum = feed(
        mixed_parts, mine, own_cotangent, w_out, part, w_up, w_down,
        {
            "out_bias": as_row(out_bias),
            "gain": as_row(ffn_gain),
            "shift": as_row(ffn_shift),
            "down_bias": as_row(down_bias),
        },
        as_row(up_bias),
    )
    local = rows * size

    def flat(values):
        return values.reshape(-1, values.shape[-1])

    row_count = lax.psum(1, row_axis)
    rows_group = (row_axis, 1, row_count, lax.axis_index(row_axis))
    chips_group = (POS, parts, rows, owner)
    own_steps = [(POS, m * parts, (owner // m) % 2) for m in bits(rows)]
    part_steps = [(POS, m, (part // m) % 2) for m in bits(parts)]
    wide = w_up.shape[1]
    near = [m for m in range(1, rows) if m & (m - 1) == 0]
    far = [m for m in range(1, rows) if m & (m - 1)]

    received = [g if s == 0 else swap(g, POS, s) for s, g in enumerate(grad_mixed)]
    layer_slabs = {m: send_back(layer_out, m) for m in [0] + near}
    stacked = jnp.stack(mixed_parts)
    mixed = jnp.concatenate([flat(take(stacked, g ^ part)) for g in range(parts)], axis=1)
    up = jnp.concatenate(
        [
            matmul(flat(act_two), flat(grad_upper), TN).astype(BF16),
            matmul(mixed, flat(grad_attn), TN).astype(BF16),
        ],
        axis=1,
    )
    up, received, layer_slabs, layer_out, hidden = close(
        up, received, layer_slabs, layer_out, hidden
    )
    for step in part_steps:
        up = halve(up, step)
    layer_slabs.update({m: send_back(layer_out, m) for m in far})
    down = matmul(flat(hidden), flat(own_cotangent), TN).astype(BF16)
    up, down, received, layer_slabs = close(up, down, received, layer_slabs)
    up_sum_all = lax.psum(up, (row_axis, "own"))
    for step in part_steps:
        down = halve(down, step)
    layer_home = arrange([layer_slabs[m] for m in range(rows)])
    grad_t = jnp.concatenate(received, axis=0).transpose(0, 2, 1)
    pair = [down[: down.shape[0] // 2], down[down.shape[0] // 2 :]]
    orders = [own_steps, own_steps[::-1]]
    pair, grad_t, layer_home = close(pair, grad_t, layer_home)

    grads, shares = [], []
    done = 0
    for h, count in groups:
        pair = [halve(p, o[done]) if done < len(o) else p for p, o in zip(pair, orders)]
        done += 1
        shares = [scatter(q, chips_group) if i == len(shares) - 1 else q for i, q in enumerate(shares)]
        grad = attention_backward(
            phys, flags, query_t, grad_t, out_t, lse, info, key, key_t, value, count, h
        )
        grads, grad_t, pair, shares = close(grads + [grad], grad_t, pair, shares)
        shares.append(matmul(flat(act_one), flat(grad), TN).astype(BF16))
        if len(grads) < len(groups):
            grad_t, pair, shares = close(grad_t, pair, shares)
    while done < len(own_steps):
        pair = [halve(p, o[done]) for p, o in zip(pair, orders)]
        done += 1

    def column_sums(which):
        return jnp.concatenate(
            [
                jnp.sum(flat(g)[:, which * n : (which + 1) * n].astype(F32), axis=0)
                for g, n in zip(grads, spans)
            ]
        )

    def placed(values):
        return lax.dynamic_update_slice_in_dim(jnp.zeros((model,), F32), values, part * width, 0)

    both = scatter(jnp.concatenate(pair, axis=1), rows_group)
    shares[-1] = scatter(shares[-1], chips_group)
    grad_act = sum(matmul(flat(g), w, NT) for g, w in zip(grads, w_groups))
    grad_act_own = grad_act[:local]
    for s in range(1, parts):
        sent = grad_act[s * local : (s + 1) * local].astype(BF16)
        grad_act_own = grad_act_own + swap(sent, POS, s).astype(F32)
    sums_q, sums_v = placed(column_sums(0)), placed(column_sums(2))
    both, shares, grad_act_own, sums_q, sums_v = close(both, shares, grad_act_own, sums_q, sums_v)

    both = gather(both, rows_group)
    share = scatter(jnp.concatenate(shares, axis=1), rows_group)
    inputs = flat(mine).astype(F32)
    _, norm_one_pull = jax.vjp(layer_norm, inputs, attn_gain.astype(F32), attn_shift.astype(F32))
    grad_input_norm, grad_attn_gain, grad_attn_shift = norm_one_pull(grad_act_own)
    tokens_grad = (flat(grad_resid) + grad_input_norm).astype(BF16).reshape(rows, size, model)
    small = jnp.concatenate(
        [
            grad_attn_gain,
            grad_attn_shift,
            sums_q,
            sums_v,
            sums[:4].reshape(-1),
            up_sum[0],
        ]
    )
    both, share, tokens_grad, small = close(both, share, tokens_grad, small)

    small_steps = part_steps + own_steps + [(row_axis, m, None) for m in bits(row_count)]

    def small_step(values):
        if small_steps:
            axis, mask, _ = small_steps.pop(0)
            values = values + swap(values, axis, mask)
        return values

    pair = [both[:, :model], both[:, model:]]
    token_slabs = {}
    waves = [[0] + near, far]
    for stage in reversed(range(len(own_steps))):
        pair = [double(p, o[stage]) for p, o in zip(pair, orders)]
        if stage == len(own_steps) - 1:
            share = gather(share, rows_group)
        if stage == 0:
            share = gather(share, chips_group)
        if waves:
            token_slabs.update({m: send_back(tokens_grad, m) for m in waves.pop(0)})
        small = small_step(small)
        pair, share, small, token_slabs, tokens_grad = close(
            pair, share, small, token_slabs, tokens_grad
        )
    for wave in waves:
        token_slabs.update({m: send_back(tokens_grad, m) for m in wave})

    down = jnp.concatenate(pair, axis=0)
    up = up_sum_all
    for step in part_steps[:0:-1]:
        down, up = double(down, step), double(up, step)
    axis, mask, bit = part_steps[0]
    other_down, other_up = swap(down, axis, mask), swap(up, axis, mask)
    pieces = [share] + [swap(share, POS, s) for s in range(1, parts)]
    (sum_w_down,) = join([down], [other_down], bit, ((0, 0, 0, 0, model),), (model,))
    sum_w_up, sum_w_out = join(
        [up], [other_up], bit, ((0, 0, 0, 0, wide), (0, wide, 1, 0, model)), (wide, model)
    )
    tokens_home = arrange([token_slabs[m] for m in range(rows)])
    sum_w_qkv = spread(pieces, part, spans)
    while small_steps:
        small = small_step(small)

    vectors = small[: 8 * model].reshape(8, model)
    return (
        layer_home,
        tokens_home,
        vectors[0],
        vectors[1],
        sum_w_qkv,
        vectors[2],
        vectors[3],
        sum_w_out,
        vectors[4],
        vectors[5],
        vectors[6],
        sum_w_up,
        small[8 * model :],
        sum_w_down,
        vectors[7],
    )


def solution(mesh):
    def run(tokens, *others):
        count = mesh.shape["rows"]
        rows = tokens.shape[0] // count
        split = Mesh(mesh.devices.reshape(count, rows, -1), ("rows", *POS))
        in_specs = (
            P("rows", POS, None),
            P("rows", POS),
            P("rows", None),
            P("rows", None),
            P("rows", None, None),
            P("rows"),
            *([P()] * 13),
            P("rows", POS, None),
        )
        out_specs = (P("rows", POS, None), P("rows", POS, None), *([P()] * 13))
        return jax.shard_map(
            functools.partial(per_device, "rows"),
            mesh=split,
            in_specs=in_specs,
            out_specs=out_specs,
            check_vma=False,
        )(tokens, *others)

    return run
```

```python
import functools

import jax
import jax.numpy as jnp
from jax import lax
from jax.experimental import pallas as pl
from jax.experimental.pallas import tpu as pltpu
from jax.sharding import PartitionSpec as P

HEAD_DIM = 64
EPS = 1e-05
NEG = -1e30
GELU_C = 0.7978845608028654
F32 = jnp.float32
BF16 = jnp.bfloat16
VMEM_LIMIT = 60 * 1024 * 1024
NT = (((1,), (1,)), ((), ()))
TN = (((0,), (0,)), ((), ()))


def layer_norm(values, gain, shift):
    center = values - jnp.mean(values, axis=-1, keepdims=True)
    spread = jnp.mean(center * center, axis=-1, keepdims=True)
    return center * lax.rsqrt(spread + EPS) * gain + shift


def gelu_tanh(values):
    return 0.5 * values * (1.0 + jnp.tanh(GELU_C * (values + 0.044715 * values * values * values)))


def matmul(left, right, dims=(((1,), (0,)), ((), ()))):
    return lax.dot_general(left, right, dims, preferred_element_type=F32)


def head_pairs(heads):
    return [(h // 2, min(128, heads * HEAD_DIM - (h // 2) * 128)) for h in range(heads)]


def mask_bias(info_ref, key_start, size):
    prefix_start, prefix_end = info_ref[0, 0:1, :], info_ref[0, 1:2, :]
    own_start, query_place = info_ref[0, 2:3, :], info_ref[0, 3:4, :]
    key_place = key_start + lax.broadcasted_iota(jnp.int32, (size, size), 0)
    allowed = ((key_place >= prefix_start) & (key_place < prefix_end)) | (
        (key_place >= own_start) & (key_place <= query_place)
    )
    return jnp.where(allowed, 0.0, NEG).astype(F32)


def fill_padded(source_ref, target_ref, heads):
    for h, (pair, width) in enumerate(head_pairs(heads)):
        rows = source_ref[0, pair * 128 : pair * 128 + width, :]
        if width == 128:
            keep = (lax.broadcasted_iota(jnp.int32, rows.shape, 0) // HEAD_DIM) == (h % 2)
            rows = jnp.where(keep, rows, jnp.zeros_like(rows))
        target_ref[h, 0:width, :] = rows


def forward_kernel(
    heads, blocks, phys_ref, flag_ref, query_t_ref, key_ref, value_t_ref, info_ref,
    mixed_ref, out_t_ref, lse_ref, bias_sc, top_sc, total_sc, acc_sc, query_sc,
):
    size = query_t_ref.shape[2]
    i = pl.program_id(0)
    fill_padded(query_t_ref, query_sc, heads)
    top_sc[...] = jnp.full_like(top_sc, NEG)
    total_sc[...] = jnp.zeros_like(total_sc)
    acc_sc[...] = jnp.zeros_like(acc_sc)

    @pl.loop(0, i + 1)
    def _(j):
        @pl.when(flag_ref[i * blocks + j] > 0)
        def _():
            at = phys_ref[j]
            bias_sc[...] = mask_bias(info_ref, j * size, size)
            for h, (pair, width) in enumerate(head_pairs(heads)):
                rows = slice(h * HEAD_DIM, (h + 1) * HEAD_DIM)
                scores = (
                    matmul(key_ref[at, :, pair * 128 : pair * 128 + width], query_sc[h, 0:width, :])
                    + bias_sc[...]
                )
                old = top_sc[h]
                top = jnp.maximum(old, jnp.max(scores, axis=0, keepdims=True))
                shrink = jnp.exp(old - top)
                weights = jnp.exp(scores - top)
                total_sc[h] = shrink * total_sc[h] + jnp.sum(weights, axis=0, keepdims=True)
                top_sc[h] = top
                acc_sc[rows, :] = shrink * acc_sc[rows, :] + matmul(
                    value_t_ref[at, rows, :], weights.astype(BF16)
                )

    for h in range(heads):
        rows = slice(h * HEAD_DIM, (h + 1) * HEAD_DIM)
        out_t_ref[0, rows, :] = acc_sc[rows, :] / total_sc[h]
        lse_ref[0, h : h + 1, :] = top_sc[h] + jnp.log(total_sc[h])
    mixed_ref[0] = out_t_ref[0].T.astype(BF16)


def attention_forward(phys, flags, query_t, key, value_t, info, heads):
    blocks, width, size = query_t.shape
    lse_rows = -(-heads // 8) * 8
    whole = pl.Buffered(1)
    spec = pltpu.PrefetchScalarGridSpec(
        num_scalar_prefetch=2,
        grid=(blocks,),
        in_specs=[
            pl.BlockSpec((1, width, size), lambda i, p, f: (p[i], 0, 0)),
            pl.BlockSpec((blocks, size, width), lambda i, p, f: (0, 0, 0), pipeline_mode=whole),
            pl.BlockSpec((blocks, width, size), lambda i, p, f: (0, 0, 0), pipeline_mode=whole),
            pl.BlockSpec((1, 8, size), lambda i, p, f: (i, 0, 0)),
        ],
        out_specs=[
            pl.BlockSpec((1, size, width), lambda i, p, f: (p[i], 0, 0)),
            pl.BlockSpec((1, width, size), lambda i, p, f: (p[i], 0, 0)),
            pl.BlockSpec((1, lse_rows, size), lambda i, p, f: (p[i], 0, 0)),
        ],
        scratch_shapes=[
            pltpu.VMEM((size, size), F32),
            pltpu.VMEM((heads, 1, size), F32),
            pltpu.VMEM((heads, 1, size), F32),
            pltpu.VMEM((width, size), F32),
            pltpu.VMEM((heads, 128, size), BF16),
        ],
    )
    pairs = heads * blocks * (blocks + 1) // 2 * size * size
    return pl.pallas_call(
        functools.partial(forward_kernel, heads, blocks),
        grid_spec=spec,
        out_shape=(
            jax.ShapeDtypeStruct((blocks, size, width), BF16),
            jax.ShapeDtypeStruct((blocks, width, size), F32),
            jax.ShapeDtypeStruct((blocks, lse_rows, size), F32),
        ),
        compiler_params=pltpu.CompilerParams(
            dimension_semantics=("arbitrary",), vmem_limit_bytes=VMEM_LIMIT
        ),
        cost_estimate=pl.CostEstimate(
            flops=pairs * 4 * 128, transcendentals=pairs, bytes_accessed=blocks * size * width * 16
        ),
        name="attention_forward",
    )(phys, flags, query_t, key, value_t, info)


def backward_kernel(
    heads, first, blocks, phys_ref, flag_ref, query_t_ref, grad_t_ref, out_t_ref, lse_ref, info_ref,
    key_ref, key_t_ref, value_ref, grads_ref,
    bias_sc, query_grad_sc, key_grad_sc, value_grad_sc, query_sc, grad_sc, delta_sc,
):
    size = query_t_ref.shape[2]
    span = heads * HEAD_DIM
    i = pl.program_id(0)

    @pl.when(i == 0)
    def _():
        key_grad_sc[...] = jnp.zeros_like(key_grad_sc)
        value_grad_sc[...] = jnp.zeros_like(value_grad_sc)

    fill_padded(query_t_ref, query_sc, heads)
    fill_padded(grad_t_ref, grad_sc, heads)
    query_grad_sc[...] = jnp.zeros_like(query_grad_sc)
    for h in range(heads):
        rows = slice(h * HEAD_DIM, (h + 1) * HEAD_DIM)
        delta_sc[h] = jnp.sum(
            grad_t_ref[0, rows, :].astype(F32) * out_t_ref[0, rows, :], axis=0, keepdims=True
        )

    @pl.loop(0, i + 1)
    def _(j):
        @pl.when(flag_ref[i * blocks + j] > 0)
        def _():
            at = phys_ref[j]
            bias_sc[...] = mask_bias(info_ref, j * size, size)
            for h, (pair, width) in enumerate(head_pairs(heads)):
                rows = slice(h * HEAD_DIM, (h + 1) * HEAD_DIM)
                lanes = slice(pair * 128, pair * 128 + width)
                scores = matmul(key_ref[at, :, lanes], query_sc[h, 0:width, :]) + bias_sc[...]
                probs = jnp.exp(scores - lse_ref[0, first + h : first + h + 1, :])
                grad_probs = matmul(value_ref[at, :, lanes], grad_sc[h, 0:width, :])
                grad_scores = (probs * (grad_probs - delta_sc[h])).astype(BF16)
                query_grad_sc[rows, :] += matmul(key_t_ref[at, rows, :], grad_scores)
                value_grad_sc[at, rows, :] += matmul(
                    grad_t_ref[0, rows, :], probs.astype(BF16), NT
                )
                key_grad_sc[at, rows, :] += matmul(query_t_ref[0, rows, :], grad_scores, NT)

    grads_ref[phys_ref[i], :, 0:span] = (query_grad_sc[...] * 0.125).T.astype(BF16)

    @pl.when(i == blocks - 1)
    def _():
        for block in range(blocks):
            grads_ref[block, :, span : 2 * span] = key_grad_sc[block].T.astype(BF16)
            grads_ref[block, :, 2 * span :] = value_grad_sc[block].T.astype(BF16)


def attention_backward(
    phys, flags, query_t, grad_t, out_t, lse, info, key, key_t, value, heads, first
):
    blocks, _, size = query_t.shape
    span = heads * HEAD_DIM
    c = first // heads
    moving_t = pl.BlockSpec((1, span, size), lambda i, p, f: (p[i], c, 0))
    whole = pl.BlockSpec(
        (blocks, size, span), lambda i, p, f: (0, 0, c), pipeline_mode=pl.Buffered(1)
    )
    whole_t = pl.BlockSpec(
        (blocks, span, size), lambda i, p, f: (0, c, 0), pipeline_mode=pl.Buffered(1)
    )
    spec = pltpu.PrefetchScalarGridSpec(
        num_scalar_prefetch=2,
        grid=(blocks,),
        in_specs=[
            moving_t,
            moving_t,
            moving_t,
            pl.BlockSpec((1, lse.shape[1], size), lambda i, p, f: (p[i], 0, 0)),
            pl.BlockSpec((1, 8, size), lambda i, p, f: (i, 0, 0)),
            whole,
            whole_t,
            whole,
        ],
        out_specs=pl.BlockSpec(
            (blocks, size, 3 * span), lambda i, p, f: (0, 0, 0), pipeline_mode=pl.Buffered(1)
        ),
        scratch_shapes=[
            pltpu.VMEM((size, size), F32),
            pltpu.VMEM((span, size), F32),
            pltpu.VMEM((blocks, span, size), F32),
            pltpu.VMEM((blocks, span, size), F32),
            pltpu.VMEM((heads, 128, size), BF16),
            pltpu.VMEM((heads, 128, size), BF16),
            pltpu.VMEM((heads, 1, size), F32),
        ],
    )
    pairs = heads * blocks * (blocks + 1) // 2 * size * size
    return pl.pallas_call(
        functools.partial(backward_kernel, heads, first, blocks),
        grid_spec=spec,
        out_shape=jax.ShapeDtypeStruct((blocks, size, 3 * span), BF16),
        compiler_params=pltpu.CompilerParams(
            dimension_semantics=("arbitrary",), vmem_limit_bytes=VMEM_LIMIT
        ),
        cost_estimate=pl.CostEstimate(
            flops=pairs * 10 * 128, transcendentals=pairs, bytes_accessed=blocks * size * span * 20
        ),
        name="attention_backward",
    )(phys, flags, query_t, grad_t, out_t, lse, info, key, key_t, value)


def project_kernel(
    width, x_ref, gain_ref, shift_ref, w_ref, bias_q_ref, bias_v_ref,
    act_ref, query_t_ref, key_ref, key_t_ref, value_ref, value_t_ref,
):
    act = layer_norm(x_ref[0].astype(F32), gain_ref[...], shift_ref[...]).astype(BF16)
    act_ref[0] = act
    query = (matmul(act, w_ref[:, :width]) + bias_q_ref[...]).astype(BF16).astype(F32) * 0.125
    query_t_ref[0] = query.T.astype(BF16)
    key = matmul(act, w_ref[:, width : 2 * width])
    key_ref[0] = key.astype(BF16)
    key_t_ref[0] = key.T.astype(BF16)
    value = matmul(act, w_ref[:, 2 * width :]) + bias_v_ref[...]
    value_ref[0] = value.astype(BF16)
    value_t_ref[0] = value.T.astype(BF16)


def project(x, gain, shift, weight, bias_q, bias_v):
    blocks, size, model = x.shape
    width = bias_q.shape[1]
    still = lambda i: (0, 0)
    step = lambda i: (i, 0, 0)
    straight, turned = (
        jax.ShapeDtypeStruct((blocks, size, width), BF16),
        jax.ShapeDtypeStruct((blocks, width, size), BF16),
    )
    wide, tall = pl.BlockSpec((1, size, width), step), pl.BlockSpec((1, width, size), step)
    return pl.pallas_call(
        functools.partial(project_kernel, width),
        grid=(blocks,),
        in_specs=[
            pl.BlockSpec((1, size, model), step),
            pl.BlockSpec((1, model), still),
            pl.BlockSpec((1, model), still),
            pl.BlockSpec(weight.shape, still, pipeline_mode=pl.Buffered(1)),
            pl.BlockSpec((1, width), still),
            pl.BlockSpec((1, width), still),
        ],
        out_specs=[pl.BlockSpec((1, size, model), step), tall, wide, tall, wide, tall],
        out_shape=(
            jax.ShapeDtypeStruct((blocks, size, model), BF16),
            turned, straight, turned, straight, turned,
        ),
        compiler_params=pltpu.CompilerParams(
            dimension_semantics=("arbitrary",), vmem_limit_bytes=VMEM_LIMIT
        ),
        cost_estimate=pl.CostEstimate(
            flops=2 * blocks * size * model * 3 * width,
            transcendentals=blocks * size,
            bytes_accessed=blocks * size * (4 * model + 10 * width),
        ),
        name="project",
    )(x, gain, shift, weight, bias_q, bias_v)


def feed_kernel(
    parts, pieces, *refs
):
    mixed_refs, refs = refs[:parts], refs[parts:]
    x_ref, cot_ref, refs = refs[0], refs[1], refs[2:]
    w_out_refs, refs = refs[:parts], refs[parts:]
    (w_up_ref, w_down_ref, out_bias_ref, gain_ref, shift_ref, up_bias_ref, down_bias_ref), refs = (
        refs[:7], refs[7:],
    )
    act_ref, hidden_ref, grad_upper_ref, layer_ref, grad_resid_ref, grad_attn_ref = refs[:6]
    refs = refs[6:]
    grad_mixed_refs, refs = refs[:parts], refs[parts:]
    sums_ref, up_sum_ref, layer_sc, back_sc = refs
    first = pl.program_id(0) == 0

    @pl.when(first)
    def _():
        sums_ref[...] = jnp.zeros_like(sums_ref)
        up_sum_ref[...] = jnp.zeros_like(up_sum_ref)

    attn = out_bias_ref[...]
    for mixed_ref, w_ref in zip(mixed_refs, w_out_refs):
        attn = attn + matmul(mixed_ref[0], w_ref[...])
    resid = x_ref[0].astype(F32) + attn
    center = resid - jnp.mean(resid, axis=-1, keepdims=True)
    root = lax.rsqrt(jnp.mean(center * center, axis=-1, keepdims=True) + EPS)
    normed = center * root
    gain = gain_ref[...]
    act_ref[0] = (normed * gain + shift_ref[...]).astype(BF16)
    layer_sc[...] = resid + down_bias_ref[...]
    back_sc[...] = jnp.zeros_like(back_sc)
    span = w_up_ref.shape[1] // pieces

    for c in range(pieces):
        lanes = slice(c * span, (c + 1) * span)
        upper = matmul(act_ref[0], w_up_ref[:, lanes]) + up_bias_ref[:, lanes]
        square = upper * upper
        bend = jnp.tanh(GELU_C * upper * (1.0 + 0.044715 * square))
        half = 0.5 * (1.0 + bend)
        hidden = (upper * half).astype(BF16)
        hidden_ref[0, :, lanes] = hidden
        slope = half + 0.5 * GELU_C * upper * (1.0 - bend * bend) * (1.0 + 0.134145 * square)
        grad_upper = (matmul(cot_ref[0], w_down_ref[lanes, :], NT) * slope).astype(BF16)
        grad_upper_ref[0, :, lanes] = grad_upper
        up_sum_ref[0:1, lanes] += jnp.sum(grad_upper.astype(F32), axis=0, keepdims=True)
        layer_sc[...] += matmul(hidden, w_down_ref[lanes, :])
        back_sc[...] += matmul(grad_upper, w_up_ref[:, lanes], NT)

    layer_ref[0] = layer_sc[...].astype(BF16)
    back = back_sc[...]
    scaled = back * gain
    grad_out = cot_ref[0].astype(F32)
    grad_resid = grad_out + root * (
        scaled
        - jnp.mean(scaled, axis=-1, keepdims=True)
        - normed * jnp.mean(scaled * normed, axis=-1, keepdims=True)
    )
    grad_resid_ref[0] = grad_resid
    grad_attn = grad_resid.astype(BF16)
    grad_attn_ref[0] = grad_attn
    for w_ref, grad_mixed_ref in zip(w_out_refs, grad_mixed_refs):
        grad_mixed_ref[0] = matmul(grad_attn, w_ref[...], NT).astype(BF16)
    sums_ref[0:1, :] += jnp.sum(grad_attn.astype(F32), axis=0, keepdims=True)
    sums_ref[1:2, :] += jnp.sum(back * normed, axis=0, keepdims=True)
    sums_ref[2:3, :] += jnp.sum(back, axis=0, keepdims=True)
    sums_ref[3:4, :] += jnp.sum(grad_out, axis=0, keepdims=True)


def feed(mixed, x, cotangent, w_out, part, w_up, w_down, vectors, up_bias):
    parts = len(mixed)
    rows, size, model = x.shape
    width = mixed[0].shape[2]
    wide = w_up.shape[1]
    still = lambda i, p: (0, 0)
    step = lambda i, p: (i, 0, 0)
    once = pl.Buffered(1)
    slab = pl.BlockSpec((1, size, model), step)
    head_slab = pl.BlockSpec((1, size, width), step)
    wide_slab = pl.BlockSpec((1, size, wide), step)
    vector = pl.BlockSpec((1, model), still)
    w_out_specs = [
        pl.BlockSpec((width, model), lambda i, p, s=s: (p[0] ^ s, 0), pipeline_mode=once)
        for s in range(parts)
    ]

    def body(p_ref, *refs):
        feed_kernel(parts, wide // model, *refs)

    shape = jax.ShapeDtypeStruct
    out = pl.pallas_call(
        body,
        grid_spec=pltpu.PrefetchScalarGridSpec(
            num_scalar_prefetch=1,
            grid=(rows,),
            in_specs=[head_slab] * parts
            + [slab, slab]
            + w_out_specs
            + [
                pl.BlockSpec(w_up.shape, still, pipeline_mode=once),
                pl.BlockSpec(w_down.shape, still, pipeline_mode=once),
                vector,
                vector,
                vector,
                pl.BlockSpec((1, wide), still),
                vector,
            ],
            out_specs=[slab, wide_slab, wide_slab, slab, slab, slab]
            + [head_slab] * parts
            + [pl.BlockSpec((8, model), still), pl.BlockSpec((8, wide), still)],
            scratch_shapes=[
                pltpu.VMEM((size, model), F32),
                pltpu.VMEM((size, model), F32),
            ],
        ),
        out_shape=[
            shape((rows, size, model), BF16),
            shape((rows, size, wide), BF16),
            shape((rows, size, wide), BF16),
            shape((rows, size, model), BF16),
            shape((rows, size, model), F32),
            shape((rows, size, model), BF16),
        ]
        + [shape((rows, size, width), BF16)] * parts
        + [shape((8, model), F32), shape((8, wide), F32)],
        compiler_params=pltpu.CompilerParams(
            dimension_semantics=("arbitrary",), vmem_limit_bytes=VMEM_LIMIT
        ),
        cost_estimate=pl.CostEstimate(
            flops=2 * rows * size * model * (4 * wide + 2 * model),
            transcendentals=rows * size * wide,
            bytes_accessed=rows * size * (4 * wide + 16 * model),
        ),
        name="feed",
    )(
        part.reshape(1), *mixed, x, cotangent, *([w_out] * parts), w_up, w_down,
        vectors["out_bias"], vectors["gain"], vectors["shift"], up_bias, vectors["down_bias"],
    )
    return out[:6], out[6 : 6 + parts], out[6 + parts], out[7 + parts]


def join_kernel(sources, moves, bit_ref, *refs):
    mine_refs, other_refs, out_refs = refs[:sources], refs[sources : 2 * sources], refs[2 * sources :]
    mine = pl.program_id(0) == bit_ref[0]
    for source, begin, out, place, count in moves:
        lanes = slice(begin, begin + count)
        out_refs[out][:, place : place + count] = jnp.where(
            mine, mine_refs[source][:, lanes], other_refs[source][:, lanes]
        ).astype(F32)


def join(mine, other, bit, moves, widths):
    count = mine[0].shape[0]
    largest = 384 if sum(widths) <= 1024 else 192
    tall = next(t for t in (largest, 192, 96, 48, count) if count % t == 0)
    steps = count // tall

    def mine_map(h, i, b):
        return jnp.where(h == b[0], i, jnp.where(h < b[0], 0, steps - 1)), 0

    def other_map(h, i, b):
        return jnp.where(h != b[0], i, jnp.where(h < 1 - b[0], 0, steps - 1)), 0

    columns = sum(widths)
    return pl.pallas_call(
        functools.partial(join_kernel, len(mine), moves),
        grid_spec=pltpu.PrefetchScalarGridSpec(
            num_scalar_prefetch=1,
            grid=(2, steps),
            in_specs=[pl.BlockSpec((tall, m.shape[1]), mine_map) for m in mine]
            + [pl.BlockSpec((tall, m.shape[1]), other_map) for m in mine],
            out_specs=[
                pl.BlockSpec((tall, n), lambda h, i, b: (h * steps + i, 0)) for n in widths
            ],
        ),
        out_shape=[jax.ShapeDtypeStruct((2 * count, n), F32) for n in widths],
        compiler_params=pltpu.CompilerParams(
            dimension_semantics=("arbitrary", "arbitrary"), vmem_limit_bytes=VMEM_LIMIT
        ),
        cost_estimate=pl.CostEstimate(
            flops=2 * count * columns, transcendentals=0, bytes_accessed=12 * count * columns
        ),
        name="join",
    )(bit.reshape(1), *mine, *other)


def spread_kernel(parts, spans, part_ref, *refs):
    out_ref, refs = refs[-1], refs[:-1]
    part = part_ref[0]
    begin = 0
    for which in range(3):
        for p in range(parts):
            for g, span in enumerate(spans):
                piece = None
                for s in range(parts):
                    here = refs[s * len(spans) + g][:, which * span : (which + 1) * span]
                    piece = here if piece is None else jnp.where((part ^ p) == s, here, piece)
                out_ref[:, begin : begin + span] = piece.astype(F32)
                begin += span


def spread(pieces, part, spans):
    parts = len(pieces)
    count = pieces[0][0].shape[0]
    tall = next(t for t in (192, 96, 48, count) if count % t == 0)
    flat = [p for piece in pieces for p in piece]
    columns = 3 * parts * sum(spans)
    return pl.pallas_call(
        functools.partial(spread_kernel, parts, spans),
        grid_spec=pltpu.PrefetchScalarGridSpec(
            num_scalar_prefetch=1,
            grid=(count // tall,),
            in_specs=[pl.BlockSpec((tall, p.shape[1]), lambda i, b: (i, 0)) for p in flat],
            out_specs=pl.BlockSpec((tall, columns), lambda i, b: (i, 0)),
        ),
        out_shape=jax.ShapeDtypeStruct((count, columns), F32),
        compiler_params=pltpu.CompilerParams(
            dimension_semantics=("arbitrary",), vmem_limit_bytes=VMEM_LIMIT
        ),
        cost_estimate=pl.CostEstimate(
            flops=count * columns, transcendentals=0, bytes_accessed=6 * count * columns
        ),
        name="spread",
    )(part.reshape(1), *flat)


def layout_kernel(owner_ref, sizes_ref, prefixes_ref, lens_ref, padding_ref, info_ref, flags_ref):
    blocks, _, size = info_ref.shape
    groups, slots = lens_ref.shape[1:]
    row = owner_ref[0]
    places = lax.broadcasted_iota(jnp.int32, (blocks, size), 0) * size + lax.broadcasted_iota(
        jnp.int32, (blocks, size), 1
    )
    filled = blocks * size - padding_ref[row]
    prefix_start = jnp.full((blocks, size), filled, jnp.int32)
    prefix_end, own_start = prefix_start, prefix_start
    start = jnp.int32(0)
    for g in range(groups):
        body = start + prefixes_ref[row, g]
        end = jnp.int32(0)
        base = jnp.zeros((blocks, size), jnp.int32)
        for j in range(slots):
            end = end + jnp.where(j < sizes_ref[row, g], lens_ref[row, g, j], 0)
            base = jnp.where(places - body >= end, end, base)
        stop = body + end
        member = (places >= start) & (places < stop) & (places < filled)
        solution = places >= body
        prefix_start = jnp.where(member, start, prefix_start)
        prefix_end = jnp.where(member, jnp.where(solution, body, start), prefix_end)
        own_start = jnp.where(member, jnp.where(solution, body + base, start), own_start)
        start = stop
    info_ref[...] = jnp.zeros_like(info_ref)
    for i, values in enumerate((prefix_start, prefix_end, own_start, places)):
        info_ref[:, i, :] = values
    lane = lax.broadcasted_iota(jnp.int32, flags_ref.shape, 1)
    flags = jnp.zeros(flags_ref.shape, jnp.int32)
    for j in range(blocks):
        low, high = j * size, (j + 1) * size
        need = (jnp.maximum(prefix_start, low) < jnp.minimum(prefix_end, high)) | (
            jnp.maximum(own_start, low) < jnp.minimum(places + 1, high)
        )
        any_need = jnp.max(jnp.where(need, 1, 0), axis=1, keepdims=True)
        flags = jnp.where(lane == j, any_need, flags)
    flags_ref[...] = flags


def row_layout(owner, sizes, prefixes, lens, padding, blocks, size):
    scalars = pl.BlockSpec(memory_space=pltpu.SMEM)
    info, flags = pl.pallas_call(
        layout_kernel,
        in_specs=[scalars] * 5,
        out_shape=(
            jax.ShapeDtypeStruct((blocks, 8, size), jnp.int32),
            jax.ShapeDtypeStruct((blocks, 128), jnp.int32),
        ),
        name="row_layout",
    )(owner.reshape(1).astype(jnp.int32), sizes, prefixes, lens, padding)
    return info, flags[:, :blocks].reshape(-1)


def swap(values, axis, mask):
    count = lax.axis_size(axis)
    return lax.ppermute(values, axis, [(i, i ^ mask) for i in range(count)])


def bits(count):
    return [1 << b for b in range(count.bit_length() - 1)]


def take(values, index):
    return lax.dynamic_index_in_dim(values, index, 0, keepdims=False)


def halve(values, step):
    axis, mask, bit = step
    two = values.reshape(2, values.shape[0] // 2, *values.shape[1:])
    arrived = swap(take(two, 1 - bit), axis, mask)
    return (take(two, bit).astype(F32) + arrived.astype(F32)).astype(values.dtype)


def double(values, step):
    axis, mask, bit = step
    arrived = swap(values, axis, mask)
    first = jnp.where(bit == 0, values, arrived)
    second = jnp.where(bit == 0, arrived, values)
    return jnp.concatenate([first, second], axis=0)


def gate(values, waits):
    count = len(values)
    anywhere = pl.BlockSpec(memory_space=pl.ANY)

    def body(*refs):
        pass

    out = pl.pallas_call(
        body,
        in_specs=[anywhere] * (count + len(waits)),
        out_specs=[anywhere] * count,
        out_shape=[jax.ShapeDtypeStruct(v.shape, v.dtype) for v in values],
        input_output_aliases={i: i for i in range(count)},
        name="gate",
    )(*values, *waits)
    return list(out)


class Chain:
    def __init__(self, values, down, up):
        self.values = values
        self.left = [(halve, step) for step in down] + [(double, step) for step in up]

    def advance(self):
        if self.left:
            move, step = self.left.pop(0)
            self.values = move(self.values, step)


def close(chains, *others):
    tied, others = lax.optimization_barrier(([c.values for c in chains], others))
    for chain, values in zip(chains, tied):
        chain.values = values
    return others


def per_device(
    row_axis,
    tokens,
    segment_ids,
    group_sizes,
    prefix_lens,
    solution_lens,
    padding_counts,
    attn_gain,
    attn_shift,
    w_qkv,
    query_bias,
    value_bias,
    w_out,
    out_bias,
    ffn_gain,
    ffn_shift,
    w_up,
    up_bias,
    w_down,
    down_bias,
    cotangent,
):
    rows, size, model = tokens.shape
    devices = lax.axis_size("pos")
    parts = devices // rows
    blocks = devices
    heads = model // HEAD_DIM // parts
    width = heads * HEAD_DIM
    place = lax.axis_index("pos")
    owner, part = place // parts, place % parts

    def bring(values):
        return jnp.stack(
            [
                swap(take(values, owner ^ m), "pos", m * parts) if m else take(values, owner)
                for m in range(rows)
            ]
        )

    def send_back(values, m):
        return swap(values[m], "pos", m * parts) if m else values[m]

    def arrange(slabs):
        out = jnp.zeros((rows, *slabs[0].shape), slabs[0].dtype)
        for m, slab in enumerate(slabs):
            out = lax.dynamic_update_index_in_dim(out, slab, owner ^ m, 0)
        return out

    info, flags = row_layout(
        owner, group_sizes, prefix_lens, solution_lens, padding_counts, blocks, size
    )
    order = jnp.arange(blocks, dtype=jnp.int32)
    phys = (((order % parts) ^ part) * rows + ((order // parts) ^ owner)).astype(jnp.int32)

    def my_columns(start, first=0, count=None):
        begin = start * model + part * width + first
        return lax.dynamic_slice_in_dim(w_qkv, begin, count or width, 1)

    def as_row(vector):
        return vector.astype(F32).reshape(1, -1)

    groups = [(0, 4), (4, 2)] if heads == 6 else [(0, heads)]
    spans = [count * HEAD_DIM for _, count in groups]
    w_mine = jnp.concatenate([my_columns(n) for n in range(3)], axis=1)
    w_groups = [
        jnp.concatenate([my_columns(n, h * HEAD_DIM, c * HEAD_DIM) for n in range(3)], axis=1)
        for h, c in groups
    ]
    bias_q = lax.dynamic_slice_in_dim(query_bias, part * width, width, 0)
    bias_v = lax.dynamic_slice_in_dim(value_bias, part * width, width, 0)

    mine = bring(tokens)
    row = jnp.concatenate([mine] + [swap(mine, "pos", s) for s in range(1, parts)], axis=0)
    cotangent, row = lax.optimization_barrier((cotangent, row))
    own_cotangent = bring(cotangent)
    act_one, query_t, key, key_t, value, value_t = project(
        row, as_row(attn_gain), as_row(attn_shift), w_mine, as_row(bias_q), as_row(bias_v)
    )
    mixed_all, out_t, lse = attention_forward(
        phys, flags, query_t, key, value_t, info, heads
    )
    mixed_all, own_cotangent = lax.optimization_barrier((mixed_all, own_cotangent))
    mixed_parts = []
    for s in range(parts):
        piece = mixed_all[s * rows : (s + 1) * rows]
        mixed_parts.append(swap(piece, "pos", s) if s else piece)

    (act_two, hidden, grad_upper, layer_out, grad_resid, grad_attn), grad_mixed, sums, up_sum = feed(
        mixed_parts, mine, own_cotangent, w_out, part, w_up, w_down,
        {
            "out_bias": as_row(out_bias),
            "gain": as_row(ffn_gain),
            "shift": as_row(ffn_shift),
            "down_bias": as_row(down_bias),
        },
        as_row(up_bias),
    )
    local = rows * size

    def flat(values):
        return values.reshape(-1, values.shape[-1])

    row_place = lax.axis_index(row_axis)
    row_steps = [(row_axis, m, (row_place // m) % 2) for m in bits(lax.axis_size(row_axis))]
    own_steps = [("pos", m * parts, (owner // m) % 2) for m in bits(rows)]
    part_steps = [("pos", m, (part // m) % 2) for m in bits(parts)]
    turning, last = own_steps + row_steps[:1], row_steps[1:]

    def order(turn):
        turn %= len(turning)
        return turning[turn:] + turning[:turn] + last

    def chain(values, turn, parted=True):
        down = order(turn)
        up = down[::-1] + (part_steps[:0:-1] if parted else [])
        return Chain(values, (part_steps if parted else []) + down, up)

    wide = w_up.shape[1]
    cut = wide * 2 // 3
    near = [m for m in range(1, rows) if m & (m - 1) == 0]
    far = [m for m in range(1, rows) if m & (m - 1)]

    received = [g if s == 0 else swap(g, "pos", s) for s, g in enumerate(grad_mixed)]
    layer_slabs = {m: send_back(layer_out, m) for m in [0] + near}
    down = chain(matmul(flat(hidden), flat(own_cotangent), TN).astype(BF16), 0)
    received, layer_slabs, layer_out, grad_upper = close(
        [down], received, layer_slabs, layer_out, grad_upper
    )
    down.advance()
    layer_slabs.update({m: send_back(layer_out, m) for m in far})
    stacked = jnp.stack(mixed_parts)
    mixed = jnp.concatenate([flat(take(stacked, g ^ part)) for g in range(parts)], axis=1)
    grad_up_flat = flat(grad_upper)
    up_one = chain(matmul(flat(act_two), grad_up_flat[:, :cut], TN).astype(BF16), 1)
    up_two = chain(
        jnp.concatenate(
            [
                matmul(flat(act_two), grad_up_flat[:, cut:], TN).astype(BF16),
                matmul(mixed, flat(grad_attn), TN).astype(BF16),
            ],
            axis=1,
        ),
        2,
    )
    chains = [down, up_one, up_two]
    received, layer_slabs = close(chains, received, layer_slabs)
    layer_home = arrange([layer_slabs[m] for m in range(rows)])
    up_one.advance()
    up_two.advance()
    for _ in part_steps[1:]:
        for c in chains:
            c.advance()
    grad_t = jnp.concatenate(received, axis=0).transpose(0, 2, 1)
    grad_t, layer_home = close(chains, grad_t, layer_home)

    grads, shares = [], []
    for h, count in groups:
        for c in chains + shares:
            c.advance()
        grad = attention_backward(
            phys, flags, query_t, grad_t, out_t, lse, info, key, key_t, value, count, h
        )
        grad, grad_t = close(chains + shares, grad, grad_t)
        grads.append(grad)
        if len(grads) == len(groups):
            grads = gate(grads, [c.values for c in chains + shares])
            grad = grads[-1]
        shares.append(chain(matmul(flat(act_one), flat(grad), TN).astype(BF16), 0, False))
        if len(grads) < len(groups):
            (grad_t,) = close(chains + shares, grad_t)

    def column_sums(which):
        return jnp.concatenate(
            [
                jnp.sum(flat(g)[:, which * n : (which + 1) * n].astype(F32), axis=0)
                for g, n in zip(grads, spans)
            ]
        )

    def placed(values):
        return lax.dynamic_update_slice_in_dim(jnp.zeros((model,), F32), values, part * width, 0)

    for c in chains + shares:
        c.advance()
    grad_act = sum(matmul(flat(g), w, NT) for g, w in zip(grads, w_groups))
    grad_act_own = grad_act[:local]
    for s in range(1, parts):
        sent = grad_act[s * local : (s + 1) * local].astype(BF16)
        grad_act_own = grad_act_own + swap(sent, "pos", s).astype(F32)
    sums_q, sums_v = placed(column_sums(0)), placed(column_sums(2))
    grad_act_own, sums_q, sums_v = close(chains + shares, grad_act_own, sums_q, sums_v)

    for c in chains + shares:
        c.advance()
    inputs = flat(mine).astype(F32)
    _, norm_one_pull = jax.vjp(layer_norm, inputs, attn_gain.astype(F32), attn_shift.astype(F32))
    grad_input_norm, grad_attn_gain, grad_attn_shift = norm_one_pull(grad_act_own)
    tokens_grad = (flat(grad_resid) + grad_input_norm).astype(BF16).reshape(rows, size, model)
    small = jnp.concatenate(
        [
            grad_attn_gain,
            grad_attn_shift,
            sums_q,
            sums_v,
            sums[:4].reshape(-1),
            up_sum[0],
        ]
    )
    tokens_grad, small = close(chains + shares, tokens_grad, small)

    small_steps = part_steps + own_steps + row_steps
    token_slabs = {}
    waves = [[0] + near, far]
    while any(c.left for c in chains):
        for c in chains + shares:
            c.advance()
        if small_steps:
            axis, mask, _ = small_steps.pop(0)
            small = small + swap(small, axis, mask)
        if waves:
            token_slabs.update({m: send_back(tokens_grad, m) for m in waves.pop(0)})
        small, token_slabs, tokens_grad = close(chains + shares, small, token_slabs, tokens_grad)

    axis, mask, bit = part_steps[0]
    others = [swap(c.values, axis, mask) for c in chains]
    for c in shares:
        c.advance()
    (sum_w_down,) = join([down.values], others[:1], bit, ((0, 0, 0, 0, model),), (model,))
    sum_w_up, sum_w_out = join(
        [up_one.values, up_two.values],
        others[1:],
        bit,
        ((0, 0, 0, 0, cut), (1, 0, 0, cut, wide - cut), (1, wide - cut, 1, 0, model)),
        (wide, model),
    )
    tokens_home = arrange([token_slabs[m] for m in range(rows)])
    while any(c.left for c in shares):
        for c in shares:
            c.advance()
    for axis, mask, _ in small_steps:
        small = small + swap(small, axis, mask)
    summed = gate([c.values for c in shares], [sum_w_down, sum_w_up, sum_w_out])
    pieces = [summed] + [[swap(g, "pos", s) for g in summed] for s in range(1, parts)]
    sum_w_qkv = spread(pieces, part, spans)

    vectors = small[: 8 * model].reshape(8, model)
    return (
        layer_home,
        tokens_home,
        vectors[0],
        vectors[1],
        sum_w_qkv,
        vectors[2],
        vectors[3],
        sum_w_out,
        vectors[4],
        vectors[5],
        vectors[6],
        sum_w_up,
        small[8 * model :],
        sum_w_down,
        vectors[7],
    )


def solution(mesh):
    in_specs = (
        P("rows", "pos", None),
        P("rows", "pos"),
        P("rows", None),
        P("rows", None),
        P("rows", None, None),
        P("rows"),
        *([P()] * 13),
        P("rows", "pos", None),
    )
    out_specs = (P("rows", "pos", None), P("rows", "pos", None), *([P()] * 13))
    return jax.shard_map(
        functools.partial(per_device, "rows"),
        mesh=mesh,
        in_specs=in_specs,
        out_specs=out_specs,
        check_vma=False,
    )
```

```python
import functools

import jax
import jax.numpy as jnp
from jax import lax
from jax.experimental import pallas as pl
from jax.experimental.pallas import tpu as pltpu
from jax.sharding import PartitionSpec as P

HEAD_DIM = 64
EPS = 1e-05
NEG = -1e30
GELU_C = 0.7978845608028654
F32 = jnp.float32
BF16 = jnp.bfloat16
VMEM_LIMIT = 60 * 1024 * 1024
FREE = pl.CostEstimate(flops=0, transcendentals=0, bytes_accessed=0)
NT = (((1,), (1,)), ((), ()))
TN = (((0,), (0,)), ((), ()))


def layer_norm(values, gain, shift):
    center = values - jnp.mean(values, axis=-1, keepdims=True)
    spread = jnp.mean(center * center, axis=-1, keepdims=True)
    return center * lax.rsqrt(spread + EPS) * gain + shift


def gelu_tanh(values):
    return 0.5 * values * (1.0 + jnp.tanh(GELU_C * (values + 0.044715 * values * values * values)))


def matmul(left, right, dims=(((1,), (0,)), ((), ()))):
    return lax.dot_general(left, right, dims, preferred_element_type=F32)


def head_pairs(heads):
    return [(h // 2, min(128, heads * HEAD_DIM - (h // 2) * 128)) for h in range(heads)]


def mask_bias(info_ref, key_start, size):
    prefix_start, prefix_end = info_ref[0, 0:1, :], info_ref[0, 1:2, :]
    own_start, query_place = info_ref[0, 2:3, :], info_ref[0, 3:4, :]
    key_place = key_start + lax.broadcasted_iota(jnp.int32, (size, size), 0)
    allowed = ((key_place >= prefix_start) & (key_place < prefix_end)) | (
        (key_place >= own_start) & (key_place <= query_place)
    )
    return jnp.where(allowed, 0.0, NEG).astype(F32)


def fill_padded(source_ref, target_ref, heads):
    for h, (pair, width) in enumerate(head_pairs(heads)):
        rows = source_ref[0, pair * 128 : pair * 128 + width, :]
        if width == 128:
            keep = (lax.broadcasted_iota(jnp.int32, rows.shape, 0) // HEAD_DIM) == (h % 2)
            rows = jnp.where(keep, rows, jnp.zeros_like(rows))
        target_ref[h, 0:width, :] = rows


def forward_kernel(
    heads, blocks, phys_ref, flag_ref, query_t_ref, key_ref, value_t_ref, info_ref,
    mixed_ref, out_t_ref, lse_ref, bias_sc, top_sc, total_sc, acc_sc, query_sc,
):
    size = query_t_ref.shape[2]
    i = pl.program_id(0)
    fill_padded(query_t_ref, query_sc, heads)
    top_sc[...] = jnp.full_like(top_sc, NEG)
    total_sc[...] = jnp.zeros_like(total_sc)
    acc_sc[...] = jnp.zeros_like(acc_sc)

    @pl.loop(0, i + 1)
    def _(j):
        @pl.when(flag_ref[i * blocks + j] > 0)
        def _():
            at = phys_ref[j]
            bias_sc[...] = mask_bias(info_ref, j * size, size)
            for h, (pair, width) in enumerate(head_pairs(heads)):
                rows = slice(h * HEAD_DIM, (h + 1) * HEAD_DIM)
                scores = (
                    matmul(key_ref[at, :, pair * 128 : pair * 128 + width], query_sc[h, 0:width, :])
                    + bias_sc[...]
                )
                old = top_sc[h]
                top = jnp.maximum(old, jnp.max(scores, axis=0, keepdims=True))
                shrink = jnp.exp(old - top)
                weights = jnp.exp(scores - top)
                total_sc[h] = shrink * total_sc[h] + jnp.sum(weights, axis=0, keepdims=True)
                top_sc[h] = top
                acc_sc[rows, :] = shrink * acc_sc[rows, :] + matmul(
                    value_t_ref[at, rows, :], weights.astype(BF16)
                )

    for h in range(heads):
        rows = slice(h * HEAD_DIM, (h + 1) * HEAD_DIM)
        out_t_ref[0, rows, :] = acc_sc[rows, :] / total_sc[h]
        lse_ref[0, h : h + 1, :] = top_sc[h] + jnp.log(total_sc[h])
    mixed_ref[0] = out_t_ref[0].T.astype(BF16)


def attention_forward(phys, flags, query_t, key, value_t, info, heads):
    blocks, width, size = query_t.shape
    lse_rows = -(-heads // 8) * 8
    whole = pl.Buffered(1)
    spec = pltpu.PrefetchScalarGridSpec(
        num_scalar_prefetch=2,
        grid=(blocks,),
        in_specs=[
            pl.BlockSpec((1, width, size), lambda i, p, f: (p[i], 0, 0)),
            pl.BlockSpec((blocks, size, width), lambda i, p, f: (0, 0, 0), pipeline_mode=whole),
            pl.BlockSpec((blocks, width, size), lambda i, p, f: (0, 0, 0), pipeline_mode=whole),
            pl.BlockSpec((1, 8, size), lambda i, p, f: (i, 0, 0)),
        ],
        out_specs=[
            pl.BlockSpec((1, size, width), lambda i, p, f: (p[i], 0, 0)),
            pl.BlockSpec((1, width, size), lambda i, p, f: (p[i], 0, 0)),
            pl.BlockSpec((1, lse_rows, size), lambda i, p, f: (p[i], 0, 0)),
        ],
        scratch_shapes=[
            pltpu.VMEM((size, size), F32),
            pltpu.VMEM((heads, 1, size), F32),
            pltpu.VMEM((heads, 1, size), F32),
            pltpu.VMEM((width, size), F32),
            pltpu.VMEM((heads, 128, size), BF16),
        ],
    )
    pairs = heads * blocks * (blocks + 1) // 2 * size * size
    return pl.pallas_call(
        functools.partial(forward_kernel, heads, blocks),
        grid_spec=spec,
        out_shape=(
            jax.ShapeDtypeStruct((blocks, size, width), BF16),
            jax.ShapeDtypeStruct((blocks, width, size), F32),
            jax.ShapeDtypeStruct((blocks, lse_rows, size), F32),
        ),
        compiler_params=pltpu.CompilerParams(
            dimension_semantics=("arbitrary",), vmem_limit_bytes=VMEM_LIMIT
        ),
        cost_estimate=pl.CostEstimate(
            flops=pairs * 4 * 128, transcendentals=pairs, bytes_accessed=blocks * size * width * 16
        ),
        name="attention_forward",
    )(phys, flags, query_t, key, value_t, info)


def backward_kernel(
    heads, first, blocks, phys_ref, flag_ref, query_t_ref, grad_t_ref, out_t_ref, lse_ref, info_ref,
    key_ref, key_t_ref, value_ref, grads_ref,
    bias_sc, query_grad_sc, key_grad_sc, value_grad_sc, query_sc, grad_sc, delta_sc,
):
    size = query_t_ref.shape[2]
    span = heads * HEAD_DIM
    i = pl.program_id(0)

    @pl.when(i == 0)
    def _():
        key_grad_sc[...] = jnp.zeros_like(key_grad_sc)
        value_grad_sc[...] = jnp.zeros_like(value_grad_sc)

    fill_padded(query_t_ref, query_sc, heads)
    fill_padded(grad_t_ref, grad_sc, heads)
    query_grad_sc[...] = jnp.zeros_like(query_grad_sc)
    for h in range(heads):
        rows = slice(h * HEAD_DIM, (h + 1) * HEAD_DIM)
        delta_sc[h] = jnp.sum(
            grad_t_ref[0, rows, :].astype(F32) * out_t_ref[0, rows, :], axis=0, keepdims=True
        )

    @pl.loop(0, i + 1)
    def _(j):
        @pl.when(flag_ref[i * blocks + j] > 0)
        def _():
            at = phys_ref[j]
            bias_sc[...] = mask_bias(info_ref, j * size, size)
            for h, (pair, width) in enumerate(head_pairs(heads)):
                rows = slice(h * HEAD_DIM, (h + 1) * HEAD_DIM)
                lanes = slice(pair * 128, pair * 128 + width)
                scores = matmul(key_ref[at, :, lanes], query_sc[h, 0:width, :]) + bias_sc[...]
                probs = jnp.exp(scores - lse_ref[0, first + h : first + h + 1, :])
                grad_probs = matmul(value_ref[at, :, lanes], grad_sc[h, 0:width, :])
                grad_scores = (probs * (grad_probs - delta_sc[h])).astype(BF16)
                query_grad_sc[rows, :] += matmul(key_t_ref[at, rows, :], grad_scores)
                value_grad_sc[at, rows, :] += matmul(
                    grad_t_ref[0, rows, :], probs.astype(BF16), NT
                )
                key_grad_sc[at, rows, :] += matmul(query_t_ref[0, rows, :], grad_scores, NT)

    grads_ref[phys_ref[i], :, 0:span] = (query_grad_sc[...] * 0.125).T.astype(BF16)

    @pl.when(i == blocks - 1)
    def _():
        for block in range(blocks):
            grads_ref[block, :, span : 2 * span] = key_grad_sc[block].T.astype(BF16)
            grads_ref[block, :, 2 * span :] = value_grad_sc[block].T.astype(BF16)


def attention_backward(
    phys, flags, query_t, grad_t, out_t, lse, info, key, key_t, value, heads, first
):
    blocks, _, size = query_t.shape
    span = heads * HEAD_DIM
    c = first // heads
    moving_t = pl.BlockSpec((1, span, size), lambda i, p, f: (p[i], c, 0))
    whole = pl.BlockSpec(
        (blocks, size, span), lambda i, p, f: (0, 0, c), pipeline_mode=pl.Buffered(1)
    )
    whole_t = pl.BlockSpec(
        (blocks, span, size), lambda i, p, f: (0, c, 0), pipeline_mode=pl.Buffered(1)
    )
    spec = pltpu.PrefetchScalarGridSpec(
        num_scalar_prefetch=2,
        grid=(blocks,),
        in_specs=[
            moving_t,
            moving_t,
            moving_t,
            pl.BlockSpec((1, lse.shape[1], size), lambda i, p, f: (p[i], 0, 0)),
            pl.BlockSpec((1, 8, size), lambda i, p, f: (i, 0, 0)),
            whole,
            whole_t,
            whole,
        ],
        out_specs=pl.BlockSpec(
            (blocks, size, 3 * span), lambda i, p, f: (0, 0, 0), pipeline_mode=pl.Buffered(1)
        ),
        scratch_shapes=[
            pltpu.VMEM((size, size), F32),
            pltpu.VMEM((span, size), F32),
            pltpu.VMEM((blocks, span, size), F32),
            pltpu.VMEM((blocks, span, size), F32),
            pltpu.VMEM((heads, 128, size), BF16),
            pltpu.VMEM((heads, 128, size), BF16),
            pltpu.VMEM((heads, 1, size), F32),
        ],
    )
    pairs = heads * blocks * (blocks + 1) // 2 * size * size
    return pl.pallas_call(
        functools.partial(backward_kernel, heads, first, blocks),
        grid_spec=spec,
        out_shape=jax.ShapeDtypeStruct((blocks, size, 3 * span), BF16),
        compiler_params=pltpu.CompilerParams(
            dimension_semantics=("arbitrary",), vmem_limit_bytes=VMEM_LIMIT
        ),
        cost_estimate=pl.CostEstimate(
            flops=pairs * 10 * 128, transcendentals=pairs, bytes_accessed=blocks * size * span * 20
        ),
        name="attention_backward",
    )(phys, flags, query_t, grad_t, out_t, lse, info, key, key_t, value)


def project_kernel(
    width, x_ref, gain_ref, shift_ref, w_ref, bias_q_ref, bias_v_ref,
    act_ref, query_t_ref, key_ref, key_t_ref, value_ref, value_t_ref,
):
    act = layer_norm(x_ref[0].astype(F32), gain_ref[...], shift_ref[...]).astype(BF16)
    act_ref[0] = act
    query = (matmul(act, w_ref[:, :width]) + bias_q_ref[...]).astype(BF16).astype(F32) * 0.125
    query_t_ref[0] = query.T.astype(BF16)
    key = matmul(act, w_ref[:, width : 2 * width])
    key_ref[0] = key.astype(BF16)
    key_t_ref[0] = key.T.astype(BF16)
    value = matmul(act, w_ref[:, 2 * width :]) + bias_v_ref[...]
    value_ref[0] = value.astype(BF16)
    value_t_ref[0] = value.T.astype(BF16)


def project(x, gain, shift, weight, bias_q, bias_v):
    blocks, size, model = x.shape
    width = bias_q.shape[1]
    still = lambda i: (0, 0)
    step = lambda i: (i, 0, 0)
    straight, turned = (
        jax.ShapeDtypeStruct((blocks, size, width), BF16),
        jax.ShapeDtypeStruct((blocks, width, size), BF16),
    )
    wide, tall = pl.BlockSpec((1, size, width), step), pl.BlockSpec((1, width, size), step)
    return pl.pallas_call(
        functools.partial(project_kernel, width),
        grid=(blocks,),
        in_specs=[
            pl.BlockSpec((1, size, model), step),
            pl.BlockSpec((1, model), still),
            pl.BlockSpec((1, model), still),
            pl.BlockSpec(weight.shape, still, pipeline_mode=pl.Buffered(1)),
            pl.BlockSpec((1, width), still),
            pl.BlockSpec((1, width), still),
        ],
        out_specs=[pl.BlockSpec((1, size, model), step), tall, wide, tall, wide, tall],
        out_shape=(
            jax.ShapeDtypeStruct((blocks, size, model), BF16),
            turned, straight, turned, straight, turned,
        ),
        compiler_params=pltpu.CompilerParams(
            dimension_semantics=("arbitrary",), vmem_limit_bytes=VMEM_LIMIT
        ),
        cost_estimate=pl.CostEstimate(
            flops=2 * blocks * size * model * 3 * width,
            transcendentals=blocks * size,
            bytes_accessed=blocks * size * (4 * model + 10 * width),
        ),
        name="project",
    )(x, gain, shift, weight, bias_q, bias_v)


def feed_kernel(
    parts, pieces, *refs
):
    mixed_refs, refs = refs[:parts], refs[parts:]
    x_ref, cot_ref, refs = refs[0], refs[1], refs[2:]
    w_out_refs, refs = refs[:parts], refs[parts:]
    (w_up_ref, w_down_ref, out_bias_ref, gain_ref, shift_ref, up_bias_ref, down_bias_ref), refs = (
        refs[:7], refs[7:],
    )
    act_ref, hidden_ref, grad_upper_ref, layer_ref, grad_resid_ref, grad_attn_ref = refs[:6]
    refs = refs[6:]
    grad_mixed_refs, refs = refs[:parts], refs[parts:]
    sums_ref, up_sum_ref, layer_sc, back_sc = refs
    first = pl.program_id(0) == 0

    @pl.when(first)
    def _():
        sums_ref[...] = jnp.zeros_like(sums_ref)
        up_sum_ref[...] = jnp.zeros_like(up_sum_ref)

    attn = out_bias_ref[...]
    for mixed_ref, w_ref in zip(mixed_refs, w_out_refs):
        attn = attn + matmul(mixed_ref[0], w_ref[...])
    resid = x_ref[0].astype(F32) + attn
    center = resid - jnp.mean(resid, axis=-1, keepdims=True)
    root = lax.rsqrt(jnp.mean(center * center, axis=-1, keepdims=True) + EPS)
    normed = center * root
    gain = gain_ref[...]
    act_ref[0] = (normed * gain + shift_ref[...]).astype(BF16)
    layer_sc[...] = resid + down_bias_ref[...]
    back_sc[...] = jnp.zeros_like(back_sc)
    span = w_up_ref.shape[1] // pieces

    for c in range(pieces):
        lanes = slice(c * span, (c + 1) * span)
        upper = matmul(act_ref[0], w_up_ref[:, lanes]) + up_bias_ref[:, lanes]
        square = upper * upper
        bend = jnp.tanh(GELU_C * upper * (1.0 + 0.044715 * square))
        half = 0.5 * (1.0 + bend)
        hidden = (upper * half).astype(BF16)
        hidden_ref[0, :, lanes] = hidden
        slope = half + 0.5 * GELU_C * upper * (1.0 - bend * bend) * (1.0 + 0.134145 * square)
        grad_upper = (matmul(cot_ref[0], w_down_ref[lanes, :], NT) * slope).astype(BF16)
        grad_upper_ref[0, :, lanes] = grad_upper
        up_sum_ref[0:1, lanes] += jnp.sum(grad_upper.astype(F32), axis=0, keepdims=True)
        layer_sc[...] += matmul(hidden, w_down_ref[lanes, :])
        back_sc[...] += matmul(grad_upper, w_up_ref[:, lanes], NT)

    layer_ref[0] = layer_sc[...].astype(BF16)
    back = back_sc[...]
    scaled = back * gain
    grad_out = cot_ref[0].astype(F32)
    grad_resid = grad_out + root * (
        scaled
        - jnp.mean(scaled, axis=-1, keepdims=True)
        - normed * jnp.mean(scaled * normed, axis=-1, keepdims=True)
    )
    grad_resid_ref[0] = grad_resid
    grad_attn = grad_resid.astype(BF16)
    grad_attn_ref[0] = grad_attn
    for w_ref, grad_mixed_ref in zip(w_out_refs, grad_mixed_refs):
        grad_mixed_ref[0] = matmul(grad_attn, w_ref[...], NT).astype(BF16)
    sums_ref[0:1, :] += jnp.sum(grad_attn.astype(F32), axis=0, keepdims=True)
    sums_ref[1:2, :] += jnp.sum(back * normed, axis=0, keepdims=True)
    sums_ref[2:3, :] += jnp.sum(back, axis=0, keepdims=True)
    sums_ref[3:4, :] += jnp.sum(grad_out, axis=0, keepdims=True)


def feed(mixed, x, cotangent, w_out, part, w_up, w_down, vectors, up_bias):
    parts = len(mixed)
    rows, size, model = x.shape
    width = mixed[0].shape[2]
    wide = w_up.shape[1]
    still = lambda i, p: (0, 0)
    step = lambda i, p: (i, 0, 0)
    once = pl.Buffered(1)
    slab = pl.BlockSpec((1, size, model), step)
    head_slab = pl.BlockSpec((1, size, width), step)
    wide_slab = pl.BlockSpec((1, size, wide), step)
    vector = pl.BlockSpec((1, model), still)
    w_out_specs = [
        pl.BlockSpec((width, model), lambda i, p, s=s: (p[0] ^ s, 0), pipeline_mode=once)
        for s in range(parts)
    ]

    def body(p_ref, *refs):
        feed_kernel(parts, wide // model, *refs)

    shape = jax.ShapeDtypeStruct
    out = pl.pallas_call(
        body,
        grid_spec=pltpu.PrefetchScalarGridSpec(
            num_scalar_prefetch=1,
            grid=(rows,),
            in_specs=[head_slab] * parts
            + [slab, slab]
            + w_out_specs
            + [
                pl.BlockSpec(w_up.shape, still, pipeline_mode=once),
                pl.BlockSpec(w_down.shape, still, pipeline_mode=once),
                vector,
                vector,
                vector,
                pl.BlockSpec((1, wide), still),
                vector,
            ],
            out_specs=[slab, wide_slab, wide_slab, slab, slab, slab]
            + [head_slab] * parts
            + [pl.BlockSpec((8, model), still), pl.BlockSpec((8, wide), still)],
            scratch_shapes=[
                pltpu.VMEM((size, model), F32),
                pltpu.VMEM((size, model), F32),
            ],
        ),
        out_shape=[
            shape((rows, size, model), BF16),
            shape((rows, size, wide), BF16),
            shape((rows, size, wide), BF16),
            shape((rows, size, model), BF16),
            shape((rows, size, model), F32),
            shape((rows, size, model), BF16),
        ]
        + [shape((rows, size, width), BF16)] * parts
        + [shape((8, model), F32), shape((8, wide), F32)],
        compiler_params=pltpu.CompilerParams(
            dimension_semantics=("arbitrary",), vmem_limit_bytes=VMEM_LIMIT
        ),
        cost_estimate=pl.CostEstimate(
            flops=2 * rows * size * model * (4 * wide + 2 * model),
            transcendentals=rows * size * wide,
            bytes_accessed=rows * size * (4 * wide + 16 * model),
        ),
        name="feed",
    )(
        part.reshape(1), *mixed, x, cotangent, *([w_out] * parts), w_up, w_down,
        vectors["out_bias"], vectors["gain"], vectors["shift"], up_bias, vectors["down_bias"],
    )
    return out[:6], out[6 : 6 + parts], out[6 + parts], out[7 + parts]


def join_kernel(sources, moves, bit_ref, token_ref, *refs):
    mine_refs, other_refs, out_refs = refs[:sources], refs[sources : 2 * sources], refs[2 * sources :]
    mine = pl.program_id(0) == bit_ref[0]
    for source, begin, out, place, count in moves:
        lanes = slice(begin, begin + count)
        out_refs[out][:, place : place + count] = jnp.where(
            mine, mine_refs[source][:, lanes], other_refs[source][:, lanes]
        ).astype(F32)
    out_refs[-1][0] = token_ref[0]


def join(mine, other, bit, moves, widths, token):
    count = mine[0].shape[0]
    largest = 384 if sum(widths) <= 1024 else 192
    tall = next(t for t in (largest, 192, 96, 48, count) if count % t == 0)
    steps = count // tall

    def mine_map(h, i, b, t):
        return jnp.where(h == b[0], i, jnp.where(h < b[0], 0, steps - 1)), 0

    def other_map(h, i, b, t):
        return jnp.where(h != b[0], i, jnp.where(h < 1 - b[0], 0, steps - 1)), 0

    return pl.pallas_call(
        functools.partial(join_kernel, len(mine), moves),
        grid_spec=pltpu.PrefetchScalarGridSpec(
            num_scalar_prefetch=2,
            grid=(2, steps),
            in_specs=[pl.BlockSpec((tall, m.shape[1]), mine_map) for m in mine]
            + [pl.BlockSpec((tall, m.shape[1]), other_map) for m in mine],
            out_specs=[
                pl.BlockSpec((tall, n), lambda h, i, b, t: (h * steps + i, 0)) for n in widths
            ]
            + [pl.BlockSpec(memory_space=pltpu.SMEM)],
        ),
        out_shape=[jax.ShapeDtypeStruct((2 * count, n), F32) for n in widths]
        + [jax.ShapeDtypeStruct((1,), jnp.int32)],
        compiler_params=pltpu.CompilerParams(
            dimension_semantics=("arbitrary", "arbitrary"), vmem_limit_bytes=VMEM_LIMIT
        ),
        cost_estimate=FREE,
        name="join",
    )(bit.reshape(1), token, *mine, *other)


def project_back_kernel(groups, rows, probe_ref, act_ref, *refs):
    grad_refs, w_refs, refs = refs[:groups], refs[groups : 2 * groups], refs[2 * groups :]
    own_ref, sent_ref, share_ref, sums_refs, share_sc = refs[0], refs[1], refs[2], refs[3:-1], refs[-1]
    i = pl.program_id(0)
    total = matmul(grad_refs[0][0], w_refs[0][...], NT)
    for grad_ref, w_ref in zip(grad_refs[1:], w_refs[1:]):
        total = total + matmul(grad_ref[0], w_ref[...], NT)

    @pl.when(i < rows)
    def _():
        own_ref[0] = total

    @pl.when(i >= rows)
    def _():
        sent_ref[0] = total.astype(BF16)

    @pl.when(i == 0)
    def _():
        share_sc[...] = jnp.zeros_like(share_sc)
        for sums_ref in sums_refs:
            sums_ref[...] = jnp.zeros_like(sums_ref)

    share_sc[...] += matmul(act_ref[0], grad_refs[-1][0], TN)

    @pl.when(i == pl.num_programs(0) - 1)
    def _():
        share_ref[...] = share_sc[...].astype(BF16)

    for grad_ref, sums_ref in zip(grad_refs, sums_refs):
        sums_ref[0:1, :] += jnp.sum(grad_ref[0].astype(F32), axis=0, keepdims=True)


def project_back(grads, weights, act, rows, probe):
    blocks, size, _ = grads[0].shape
    model = weights[0].shape[0]
    still = lambda i: (0, 0)
    shape = jax.ShapeDtypeStruct
    out = pl.pallas_call(
        functools.partial(project_back_kernel, len(grads), rows),
        grid=(blocks,),
        in_specs=[
            pl.BlockSpec(memory_space=pltpu.SMEM),
            pl.BlockSpec((1, size, act.shape[2]), lambda i: (i, 0, 0)),
        ]
        + [pl.BlockSpec((1, size, g.shape[2]), lambda i: (i, 0, 0)) for g in grads]
        + [pl.BlockSpec(w.shape, still) for w in weights],
        out_specs=[
            pl.BlockSpec((1, size, model), lambda i: (jnp.minimum(i, rows - 1), 0, 0)),
            pl.BlockSpec((1, size, model), lambda i: (jnp.maximum(i - rows, 0), 0, 0)),
            pl.BlockSpec((model, grads[-1].shape[2]), still),
        ]
        + [pl.BlockSpec((8, g.shape[2]), still) for g in grads],
        out_shape=[
            shape((rows, size, model), F32),
            shape((blocks - rows, size, model), BF16),
            shape((model, grads[-1].shape[2]), BF16),
        ]
        + [shape((8, g.shape[2]), F32) for g in grads],
        scratch_shapes=[pltpu.VMEM((model, grads[-1].shape[2]), F32)],
        compiler_params=pltpu.CompilerParams(
            dimension_semantics=("arbitrary",), vmem_limit_bytes=VMEM_LIMIT
        ),
        cost_estimate=FREE,
        name="project_back",
    )(probe, act, *grads, *weights)
    return out[0], out[1], out[2], [sums[0] for sums in out[3:]]


def norm_back_kernel(count, x_ref, own_ref, *refs):
    arrived_refs, (resid_ref, gain_ref, tokens_ref, sums_ref) = refs[:count], refs[count:]

    @pl.when(pl.program_id(0) == 0)
    def _():
        sums_ref[...] = jnp.zeros_like(sums_ref)

    values = x_ref[0].astype(F32)
    center = values - jnp.mean(values, axis=-1, keepdims=True)
    root = lax.rsqrt(jnp.mean(center * center, axis=-1, keepdims=True) + EPS)
    normed = center * root
    back = own_ref[0]
    for arrived_ref in arrived_refs:
        back = back + arrived_ref[0].astype(F32)
    scaled = back * gain_ref[...]
    grad = root * (
        scaled
        - jnp.mean(scaled, axis=-1, keepdims=True)
        - normed * jnp.mean(scaled * normed, axis=-1, keepdims=True)
    )
    tokens_ref[0] = (resid_ref[0] + grad).astype(BF16)
    sums_ref[0:1, :] += jnp.sum(back * normed, axis=0, keepdims=True)
    sums_ref[1:2, :] += jnp.sum(back, axis=0, keepdims=True)


def norm_back(x, own, arrived, grad_resid, gain):
    rows, size, model = x.shape
    slab = pl.BlockSpec((1, size, model), lambda i: (i, 0, 0))
    return pl.pallas_call(
        functools.partial(norm_back_kernel, len(arrived)),
        grid=(rows,),
        in_specs=[slab] * (3 + len(arrived)) + [pl.BlockSpec((1, model), lambda i: (0, 0))],
        out_specs=[slab, pl.BlockSpec((8, model), lambda i: (0, 0))],
        out_shape=[
            jax.ShapeDtypeStruct((rows, size, model), BF16),
            jax.ShapeDtypeStruct((8, model), F32),
        ],
        compiler_params=pltpu.CompilerParams(
            dimension_semantics=("arbitrary",), vmem_limit_bytes=VMEM_LIMIT
        ),
        cost_estimate=FREE,
        name="norm_back",
    )(x, own, *arrived, grad_resid, gain)


def spread_kernel(parts, spans, part_ref, *refs):
    out_ref, refs = refs[-1], refs[:-1]
    part = part_ref[0]
    begin = 0
    for which in range(3):
        for p in range(parts):
            for g, span in enumerate(spans):
                piece = None
                for s in range(parts):
                    here = refs[s * len(spans) + g][:, which * span : (which + 1) * span]
                    piece = here if piece is None else jnp.where((part ^ p) == s, here, piece)
                out_ref[:, begin : begin + span] = piece.astype(F32)
                begin += span


def spread(pieces, part, spans):
    parts = len(pieces)
    count = pieces[0][0].shape[0]
    tall = next(t for t in (192, 96, 48, count) if count % t == 0)
    flat = [p for piece in pieces for p in piece]
    columns = 3 * parts * sum(spans)
    return pl.pallas_call(
        functools.partial(spread_kernel, parts, spans),
        grid_spec=pltpu.PrefetchScalarGridSpec(
            num_scalar_prefetch=1,
            grid=(count // tall,),
            in_specs=[pl.BlockSpec((tall, p.shape[1]), lambda i, b: (i, 0)) for p in flat],
            out_specs=pl.BlockSpec((tall, columns), lambda i, b: (i, 0)),
        ),
        out_shape=jax.ShapeDtypeStruct((count, columns), F32),
        compiler_params=pltpu.CompilerParams(
            dimension_semantics=("arbitrary",), vmem_limit_bytes=VMEM_LIMIT
        ),
        cost_estimate=pl.CostEstimate(
            flops=count * columns, transcendentals=0, bytes_accessed=6 * count * columns
        ),
        name="spread",
    )(part.reshape(1), *flat)


def layout_kernel(owner_ref, sizes_ref, prefixes_ref, lens_ref, padding_ref, info_ref, flags_ref):
    blocks, _, size = info_ref.shape
    groups, slots = lens_ref.shape[1:]
    row = owner_ref[0]
    places = lax.broadcasted_iota(jnp.int32, (blocks, size), 0) * size + lax.broadcasted_iota(
        jnp.int32, (blocks, size), 1
    )
    filled = blocks * size - padding_ref[row]
    prefix_start = jnp.full((blocks, size), filled, jnp.int32)
    prefix_end, own_start = prefix_start, prefix_start
    start = jnp.int32(0)
    for g in range(groups):
        body = start + prefixes_ref[row, g]
        end = jnp.int32(0)
        base = jnp.zeros((blocks, size), jnp.int32)
        for j in range(slots):
            end = end + jnp.where(j < sizes_ref[row, g], lens_ref[row, g, j], 0)
            base = jnp.where(places - body >= end, end, base)
        stop = body + end
        member = (places >= start) & (places < stop) & (places < filled)
        solution = places >= body
        prefix_start = jnp.where(member, start, prefix_start)
        prefix_end = jnp.where(member, jnp.where(solution, body, start), prefix_end)
        own_start = jnp.where(member, jnp.where(solution, body + base, start), own_start)
        start = stop
    info_ref[...] = jnp.zeros_like(info_ref)
    for i, values in enumerate((prefix_start, prefix_end, own_start, places)):
        info_ref[:, i, :] = values
    lane = lax.broadcasted_iota(jnp.int32, flags_ref.shape, 1)
    flags = jnp.zeros(flags_ref.shape, jnp.int32)
    for j in range(blocks):
        low, high = j * size, (j + 1) * size
        need = (jnp.maximum(prefix_start, low) < jnp.minimum(prefix_end, high)) | (
            jnp.maximum(own_start, low) < jnp.minimum(places + 1, high)
        )
        any_need = jnp.max(jnp.where(need, 1, 0), axis=1, keepdims=True)
        flags = jnp.where(lane == j, any_need, flags)
    flags_ref[...] = flags


def row_layout(owner, sizes, prefixes, lens, padding, blocks, size):
    scalars = pl.BlockSpec(memory_space=pltpu.SMEM)
    info, flags = pl.pallas_call(
        layout_kernel,
        in_specs=[scalars] * 5,
        out_shape=(
            jax.ShapeDtypeStruct((blocks, 8, size), jnp.int32),
            jax.ShapeDtypeStruct((blocks, 128), jnp.int32),
        ),
        name="row_layout",
    )(owner.reshape(1).astype(jnp.int32), sizes, prefixes, lens, padding)
    return info, flags[:, :blocks].reshape(-1)


def swap(values, axis, mask):
    count = lax.axis_size(axis)
    return lax.ppermute(values, axis, [(i, i ^ mask) for i in range(count)])


def bits(count):
    return [1 << b for b in range(count.bit_length() - 1)]


def take(values, index):
    return lax.dynamic_index_in_dim(values, index, 0, keepdims=False)


def halve(values, step):
    axis, mask, bit = step
    two = values.reshape(2, values.shape[0] // 2, *values.shape[1:])
    arrived = swap(take(two, 1 - bit), axis, mask)
    return (take(two, bit).astype(F32) + arrived.astype(F32)).astype(values.dtype)


def double(values, step):
    axis, mask, bit = step
    arrived = swap(values, axis, mask)
    first = jnp.where(bit == 0, values, arrived)
    second = jnp.where(bit == 0, arrived, values)
    return jnp.concatenate([first, second], axis=0)


class Chain:
    def __init__(self, values, down, up):
        self.values = values
        self.left = [(halve, step) for step in down] + [(double, step) for step in up]

    def advance(self):
        if self.left:
            move, step = self.left.pop(0)
            self.values = move(self.values, step)


def close(chains, *others):
    tied, others = lax.optimization_barrier(([c.values for c in chains], others))
    for chain, values in zip(chains, tied):
        chain.values = values
    return others


def per_device(
    row_axis,
    tokens,
    segment_ids,
    group_sizes,
    prefix_lens,
    solution_lens,
    padding_counts,
    attn_gain,
    attn_shift,
    w_qkv,
    query_bias,
    value_bias,
    w_out,
    out_bias,
    ffn_gain,
    ffn_shift,
    w_up,
    up_bias,
    w_down,
    down_bias,
    cotangent,
):
    rows, size, model = tokens.shape
    devices = lax.axis_size("pos")
    parts = devices // rows
    blocks = devices
    heads = model // HEAD_DIM // parts
    width = heads * HEAD_DIM
    place = lax.axis_index("pos")
    owner, part = place // parts, place % parts

    def bring(values):
        return jnp.stack(
            [
                swap(take(values, owner ^ m), "pos", m * parts) if m else take(values, owner)
                for m in range(rows)
            ]
        )

    def send_back(values, m):
        return swap(values[m], "pos", m * parts) if m else values[m]

    def arrange(slabs):
        out = jnp.zeros((rows, *slabs[0].shape), slabs[0].dtype)
        for m, slab in enumerate(slabs):
            out = lax.dynamic_update_index_in_dim(out, slab, owner ^ m, 0)
        return out

    info, flags = row_layout(
        owner, group_sizes, prefix_lens, solution_lens, padding_counts, blocks, size
    )
    order = jnp.arange(blocks, dtype=jnp.int32)
    phys = (((order % parts) ^ part) * rows + ((order // parts) ^ owner)).astype(jnp.int32)

    def my_columns(start, first=0, count=None):
        begin = start * model + part * width + first
        return lax.dynamic_slice_in_dim(w_qkv, begin, count or width, 1)

    def as_row(vector):
        return vector.astype(F32).reshape(1, -1)

    groups = [(0, 4), (4, 2)] if heads == 6 else [(0, heads)]
    spans = [count * HEAD_DIM for _, count in groups]
    w_mine = jnp.concatenate([my_columns(n) for n in range(3)], axis=1)
    w_groups = [
        jnp.concatenate([my_columns(n, h * HEAD_DIM, c * HEAD_DIM) for n in range(3)], axis=1)
        for h, c in groups
    ]
    bias_q = lax.dynamic_slice_in_dim(query_bias, part * width, width, 0)
    bias_v = lax.dynamic_slice_in_dim(value_bias, part * width, width, 0)

    mine = bring(tokens)
    row = jnp.concatenate([mine] + [swap(mine, "pos", s) for s in range(1, parts)], axis=0)
    cotangent, row = lax.optimization_barrier((cotangent, row))
    own_cotangent = bring(cotangent)
    act_one, query_t, key, key_t, value, value_t = project(
        row, as_row(attn_gain), as_row(attn_shift), w_mine, as_row(bias_q), as_row(bias_v)
    )
    mixed_all, out_t, lse = attention_forward(
        phys, flags, query_t, key, value_t, info, heads
    )
    mixed_all, own_cotangent = lax.optimization_barrier((mixed_all, own_cotangent))
    mixed_parts = []
    for s in range(parts):
        piece = mixed_all[s * rows : (s + 1) * rows]
        mixed_parts.append(swap(piece, "pos", s) if s else piece)

    (act_two, hidden, grad_upper, layer_out, grad_resid, grad_attn), grad_mixed, sums, up_sum = feed(
        mixed_parts, mine, own_cotangent, w_out, part, w_up, w_down,
        {
            "out_bias": as_row(out_bias),
            "gain": as_row(ffn_gain),
            "shift": as_row(ffn_shift),
            "down_bias": as_row(down_bias),
        },
        as_row(up_bias),
    )
    local = rows * size

    def flat(values):
        return values.reshape(-1, values.shape[-1])

    row_place = lax.axis_index(row_axis)
    row_steps = [(row_axis, m, (row_place // m) % 2) for m in bits(lax.axis_size(row_axis))]
    own_steps = [("pos", m * parts, (owner // m) % 2) for m in bits(rows)]
    part_steps = [("pos", m, (part // m) % 2) for m in bits(parts)]
    turning, last = own_steps + row_steps[:1], row_steps[1:]

    def order(turn):
        turn %= len(turning)
        return turning[turn:] + turning[:turn] + last

    def chain(values, turn, parted=True):
        down = order(turn)
        up = down[::-1] + (part_steps[:0:-1] if parted else [])
        return Chain(values, (part_steps if parted else []) + down, up)

    wide = w_up.shape[1]
    cut = wide * 2 // 3
    near = [m for m in range(1, rows) if m & (m - 1) == 0]
    far = [m for m in range(1, rows) if m & (m - 1)]

    received = [g if s == 0 else swap(g, "pos", s) for s, g in enumerate(grad_mixed)]
    layer_slabs = {m: send_back(layer_out, m) for m in [0] + near}
    down = chain(matmul(flat(hidden), flat(own_cotangent), TN).astype(BF16), 0)
    received, layer_slabs, layer_out, grad_upper = close(
        [down], received, layer_slabs, layer_out, grad_upper
    )
    down.advance()
    layer_slabs.update({m: send_back(layer_out, m) for m in far})
    stacked = jnp.stack(mixed_parts)
    mixed = jnp.concatenate([flat(take(stacked, g ^ part)) for g in range(parts)], axis=1)
    grad_up_flat = flat(grad_upper)
    up_one = chain(matmul(flat(act_two), grad_up_flat[:, :cut], TN).astype(BF16), 1)
    up_two = chain(
        jnp.concatenate(
            [
                matmul(flat(act_two), grad_up_flat[:, cut:], TN).astype(BF16),
                matmul(mixed, flat(grad_attn), TN).astype(BF16),
            ],
            axis=1,
        ),
        2,
    )
    chains = [down, up_one, up_two]
    received, layer_slabs = close(chains, received, layer_slabs)
    layer_home = arrange([layer_slabs[m] for m in range(rows)])
    up_one.advance()
    up_two.advance()
    for _ in part_steps[1:]:
        for c in chains:
            c.advance()
    grad_t = jnp.concatenate(received, axis=0).transpose(0, 2, 1)
    grad_t, layer_home = close(chains, grad_t, layer_home)

    grads, shares = [], []
    for h, count in groups:
        for c in chains + shares:
            c.advance()
        grad = attention_backward(
            phys, flags, query_t, grad_t, out_t, lse, info, key, key_t, value, count, h
        )
        grad, grad_t = close(chains + shares, grad, grad_t)
        grads.append(grad)
        if len(grads) < len(groups):
            shares.append(chain(matmul(flat(act_one), flat(grad), TN).astype(BF16), 0, False))
            (grad_t,) = close(chains + shares, grad_t)

    def placed(values):
        return lax.dynamic_update_slice_in_dim(jnp.zeros((model,), F32), values, part * width, 0)

    probe = jnp.stack([c.values[0, 0] for c in chains + shares]).astype(F32)
    own_act, sent_act, last_share, sums_grads = project_back(
        grads, w_groups, act_one, rows, probe
    )
    shares.append(chain(last_share, 0, False))
    for c in chains + shares:
        c.advance()
    arrived_act = [
        swap(sent_act[(s - 1) * rows : s * rows], "pos", s) for s in range(1, parts)
    ]

    def column_sums(which):
        return jnp.concatenate(
            [g[which * n : (which + 1) * n] for g, n in zip(sums_grads, spans)]
        )

    sums_q, sums_v = placed(column_sums(0)), placed(column_sums(2))
    own_act, arrived_act, sums_q, sums_v = close(
        chains + shares, own_act, arrived_act, sums_q, sums_v
    )

    for c in chains + shares:
        c.advance()
    tokens_grad, norm_sums = norm_back(mine, own_act, arrived_act, grad_resid, as_row(attn_gain))
    small = jnp.concatenate(
        [
            norm_sums[0],
            norm_sums[1],
            sums_q,
            sums_v,
            sums[:4].reshape(-1),
            up_sum[0],
        ]
    )
    tokens_grad, small = close(chains + shares, tokens_grad, small)

    small_steps = part_steps + own_steps + row_steps
    token_slabs = {}
    waves = [[0] + near, far]
    while any(c.left for c in chains):
        for c in chains + shares:
            c.advance()
        if small_steps:
            axis, mask, _ = small_steps.pop(0)
            small = small + swap(small, axis, mask)
        if waves:
            token_slabs.update({m: send_back(tokens_grad, m) for m in waves.pop(0)})
        small, token_slabs, tokens_grad = close(chains + shares, small, token_slabs, tokens_grad)

    axis, mask, bit = part_steps[0]
    others = [swap(c.values, axis, mask) for c in chains]
    token = own_steps[0][2].astype(jnp.int32).reshape(1)
    sum_w_down, token = join(
        [down.values], others[:1], bit, ((0, 0, 0, 0, model),), (model,), token
    )
    sum_w_up, sum_w_out, token = join(
        [up_one.values, up_two.values],
        others[1:],
        bit,
        ((0, 0, 0, 0, cut), (1, 0, 0, cut, wide - cut), (1, wide - cut, 1, 0, model)),
        (wide, model),
        token,
    )
    for c in shares:
        if c.left:
            move, (axis_last, mask_last, _) = c.left[-1]
            c.left[-1] = (move, (axis_last, mask_last, token[0]))
    tokens_home = arrange([token_slabs[m] for m in range(rows)])
    while any(c.left for c in shares):
        for c in shares:
            c.advance()
    for axis, mask, _ in small_steps:
        small = small + swap(small, axis, mask)
    summed = [c.values for c in shares]
    pieces = [summed] + [[swap(g, "pos", s) for g in summed] for s in range(1, parts)]
    sum_w_qkv = spread(pieces, part, spans)

    vectors = small[: 8 * model].reshape(8, model)
    return (
        layer_home,
        tokens_home,
        vectors[0],
        vectors[1],
        sum_w_qkv,
        vectors[2],
        vectors[3],
        sum_w_out,
        vectors[4],
        vectors[5],
        vectors[6],
        sum_w_up,
        small[8 * model :],
        sum_w_down,
        vectors[7],
    )


def solution(mesh):
    in_specs = (
        P("rows", "pos", None),
        P("rows", "pos"),
        P("rows", None),
        P("rows", None),
        P("rows", None, None),
        P("rows"),
        *([P()] * 13),
        P("rows", "pos", None),
    )
    out_specs = (P("rows", "pos", None), P("rows", "pos", None), *([P()] * 13))
    return jax.shard_map(
        functools.partial(per_device, "rows"),
        mesh=mesh,
        in_specs=in_specs,
        out_specs=out_specs,
        check_vma=False,
    )
```

```python
import functools

import jax
import jax.numpy as jnp
from jax import lax
from jax.experimental import pallas as pl
from jax.experimental.pallas import tpu as pltpu
from jax.sharding import PartitionSpec as P

HEAD_DIM = 64
EPS = 1e-05
NEG = -1e30
GELU_C = 0.7978845608028654
F32 = jnp.float32
BF16 = jnp.bfloat16
VMEM_LIMIT = 60 * 1024 * 1024
FREE = pl.CostEstimate(flops=0, transcendentals=0, bytes_accessed=0)
NT = (((1,), (1,)), ((), ()))
TN = (((0,), (0,)), ((), ()))


def layer_norm(values, gain, shift):
    center = values - jnp.mean(values, axis=-1, keepdims=True)
    spread = jnp.mean(center * center, axis=-1, keepdims=True)
    return center * lax.rsqrt(spread + EPS) * gain + shift


def gelu_tanh(values):
    return 0.5 * values * (1.0 + jnp.tanh(GELU_C * (values + 0.044715 * values * values * values)))


def matmul(left, right, dims=(((1,), (0,)), ((), ()))):
    return lax.dot_general(left, right, dims, preferred_element_type=F32)


def head_pairs(heads):
    return [(h // 2, min(128, heads * HEAD_DIM - (h // 2) * 128)) for h in range(heads)]


def mask_bias(info_ref, key_start, size):
    prefix_start, prefix_end = info_ref[0, 0:1, :], info_ref[0, 1:2, :]
    own_start, query_place = info_ref[0, 2:3, :], info_ref[0, 3:4, :]
    key_place = key_start + lax.broadcasted_iota(jnp.int32, (size, size), 0)
    allowed = ((key_place >= prefix_start) & (key_place < prefix_end)) | (
        (key_place >= own_start) & (key_place <= query_place)
    )
    return jnp.where(allowed, 0.0, NEG).astype(F32)


def fill_padded(source_ref, target_ref, heads):
    for h, (pair, width) in enumerate(head_pairs(heads)):
        rows = source_ref[0, pair * 128 : pair * 128 + width, :]
        if width == 128:
            keep = (lax.broadcasted_iota(jnp.int32, rows.shape, 0) // HEAD_DIM) == (h % 2)
            rows = jnp.where(keep, rows, jnp.zeros_like(rows))
        target_ref[h, 0:width, :] = rows


def forward_kernel(
    heads, blocks, phys_ref, flag_ref, query_t_ref, key_ref, value_t_ref, info_ref,
    mixed_ref, out_t_ref, lse_ref, bias_sc, top_sc, total_sc, acc_sc, query_sc,
):
    size = query_t_ref.shape[2]
    i = pl.program_id(0)
    fill_padded(query_t_ref, query_sc, heads)
    top_sc[...] = jnp.full_like(top_sc, NEG)
    total_sc[...] = jnp.zeros_like(total_sc)
    acc_sc[...] = jnp.zeros_like(acc_sc)

    @pl.loop(0, i + 1)
    def _(j):
        @pl.when(flag_ref[i * blocks + j] > 0)
        def _():
            at = phys_ref[j]
            bias_sc[...] = mask_bias(info_ref, j * size, size)
            for h, (pair, width) in enumerate(head_pairs(heads)):
                rows = slice(h * HEAD_DIM, (h + 1) * HEAD_DIM)
                scores = (
                    matmul(key_ref[at, :, pair * 128 : pair * 128 + width], query_sc[h, 0:width, :])
                    + bias_sc[...]
                )
                old = top_sc[h]
                top = jnp.maximum(old, jnp.max(scores, axis=0, keepdims=True))
                shrink = jnp.exp(old - top)
                weights = jnp.exp(scores - top)
                total_sc[h] = shrink * total_sc[h] + jnp.sum(weights, axis=0, keepdims=True)
                top_sc[h] = top
                acc_sc[rows, :] = shrink * acc_sc[rows, :] + matmul(
                    value_t_ref[at, rows, :], weights.astype(BF16)
                )

    for h in range(heads):
        rows = slice(h * HEAD_DIM, (h + 1) * HEAD_DIM)
        out_t_ref[0, rows, :] = acc_sc[rows, :] / total_sc[h]
        lse_ref[0, h : h + 1, :] = top_sc[h] + jnp.log(total_sc[h])
    mixed_ref[0] = out_t_ref[0].T.astype(BF16)


def attention_forward(phys, flags, query_t, key, value_t, info, heads):
    blocks, width, size = query_t.shape
    lse_rows = -(-heads // 8) * 8
    whole = pl.Buffered(1)
    spec = pltpu.PrefetchScalarGridSpec(
        num_scalar_prefetch=2,
        grid=(blocks,),
        in_specs=[
            pl.BlockSpec((1, width, size), lambda i, p, f: (p[i], 0, 0)),
            pl.BlockSpec((blocks, size, width), lambda i, p, f: (0, 0, 0), pipeline_mode=whole),
            pl.BlockSpec((blocks, width, size), lambda i, p, f: (0, 0, 0), pipeline_mode=whole),
            pl.BlockSpec((1, 8, size), lambda i, p, f: (i, 0, 0)),
        ],
        out_specs=[
            pl.BlockSpec((1, size, width), lambda i, p, f: (p[i], 0, 0)),
            pl.BlockSpec((1, width, size), lambda i, p, f: (p[i], 0, 0)),
            pl.BlockSpec((1, lse_rows, size), lambda i, p, f: (p[i], 0, 0)),
        ],
        scratch_shapes=[
            pltpu.VMEM((size, size), F32),
            pltpu.VMEM((heads, 1, size), F32),
            pltpu.VMEM((heads, 1, size), F32),
            pltpu.VMEM((width, size), F32),
            pltpu.VMEM((heads, 128, size), BF16),
        ],
    )
    pairs = heads * blocks * (blocks + 1) // 2 * size * size
    return pl.pallas_call(
        functools.partial(forward_kernel, heads, blocks),
        grid_spec=spec,
        out_shape=(
            jax.ShapeDtypeStruct((blocks, size, width), BF16),
            jax.ShapeDtypeStruct((blocks, width, size), F32),
            jax.ShapeDtypeStruct((blocks, lse_rows, size), F32),
        ),
        compiler_params=pltpu.CompilerParams(
            dimension_semantics=("arbitrary",), vmem_limit_bytes=VMEM_LIMIT
        ),
        cost_estimate=pl.CostEstimate(
            flops=pairs * 4 * 128, transcendentals=pairs, bytes_accessed=blocks * size * width * 16
        ),
        name="attention_forward",
    )(phys, flags, query_t, key, value_t, info)


def backward_kernel(
    heads, first, blocks, phys_ref, flag_ref, query_t_ref, grad_t_ref, out_t_ref, lse_ref, info_ref,
    key_ref, key_t_ref, value_ref, grads_ref,
    bias_sc, query_grad_sc, key_grad_sc, value_grad_sc, query_sc, grad_sc, delta_sc,
):
    size = query_t_ref.shape[2]
    span = heads * HEAD_DIM
    i = pl.program_id(0)

    @pl.when(i == 0)
    def _():
        key_grad_sc[...] = jnp.zeros_like(key_grad_sc)
        value_grad_sc[...] = jnp.zeros_like(value_grad_sc)

    fill_padded(query_t_ref, query_sc, heads)
    fill_padded(grad_t_ref, grad_sc, heads)
    query_grad_sc[...] = jnp.zeros_like(query_grad_sc)
    for h in range(heads):
        rows = slice(h * HEAD_DIM, (h + 1) * HEAD_DIM)
        delta_sc[h] = jnp.sum(
            grad_t_ref[0, rows, :].astype(F32) * out_t_ref[0, rows, :], axis=0, keepdims=True
        )

    @pl.loop(0, i + 1)
    def _(j):
        @pl.when(flag_ref[i * blocks + j] > 0)
        def _():
            at = phys_ref[j]
            bias_sc[...] = mask_bias(info_ref, j * size, size)
            for h, (pair, width) in enumerate(head_pairs(heads)):
                rows = slice(h * HEAD_DIM, (h + 1) * HEAD_DIM)
                lanes = slice(pair * 128, pair * 128 + width)
                scores = matmul(key_ref[at, :, lanes], query_sc[h, 0:width, :]) + bias_sc[...]
                probs = jnp.exp(scores - lse_ref[0, first + h : first + h + 1, :])
                grad_probs = matmul(value_ref[at, :, lanes], grad_sc[h, 0:width, :])
                grad_scores = (probs * (grad_probs - delta_sc[h])).astype(BF16)
                query_grad_sc[rows, :] += matmul(key_t_ref[at, rows, :], grad_scores)
                value_grad_sc[at, rows, :] += matmul(
                    grad_t_ref[0, rows, :], probs.astype(BF16), NT
                )
                key_grad_sc[at, rows, :] += matmul(query_t_ref[0, rows, :], grad_scores, NT)

    grads_ref[phys_ref[i], :, 0:span] = (query_grad_sc[...] * 0.125).T.astype(BF16)

    @pl.when(i == blocks - 1)
    def _():
        for block in range(blocks):
            grads_ref[block, :, span : 2 * span] = key_grad_sc[block].T.astype(BF16)
            grads_ref[block, :, 2 * span :] = value_grad_sc[block].T.astype(BF16)


def attention_backward(
    phys, flags, query_t, grad_t, out_t, lse, info, key, key_t, value, heads, first
):
    blocks, _, size = query_t.shape
    span = heads * HEAD_DIM
    c = first // heads
    moving_t = pl.BlockSpec((1, span, size), lambda i, p, f: (p[i], c, 0))
    whole = pl.BlockSpec(
        (blocks, size, span), lambda i, p, f: (0, 0, c), pipeline_mode=pl.Buffered(1)
    )
    whole_t = pl.BlockSpec(
        (blocks, span, size), lambda i, p, f: (0, c, 0), pipeline_mode=pl.Buffered(1)
    )
    spec = pltpu.PrefetchScalarGridSpec(
        num_scalar_prefetch=2,
        grid=(blocks,),
        in_specs=[
            moving_t,
            moving_t,
            moving_t,
            pl.BlockSpec((1, lse.shape[1], size), lambda i, p, f: (p[i], 0, 0)),
            pl.BlockSpec((1, 8, size), lambda i, p, f: (i, 0, 0)),
            whole,
            whole_t,
            whole,
        ],
        out_specs=pl.BlockSpec(
            (blocks, size, 3 * span), lambda i, p, f: (0, 0, 0), pipeline_mode=pl.Buffered(1)
        ),
        scratch_shapes=[
            pltpu.VMEM((size, size), F32),
            pltpu.VMEM((span, size), F32),
            pltpu.VMEM((blocks, span, size), F32),
            pltpu.VMEM((blocks, span, size), F32),
            pltpu.VMEM((heads, 128, size), BF16),
            pltpu.VMEM((heads, 128, size), BF16),
            pltpu.VMEM((heads, 1, size), F32),
        ],
    )
    pairs = heads * blocks * (blocks + 1) // 2 * size * size
    return pl.pallas_call(
        functools.partial(backward_kernel, heads, first, blocks),
        grid_spec=spec,
        out_shape=jax.ShapeDtypeStruct((blocks, size, 3 * span), BF16),
        compiler_params=pltpu.CompilerParams(
            dimension_semantics=("arbitrary",), vmem_limit_bytes=VMEM_LIMIT
        ),
        cost_estimate=pl.CostEstimate(
            flops=pairs * 10 * 128, transcendentals=pairs, bytes_accessed=blocks * size * span * 20
        ),
        name="attention_backward",
    )(phys, flags, query_t, grad_t, out_t, lse, info, key, key_t, value)


def project_kernel(
    width, x_ref, gain_ref, shift_ref, w_ref, bias_q_ref, bias_v_ref,
    act_ref, query_t_ref, key_ref, key_t_ref, value_ref, value_t_ref,
):
    act = layer_norm(x_ref[0].astype(F32), gain_ref[...], shift_ref[...]).astype(BF16)
    act_ref[0] = act
    query = (matmul(act, w_ref[:, :width]) + bias_q_ref[...]).astype(BF16).astype(F32) * 0.125
    query_t_ref[0] = query.T.astype(BF16)
    key = matmul(act, w_ref[:, width : 2 * width])
    key_ref[0] = key.astype(BF16)
    key_t_ref[0] = key.T.astype(BF16)
    value = matmul(act, w_ref[:, 2 * width :]) + bias_v_ref[...]
    value_ref[0] = value.astype(BF16)
    value_t_ref[0] = value.T.astype(BF16)


def project(x, gain, shift, weight, bias_q, bias_v):
    blocks, size, model = x.shape
    width = bias_q.shape[1]
    still = lambda i: (0, 0)
    step = lambda i: (i, 0, 0)
    straight, turned = (
        jax.ShapeDtypeStruct((blocks, size, width), BF16),
        jax.ShapeDtypeStruct((blocks, width, size), BF16),
    )
    wide, tall = pl.BlockSpec((1, size, width), step), pl.BlockSpec((1, width, size), step)
    return pl.pallas_call(
        functools.partial(project_kernel, width),
        grid=(blocks,),
        in_specs=[
            pl.BlockSpec((1, size, model), step),
            pl.BlockSpec((1, model), still),
            pl.BlockSpec((1, model), still),
            pl.BlockSpec(weight.shape, still, pipeline_mode=pl.Buffered(1)),
            pl.BlockSpec((1, width), still),
            pl.BlockSpec((1, width), still),
        ],
        out_specs=[pl.BlockSpec((1, size, model), step), tall, wide, tall, wide, tall],
        out_shape=(
            jax.ShapeDtypeStruct((blocks, size, model), BF16),
            turned, straight, turned, straight, turned,
        ),
        compiler_params=pltpu.CompilerParams(
            dimension_semantics=("arbitrary",), vmem_limit_bytes=VMEM_LIMIT
        ),
        cost_estimate=pl.CostEstimate(
            flops=2 * blocks * size * model * 3 * width,
            transcendentals=blocks * size,
            bytes_accessed=blocks * size * (4 * model + 10 * width),
        ),
        name="project",
    )(x, gain, shift, weight, bias_q, bias_v)


def feed_kernel(
    parts, pieces, *refs
):
    mixed_refs, refs = refs[:parts], refs[parts:]
    x_ref, cot_ref, refs = refs[0], refs[1], refs[2:]
    w_out_refs, refs = refs[:parts], refs[parts:]
    (w_up_ref, w_down_ref, out_bias_ref, gain_ref, shift_ref, up_bias_ref, down_bias_ref), refs = (
        refs[:7], refs[7:],
    )
    act_ref, hidden_ref, grad_upper_ref, layer_ref, grad_resid_ref, grad_attn_ref = refs[:6]
    refs = refs[6:]
    grad_mixed_refs, refs = refs[:parts], refs[parts:]
    sums_ref, up_sum_ref, layer_sc, back_sc = refs
    first = pl.program_id(0) == 0

    @pl.when(first)
    def _():
        sums_ref[...] = jnp.zeros_like(sums_ref)
        up_sum_ref[...] = jnp.zeros_like(up_sum_ref)

    attn = out_bias_ref[...]
    for mixed_ref, w_ref in zip(mixed_refs, w_out_refs):
        attn = attn + matmul(mixed_ref[0], w_ref[...])
    resid = x_ref[0].astype(F32) + attn
    center = resid - jnp.mean(resid, axis=-1, keepdims=True)
    root = lax.rsqrt(jnp.mean(center * center, axis=-1, keepdims=True) + EPS)
    normed = center * root
    gain = gain_ref[...]
    act_ref[0] = (normed * gain + shift_ref[...]).astype(BF16)
    layer_sc[...] = resid + down_bias_ref[...]
    back_sc[...] = jnp.zeros_like(back_sc)
    span = w_up_ref.shape[1] // pieces

    for c in range(pieces):
        lanes = slice(c * span, (c + 1) * span)
        upper = matmul(act_ref[0], w_up_ref[:, lanes]) + up_bias_ref[:, lanes]
        square = upper * upper
        bend = jnp.tanh(GELU_C * upper * (1.0 + 0.044715 * square))
        half = 0.5 * (1.0 + bend)
        hidden = (upper * half).astype(BF16)
        hidden_ref[0, :, lanes] = hidden
        slope = half + 0.5 * GELU_C * upper * (1.0 - bend * bend) * (1.0 + 0.134145 * square)
        grad_upper = (matmul(cot_ref[0], w_down_ref[lanes, :], NT) * slope).astype(BF16)
        grad_upper_ref[0, :, lanes] = grad_upper
        up_sum_ref[0:1, lanes] += jnp.sum(grad_upper.astype(F32), axis=0, keepdims=True)
        layer_sc[...] += matmul(hidden, w_down_ref[lanes, :])
        back_sc[...] += matmul(grad_upper, w_up_ref[:, lanes], NT)

    layer_ref[0] = layer_sc[...].astype(BF16)
    back = back_sc[...]
    scaled = back * gain
    grad_out = cot_ref[0].astype(F32)
    grad_resid = grad_out + root * (
        scaled
        - jnp.mean(scaled, axis=-1, keepdims=True)
        - normed * jnp.mean(scaled * normed, axis=-1, keepdims=True)
    )
    grad_resid_ref[0] = grad_resid
    grad_attn = grad_resid.astype(BF16)
    grad_attn_ref[0] = grad_attn
    for w_ref, grad_mixed_ref in zip(w_out_refs, grad_mixed_refs):
        grad_mixed_ref[0] = matmul(grad_attn, w_ref[...], NT).astype(BF16)
    sums_ref[0:1, :] += jnp.sum(grad_attn.astype(F32), axis=0, keepdims=True)
    sums_ref[1:2, :] += jnp.sum(back * normed, axis=0, keepdims=True)
    sums_ref[2:3, :] += jnp.sum(back, axis=0, keepdims=True)
    sums_ref[3:4, :] += jnp.sum(grad_out, axis=0, keepdims=True)


def feed(mixed, x, cotangent, w_out, part, w_up, w_down, vectors, up_bias):
    parts = len(mixed)
    rows, size, model = x.shape
    width = mixed[0].shape[2]
    wide = w_up.shape[1]
    still = lambda i, p: (0, 0)
    step = lambda i, p: (i, 0, 0)
    once = pl.Buffered(1)
    slab = pl.BlockSpec((1, size, model), step)
    head_slab = pl.BlockSpec((1, size, width), step)
    wide_slab = pl.BlockSpec((1, size, wide), step)
    vector = pl.BlockSpec((1, model), still)
    w_out_specs = [
        pl.BlockSpec((width, model), lambda i, p, s=s: (p[0] ^ s, 0), pipeline_mode=once)
        for s in range(parts)
    ]

    def body(p_ref, *refs):
        feed_kernel(parts, wide // model, *refs)

    shape = jax.ShapeDtypeStruct
    out = pl.pallas_call(
        body,
        grid_spec=pltpu.PrefetchScalarGridSpec(
            num_scalar_prefetch=1,
            grid=(rows,),
            in_specs=[head_slab] * parts
            + [slab, slab]
            + w_out_specs
            + [
                pl.BlockSpec(w_up.shape, still, pipeline_mode=once),
                pl.BlockSpec(w_down.shape, still, pipeline_mode=once),
                vector,
                vector,
                vector,
                pl.BlockSpec((1, wide), still),
                vector,
            ],
            out_specs=[slab, wide_slab, wide_slab, slab, slab, slab]
            + [head_slab] * parts
            + [pl.BlockSpec((8, model), still), pl.BlockSpec((8, wide), still)],
            scratch_shapes=[
                pltpu.VMEM((size, model), F32),
                pltpu.VMEM((size, model), F32),
            ],
        ),
        out_shape=[
            shape((rows, size, model), BF16),
            shape((rows, size, wide), BF16),
            shape((rows, size, wide), BF16),
            shape((rows, size, model), BF16),
            shape((rows, size, model), F32),
            shape((rows, size, model), BF16),
        ]
        + [shape((rows, size, width), BF16)] * parts
        + [shape((8, model), F32), shape((8, wide), F32)],
        compiler_params=pltpu.CompilerParams(
            dimension_semantics=("arbitrary",), vmem_limit_bytes=VMEM_LIMIT
        ),
        cost_estimate=pl.CostEstimate(
            flops=2 * rows * size * model * (4 * wide + 2 * model),
            transcendentals=rows * size * wide,
            bytes_accessed=rows * size * (4 * wide + 16 * model),
        ),
        name="feed",
    )(
        part.reshape(1), *mixed, x, cotangent, *([w_out] * parts), w_up, w_down,
        vectors["out_bias"], vectors["gain"], vectors["shift"], up_bias, vectors["down_bias"],
    )
    return out[:6], out[6 : 6 + parts], out[6 + parts], out[7 + parts]


def join_kernel(sources, moves, bit_ref, token_ref, *refs):
    mine_refs, other_refs, out_refs = refs[:sources], refs[sources : 2 * sources], refs[2 * sources :]
    mine = pl.program_id(0) == bit_ref[0]
    for source, begin, out, place, count in moves:
        lanes = slice(begin, begin + count)
        out_refs[out][:, place : place + count] = jnp.where(
            mine, mine_refs[source][:, lanes], other_refs[source][:, lanes]
        ).astype(F32)
    out_refs[-1][0] = token_ref[0]


def join(mine, other, bit, moves, widths, token):
    count = mine[0].shape[0]
    largest = 384 if sum(widths) <= 1024 else 192
    tall = next(t for t in (largest, 192, 96, 48, count) if count % t == 0)
    steps = count // tall

    def mine_map(h, i, b, t):
        return jnp.where(h == b[0], i, jnp.where(h < b[0], 0, steps - 1)), 0

    def other_map(h, i, b, t):
        return jnp.where(h != b[0], i, jnp.where(h < 1 - b[0], 0, steps - 1)), 0

    return pl.pallas_call(
        functools.partial(join_kernel, len(mine), moves),
        grid_spec=pltpu.PrefetchScalarGridSpec(
            num_scalar_prefetch=2,
            grid=(2, steps),
            in_specs=[pl.BlockSpec((tall, m.shape[1]), mine_map) for m in mine]
            + [pl.BlockSpec((tall, m.shape[1]), other_map) for m in mine],
            out_specs=[
                pl.BlockSpec((tall, n), lambda h, i, b, t: (h * steps + i, 0)) for n in widths
            ]
            + [pl.BlockSpec(memory_space=pltpu.SMEM)],
        ),
        out_shape=[jax.ShapeDtypeStruct((2 * count, n), F32) for n in widths]
        + [jax.ShapeDtypeStruct((1,), jnp.int32)],
        compiler_params=pltpu.CompilerParams(
            dimension_semantics=("arbitrary", "arbitrary"), vmem_limit_bytes=VMEM_LIMIT
        ),
        cost_estimate=FREE,
        name="join",
    )(bit.reshape(1), token, *mine, *other)


def project_back_kernel(groups, rows, probe_ref, act_ref, *refs):
    grad_refs, w_refs, refs = refs[:groups], refs[groups : 2 * groups], refs[2 * groups :]
    own_ref, sent_ref, share_ref, sums_refs, share_sc = refs[0], refs[1], refs[2], refs[3:-1], refs[-1]
    i = pl.program_id(0)

    def flat(ref):
        return ref[...].reshape(-1, ref.shape[-1])

    total = matmul(flat(grad_refs[0]), w_refs[0][...], NT)
    for grad_ref, w_ref in zip(grad_refs[1:], w_refs[1:]):
        total = total + matmul(flat(grad_ref), w_ref[...], NT)

    @pl.when(i < rows)
    def _():
        own_ref[...] = total.reshape(own_ref.shape)

    @pl.when(i >= rows)
    def _():
        sent_ref[...] = total.astype(BF16).reshape(sent_ref.shape)

    @pl.when(i == 0)
    def _():
        share_sc[...] = jnp.zeros_like(share_sc)
        for sums_ref in sums_refs:
            sums_ref[...] = jnp.zeros_like(sums_ref)

    share_sc[...] += matmul(flat(act_ref), flat(grad_refs[-1]), TN)

    @pl.when(i == pl.num_programs(0) - 1)
    def _():
        share_ref[...] = share_sc[...].astype(BF16)

    for grad_ref, sums_ref in zip(grad_refs, sums_refs):
        sums_ref[0:1, :] += jnp.sum(flat(grad_ref).astype(F32), axis=0, keepdims=True)


def project_back(grads, weights, act, rows, probe):
    blocks, size, _ = grads[0].shape
    step = 2 if rows % 2 == 0 else 1
    turn = rows // step
    model = weights[0].shape[0]
    still = lambda i: (0, 0)
    shape = jax.ShapeDtypeStruct
    out = pl.pallas_call(
        functools.partial(project_back_kernel, len(grads), turn),
        grid=(blocks // step,),
        in_specs=[
            pl.BlockSpec(memory_space=pltpu.SMEM),
            pl.BlockSpec((step, size, act.shape[2]), lambda i: (i, 0, 0)),
        ]
        + [pl.BlockSpec((step, size, g.shape[2]), lambda i: (i, 0, 0)) for g in grads]
        + [pl.BlockSpec(w.shape, still) for w in weights],
        out_specs=[
            pl.BlockSpec((step, size, model), lambda i: (jnp.minimum(i, turn - 1), 0, 0)),
            pl.BlockSpec((step, size, model), lambda i: (jnp.maximum(i - turn, 0), 0, 0)),
            pl.BlockSpec((model, grads[-1].shape[2]), still),
        ]
        + [pl.BlockSpec((8, g.shape[2]), still) for g in grads],
        out_shape=[
            shape((rows, size, model), F32),
            shape((blocks - rows, size, model), BF16),
            shape((model, grads[-1].shape[2]), BF16),
        ]
        + [shape((8, g.shape[2]), F32) for g in grads],
        scratch_shapes=[pltpu.VMEM((model, grads[-1].shape[2]), F32)],
        compiler_params=pltpu.CompilerParams(
            dimension_semantics=("arbitrary",), vmem_limit_bytes=VMEM_LIMIT
        ),
        cost_estimate=FREE,
        name="project_back",
    )(probe, act, *grads, *weights)
    return out[0], out[1], out[2], [sums[0] for sums in out[3:]]


def norm_back_kernel(count, x_ref, own_ref, *refs):
    arrived_refs, (resid_ref, gain_ref, tokens_ref, sums_ref) = refs[:count], refs[count:]

    @pl.when(pl.program_id(0) == 0)
    def _():
        sums_ref[...] = jnp.zeros_like(sums_ref)

    values = x_ref[0].astype(F32)
    center = values - jnp.mean(values, axis=-1, keepdims=True)
    root = lax.rsqrt(jnp.mean(center * center, axis=-1, keepdims=True) + EPS)
    normed = center * root
    back = own_ref[0]
    for arrived_ref in arrived_refs:
        back = back + arrived_ref[0].astype(F32)
    scaled = back * gain_ref[...]
    grad = root * (
        scaled
        - jnp.mean(scaled, axis=-1, keepdims=True)
        - normed * jnp.mean(scaled * normed, axis=-1, keepdims=True)
    )
    tokens_ref[0] = (resid_ref[0] + grad).astype(BF16)
    sums_ref[0:1, :] += jnp.sum(back * normed, axis=0, keepdims=True)
    sums_ref[1:2, :] += jnp.sum(back, axis=0, keepdims=True)


def norm_back(x, own, arrived, grad_resid, gain):
    rows, size, model = x.shape
    slab = pl.BlockSpec((1, size, model), lambda i: (i, 0, 0))
    return pl.pallas_call(
        functools.partial(norm_back_kernel, len(arrived)),
        grid=(rows,),
        in_specs=[slab] * (3 + len(arrived)) + [pl.BlockSpec((1, model), lambda i: (0, 0))],
        out_specs=[slab, pl.BlockSpec((8, model), lambda i: (0, 0))],
        out_shape=[
            jax.ShapeDtypeStruct((rows, size, model), BF16),
            jax.ShapeDtypeStruct((8, model), F32),
        ],
        compiler_params=pltpu.CompilerParams(
            dimension_semantics=("arbitrary",), vmem_limit_bytes=VMEM_LIMIT
        ),
        cost_estimate=FREE,
        name="norm_back",
    )(x, own, *arrived, grad_resid, gain)


def spread_kernel(parts, spans, part_ref, *refs):
    out_ref, refs = refs[-1], refs[:-1]
    part = part_ref[0]
    begin = 0
    for which in range(3):
        for p in range(parts):
            for g, span in enumerate(spans):
                piece = None
                for s in range(parts):
                    here = refs[s * len(spans) + g][:, which * span : (which + 1) * span]
                    piece = here if piece is None else jnp.where((part ^ p) == s, here, piece)
                out_ref[:, begin : begin + span] = piece.astype(F32)
                begin += span


def spread(pieces, part, spans):
    parts = len(pieces)
    count = pieces[0][0].shape[0]
    tall = next(t for t in (192, 96, 48, count) if count % t == 0)
    flat = [p for piece in pieces for p in piece]
    columns = 3 * parts * sum(spans)
    return pl.pallas_call(
        functools.partial(spread_kernel, parts, spans),
        grid_spec=pltpu.PrefetchScalarGridSpec(
            num_scalar_prefetch=1,
            grid=(count // tall,),
            in_specs=[pl.BlockSpec((tall, p.shape[1]), lambda i, b: (i, 0)) for p in flat],
            out_specs=pl.BlockSpec((tall, columns), lambda i, b: (i, 0)),
        ),
        out_shape=jax.ShapeDtypeStruct((count, columns), F32),
        compiler_params=pltpu.CompilerParams(
            dimension_semantics=("arbitrary",), vmem_limit_bytes=VMEM_LIMIT
        ),
        cost_estimate=pl.CostEstimate(
            flops=count * columns, transcendentals=0, bytes_accessed=6 * count * columns
        ),
        name="spread",
    )(part.reshape(1), *flat)


def layout_kernel(owner_ref, sizes_ref, prefixes_ref, lens_ref, padding_ref, info_ref, flags_ref):
    blocks, _, size = info_ref.shape
    groups, slots = lens_ref.shape[1:]
    row = owner_ref[0]
    places = lax.broadcasted_iota(jnp.int32, (blocks, size), 0) * size + lax.broadcasted_iota(
        jnp.int32, (blocks, size), 1
    )
    filled = blocks * size - padding_ref[row]
    prefix_start = jnp.full((blocks, size), filled, jnp.int32)
    prefix_end, own_start = prefix_start, prefix_start
    start = jnp.int32(0)
    for g in range(groups):
        body = start + prefixes_ref[row, g]
        end = jnp.int32(0)
        base = jnp.zeros((blocks, size), jnp.int32)
        for j in range(slots):
            end = end + jnp.where(j < sizes_ref[row, g], lens_ref[row, g, j], 0)
            base = jnp.where(places - body >= end, end, base)
        stop = body + end
        member = (places >= start) & (places < stop) & (places < filled)
        solution = places >= body
        prefix_start = jnp.where(member, start, prefix_start)
        prefix_end = jnp.where(member, jnp.where(solution, body, start), prefix_end)
        own_start = jnp.where(member, jnp.where(solution, body + base, start), own_start)
        start = stop
    info_ref[...] = jnp.zeros_like(info_ref)
    for i, values in enumerate((prefix_start, prefix_end, own_start, places)):
        info_ref[:, i, :] = values
    lane = lax.broadcasted_iota(jnp.int32, flags_ref.shape, 1)
    flags = jnp.zeros(flags_ref.shape, jnp.int32)
    for j in range(blocks):
        low, high = j * size, (j + 1) * size
        need = (jnp.maximum(prefix_start, low) < jnp.minimum(prefix_end, high)) | (
            jnp.maximum(own_start, low) < jnp.minimum(places + 1, high)
        )
        any_need = jnp.max(jnp.where(need, 1, 0), axis=1, keepdims=True)
        flags = jnp.where(lane == j, any_need, flags)
    flags_ref[...] = flags


def row_layout(owner, sizes, prefixes, lens, padding, blocks, size):
    scalars = pl.BlockSpec(memory_space=pltpu.SMEM)
    info, flags = pl.pallas_call(
        layout_kernel,
        in_specs=[scalars] * 5,
        out_shape=(
            jax.ShapeDtypeStruct((blocks, 8, size), jnp.int32),
            jax.ShapeDtypeStruct((blocks, 128), jnp.int32),
        ),
        name="row_layout",
    )(owner.reshape(1).astype(jnp.int32), sizes, prefixes, lens, padding)
    return info, flags[:, :blocks].reshape(-1)


def swap(values, axis, mask):
    count = lax.axis_size(axis)
    return lax.ppermute(values, axis, [(i, i ^ mask) for i in range(count)])


def bits(count):
    return [1 << b for b in range(count.bit_length() - 1)]


def take(values, index):
    return lax.dynamic_index_in_dim(values, index, 0, keepdims=False)


def halve(values, step):
    axis, mask, bit = step
    two = values.reshape(2, values.shape[0] // 2, *values.shape[1:])
    arrived = swap(take(two, 1 - bit), axis, mask)
    return (take(two, bit).astype(F32) + arrived.astype(F32)).astype(values.dtype)


def double(values, step):
    axis, mask, bit = step
    arrived = swap(values, axis, mask)
    first = jnp.where(bit == 0, values, arrived)
    second = jnp.where(bit == 0, arrived, values)
    return jnp.concatenate([first, second], axis=0)


class Chain:
    def __init__(self, values, down, up):
        self.values = values
        self.left = [(halve, step) for step in down] + [(double, step) for step in up]

    def advance(self):
        if self.left:
            move, step = self.left.pop(0)
            self.values = move(self.values, step)


def close(chains, *others):
    others, tied = lax.optimization_barrier((others, [c.values for c in chains[::-1]]))
    for chain, values in zip(chains[::-1], tied):
        chain.values = values
    return others


def per_device(
    row_axis,
    tokens,
    segment_ids,
    group_sizes,
    prefix_lens,
    solution_lens,
    padding_counts,
    attn_gain,
    attn_shift,
    w_qkv,
    query_bias,
    value_bias,
    w_out,
    out_bias,
    ffn_gain,
    ffn_shift,
    w_up,
    up_bias,
    w_down,
    down_bias,
    cotangent,
):
    rows, size, model = tokens.shape
    devices = lax.axis_size("pos")
    parts = devices // rows
    blocks = devices
    heads = model // HEAD_DIM // parts
    width = heads * HEAD_DIM
    place = lax.axis_index("pos")
    owner, part = place // parts, place % parts

    def bring(values):
        return jnp.stack(
            [
                swap(take(values, owner ^ m), "pos", m * parts) if m else take(values, owner)
                for m in range(rows)
            ]
        )

    def send_back(values, m):
        return swap(values[m], "pos", m * parts) if m else values[m]

    def arrange(slabs):
        out = jnp.zeros((rows, *slabs[0].shape), slabs[0].dtype)
        for m, slab in enumerate(slabs):
            out = lax.dynamic_update_index_in_dim(out, slab, owner ^ m, 0)
        return out

    info, flags = row_layout(
        owner, group_sizes, prefix_lens, solution_lens, padding_counts, blocks, size
    )
    order = jnp.arange(blocks, dtype=jnp.int32)
    phys = (((order % parts) ^ part) * rows + ((order // parts) ^ owner)).astype(jnp.int32)

    def my_columns(start, first=0, count=None):
        begin = start * model + part * width + first
        return lax.dynamic_slice_in_dim(w_qkv, begin, count or width, 1)

    def as_row(vector):
        return vector.astype(F32).reshape(1, -1)

    groups = [(0, 4), (4, 2)] if heads == 6 else [(0, heads)]
    spans = [count * HEAD_DIM for _, count in groups]
    w_mine = jnp.concatenate([my_columns(n) for n in range(3)], axis=1)
    w_groups = [
        jnp.concatenate([my_columns(n, h * HEAD_DIM, c * HEAD_DIM) for n in range(3)], axis=1)
        for h, c in groups
    ]
    bias_q = lax.dynamic_slice_in_dim(query_bias, part * width, width, 0)
    bias_v = lax.dynamic_slice_in_dim(value_bias, part * width, width, 0)

    mine = bring(tokens)
    row = jnp.concatenate([mine] + [swap(mine, "pos", s) for s in range(1, parts)], axis=0)
    cotangent, row = lax.optimization_barrier((cotangent, row))
    own_cotangent = bring(cotangent)
    act_one, query_t, key, key_t, value, value_t = project(
        row, as_row(attn_gain), as_row(attn_shift), w_mine, as_row(bias_q), as_row(bias_v)
    )
    mixed_all, out_t, lse = attention_forward(
        phys, flags, query_t, key, value_t, info, heads
    )
    mixed_all, own_cotangent = lax.optimization_barrier((mixed_all, own_cotangent))
    mixed_parts = []
    for s in range(parts):
        piece = mixed_all[s * rows : (s + 1) * rows]
        mixed_parts.append(swap(piece, "pos", s) if s else piece)

    (act_two, hidden, grad_upper, layer_out, grad_resid, grad_attn), grad_mixed, sums, up_sum = feed(
        mixed_parts, mine, own_cotangent, w_out, part, w_up, w_down,
        {
            "out_bias": as_row(out_bias),
            "gain": as_row(ffn_gain),
            "shift": as_row(ffn_shift),
            "down_bias": as_row(down_bias),
        },
        as_row(up_bias),
    )
    local = rows * size

    def flat(values):
        return values.reshape(-1, values.shape[-1])

    row_place = lax.axis_index(row_axis)
    row_steps = [(row_axis, m, (row_place // m) % 2) for m in bits(lax.axis_size(row_axis))]
    own_steps = [("pos", m * parts, (owner // m) % 2) for m in bits(rows)]
    part_steps = [("pos", m, (part // m) % 2) for m in bits(parts)]
    turning, last = own_steps + row_steps[:1], row_steps[1:]

    def order(turn):
        turn %= len(turning)
        return turning[turn:] + turning[:turn] + last

    def chain(values, turn, parted=True):
        down = order(turn)
        up = down[::-1] + (part_steps[:0:-1] if parted else [])
        return Chain(values, (part_steps if parted else []) + down, up)

    wide = w_up.shape[1]
    cut = wide * 2 // 3
    near = [m for m in range(1, rows) if m & (m - 1) == 0]
    far = [m for m in range(1, rows) if m & (m - 1)]

    received = [g if s == 0 else swap(g, "pos", s) for s, g in enumerate(grad_mixed)]
    layer_slabs = {m: send_back(layer_out, m) for m in [0] + near}
    down = chain(matmul(flat(hidden), flat(own_cotangent), TN).astype(BF16), 0)
    received, layer_slabs, layer_out, grad_upper = close(
        [down], received, layer_slabs, layer_out, grad_upper
    )
    down.advance()
    layer_slabs.update({m: send_back(layer_out, m) for m in far})
    stacked = jnp.stack(mixed_parts)
    mixed = jnp.concatenate([flat(take(stacked, g ^ part)) for g in range(parts)], axis=1)
    grad_up_flat = flat(grad_upper)
    up_one = chain(matmul(flat(act_two), grad_up_flat[:, :cut], TN).astype(BF16), 1)
    up_two = chain(
        jnp.concatenate(
            [
                matmul(flat(act_two), grad_up_flat[:, cut:], TN).astype(BF16),
                matmul(mixed, flat(grad_attn), TN).astype(BF16),
            ],
            axis=1,
        ),
        2,
    )
    chains = [down, up_one, up_two]
    received, layer_slabs = close(chains, received, layer_slabs)
    layer_home = arrange([layer_slabs[m] for m in range(rows)])
    up_one.advance()
    up_two.advance()
    for _ in part_steps[1:]:
        for c in chains:
            c.advance()
    grad_t = jnp.concatenate(received, axis=0).transpose(0, 2, 1)
    grad_t, layer_home = close(chains, grad_t, layer_home)

    grads, shares = [], []
    for h, count in groups:
        for c in shares[::-1] + chains[::-1]:
            c.advance()
        grad = attention_backward(
            phys, flags, query_t, grad_t, out_t, lse, info, key, key_t, value, count, h
        )
        grad, grad_t = close(chains + shares, grad, grad_t)
        grads.append(grad)
        if len(grads) < len(groups):
            shares.append(chain(matmul(flat(act_one), flat(grad), TN).astype(BF16), 0, False))
            (grad_t,) = close(chains + shares, grad_t)

    def placed(values):
        return lax.dynamic_update_slice_in_dim(jnp.zeros((model,), F32), values, part * width, 0)

    probe = jnp.stack([c.values[0, 0] for c in chains + shares]).astype(F32)
    own_act, sent_act, last_share, sums_grads = project_back(
        grads, w_groups, act_one, rows, probe
    )
    shares.append(chain(last_share, 0, False))
    for c in shares[::-1] + chains[::-1]:
        c.advance()
    arrived_act = [
        swap(sent_act[(s - 1) * rows : s * rows], "pos", s) for s in range(1, parts)
    ]

    def column_sums(which):
        return jnp.concatenate(
            [g[which * n : (which + 1) * n] for g, n in zip(sums_grads, spans)]
        )

    sums_q, sums_v = placed(column_sums(0)), placed(column_sums(2))
    own_act, arrived_act, sums_q, sums_v = close(
        chains + shares, own_act, arrived_act, sums_q, sums_v
    )

    for c in shares[::-1] + chains[::-1]:
        c.advance()
    tokens_grad, norm_sums = norm_back(mine, own_act, arrived_act, grad_resid, as_row(attn_gain))
    small = jnp.concatenate(
        [
            norm_sums[0],
            norm_sums[1],
            sums_q,
            sums_v,
            sums[:4].reshape(-1),
            up_sum[0],
        ]
    )
    tokens_grad, small = close(chains + shares, tokens_grad, small)

    small_steps = part_steps + own_steps + row_steps
    token_slabs = {}
    waves = [[0] + near, far]
    while any(c.left for c in chains):
        if small_steps:
            axis, mask, _ = small_steps.pop(0)
            small = small + swap(small, axis, mask)
        if waves:
            token_slabs.update({m: send_back(tokens_grad, m) for m in waves.pop(0)})
        for c in shares[::-1] + chains[::-1]:
            c.advance()
        small, token_slabs, tokens_grad = close(chains + shares, small, token_slabs, tokens_grad)

    axis, mask, bit = part_steps[0]
    others = [swap(c.values, axis, mask) for c in chains[::-1]][::-1]
    token = own_steps[0][2].astype(jnp.int32).reshape(1)
    sum_w_down, token = join(
        [down.values], others[:1], bit, ((0, 0, 0, 0, model),), (model,), token
    )
    sum_w_up, sum_w_out, token = join(
        [up_one.values, up_two.values],
        others[1:],
        bit,
        ((0, 0, 0, 0, cut), (1, 0, 0, cut, wide - cut), (1, wide - cut, 1, 0, model)),
        (wide, model),
        token,
    )
    for c in shares:
        if c.left:
            move, (axis_last, mask_last, _) = c.left[-1]
            c.left[-1] = (move, (axis_last, mask_last, token[0]))
    tokens_home = arrange([token_slabs[m] for m in range(rows)])
    while any(c.left for c in shares):
        for c in shares:
            c.advance()
    for axis, mask, _ in small_steps:
        small = small + swap(small, axis, mask)
    summed = [c.values for c in shares]
    pieces = [summed] + [[swap(g, "pos", s) for g in summed] for s in range(1, parts)]
    sum_w_qkv = spread(pieces, part, spans)

    vectors = small[: 8 * model].reshape(8, model)
    return (
        layer_home,
        tokens_home,
        vectors[0],
        vectors[1],
        sum_w_qkv,
        vectors[2],
        vectors[3],
        sum_w_out,
        vectors[4],
        vectors[5],
        vectors[6],
        sum_w_up,
        small[8 * model :],
        sum_w_down,
        vectors[7],
    )


def solution(mesh):
    in_specs = (
        P("rows", "pos", None),
        P("rows", "pos"),
        P("rows", None),
        P("rows", None),
        P("rows", None, None),
        P("rows"),
        *([P()] * 13),
        P("rows", "pos", None),
    )
    out_specs = (P("rows", "pos", None), P("rows", "pos", None), *([P()] * 13))
    return jax.shard_map(
        functools.partial(per_device, "rows"),
        mesh=mesh,
        in_specs=in_specs,
        out_specs=out_specs,
        check_vma=False,
    )
```

```python
import functools

import jax
import jax.numpy as jnp
from jax import lax
from jax.experimental import pallas as pl
from jax.experimental.pallas import tpu as pltpu
from jax.sharding import PartitionSpec as P

HEAD_DIM = 64
EPS = 1e-05
NEG = -1e30
GELU_C = 0.7978845608028654
F32 = jnp.float32
BF16 = jnp.bfloat16
VMEM_LIMIT = 60 * 1024 * 1024
FREE = pl.CostEstimate(flops=0, transcendentals=0, bytes_accessed=0)
NT = (((1,), (1,)), ((), ()))
TN = (((0,), (0,)), ((), ()))


def layer_norm(values, gain, shift):
    center = values - jnp.mean(values, axis=-1, keepdims=True)
    spread = jnp.mean(center * center, axis=-1, keepdims=True)
    return center * lax.rsqrt(spread + EPS) * gain + shift


def gelu_tanh(values):
    return 0.5 * values * (1.0 + jnp.tanh(GELU_C * (values + 0.044715 * values * values * values)))


def matmul(left, right, dims=(((1,), (0,)), ((), ()))):
    return lax.dot_general(left, right, dims, preferred_element_type=F32)


def head_pairs(heads):
    return [(h // 2, min(128, heads * HEAD_DIM - (h // 2) * 128)) for h in range(heads)]


def mask_bias(info_ref, key_start, size):
    prefix_start, prefix_end = info_ref[0, 0:1, :], info_ref[0, 1:2, :]
    own_start, query_place = info_ref[0, 2:3, :], info_ref[0, 3:4, :]
    key_place = key_start + lax.broadcasted_iota(jnp.int32, (size, size), 0)
    allowed = ((key_place >= prefix_start) & (key_place < prefix_end)) | (
        (key_place >= own_start) & (key_place <= query_place)
    )
    return jnp.where(allowed, 0.0, NEG).astype(F32)


def fill_padded(source_ref, target_ref, heads):
    for h, (pair, width) in enumerate(head_pairs(heads)):
        rows = source_ref[0, pair * 128 : pair * 128 + width, :]
        if width == 128:
            keep = (lax.broadcasted_iota(jnp.int32, rows.shape, 0) // HEAD_DIM) == (h % 2)
            rows = jnp.where(keep, rows, jnp.zeros_like(rows))
        target_ref[h, 0:width, :] = rows


def forward_kernel(
    heads, blocks, phys_ref, flag_ref, query_t_ref, key_ref, value_t_ref, info_ref,
    mixed_ref, out_t_ref, lse_ref, bias_sc, top_sc, total_sc, acc_sc, query_sc,
):
    size = query_t_ref.shape[2]
    i = pl.program_id(0)
    fill_padded(query_t_ref, query_sc, heads)
    top_sc[...] = jnp.full_like(top_sc, NEG)
    total_sc[...] = jnp.zeros_like(total_sc)
    acc_sc[...] = jnp.zeros_like(acc_sc)

    @pl.loop(0, i + 1)
    def _(j):
        @pl.when(flag_ref[i * blocks + j] > 0)
        def _():
            at = phys_ref[j]
            bias_sc[...] = mask_bias(info_ref, j * size, size)
            for h, (pair, width) in enumerate(head_pairs(heads)):
                rows = slice(h * HEAD_DIM, (h + 1) * HEAD_DIM)
                scores = (
                    matmul(key_ref[at, :, pair * 128 : pair * 128 + width], query_sc[h, 0:width, :])
                    + bias_sc[...]
                )
                old = top_sc[h]
                top = jnp.maximum(old, jnp.max(scores, axis=0, keepdims=True))
                shrink = jnp.exp(old - top)
                weights = jnp.exp(scores - top)
                total_sc[h] = shrink * total_sc[h] + jnp.sum(weights, axis=0, keepdims=True)
                top_sc[h] = top
                acc_sc[rows, :] = shrink * acc_sc[rows, :] + matmul(
                    value_t_ref[at, rows, :], weights.astype(BF16)
                )

    for h in range(heads):
        rows = slice(h * HEAD_DIM, (h + 1) * HEAD_DIM)
        out_t_ref[0, rows, :] = acc_sc[rows, :] / total_sc[h]
        lse_ref[0, h : h + 1, :] = top_sc[h] + jnp.log(total_sc[h])
    mixed_ref[0] = out_t_ref[0].T.astype(BF16)


def attention_forward(phys, flags, query_t, key, value_t, info, heads):
    blocks, width, size = query_t.shape
    lse_rows = -(-heads // 8) * 8
    whole = pl.Buffered(1)
    spec = pltpu.PrefetchScalarGridSpec(
        num_scalar_prefetch=2,
        grid=(blocks,),
        in_specs=[
            pl.BlockSpec((1, width, size), lambda i, p, f: (p[i], 0, 0)),
            pl.BlockSpec((blocks, size, width), lambda i, p, f: (0, 0, 0), pipeline_mode=whole),
            pl.BlockSpec((blocks, width, size), lambda i, p, f: (0, 0, 0), pipeline_mode=whole),
            pl.BlockSpec((1, 8, size), lambda i, p, f: (i, 0, 0)),
        ],
        out_specs=[
            pl.BlockSpec((1, size, width), lambda i, p, f: (p[i], 0, 0)),
            pl.BlockSpec((1, width, size), lambda i, p, f: (p[i], 0, 0)),
            pl.BlockSpec((1, lse_rows, size), lambda i, p, f: (p[i], 0, 0)),
        ],
        scratch_shapes=[
            pltpu.VMEM((size, size), F32),
            pltpu.VMEM((heads, 1, size), F32),
            pltpu.VMEM((heads, 1, size), F32),
            pltpu.VMEM((width, size), F32),
            pltpu.VMEM((heads, 128, size), BF16),
        ],
    )
    pairs = heads * blocks * (blocks + 1) // 2 * size * size
    return pl.pallas_call(
        functools.partial(forward_kernel, heads, blocks),
        grid_spec=spec,
        out_shape=(
            jax.ShapeDtypeStruct((blocks, size, width), BF16),
            jax.ShapeDtypeStruct((blocks, width, size), F32),
            jax.ShapeDtypeStruct((blocks, lse_rows, size), F32),
        ),
        compiler_params=pltpu.CompilerParams(
            dimension_semantics=("arbitrary",), vmem_limit_bytes=VMEM_LIMIT
        ),
        cost_estimate=pl.CostEstimate(
            flops=pairs * 4 * 128, transcendentals=pairs, bytes_accessed=blocks * size * width * 16
        ),
        name="attention_forward",
    )(phys, flags, query_t, key, value_t, info)


def backward_kernel(
    heads, first, blocks, phys_ref, flag_ref, query_t_ref, grad_t_ref, out_t_ref, lse_ref, info_ref,
    key_ref, key_t_ref, value_ref, grads_ref,
    bias_sc, query_grad_sc, key_grad_sc, value_grad_sc, query_sc, grad_sc, delta_sc,
):
    size = query_t_ref.shape[2]
    span = heads * HEAD_DIM
    i = pl.program_id(0)

    @pl.when(i == 0)
    def _():
        key_grad_sc[...] = jnp.zeros_like(key_grad_sc)
        value_grad_sc[...] = jnp.zeros_like(value_grad_sc)

    fill_padded(query_t_ref, query_sc, heads)
    fill_padded(grad_t_ref, grad_sc, heads)
    query_grad_sc[...] = jnp.zeros_like(query_grad_sc)
    for h in range(heads):
        rows = slice(h * HEAD_DIM, (h + 1) * HEAD_DIM)
        delta_sc[h] = jnp.sum(
            grad_t_ref[0, rows, :].astype(F32) * out_t_ref[0, rows, :], axis=0, keepdims=True
        )

    @pl.loop(0, i + 1)
    def _(j):
        @pl.when(flag_ref[i * blocks + j] > 0)
        def _():
            at = phys_ref[j]
            bias_sc[...] = mask_bias(info_ref, j * size, size)
            for h, (pair, width) in enumerate(head_pairs(heads)):
                rows = slice(h * HEAD_DIM, (h + 1) * HEAD_DIM)
                lanes = slice(pair * 128, pair * 128 + width)
                scores = matmul(key_ref[at, :, lanes], query_sc[h, 0:width, :]) + bias_sc[...]
                probs = jnp.exp(scores - lse_ref[0, first + h : first + h + 1, :])
                grad_probs = matmul(value_ref[at, :, lanes], grad_sc[h, 0:width, :])
                grad_scores = (probs * (grad_probs - delta_sc[h])).astype(BF16)
                query_grad_sc[rows, :] += matmul(key_t_ref[at, rows, :], grad_scores)
                value_grad_sc[at, rows, :] += matmul(
                    grad_t_ref[0, rows, :], probs.astype(BF16), NT
                )
                key_grad_sc[at, rows, :] += matmul(query_t_ref[0, rows, :], grad_scores, NT)

    grads_ref[phys_ref[i], :, 0:span] = (query_grad_sc[...] * 0.125).T.astype(BF16)

    @pl.when(i == blocks - 1)
    def _():
        for block in range(blocks):
            grads_ref[block, :, span : 2 * span] = key_grad_sc[block].T.astype(BF16)
            grads_ref[block, :, 2 * span :] = value_grad_sc[block].T.astype(BF16)


def attention_backward(
    phys, flags, query_t, grad_t, out_t, lse, info, key, key_t, value, heads, first
):
    blocks, _, size = query_t.shape
    span = heads * HEAD_DIM
    c = first // heads
    moving_t = pl.BlockSpec((1, span, size), lambda i, p, f: (p[i], c, 0))
    whole = pl.BlockSpec(
        (blocks, size, span), lambda i, p, f: (0, 0, c), pipeline_mode=pl.Buffered(1)
    )
    whole_t = pl.BlockSpec(
        (blocks, span, size), lambda i, p, f: (0, c, 0), pipeline_mode=pl.Buffered(1)
    )
    spec = pltpu.PrefetchScalarGridSpec(
        num_scalar_prefetch=2,
        grid=(blocks,),
        in_specs=[
            moving_t,
            moving_t,
            moving_t,
            pl.BlockSpec((1, lse.shape[1], size), lambda i, p, f: (p[i], 0, 0)),
            pl.BlockSpec((1, 8, size), lambda i, p, f: (i, 0, 0)),
            whole,
            whole_t,
            whole,
        ],
        out_specs=pl.BlockSpec(
            (blocks, size, 3 * span), lambda i, p, f: (0, 0, 0), pipeline_mode=pl.Buffered(1)
        ),
        scratch_shapes=[
            pltpu.VMEM((size, size), F32),
            pltpu.VMEM((span, size), F32),
            pltpu.VMEM((blocks, span, size), F32),
            pltpu.VMEM((blocks, span, size), F32),
            pltpu.VMEM((heads, 128, size), BF16),
            pltpu.VMEM((heads, 128, size), BF16),
            pltpu.VMEM((heads, 1, size), F32),
        ],
    )
    pairs = heads * blocks * (blocks + 1) // 2 * size * size
    return pl.pallas_call(
        functools.partial(backward_kernel, heads, first, blocks),
        grid_spec=spec,
        out_shape=jax.ShapeDtypeStruct((blocks, size, 3 * span), BF16),
        compiler_params=pltpu.CompilerParams(
            dimension_semantics=("arbitrary",), vmem_limit_bytes=VMEM_LIMIT
        ),
        cost_estimate=pl.CostEstimate(
            flops=pairs * 10 * 128, transcendentals=pairs, bytes_accessed=blocks * size * span * 20
        ),
        name="attention_backward",
    )(phys, flags, query_t, grad_t, out_t, lse, info, key, key_t, value)


def project_kernel(
    width, x_ref, gain_ref, shift_ref, w_ref, bias_q_ref, bias_v_ref,
    act_ref, query_t_ref, key_ref, key_t_ref, value_ref, value_t_ref,
):
    act = layer_norm(x_ref[0].astype(F32), gain_ref[...], shift_ref[...]).astype(BF16)
    act_ref[0] = act
    query = (matmul(act, w_ref[:, :width]) + bias_q_ref[...]).astype(BF16).astype(F32) * 0.125
    query_t_ref[0] = query.T.astype(BF16)
    key = matmul(act, w_ref[:, width : 2 * width])
    key_ref[0] = key.astype(BF16)
    key_t_ref[0] = key.T.astype(BF16)
    value = matmul(act, w_ref[:, 2 * width :]) + bias_v_ref[...]
    value_ref[0] = value.astype(BF16)
    value_t_ref[0] = value.T.astype(BF16)


def project(x, gain, shift, weight, bias_q, bias_v):
    blocks, size, model = x.shape
    width = bias_q.shape[1]
    still = lambda i: (0, 0)
    step = lambda i: (i, 0, 0)
    straight, turned = (
        jax.ShapeDtypeStruct((blocks, size, width), BF16),
        jax.ShapeDtypeStruct((blocks, width, size), BF16),
    )
    wide, tall = pl.BlockSpec((1, size, width), step), pl.BlockSpec((1, width, size), step)
    return pl.pallas_call(
        functools.partial(project_kernel, width),
        grid=(blocks,),
        in_specs=[
            pl.BlockSpec((1, size, model), step),
            pl.BlockSpec((1, model), still),
            pl.BlockSpec((1, model), still),
            pl.BlockSpec(weight.shape, still, pipeline_mode=pl.Buffered(1)),
            pl.BlockSpec((1, width), still),
            pl.BlockSpec((1, width), still),
        ],
        out_specs=[pl.BlockSpec((1, size, model), step), tall, wide, tall, wide, tall],
        out_shape=(
            jax.ShapeDtypeStruct((blocks, size, model), BF16),
            turned, straight, turned, straight, turned,
        ),
        compiler_params=pltpu.CompilerParams(
            dimension_semantics=("arbitrary",), vmem_limit_bytes=VMEM_LIMIT
        ),
        cost_estimate=pl.CostEstimate(
            flops=2 * blocks * size * model * 3 * width,
            transcendentals=blocks * size,
            bytes_accessed=blocks * size * (4 * model + 10 * width),
        ),
        name="project",
    )(x, gain, shift, weight, bias_q, bias_v)


def feed_kernel(
    parts, pieces, *refs
):
    mixed_refs, refs = refs[:parts], refs[parts:]
    x_ref, cot_ref, refs = refs[0], refs[1], refs[2:]
    w_out_refs, refs = refs[:parts], refs[parts:]
    (w_up_ref, w_down_ref, out_bias_ref, gain_ref, shift_ref, up_bias_ref, down_bias_ref), refs = (
        refs[:7], refs[7:],
    )
    act_ref, hidden_ref, grad_upper_ref, layer_ref, grad_resid_ref, grad_attn_ref = refs[:6]
    refs = refs[6:]
    grad_mixed_refs, refs = refs[:parts], refs[parts:]
    sums_ref, up_sum_ref, layer_sc, back_sc = refs
    first = pl.program_id(0) == 0

    @pl.when(first)
    def _():
        sums_ref[...] = jnp.zeros_like(sums_ref)
        up_sum_ref[...] = jnp.zeros_like(up_sum_ref)

    attn = out_bias_ref[...]
    for mixed_ref, w_ref in zip(mixed_refs, w_out_refs):
        attn = attn + matmul(mixed_ref[0], w_ref[...])
    resid = x_ref[0].astype(F32) + attn
    center = resid - jnp.mean(resid, axis=-1, keepdims=True)
    root = lax.rsqrt(jnp.mean(center * center, axis=-1, keepdims=True) + EPS)
    normed = center * root
    gain = gain_ref[...]
    act_ref[0] = (normed * gain + shift_ref[...]).astype(BF16)
    layer_sc[...] = resid + down_bias_ref[...]
    back_sc[...] = jnp.zeros_like(back_sc)
    span = w_up_ref.shape[1] // pieces

    for c in range(pieces):
        lanes = slice(c * span, (c + 1) * span)
        upper = matmul(act_ref[0], w_up_ref[:, lanes]) + up_bias_ref[:, lanes]
        square = upper * upper
        bend = jnp.tanh(GELU_C * upper * (1.0 + 0.044715 * square))
        half = 0.5 * (1.0 + bend)
        hidden = (upper * half).astype(BF16)
        hidden_ref[0, :, lanes] = hidden
        slope = half + 0.5 * GELU_C * upper * (1.0 - bend * bend) * (1.0 + 0.134145 * square)
        grad_upper = (matmul(cot_ref[0], w_down_ref[lanes, :], NT) * slope).astype(BF16)
        grad_upper_ref[0, :, lanes] = grad_upper
        up_sum_ref[0:1, lanes] += jnp.sum(grad_upper.astype(F32), axis=0, keepdims=True)
        layer_sc[...] += matmul(hidden, w_down_ref[lanes, :])
        back_sc[...] += matmul(grad_upper, w_up_ref[:, lanes], NT)

    layer_ref[0] = layer_sc[...].astype(BF16)
    back = back_sc[...]
    scaled = back * gain
    grad_out = cot_ref[0].astype(F32)
    grad_resid = grad_out + root * (
        scaled
        - jnp.mean(scaled, axis=-1, keepdims=True)
        - normed * jnp.mean(scaled * normed, axis=-1, keepdims=True)
    )
    grad_resid_ref[0] = grad_resid
    grad_attn = grad_resid.astype(BF16)
    grad_attn_ref[0] = grad_attn
    for w_ref, grad_mixed_ref in zip(w_out_refs, grad_mixed_refs):
        grad_mixed_ref[0] = matmul(grad_attn, w_ref[...], NT).astype(BF16)
    sums_ref[0:1, :] += jnp.sum(grad_attn.astype(F32), axis=0, keepdims=True)
    sums_ref[1:2, :] += jnp.sum(back * normed, axis=0, keepdims=True)
    sums_ref[2:3, :] += jnp.sum(back, axis=0, keepdims=True)
    sums_ref[3:4, :] += jnp.sum(grad_out, axis=0, keepdims=True)


def feed(mixed, x, cotangent, w_out, part, w_up, w_down, vectors, up_bias):
    parts = len(mixed)
    rows, size, model = x.shape
    width = mixed[0].shape[2]
    wide = w_up.shape[1]
    still = lambda i, p: (0, 0)
    step = lambda i, p: (i, 0, 0)
    once = pl.Buffered(1)
    slab = pl.BlockSpec((1, size, model), step)
    head_slab = pl.BlockSpec((1, size, width), step)
    wide_slab = pl.BlockSpec((1, size, wide), step)
    vector = pl.BlockSpec((1, model), still)
    w_out_specs = [
        pl.BlockSpec((width, model), lambda i, p, s=s: (p[0] ^ s, 0), pipeline_mode=once)
        for s in range(parts)
    ]

    def body(p_ref, *refs):
        feed_kernel(parts, wide // model, *refs)

    shape = jax.ShapeDtypeStruct
    out = pl.pallas_call(
        body,
        grid_spec=pltpu.PrefetchScalarGridSpec(
            num_scalar_prefetch=1,
            grid=(rows,),
            in_specs=[head_slab] * parts
            + [slab, slab]
            + w_out_specs
            + [
                pl.BlockSpec(w_up.shape, still, pipeline_mode=once),
                pl.BlockSpec(w_down.shape, still, pipeline_mode=once),
                vector,
                vector,
                vector,
                pl.BlockSpec((1, wide), still),
                vector,
            ],
            out_specs=[slab, wide_slab, wide_slab, slab, slab, slab]
            + [head_slab] * parts
            + [pl.BlockSpec((8, model), still), pl.BlockSpec((8, wide), still)],
            scratch_shapes=[
                pltpu.VMEM((size, model), F32),
                pltpu.VMEM((size, model), F32),
            ],
        ),
        out_shape=[
            shape((rows, size, model), BF16),
            shape((rows, size, wide), BF16),
            shape((rows, size, wide), BF16),
            shape((rows, size, model), BF16),
            shape((rows, size, model), F32),
            shape((rows, size, model), BF16),
        ]
        + [shape((rows, size, width), BF16)] * parts
        + [shape((8, model), F32), shape((8, wide), F32)],
        compiler_params=pltpu.CompilerParams(
            dimension_semantics=("arbitrary",), vmem_limit_bytes=VMEM_LIMIT
        ),
        cost_estimate=pl.CostEstimate(
            flops=2 * rows * size * model * (4 * wide + 2 * model),
            transcendentals=rows * size * wide,
            bytes_accessed=rows * size * (4 * wide + 16 * model),
        ),
        name="feed",
    )(
        part.reshape(1), *mixed, x, cotangent, *([w_out] * parts), w_up, w_down,
        vectors["out_bias"], vectors["gain"], vectors["shift"], up_bias, vectors["down_bias"],
    )
    return out[:6], out[6 : 6 + parts], out[6 + parts], out[7 + parts]


def join_kernel(sources, moves, bit_ref, token_ref, *refs):
    mine_refs, other_refs, out_refs = refs[:sources], refs[sources : 2 * sources], refs[2 * sources :]
    mine = pl.program_id(0) == bit_ref[0]
    for source, begin, out, place, count in moves:
        lanes = slice(begin, begin + count)
        out_refs[out][:, place : place + count] = jnp.where(
            mine, mine_refs[source][:, lanes], other_refs[source][:, lanes]
        ).astype(F32)
    out_refs[-1][0] = token_ref[0]


def join(mine, other, bit, moves, widths, token):
    count = mine[0].shape[0]
    largest = 384 if sum(widths) <= 1024 else 192
    tall = next(t for t in (largest, 192, 96, 48, count) if count % t == 0)
    steps = count // tall

    def mine_map(h, i, b, t):
        return jnp.where(h == b[0], i, jnp.where(h < b[0], 0, steps - 1)), 0

    def other_map(h, i, b, t):
        return jnp.where(h != b[0], i, jnp.where(h < 1 - b[0], 0, steps - 1)), 0

    return pl.pallas_call(
        functools.partial(join_kernel, len(mine), moves),
        grid_spec=pltpu.PrefetchScalarGridSpec(
            num_scalar_prefetch=2,
            grid=(2, steps),
            in_specs=[pl.BlockSpec((tall, m.shape[1]), mine_map) for m in mine]
            + [pl.BlockSpec((tall, m.shape[1]), other_map) for m in mine],
            out_specs=[
                pl.BlockSpec((tall, n), lambda h, i, b, t: (h * steps + i, 0)) for n in widths
            ]
            + [pl.BlockSpec(memory_space=pltpu.SMEM)],
        ),
        out_shape=[jax.ShapeDtypeStruct((2 * count, n), F32) for n in widths]
        + [jax.ShapeDtypeStruct((1,), jnp.int32)],
        compiler_params=pltpu.CompilerParams(
            dimension_semantics=("arbitrary", "arbitrary"), vmem_limit_bytes=VMEM_LIMIT
        ),
        cost_estimate=FREE,
        name="join",
    )(bit.reshape(1), token, *mine, *other)


def project_back_kernel(groups, rows, *refs):
    grad_refs, w_refs, refs = refs[:groups], refs[groups : 2 * groups], refs[2 * groups :]
    own_ref, sent_ref, sums_refs = refs[0], refs[1], refs[2:]
    i = pl.program_id(0)

    def flat(ref):
        return ref[...].reshape(-1, ref.shape[-1])

    total = matmul(flat(grad_refs[0]), w_refs[0][...], NT)
    for grad_ref, w_ref in zip(grad_refs[1:], w_refs[1:]):
        total = total + matmul(flat(grad_ref), w_ref[...], NT)

    @pl.when(i < rows)
    def _():
        own_ref[...] = total.reshape(own_ref.shape)

    @pl.when(i >= rows)
    def _():
        sent_ref[...] = total.astype(BF16).reshape(sent_ref.shape)

    @pl.when(i == 0)
    def _():
        for sums_ref in sums_refs:
            sums_ref[...] = jnp.zeros_like(sums_ref)

    for grad_ref, sums_ref in zip(grad_refs, sums_refs):
        sums_ref[0:1, :] += jnp.sum(flat(grad_ref).astype(F32), axis=0, keepdims=True)


def project_back(grads, weights, rows):
    blocks, size, _ = grads[0].shape
    step = 2 if rows % 2 == 0 else 1
    turn = rows // step
    model = weights[0].shape[0]
    still = lambda i: (0, 0)
    shape = jax.ShapeDtypeStruct
    out = pl.pallas_call(
        functools.partial(project_back_kernel, len(grads), turn),
        grid=(blocks // step,),
        in_specs=[pl.BlockSpec((step, size, g.shape[2]), lambda i: (i, 0, 0)) for g in grads]
        + [pl.BlockSpec(w.shape, still) for w in weights],
        out_specs=[
            pl.BlockSpec((step, size, model), lambda i: (jnp.minimum(i, turn - 1), 0, 0)),
            pl.BlockSpec((step, size, model), lambda i: (jnp.maximum(i - turn, 0), 0, 0)),
        ]
        + [pl.BlockSpec((8, g.shape[2]), still) for g in grads],
        out_shape=[
            shape((rows, size, model), F32),
            shape((blocks - rows, size, model), BF16),
        ]
        + [shape((8, g.shape[2]), F32) for g in grads],
        compiler_params=pltpu.CompilerParams(
            dimension_semantics=("arbitrary",), vmem_limit_bytes=VMEM_LIMIT
        ),
        cost_estimate=FREE,
        name="project_back",
    )(*grads, *weights)
    return out[0], out[1], [sums[0] for sums in out[2:]]


def norm_back_kernel(count, x_ref, own_ref, *refs):
    arrived_refs, (resid_ref, gain_ref, tokens_ref, sums_ref) = refs[:count], refs[count:]

    @pl.when(pl.program_id(0) == 0)
    def _():
        sums_ref[...] = jnp.zeros_like(sums_ref)

    values = x_ref[0].astype(F32)
    center = values - jnp.mean(values, axis=-1, keepdims=True)
    root = lax.rsqrt(jnp.mean(center * center, axis=-1, keepdims=True) + EPS)
    normed = center * root
    back = own_ref[0]
    for arrived_ref in arrived_refs:
        back = back + arrived_ref[0].astype(F32)
    scaled = back * gain_ref[...]
    grad = root * (
        scaled
        - jnp.mean(scaled, axis=-1, keepdims=True)
        - normed * jnp.mean(scaled * normed, axis=-1, keepdims=True)
    )
    tokens_ref[0] = (resid_ref[0] + grad).astype(BF16)
    sums_ref[0:1, :] += jnp.sum(back * normed, axis=0, keepdims=True)
    sums_ref[1:2, :] += jnp.sum(back, axis=0, keepdims=True)


def norm_back(x, own, arrived, grad_resid, gain):
    rows, size, model = x.shape
    slab = pl.BlockSpec((1, size, model), lambda i: (i, 0, 0))
    return pl.pallas_call(
        functools.partial(norm_back_kernel, len(arrived)),
        grid=(rows,),
        in_specs=[slab] * (3 + len(arrived)) + [pl.BlockSpec((1, model), lambda i: (0, 0))],
        out_specs=[slab, pl.BlockSpec((8, model), lambda i: (0, 0))],
        out_shape=[
            jax.ShapeDtypeStruct((rows, size, model), BF16),
            jax.ShapeDtypeStruct((8, model), F32),
        ],
        compiler_params=pltpu.CompilerParams(
            dimension_semantics=("arbitrary",), vmem_limit_bytes=VMEM_LIMIT
        ),
        cost_estimate=FREE,
        name="norm_back",
    )(x, own, *arrived, grad_resid, gain)


def spread_kernel(parts, spans, part_ref, *refs):
    out_ref, refs = refs[-1], refs[:-1]
    part = part_ref[0]
    begin = 0
    for which in range(3):
        for p in range(parts):
            for g, span in enumerate(spans):
                piece = None
                for s in range(parts):
                    here = refs[s * len(spans) + g][:, which * span : (which + 1) * span]
                    piece = here if piece is None else jnp.where((part ^ p) == s, here, piece)
                out_ref[:, begin : begin + span] = piece.astype(F32)
                begin += span


def spread(pieces, part, spans):
    parts = len(pieces)
    count = pieces[0][0].shape[0]
    tall = next(t for t in (192, 96, 48, count) if count % t == 0)
    flat = [p for piece in pieces for p in piece]
    columns = 3 * parts * sum(spans)
    return pl.pallas_call(
        functools.partial(spread_kernel, parts, spans),
        grid_spec=pltpu.PrefetchScalarGridSpec(
            num_scalar_prefetch=1,
            grid=(count // tall,),
            in_specs=[pl.BlockSpec((tall, p.shape[1]), lambda i, b: (i, 0)) for p in flat],
            out_specs=pl.BlockSpec((tall, columns), lambda i, b: (i, 0)),
        ),
        out_shape=jax.ShapeDtypeStruct((count, columns), F32),
        compiler_params=pltpu.CompilerParams(
            dimension_semantics=("arbitrary",), vmem_limit_bytes=VMEM_LIMIT
        ),
        cost_estimate=pl.CostEstimate(
            flops=count * columns, transcendentals=0, bytes_accessed=6 * count * columns
        ),
        name="spread",
    )(part.reshape(1), *flat)


def layout_kernel(owner_ref, sizes_ref, prefixes_ref, lens_ref, padding_ref, info_ref, flags_ref):
    blocks, _, size = info_ref.shape
    groups, slots = lens_ref.shape[1:]
    row = owner_ref[0]
    places = lax.broadcasted_iota(jnp.int32, (blocks, size), 0) * size + lax.broadcasted_iota(
        jnp.int32, (blocks, size), 1
    )
    filled = blocks * size - padding_ref[row]
    prefix_start = jnp.full((blocks, size), filled, jnp.int32)
    prefix_end, own_start = prefix_start, prefix_start
    start = jnp.int32(0)
    for g in range(groups):
        body = start + prefixes_ref[row, g]
        end = jnp.int32(0)
        base = jnp.zeros((blocks, size), jnp.int32)
        for j in range(slots):
            end = end + jnp.where(j < sizes_ref[row, g], lens_ref[row, g, j], 0)
            base = jnp.where(places - body >= end, end, base)
        stop = body + end
        member = (places >= start) & (places < stop) & (places < filled)
        solution = places >= body
        prefix_start = jnp.where(member, start, prefix_start)
        prefix_end = jnp.where(member, jnp.where(solution, body, start), prefix_end)
        own_start = jnp.where(member, jnp.where(solution, body + base, start), own_start)
        start = stop
    info_ref[...] = jnp.zeros_like(info_ref)
    for i, values in enumerate((prefix_start, prefix_end, own_start, places)):
        info_ref[:, i, :] = values
    lane = lax.broadcasted_iota(jnp.int32, flags_ref.shape, 1)
    flags = jnp.zeros(flags_ref.shape, jnp.int32)
    for j in range(blocks):
        low, high = j * size, (j + 1) * size
        need = (jnp.maximum(prefix_start, low) < jnp.minimum(prefix_end, high)) | (
            jnp.maximum(own_start, low) < jnp.minimum(places + 1, high)
        )
        any_need = jnp.max(jnp.where(need, 1, 0), axis=1, keepdims=True)
        flags = jnp.where(lane == j, any_need, flags)
    flags_ref[...] = flags


def row_layout(owner, sizes, prefixes, lens, padding, blocks, size):
    scalars = pl.BlockSpec(memory_space=pltpu.SMEM)
    info, flags = pl.pallas_call(
        layout_kernel,
        in_specs=[scalars] * 5,
        out_shape=(
            jax.ShapeDtypeStruct((blocks, 8, size), jnp.int32),
            jax.ShapeDtypeStruct((blocks, 128), jnp.int32),
        ),
        name="row_layout",
    )(owner.reshape(1).astype(jnp.int32), sizes, prefixes, lens, padding)
    return info, flags[:, :blocks].reshape(-1)


def swap(values, axis, mask):
    count = lax.axis_size(axis)
    return lax.ppermute(values, axis, [(i, i ^ mask) for i in range(count)])


def bits(count):
    return [1 << b for b in range(count.bit_length() - 1)]


def take(values, index):
    return lax.dynamic_index_in_dim(values, index, 0, keepdims=False)


def halve(values, step):
    axis, mask, bit = step
    two = values.reshape(2, values.shape[0] // 2, *values.shape[1:])
    arrived = swap(take(two, 1 - bit), axis, mask)
    return (take(two, bit).astype(F32) + arrived.astype(F32)).astype(values.dtype)


def double(values, step):
    axis, mask, bit = step
    arrived = swap(values, axis, mask)
    first = jnp.where(bit == 0, values, arrived)
    second = jnp.where(bit == 0, arrived, values)
    return jnp.concatenate([first, second], axis=0)


class Chain:
    def __init__(self, values, down, up):
        self.values = values
        self.left = [(halve, step) for step in down] + [(double, step) for step in up]

    def advance(self):
        if self.left:
            move, step = self.left.pop(0)
            self.values = move(self.values, step)


def close(chains, *others, early=()):
    order = chains[3:][::-1], chains[2::-1]
    others, small, early, large = lax.optimization_barrier(
        (others, [c.values for c in order[0]], early, [c.values for c in order[1]])
    )
    for chain, values in zip(order[0] + order[1], small + large):
        chain.values = values
    return (*others, *early)


def per_device(
    row_axis,
    tokens,
    segment_ids,
    group_sizes,
    prefix_lens,
    solution_lens,
    padding_counts,
    attn_gain,
    attn_shift,
    w_qkv,
    query_bias,
    value_bias,
    w_out,
    out_bias,
    ffn_gain,
    ffn_shift,
    w_up,
    up_bias,
    w_down,
    down_bias,
    cotangent,
):
    rows, size, model = tokens.shape
    devices = lax.axis_size("pos")
    parts = devices // rows
    blocks = devices
    heads = model // HEAD_DIM // parts
    width = heads * HEAD_DIM
    place = lax.axis_index("pos")
    owner, part = place // parts, place % parts

    def bring(values):
        return jnp.stack(
            [
                swap(take(values, owner ^ m), "pos", m * parts) if m else take(values, owner)
                for m in range(rows)
            ]
        )

    def send_back(values, m):
        return swap(values[m], "pos", m * parts) if m else values[m]

    def arrange(slabs):
        out = jnp.zeros((rows, *slabs[0].shape), slabs[0].dtype)
        for m, slab in enumerate(slabs):
            out = lax.dynamic_update_index_in_dim(out, slab, owner ^ m, 0)
        return out

    info, flags = row_layout(
        owner, group_sizes, prefix_lens, solution_lens, padding_counts, blocks, size
    )
    order = jnp.arange(blocks, dtype=jnp.int32)
    phys = (((order % parts) ^ part) * rows + ((order // parts) ^ owner)).astype(jnp.int32)

    def my_columns(start, first=0, count=None):
        begin = start * model + part * width + first
        return lax.dynamic_slice_in_dim(w_qkv, begin, count or width, 1)

    def as_row(vector):
        return vector.astype(F32).reshape(1, -1)

    groups = [(0, 4), (4, 2)] if heads == 6 else [(0, heads)]
    spans = [count * HEAD_DIM for _, count in groups]
    w_mine = jnp.concatenate([my_columns(n) for n in range(3)], axis=1)
    w_groups = [
        jnp.concatenate([my_columns(n, h * HEAD_DIM, c * HEAD_DIM) for n in range(3)], axis=1)
        for h, c in groups
    ]
    bias_q = lax.dynamic_slice_in_dim(query_bias, part * width, width, 0)
    bias_v = lax.dynamic_slice_in_dim(value_bias, part * width, width, 0)

    mine = bring(tokens)
    row = jnp.concatenate([mine] + [swap(mine, "pos", s) for s in range(1, parts)], axis=0)
    cotangent, row = lax.optimization_barrier((cotangent, row))
    own_cotangent = bring(cotangent)
    act_one, query_t, key, key_t, value, value_t = project(
        row, as_row(attn_gain), as_row(attn_shift), w_mine, as_row(bias_q), as_row(bias_v)
    )
    mixed_all, out_t, lse = attention_forward(
        phys, flags, query_t, key, value_t, info, heads
    )
    mixed_all, own_cotangent = lax.optimization_barrier((mixed_all, own_cotangent))
    mixed_parts = []
    for s in range(parts):
        piece = mixed_all[s * rows : (s + 1) * rows]
        mixed_parts.append(swap(piece, "pos", s) if s else piece)

    (act_two, hidden, grad_upper, layer_out, grad_resid, grad_attn), grad_mixed, sums, up_sum = feed(
        mixed_parts, mine, own_cotangent, w_out, part, w_up, w_down,
        {
            "out_bias": as_row(out_bias),
            "gain": as_row(ffn_gain),
            "shift": as_row(ffn_shift),
            "down_bias": as_row(down_bias),
        },
        as_row(up_bias),
    )
    local = rows * size

    def flat(values):
        return values.reshape(-1, values.shape[-1])

    row_place = lax.axis_index(row_axis)
    row_steps = [(row_axis, m, (row_place // m) % 2) for m in bits(lax.axis_size(row_axis))]
    own_steps = [("pos", m * parts, (owner // m) % 2) for m in bits(rows)]
    part_steps = [("pos", m, (part // m) % 2) for m in bits(parts)]
    turning, last = own_steps + row_steps[:1], row_steps[1:]

    def order(turn):
        turn %= len(turning)
        return turning[turn:] + turning[:turn] + last

    def chain(values, turn, parted=True):
        down = order(turn)
        up = down[::-1] + (part_steps[:0:-1] if parted else [])
        return Chain(values, (part_steps if parted else []) + down, up)

    wide = w_up.shape[1]
    cut = wide * 2 // 3
    near = [m for m in range(1, rows) if m & (m - 1) == 0]
    far = [m for m in range(1, rows) if m & (m - 1)]

    received = [g if s == 0 else swap(g, "pos", s) for s, g in enumerate(grad_mixed)]
    layer_slabs = {m: send_back(layer_out, m) for m in [0] + near}
    down = chain(matmul(flat(hidden), flat(own_cotangent), TN).astype(BF16), 0)
    received, layer_slabs, layer_out, grad_upper = close(
        [down], received, layer_slabs, layer_out, grad_upper
    )
    down.advance()
    layer_slabs.update({m: send_back(layer_out, m) for m in far})
    stacked = jnp.stack(mixed_parts)
    mixed = jnp.concatenate([flat(take(stacked, g ^ part)) for g in range(parts)], axis=1)
    grad_up_flat = flat(grad_upper)
    up_one = chain(matmul(flat(act_two), grad_up_flat[:, :cut], TN).astype(BF16), 1)
    up_two = chain(
        jnp.concatenate(
            [
                matmul(flat(act_two), grad_up_flat[:, cut:], TN).astype(BF16),
                matmul(mixed, flat(grad_attn), TN).astype(BF16),
            ],
            axis=1,
        ),
        2,
    )
    chains = [down, up_one, up_two]
    received, layer_slabs = close(chains, received, layer_slabs)
    layer_home = arrange([layer_slabs[m] for m in range(rows)])
    up_one.advance()
    up_two.advance()
    for _ in part_steps[1:]:
        for c in chains:
            c.advance()
    grad_t = jnp.concatenate(received, axis=0).transpose(0, 2, 1)
    grad_t, layer_home = close(chains, grad_t, layer_home)

    grads, shares = [], []
    for h, count in groups:
        for c in shares[::-1] + chains[::-1]:
            c.advance()
        grad = attention_backward(
            phys, flags, query_t, grad_t, out_t, lse, info, key, key_t, value, count, h
        )
        grad, grad_t = close(chains + shares, grad, grad_t)
        grads.append(grad)
        if len(grads) < len(groups):
            shares.append(chain(matmul(flat(act_one), flat(grad), TN).astype(BF16), 0, False))
            (grad_t,) = close(chains + shares, grad_t)

    def placed(values):
        return lax.dynamic_update_slice_in_dim(jnp.zeros((model,), F32), values, part * width, 0)

    shares.append(chain(matmul(flat(act_one), flat(grads[-1]), TN).astype(BF16), 0, False))
    for c in shares[::-1] + chains[::-1]:
        c.advance()
    own_act, sent_act, sums_grads = project_back(grads, w_groups, rows)
    arrived_act = [
        swap(sent_act[(s - 1) * rows : s * rows], "pos", s) for s in range(1, parts)
    ]

    def column_sums(which):
        return jnp.concatenate(
            [g[which * n : (which + 1) * n] for g, n in zip(sums_grads, spans)]
        )

    sums_q, sums_v = placed(column_sums(0)), placed(column_sums(2))
    own_act, arrived_act, sums_q, sums_v = close(
        chains + shares, own_act, arrived_act, sums_q, sums_v
    )

    for c in shares[::-1] + chains[::-1]:
        c.advance()
    tokens_grad, norm_sums = norm_back(mine, own_act, arrived_act, grad_resid, as_row(attn_gain))
    small = jnp.concatenate(
        [
            norm_sums[0],
            norm_sums[1],
            sums_q,
            sums_v,
            sums[:4].reshape(-1),
            up_sum[0],
        ]
    )
    tokens_grad, small = close(chains + shares, tokens_grad, small)

    small_steps = part_steps + own_steps + row_steps
    token_slabs = {0: tokens_grad[0]}
    waves = [near, far]
    while any(c.left for c in chains):
        if small_steps:
            axis, mask, _ = small_steps.pop(0)
            small = small + swap(small, axis, mask)
        for c in shares[::-1] + chains[::-1]:
            c.advance()
        wave = waves.pop(0) if waves else []
        token_slabs.update({m: send_back(tokens_grad, m) for m in wave})
        small, tokens_grad, *arrived = close(
            chains + shares, small, tokens_grad, early=tuple(token_slabs[m] for m in wave)
        )
        token_slabs.update(zip(wave, arrived))

    axis, mask, bit = part_steps[0]
    others = [swap(c.values, axis, mask) for c in chains[::-1]][::-1]
    token = own_steps[0][2].astype(jnp.int32).reshape(1)
    sum_w_down, token = join(
        [down.values], others[:1], bit, ((0, 0, 0, 0, model),), (model,), token
    )
    sum_w_up, sum_w_out, token = join(
        [up_one.values, up_two.values],
        others[1:],
        bit,
        ((0, 0, 0, 0, cut), (1, 0, 0, cut, wide - cut), (1, wide - cut, 1, 0, model)),
        (wide, model),
        token,
    )
    for c in shares:
        if c.left:
            move, (axis_last, mask_last, _) = c.left[-1]
            c.left[-1] = (move, (axis_last, mask_last, token[0]))
    tokens_home = arrange([token_slabs[m] for m in range(rows)])
    while any(c.left for c in shares):
        for c in shares:
            c.advance()
    for axis, mask, _ in small_steps:
        small = small + swap(small, axis, mask)
    summed = [c.values for c in shares]
    pieces = [summed] + [[swap(g, "pos", s) for g in summed] for s in range(1, parts)]
    sum_w_qkv = spread(pieces, part, spans)

    vectors = small[: 8 * model].reshape(8, model)
    return (
        layer_home,
        tokens_home,
        vectors[0],
        vectors[1],
        sum_w_qkv,
        vectors[2],
        vectors[3],
        sum_w_out,
        vectors[4],
        vectors[5],
        vectors[6],
        sum_w_up,
        small[8 * model :],
        sum_w_down,
        vectors[7],
    )


def solution(mesh):
    in_specs = (
        P("rows", "pos", None),
        P("rows", "pos"),
        P("rows", None),
        P("rows", None),
        P("rows", None, None),
        P("rows"),
        *([P()] * 13),
        P("rows", "pos", None),
    )
    out_specs = (P("rows", "pos", None), P("rows", "pos", None), *([P()] * 13))
    return jax.shard_map(
        functools.partial(per_device, "rows"),
        mesh=mesh,
        in_specs=in_specs,
        out_specs=out_specs,
        check_vma=False,
    )
```

```python
import functools

import jax
import jax.numpy as jnp
from jax import lax
from jax.experimental import pallas as pl
from jax.experimental.pallas import tpu as pltpu
from jax.sharding import PartitionSpec as P

HEAD_DIM = 64
EPS = 1e-05
NEG = -1e30
GELU_C = 0.7978845608028654
F32 = jnp.float32
BF16 = jnp.bfloat16
VMEM_LIMIT = 60 * 1024 * 1024
FREE = pl.CostEstimate(flops=0, transcendentals=0, bytes_accessed=0)
NT = (((1,), (1,)), ((), ()))
TN = (((0,), (0,)), ((), ()))


def layer_norm(values, gain, shift):
    center = values - jnp.mean(values, axis=-1, keepdims=True)
    spread = jnp.mean(center * center, axis=-1, keepdims=True)
    return center * lax.rsqrt(spread + EPS) * gain + shift


def gelu_tanh(values):
    return 0.5 * values * (1.0 + jnp.tanh(GELU_C * (values + 0.044715 * values * values * values)))


def matmul(left, right, dims=(((1,), (0,)), ((), ()))):
    return lax.dot_general(left, right, dims, preferred_element_type=F32)


def head_pairs(heads):
    return [(h // 2, min(128, heads * HEAD_DIM - (h // 2) * 128)) for h in range(heads)]


def mask_bias(info_ref, key_start, size):
    prefix_start, prefix_end = info_ref[0, 0:1, :], info_ref[0, 1:2, :]
    own_start, query_place = info_ref[0, 2:3, :], info_ref[0, 3:4, :]
    key_place = key_start + lax.broadcasted_iota(jnp.int32, (size, size), 0)
    allowed = ((key_place >= prefix_start) & (key_place < prefix_end)) | (
        (key_place >= own_start) & (key_place <= query_place)
    )
    return jnp.where(allowed, 0.0, NEG).astype(F32)


def fill_padded(source_ref, target_ref, heads):
    for h, (pair, width) in enumerate(head_pairs(heads)):
        rows = source_ref[0, pair * 128 : pair * 128 + width, :]
        if width == 128:
            keep = (lax.broadcasted_iota(jnp.int32, rows.shape, 0) // HEAD_DIM) == (h % 2)
            rows = jnp.where(keep, rows, jnp.zeros_like(rows))
        target_ref[h, 0:width, :] = rows


def forward_kernel(
    heads, blocks, phys_ref, flag_ref, query_t_ref, key_ref, value_t_ref, info_ref,
    mixed_ref, out_t_ref, lse_ref, bias_sc, top_sc, total_sc, acc_sc, query_sc,
):
    size = query_t_ref.shape[2]
    i = pl.program_id(0)
    fill_padded(query_t_ref, query_sc, heads)
    top_sc[...] = jnp.full_like(top_sc, NEG)
    total_sc[...] = jnp.zeros_like(total_sc)
    acc_sc[...] = jnp.zeros_like(acc_sc)

    @pl.loop(0, i + 1)
    def _(j):
        @pl.when(flag_ref[i * blocks + j] > 0)
        def _():
            at = phys_ref[j]
            bias_sc[...] = mask_bias(info_ref, j * size, size)
            for h, (pair, width) in enumerate(head_pairs(heads)):
                rows = slice(h * HEAD_DIM, (h + 1) * HEAD_DIM)
                scores = (
                    matmul(key_ref[at, :, pair * 128 : pair * 128 + width], query_sc[h, 0:width, :])
                    + bias_sc[...]
                )
                old = top_sc[h]
                top = jnp.maximum(old, jnp.max(scores, axis=0, keepdims=True))
                shrink = jnp.exp(old - top)
                weights = jnp.exp(scores - top)
                total_sc[h] = shrink * total_sc[h] + jnp.sum(weights, axis=0, keepdims=True)
                top_sc[h] = top
                acc_sc[rows, :] = shrink * acc_sc[rows, :] + matmul(
                    value_t_ref[at, rows, :], weights.astype(BF16)
                )

    for h in range(heads):
        rows = slice(h * HEAD_DIM, (h + 1) * HEAD_DIM)
        out_t_ref[0, rows, :] = acc_sc[rows, :] / total_sc[h]
        lse_ref[0, h : h + 1, :] = top_sc[h] + jnp.log(total_sc[h])
    mixed_ref[0] = out_t_ref[0].T.astype(BF16)


def attention_forward(phys, flags, query_t, key, value_t, info, heads):
    blocks, width, size = query_t.shape
    lse_rows = -(-heads // 8) * 8
    whole = pl.Buffered(1)
    spec = pltpu.PrefetchScalarGridSpec(
        num_scalar_prefetch=2,
        grid=(blocks,),
        in_specs=[
            pl.BlockSpec((1, width, size), lambda i, p, f: (p[i], 0, 0)),
            pl.BlockSpec((blocks, size, width), lambda i, p, f: (0, 0, 0), pipeline_mode=whole),
            pl.BlockSpec((blocks, width, size), lambda i, p, f: (0, 0, 0), pipeline_mode=whole),
            pl.BlockSpec((1, 8, size), lambda i, p, f: (i, 0, 0)),
        ],
        out_specs=[
            pl.BlockSpec((1, size, width), lambda i, p, f: (p[i], 0, 0)),
            pl.BlockSpec((1, width, size), lambda i, p, f: (p[i], 0, 0)),
            pl.BlockSpec((1, lse_rows, size), lambda i, p, f: (p[i], 0, 0)),
        ],
        scratch_shapes=[
            pltpu.VMEM((size, size), F32),
            pltpu.VMEM((heads, 1, size), F32),
            pltpu.VMEM((heads, 1, size), F32),
            pltpu.VMEM((width, size), F32),
            pltpu.VMEM((heads, 128, size), BF16),
        ],
    )
    pairs = heads * blocks * (blocks + 1) // 2 * size * size
    return pl.pallas_call(
        functools.partial(forward_kernel, heads, blocks),
        grid_spec=spec,
        out_shape=(
            jax.ShapeDtypeStruct((blocks, size, width), BF16),
            jax.ShapeDtypeStruct((blocks, width, size), F32),
            jax.ShapeDtypeStruct((blocks, lse_rows, size), F32),
        ),
        compiler_params=pltpu.CompilerParams(
            dimension_semantics=("arbitrary",), vmem_limit_bytes=VMEM_LIMIT
        ),
        cost_estimate=pl.CostEstimate(
            flops=pairs * 4 * 128, transcendentals=pairs, bytes_accessed=blocks * size * width * 16
        ),
        name="attention_forward",
    )(phys, flags, query_t, key, value_t, info)


def backward_kernel(
    heads, first, blocks, phys_ref, flag_ref, query_t_ref, grad_t_ref, out_t_ref, lse_ref, info_ref,
    key_ref, key_t_ref, value_ref, grads_ref,
    bias_sc, query_grad_sc, key_grad_sc, value_grad_sc, query_sc, grad_sc, delta_sc,
):
    size = query_t_ref.shape[2]
    span = heads * HEAD_DIM
    i = pl.program_id(0)

    @pl.when(i == 0)
    def _():
        key_grad_sc[...] = jnp.zeros_like(key_grad_sc)
        value_grad_sc[...] = jnp.zeros_like(value_grad_sc)

    fill_padded(query_t_ref, query_sc, heads)
    fill_padded(grad_t_ref, grad_sc, heads)
    query_grad_sc[...] = jnp.zeros_like(query_grad_sc)
    for h in range(heads):
        rows = slice(h * HEAD_DIM, (h + 1) * HEAD_DIM)
        delta_sc[h] = jnp.sum(
            grad_t_ref[0, rows, :].astype(F32) * out_t_ref[0, rows, :], axis=0, keepdims=True
        )

    @pl.loop(0, i + 1)
    def _(j):
        @pl.when(flag_ref[i * blocks + j] > 0)
        def _():
            at = phys_ref[j]
            bias_sc[...] = mask_bias(info_ref, j * size, size)
            for h, (pair, width) in enumerate(head_pairs(heads)):
                rows = slice(h * HEAD_DIM, (h + 1) * HEAD_DIM)
                lanes = slice(pair * 128, pair * 128 + width)
                scores = matmul(key_ref[at, :, lanes], query_sc[h, 0:width, :]) + bias_sc[...]
                probs = jnp.exp(scores - lse_ref[0, first + h : first + h + 1, :])
                grad_probs = matmul(value_ref[at, :, lanes], grad_sc[h, 0:width, :])
                grad_scores = (probs * (grad_probs - delta_sc[h])).astype(BF16)
                query_grad_sc[rows, :] += matmul(key_t_ref[at, rows, :], grad_scores)
                value_grad_sc[at, rows, :] += matmul(
                    grad_t_ref[0, rows, :], probs.astype(BF16), NT
                )
                key_grad_sc[at, rows, :] += matmul(query_t_ref[0, rows, :], grad_scores, NT)

    grads_ref[phys_ref[i], :, 0:span] = (query_grad_sc[...] * 0.125).T.astype(BF16)

    @pl.when(i == blocks - 1)
    def _():
        for block in range(blocks):
            grads_ref[block, :, span : 2 * span] = key_grad_sc[block].T.astype(BF16)
            grads_ref[block, :, 2 * span :] = value_grad_sc[block].T.astype(BF16)


def attention_backward(
    phys, flags, query_t, grad_t, out_t, lse, info, key, key_t, value, heads, first
):
    blocks, _, size = query_t.shape
    span = heads * HEAD_DIM
    c = first // heads
    moving_t = pl.BlockSpec((1, span, size), lambda i, p, f: (p[i], c, 0))
    whole = pl.BlockSpec(
        (blocks, size, span), lambda i, p, f: (0, 0, c), pipeline_mode=pl.Buffered(1)
    )
    whole_t = pl.BlockSpec(
        (blocks, span, size), lambda i, p, f: (0, c, 0), pipeline_mode=pl.Buffered(1)
    )
    spec = pltpu.PrefetchScalarGridSpec(
        num_scalar_prefetch=2,
        grid=(blocks,),
        in_specs=[
            moving_t,
            moving_t,
            moving_t,
            pl.BlockSpec((1, lse.shape[1], size), lambda i, p, f: (p[i], 0, 0)),
            pl.BlockSpec((1, 8, size), lambda i, p, f: (i, 0, 0)),
            whole,
            whole_t,
            whole,
        ],
        out_specs=pl.BlockSpec(
            (blocks, size, 3 * span), lambda i, p, f: (0, 0, 0), pipeline_mode=pl.Buffered(1)
        ),
        scratch_shapes=[
            pltpu.VMEM((size, size), F32),
            pltpu.VMEM((span, size), F32),
            pltpu.VMEM((blocks, span, size), F32),
            pltpu.VMEM((blocks, span, size), F32),
            pltpu.VMEM((heads, 128, size), BF16),
            pltpu.VMEM((heads, 128, size), BF16),
            pltpu.VMEM((heads, 1, size), F32),
        ],
    )
    pairs = heads * blocks * (blocks + 1) // 2 * size * size
    return pl.pallas_call(
        functools.partial(backward_kernel, heads, first, blocks),
        grid_spec=spec,
        out_shape=jax.ShapeDtypeStruct((blocks, size, 3 * span), BF16),
        compiler_params=pltpu.CompilerParams(
            dimension_semantics=("arbitrary",), vmem_limit_bytes=VMEM_LIMIT
        ),
        cost_estimate=pl.CostEstimate(
            flops=pairs * 10 * 128, transcendentals=pairs, bytes_accessed=blocks * size * span * 20
        ),
        name="attention_backward",
    )(phys, flags, query_t, grad_t, out_t, lse, info, key, key_t, value)


def project_kernel(
    width, x_ref, gain_ref, shift_ref, w_ref, bias_q_ref, bias_v_ref,
    act_ref, query_t_ref, key_ref, key_t_ref, value_ref, value_t_ref,
):
    act = layer_norm(x_ref[0].astype(F32), gain_ref[...], shift_ref[...]).astype(BF16)
    act_ref[0] = act
    query = (matmul(act, w_ref[:, :width]) + bias_q_ref[...]).astype(BF16).astype(F32) * 0.125
    query_t_ref[0] = query.T.astype(BF16)
    key = matmul(act, w_ref[:, width : 2 * width])
    key_ref[0] = key.astype(BF16)
    key_t_ref[0] = key.T.astype(BF16)
    value = matmul(act, w_ref[:, 2 * width :]) + bias_v_ref[...]
    value_ref[0] = value.astype(BF16)
    value_t_ref[0] = value.T.astype(BF16)


def project(x, gain, shift, weight, bias_q, bias_v):
    blocks, size, model = x.shape
    width = bias_q.shape[1]
    still = lambda i: (0, 0)
    step = lambda i: (i, 0, 0)
    straight, turned = (
        jax.ShapeDtypeStruct((blocks, size, width), BF16),
        jax.ShapeDtypeStruct((blocks, width, size), BF16),
    )
    wide, tall = pl.BlockSpec((1, size, width), step), pl.BlockSpec((1, width, size), step)
    return pl.pallas_call(
        functools.partial(project_kernel, width),
        grid=(blocks,),
        in_specs=[
            pl.BlockSpec((1, size, model), step),
            pl.BlockSpec((1, model), still),
            pl.BlockSpec((1, model), still),
            pl.BlockSpec(weight.shape, still, pipeline_mode=pl.Buffered(1)),
            pl.BlockSpec((1, width), still),
            pl.BlockSpec((1, width), still),
        ],
        out_specs=[pl.BlockSpec((1, size, model), step), tall, wide, tall, wide, tall],
        out_shape=(
            jax.ShapeDtypeStruct((blocks, size, model), BF16),
            turned, straight, turned, straight, turned,
        ),
        compiler_params=pltpu.CompilerParams(
            dimension_semantics=("arbitrary",), vmem_limit_bytes=VMEM_LIMIT
        ),
        cost_estimate=pl.CostEstimate(
            flops=2 * blocks * size * model * 3 * width,
            transcendentals=blocks * size,
            bytes_accessed=blocks * size * (4 * model + 10 * width),
        ),
        name="project",
    )(x, gain, shift, weight, bias_q, bias_v)


def feed_kernel(
    parts, pieces, *refs
):
    mixed_refs, refs = refs[:parts], refs[parts:]
    x_ref, cot_ref, refs = refs[0], refs[1], refs[2:]
    w_out_refs, refs = refs[:parts], refs[parts:]
    (w_up_ref, w_down_ref, out_bias_ref, gain_ref, shift_ref, up_bias_ref, down_bias_ref), refs = (
        refs[:7], refs[7:],
    )
    act_ref, hidden_ref, grad_upper_ref, layer_ref, grad_resid_ref, grad_attn_ref = refs[:6]
    refs = refs[6:]
    grad_mixed_refs, refs = refs[:parts], refs[parts:]
    sums_ref, up_sum_ref, layer_sc, back_sc = refs
    first = pl.program_id(0) == 0

    @pl.when(first)
    def _():
        sums_ref[...] = jnp.zeros_like(sums_ref)
        up_sum_ref[...] = jnp.zeros_like(up_sum_ref)

    attn = out_bias_ref[...]
    for mixed_ref, w_ref in zip(mixed_refs, w_out_refs):
        attn = attn + matmul(mixed_ref[0], w_ref[...])
    resid = x_ref[0].astype(F32) + attn
    center = resid - jnp.mean(resid, axis=-1, keepdims=True)
    root = lax.rsqrt(jnp.mean(center * center, axis=-1, keepdims=True) + EPS)
    normed = center * root
    gain = gain_ref[...]
    act_ref[0] = (normed * gain + shift_ref[...]).astype(BF16)
    layer_sc[...] = resid + down_bias_ref[...]
    back_sc[...] = jnp.zeros_like(back_sc)
    span = w_up_ref.shape[1] // pieces

    for c in range(pieces):
        lanes = slice(c * span, (c + 1) * span)
        upper = matmul(act_ref[0], w_up_ref[:, lanes]) + up_bias_ref[:, lanes]
        square = upper * upper
        bend = jnp.tanh(GELU_C * upper * (1.0 + 0.044715 * square))
        half = 0.5 * (1.0 + bend)
        hidden = (upper * half).astype(BF16)
        hidden_ref[0, :, lanes] = hidden
        slope = half + 0.5 * GELU_C * upper * (1.0 - bend * bend) * (1.0 + 0.134145 * square)
        grad_upper = (matmul(cot_ref[0], w_down_ref[lanes, :], NT) * slope).astype(BF16)
        grad_upper_ref[0, :, lanes] = grad_upper
        up_sum_ref[0:1, lanes] += jnp.sum(grad_upper.astype(F32), axis=0, keepdims=True)
        layer_sc[...] += matmul(hidden, w_down_ref[lanes, :])
        back_sc[...] += matmul(grad_upper, w_up_ref[:, lanes], NT)

    layer_ref[0] = layer_sc[...].astype(BF16)
    back = back_sc[...]
    scaled = back * gain
    grad_out = cot_ref[0].astype(F32)
    grad_resid = grad_out + root * (
        scaled
        - jnp.mean(scaled, axis=-1, keepdims=True)
        - normed * jnp.mean(scaled * normed, axis=-1, keepdims=True)
    )
    grad_resid_ref[0] = grad_resid
    grad_attn = grad_resid.astype(BF16)
    grad_attn_ref[0] = grad_attn
    for w_ref, grad_mixed_ref in zip(w_out_refs, grad_mixed_refs):
        grad_mixed_ref[0] = matmul(grad_attn, w_ref[...], NT).astype(BF16)
    sums_ref[0:1, :] += jnp.sum(grad_attn.astype(F32), axis=0, keepdims=True)
    sums_ref[1:2, :] += jnp.sum(back * normed, axis=0, keepdims=True)
    sums_ref[2:3, :] += jnp.sum(back, axis=0, keepdims=True)
    sums_ref[3:4, :] += jnp.sum(grad_out, axis=0, keepdims=True)


def feed(mixed, x, cotangent, w_out, part, w_up, w_down, vectors, up_bias):
    parts = len(mixed)
    rows, size, model = x.shape
    width = mixed[0].shape[2]
    wide = w_up.shape[1]
    still = lambda i, p: (0, 0)
    step = lambda i, p: (i, 0, 0)
    once = pl.Buffered(1)
    slab = pl.BlockSpec((1, size, model), step)
    head_slab = pl.BlockSpec((1, size, width), step)
    wide_slab = pl.BlockSpec((1, size, wide), step)
    vector = pl.BlockSpec((1, model), still)
    w_out_specs = [
        pl.BlockSpec((width, model), lambda i, p, s=s: (p[0] ^ s, 0), pipeline_mode=once)
        for s in range(parts)
    ]

    def body(p_ref, *refs):
        feed_kernel(parts, wide // model, *refs)

    shape = jax.ShapeDtypeStruct
    out = pl.pallas_call(
        body,
        grid_spec=pltpu.PrefetchScalarGridSpec(
            num_scalar_prefetch=1,
            grid=(rows,),
            in_specs=[head_slab] * parts
            + [slab, slab]
            + w_out_specs
            + [
                pl.BlockSpec(w_up.shape, still, pipeline_mode=once),
                pl.BlockSpec(w_down.shape, still, pipeline_mode=once),
                vector,
                vector,
                vector,
                pl.BlockSpec((1, wide), still),
                vector,
            ],
            out_specs=[slab, wide_slab, wide_slab, slab, slab, slab]
            + [head_slab] * parts
            + [pl.BlockSpec((8, model), still), pl.BlockSpec((8, wide), still)],
            scratch_shapes=[
                pltpu.VMEM((size, model), F32),
                pltpu.VMEM((size, model), F32),
            ],
        ),
        out_shape=[
            shape((rows, size, model), BF16),
            shape((rows, size, wide), BF16),
            shape((rows, size, wide), BF16),
            shape((rows, size, model), BF16),
            shape((rows, size, model), F32),
            shape((rows, size, model), BF16),
        ]
        + [shape((rows, size, width), BF16)] * parts
        + [shape((8, model), F32), shape((8, wide), F32)],
        compiler_params=pltpu.CompilerParams(
            dimension_semantics=("arbitrary",), vmem_limit_bytes=VMEM_LIMIT
        ),
        cost_estimate=pl.CostEstimate(
            flops=2 * rows * size * model * (4 * wide + 2 * model),
            transcendentals=rows * size * wide,
            bytes_accessed=rows * size * (4 * wide + 16 * model),
        ),
        name="feed",
    )(
        part.reshape(1), *mixed, x, cotangent, *([w_out] * parts), w_up, w_down,
        vectors["out_bias"], vectors["gain"], vectors["shift"], up_bias, vectors["down_bias"],
    )
    return out[:6], out[6 : 6 + parts], out[6 + parts], out[7 + parts]


def join_kernel(sources, moves, bit_ref, token_ref, *refs):
    mine_refs, other_refs, out_refs = refs[:sources], refs[sources : 2 * sources], refs[2 * sources :]
    mine = pl.program_id(0) == bit_ref[0]
    for source, begin, out, place, count in moves:
        lanes = slice(begin, begin + count)
        out_refs[out][:, place : place + count] = jnp.where(
            mine, mine_refs[source][:, lanes], other_refs[source][:, lanes]
        ).astype(F32)
    out_refs[-1][0] = token_ref[0]


def join(mine, other, bit, moves, widths, token):
    count = mine[0].shape[0]
    largest = 384 if sum(widths) <= 1024 else 192
    tall = next(t for t in (largest, 192, 96, 48, count) if count % t == 0)
    steps = count // tall

    def mine_map(h, i, b, t):
        return jnp.where(h == b[0], i, jnp.where(h < b[0], 0, steps - 1)), 0

    def other_map(h, i, b, t):
        return jnp.where(h != b[0], i, jnp.where(h < 1 - b[0], 0, steps - 1)), 0

    return pl.pallas_call(
        functools.partial(join_kernel, len(mine), moves),
        grid_spec=pltpu.PrefetchScalarGridSpec(
            num_scalar_prefetch=2,
            grid=(2, steps),
            in_specs=[pl.BlockSpec((tall, m.shape[1]), mine_map) for m in mine]
            + [pl.BlockSpec((tall, m.shape[1]), other_map) for m in mine],
            out_specs=[
                pl.BlockSpec((tall, n), lambda h, i, b, t: (h * steps + i, 0)) for n in widths
            ]
            + [pl.BlockSpec(memory_space=pltpu.SMEM)],
        ),
        out_shape=[jax.ShapeDtypeStruct((2 * count, n), F32) for n in widths]
        + [jax.ShapeDtypeStruct((1,), jnp.int32)],
        compiler_params=pltpu.CompilerParams(
            dimension_semantics=("arbitrary", "arbitrary"), vmem_limit_bytes=VMEM_LIMIT
        ),
        cost_estimate=FREE,
        name="join",
    )(bit.reshape(1), token, *mine, *other)


def project_back_kernel(groups, rows, *refs):
    grad_refs, w_refs, refs = refs[:groups], refs[groups : 2 * groups], refs[2 * groups :]
    own_ref, sent_ref, sums_refs = refs[0], refs[1], refs[2:]
    i = pl.program_id(0)

    def flat(ref):
        return ref[...].reshape(-1, ref.shape[-1])

    total = matmul(flat(grad_refs[0]), w_refs[0][...], NT)
    for grad_ref, w_ref in zip(grad_refs[1:], w_refs[1:]):
        total = total + matmul(flat(grad_ref), w_ref[...], NT)

    @pl.when(i < rows)
    def _():
        own_ref[...] = total.reshape(own_ref.shape)

    @pl.when(i >= rows)
    def _():
        sent_ref[...] = total.astype(BF16).reshape(sent_ref.shape)

    @pl.when(i == 0)
    def _():
        for sums_ref in sums_refs:
            sums_ref[...] = jnp.zeros_like(sums_ref)

    for grad_ref, sums_ref in zip(grad_refs, sums_refs):
        sums_ref[0:1, :] += jnp.sum(flat(grad_ref).astype(F32), axis=0, keepdims=True)


def project_back(grads, weights, rows):
    blocks, size, _ = grads[0].shape
    step = 2 if rows % 2 == 0 else 1
    turn = rows // step
    model = weights[0].shape[0]
    still = lambda i: (0, 0)
    shape = jax.ShapeDtypeStruct
    out = pl.pallas_call(
        functools.partial(project_back_kernel, len(grads), turn),
        grid=(blocks // step,),
        in_specs=[pl.BlockSpec((step, size, g.shape[2]), lambda i: (i, 0, 0)) for g in grads]
        + [pl.BlockSpec(w.shape, still) for w in weights],
        out_specs=[
            pl.BlockSpec((step, size, model), lambda i: (jnp.minimum(i, turn - 1), 0, 0)),
            pl.BlockSpec((step, size, model), lambda i: (jnp.maximum(i - turn, 0), 0, 0)),
        ]
        + [pl.BlockSpec((8, g.shape[2]), still) for g in grads],
        out_shape=[
            shape((rows, size, model), F32),
            shape((blocks - rows, size, model), BF16),
        ]
        + [shape((8, g.shape[2]), F32) for g in grads],
        compiler_params=pltpu.CompilerParams(
            dimension_semantics=("arbitrary",), vmem_limit_bytes=VMEM_LIMIT
        ),
        cost_estimate=FREE,
        name="project_back",
    )(*grads, *weights)
    return out[0], out[1], [sums[0] for sums in out[2:]]


def norm_back_kernel(count, x_ref, own_ref, *refs):
    arrived_refs, (resid_ref, gain_ref, tokens_ref, sums_ref) = refs[:count], refs[count:]

    @pl.when(pl.program_id(0) == 0)
    def _():
        sums_ref[...] = jnp.zeros_like(sums_ref)

    values = x_ref[0].astype(F32)
    center = values - jnp.mean(values, axis=-1, keepdims=True)
    root = lax.rsqrt(jnp.mean(center * center, axis=-1, keepdims=True) + EPS)
    normed = center * root
    back = own_ref[0]
    for arrived_ref in arrived_refs:
        back = back + arrived_ref[0].astype(F32)
    scaled = back * gain_ref[...]
    grad = root * (
        scaled
        - jnp.mean(scaled, axis=-1, keepdims=True)
        - normed * jnp.mean(scaled * normed, axis=-1, keepdims=True)
    )
    tokens_ref[0] = (resid_ref[0] + grad).astype(BF16)
    sums_ref[0:1, :] += jnp.sum(back * normed, axis=0, keepdims=True)
    sums_ref[1:2, :] += jnp.sum(back, axis=0, keepdims=True)


def norm_back(x, own, arrived, grad_resid, gain):
    rows, size, model = x.shape
    slab = pl.BlockSpec((1, size, model), lambda i: (i, 0, 0))
    return pl.pallas_call(
        functools.partial(norm_back_kernel, len(arrived)),
        grid=(rows,),
        in_specs=[slab] * (3 + len(arrived)) + [pl.BlockSpec((1, model), lambda i: (0, 0))],
        out_specs=[slab, pl.BlockSpec((8, model), lambda i: (0, 0))],
        out_shape=[
            jax.ShapeDtypeStruct((rows, size, model), BF16),
            jax.ShapeDtypeStruct((8, model), F32),
        ],
        compiler_params=pltpu.CompilerParams(
            dimension_semantics=("arbitrary",), vmem_limit_bytes=VMEM_LIMIT
        ),
        cost_estimate=FREE,
        name="norm_back",
    )(x, own, *arrived, grad_resid, gain)


def spread_kernel(parts, spans, part_ref, *refs):
    out_ref, refs = refs[-1], refs[:-1]
    part = part_ref[0]
    begin = 0
    for which in range(3):
        for p in range(parts):
            for g, span in enumerate(spans):
                piece = None
                for s in range(parts):
                    here = refs[s * len(spans) + g][:, which * span : (which + 1) * span]
                    piece = here if piece is None else jnp.where((part ^ p) == s, here, piece)
                out_ref[:, begin : begin + span] = piece.astype(F32)
                begin += span


def spread(pieces, part, spans):
    parts = len(pieces)
    count = pieces[0][0].shape[0]
    tall = next(t for t in (192, 96, 48, count) if count % t == 0)
    flat = [p for piece in pieces for p in piece]
    columns = 3 * parts * sum(spans)
    return pl.pallas_call(
        functools.partial(spread_kernel, parts, spans),
        grid_spec=pltpu.PrefetchScalarGridSpec(
            num_scalar_prefetch=1,
            grid=(count // tall,),
            in_specs=[pl.BlockSpec((tall, p.shape[1]), lambda i, b: (i, 0)) for p in flat],
            out_specs=pl.BlockSpec((tall, columns), lambda i, b: (i, 0)),
        ),
        out_shape=jax.ShapeDtypeStruct((count, columns), F32),
        compiler_params=pltpu.CompilerParams(
            dimension_semantics=("arbitrary",), vmem_limit_bytes=VMEM_LIMIT
        ),
        cost_estimate=pl.CostEstimate(
            flops=count * columns, transcendentals=0, bytes_accessed=6 * count * columns
        ),
        name="spread",
    )(part.reshape(1), *flat)


def layout_kernel(owner_ref, sizes_ref, prefixes_ref, lens_ref, padding_ref, info_ref, flags_ref):
    blocks, _, size = info_ref.shape
    groups, slots = lens_ref.shape[1:]
    row = owner_ref[0]
    places = lax.broadcasted_iota(jnp.int32, (blocks, size), 0) * size + lax.broadcasted_iota(
        jnp.int32, (blocks, size), 1
    )
    filled = blocks * size - padding_ref[row]
    prefix_start = jnp.full((blocks, size), filled, jnp.int32)
    prefix_end, own_start = prefix_start, prefix_start
    start = jnp.int32(0)
    for g in range(groups):
        body = start + prefixes_ref[row, g]
        end = jnp.int32(0)
        base = jnp.zeros((blocks, size), jnp.int32)
        for j in range(slots):
            end = end + jnp.where(j < sizes_ref[row, g], lens_ref[row, g, j], 0)
            base = jnp.where(places - body >= end, end, base)
        stop = body + end
        member = (places >= start) & (places < stop) & (places < filled)
        solution = places >= body
        prefix_start = jnp.where(member, start, prefix_start)
        prefix_end = jnp.where(member, jnp.where(solution, body, start), prefix_end)
        own_start = jnp.where(member, jnp.where(solution, body + base, start), own_start)
        start = stop
    info_ref[...] = jnp.zeros_like(info_ref)
    for i, values in enumerate((prefix_start, prefix_end, own_start, places)):
        info_ref[:, i, :] = values
    lane = lax.broadcasted_iota(jnp.int32, flags_ref.shape, 1)
    flags = jnp.zeros(flags_ref.shape, jnp.int32)
    for j in range(blocks):
        low, high = j * size, (j + 1) * size
        need = (jnp.maximum(prefix_start, low) < jnp.minimum(prefix_end, high)) | (
            jnp.maximum(own_start, low) < jnp.minimum(places + 1, high)
        )
        any_need = jnp.max(jnp.where(need, 1, 0), axis=1, keepdims=True)
        flags = jnp.where(lane == j, any_need, flags)
    flags_ref[...] = flags


def row_layout(owner, sizes, prefixes, lens, padding, blocks, size):
    scalars = pl.BlockSpec(memory_space=pltpu.SMEM)
    info, flags = pl.pallas_call(
        layout_kernel,
        in_specs=[scalars] * 5,
        out_shape=(
            jax.ShapeDtypeStruct((blocks, 8, size), jnp.int32),
            jax.ShapeDtypeStruct((blocks, 128), jnp.int32),
        ),
        name="row_layout",
    )(owner.reshape(1).astype(jnp.int32), sizes, prefixes, lens, padding)
    return info, flags[:, :blocks].reshape(-1)


def swap(values, axis, mask):
    count = lax.axis_size(axis)
    return lax.ppermute(values, axis, [(i, i ^ mask) for i in range(count)])


def bits(count):
    return [1 << b for b in range(count.bit_length() - 1)]


def take(values, index):
    return lax.dynamic_index_in_dim(values, index, 0, keepdims=False)


def halve(values, step):
    axis, mask, bit = step
    two = values.reshape(2, values.shape[0] // 2, *values.shape[1:])
    arrived = swap(take(two, 1 - bit), axis, mask)
    return (take(two, bit).astype(F32) + arrived.astype(F32)).astype(values.dtype)


def double(values, step):
    axis, mask, bit = step
    arrived = swap(values, axis, mask)
    first = jnp.where(bit == 0, values, arrived)
    second = jnp.where(bit == 0, arrived, values)
    return jnp.concatenate([first, second], axis=0)


class Chain:
    def __init__(self, values, down, up):
        self.values = values
        self.left = [(halve, step) for step in down] + [(double, step) for step in up]

    def advance(self):
        if self.left:
            move, step = self.left.pop(0)
            self.values = move(self.values, step)


def close(chains, *others, early=()):
    order = chains[3:][::-1], chains[2::-1]
    others, small, early, large = lax.optimization_barrier(
        (others, [c.values for c in order[0]], early, [c.values for c in order[1]])
    )
    for chain, values in zip(order[0] + order[1], small + large):
        chain.values = values
    return (*others, *early)


def per_device(
    row_axis,
    tokens,
    segment_ids,
    group_sizes,
    prefix_lens,
    solution_lens,
    padding_counts,
    attn_gain,
    attn_shift,
    w_qkv,
    query_bias,
    value_bias,
    w_out,
    out_bias,
    ffn_gain,
    ffn_shift,
    w_up,
    up_bias,
    w_down,
    down_bias,
    cotangent,
):
    rows, size, model = tokens.shape
    devices = lax.axis_size("pos")
    parts = devices // rows
    blocks = devices
    heads = model // HEAD_DIM // parts
    width = heads * HEAD_DIM
    place = lax.axis_index("pos")
    owner, part = place // parts, place % parts

    def bring(values):
        return jnp.stack(
            [
                swap(take(values, owner ^ m), "pos", m * parts) if m else take(values, owner)
                for m in range(rows)
            ]
        )

    def send_back(values, m):
        return swap(values[m], "pos", m * parts) if m else values[m]

    def arrange(slabs):
        out = jnp.zeros((rows, *slabs[0].shape), slabs[0].dtype)
        for m, slab in enumerate(slabs):
            out = lax.dynamic_update_index_in_dim(out, slab, owner ^ m, 0)
        return out

    info, flags = row_layout(
        owner, group_sizes, prefix_lens, solution_lens, padding_counts, blocks, size
    )
    order = jnp.arange(blocks, dtype=jnp.int32)
    phys = (((order % parts) ^ part) * rows + ((order // parts) ^ owner)).astype(jnp.int32)

    def my_columns(start, first=0, count=None):
        begin = start * model + part * width + first
        return lax.dynamic_slice_in_dim(w_qkv, begin, count or width, 1)

    def as_row(vector):
        return vector.astype(F32).reshape(1, -1)

    groups = [(0, 4), (4, 2)] if heads == 6 else [(0, heads)]
    spans = [count * HEAD_DIM for _, count in groups]
    w_mine = jnp.concatenate([my_columns(n) for n in range(3)], axis=1)
    w_groups = [
        jnp.concatenate([my_columns(n, h * HEAD_DIM, c * HEAD_DIM) for n in range(3)], axis=1)
        for h, c in groups
    ]
    bias_q = lax.dynamic_slice_in_dim(query_bias, part * width, width, 0)
    bias_v = lax.dynamic_slice_in_dim(value_bias, part * width, width, 0)

    mine = bring(tokens)
    row = jnp.concatenate([mine] + [swap(mine, "pos", s) for s in range(1, parts)], axis=0)
    cotangent, row = lax.optimization_barrier((cotangent, row))
    own_cotangent = bring(cotangent)
    act_one, query_t, key, key_t, value, value_t = project(
        row, as_row(attn_gain), as_row(attn_shift), w_mine, as_row(bias_q), as_row(bias_v)
    )
    mixed_all, out_t, lse = attention_forward(
        phys, flags, query_t, key, value_t, info, heads
    )
    mixed_all, own_cotangent = lax.optimization_barrier((mixed_all, own_cotangent))
    mixed_parts = []
    for s in range(parts):
        piece = mixed_all[s * rows : (s + 1) * rows]
        mixed_parts.append(swap(piece, "pos", s) if s else piece)

    (act_two, hidden, grad_upper, layer_out, grad_resid, grad_attn), grad_mixed, sums, up_sum = feed(
        mixed_parts, mine, own_cotangent, w_out, part, w_up, w_down,
        {
            "out_bias": as_row(out_bias),
            "gain": as_row(ffn_gain),
            "shift": as_row(ffn_shift),
            "down_bias": as_row(down_bias),
        },
        as_row(up_bias),
    )
    local = rows * size

    def flat(values):
        return values.reshape(-1, values.shape[-1])

    row_place = lax.axis_index(row_axis)
    row_steps = [(row_axis, m, (row_place // m) % 2) for m in bits(lax.axis_size(row_axis))]
    own_steps = [("pos", m * parts, (owner // m) % 2) for m in bits(rows)]
    part_steps = [("pos", m, (part // m) % 2) for m in bits(parts)]
    turning, last = own_steps + row_steps[:1], row_steps[1:]

    def order(turn):
        turn %= len(turning)
        return turning[turn:] + turning[:turn] + last

    def chain(values, turn, parted=True):
        down = order(turn)
        up = down[::-1] + (part_steps[:0:-1] if parted else [])
        return Chain(values, (part_steps if parted else []) + down, up)

    wide = w_up.shape[1]
    cut = wide * 2 // 3
    near = [m for m in range(1, rows) if m & (m - 1) == 0]
    far = [m for m in range(1, rows) if m & (m - 1)]

    received = [g if s == 0 else swap(g, "pos", s) for s, g in enumerate(grad_mixed)]
    layer_slabs = {m: send_back(layer_out, m) for m in [0] + near}
    down = chain(matmul(flat(hidden), flat(own_cotangent), TN).astype(BF16), 0)
    received, layer_slabs, layer_out, grad_upper = close(
        [down], received, layer_slabs, layer_out, grad_upper
    )
    down.advance()
    layer_slabs.update({m: send_back(layer_out, m) for m in far})
    stacked = jnp.stack(mixed_parts)
    mixed = jnp.concatenate([flat(take(stacked, g ^ part)) for g in range(parts)], axis=1)
    grad_up_flat = flat(grad_upper)
    up_one = chain(matmul(flat(act_two), grad_up_flat[:, :cut], TN).astype(BF16), 1)
    up_two = chain(
        jnp.concatenate(
            [
                matmul(flat(act_two), grad_up_flat[:, cut:], TN).astype(BF16),
                matmul(mixed, flat(grad_attn), TN).astype(BF16),
            ],
            axis=1,
        ),
        2,
    )
    chains = [down, up_one, up_two]
    received, layer_slabs = close(chains, received, layer_slabs)
    up_one.advance()
    up_two.advance()
    for _ in part_steps[1:]:
        for c in chains:
            c.advance()
    grad_t = jnp.concatenate(received, axis=0).transpose(0, 2, 1)
    (grad_t,) = close(chains, grad_t)

    grads, shares = [], []
    for h, count in groups:
        for c in shares[::-1] + chains[::-1]:
            c.advance()
        grad = attention_backward(
            phys, flags, query_t, grad_t, out_t, lse, info, key, key_t, value, count, h
        )
        grad, grad_t = close(chains + shares, grad, grad_t)
        grads.append(grad)
        if len(grads) < len(groups):
            shares.append(chain(matmul(flat(act_one), flat(grad), TN).astype(BF16), 0, False))
            (grad_t,) = close(chains + shares, grad_t)

    def placed(values):
        return lax.dynamic_update_slice_in_dim(jnp.zeros((model,), F32), values, part * width, 0)

    shares.append(chain(matmul(flat(act_one), flat(grads[-1]), TN).astype(BF16), 0, False))
    for c in shares[::-1] + chains[::-1]:
        c.advance()
    own_act, sent_act, sums_grads = project_back(grads, w_groups, rows)
    arrived_act = [
        swap(sent_act[(s - 1) * rows : s * rows], "pos", s) for s in range(1, parts)
    ]

    def column_sums(which):
        return jnp.concatenate(
            [g[which * n : (which + 1) * n] for g, n in zip(sums_grads, spans)]
        )

    sums_q, sums_v = placed(column_sums(0)), placed(column_sums(2))
    own_act, arrived_act, sums_q, sums_v = close(
        chains + shares, own_act, arrived_act, sums_q, sums_v
    )

    for c in shares[::-1] + chains[::-1]:
        c.advance()
    tokens_grad, norm_sums = norm_back(mine, own_act, arrived_act, grad_resid, as_row(attn_gain))
    small = jnp.concatenate(
        [
            norm_sums[0],
            norm_sums[1],
            sums_q,
            sums_v,
            sums[:4].reshape(-1),
            up_sum[0],
        ]
    )
    tokens_grad, small = close(chains + shares, tokens_grad, small)

    small_steps = part_steps + own_steps + row_steps
    token_slabs = {0: tokens_grad[0]}
    layer_home = arrange([layer_slabs[m] for m in range(rows)])
    waves = [[], near + far]
    while any(c.left for c in chains):
        if small_steps:
            axis, mask, _ = small_steps.pop(0)
            small = small + swap(small, axis, mask)
        for c in shares[::-1] + chains[::-1]:
            c.advance()
        wave = waves.pop(0) if waves else []
        token_slabs.update({m: send_back(tokens_grad, m) for m in wave})
        small, tokens_grad, layer_home, *arrived = close(
            chains + shares, small, tokens_grad, layer_home,
            early=tuple(token_slabs[m] for m in wave),
        )
        token_slabs.update(zip(wave, arrived))

    axis, mask, bit = part_steps[0]
    others = [swap(c.values, axis, mask) for c in chains[::-1]][::-1]
    token = own_steps[0][2].astype(jnp.int32).reshape(1)
    sum_w_down, token = join(
        [down.values], others[:1], bit, ((0, 0, 0, 0, model),), (model,), token
    )
    sum_w_up, sum_w_out, token = join(
        [up_one.values, up_two.values],
        others[1:],
        bit,
        ((0, 0, 0, 0, cut), (1, 0, 0, cut, wide - cut), (1, wide - cut, 1, 0, model)),
        (wide, model),
        token,
    )
    for c in shares:
        if c.left:
            move, (axis_last, mask_last, _) = c.left[-1]
            c.left[-1] = (move, (axis_last, mask_last, token[0]))
    tokens_home = arrange([token_slabs[m] for m in range(rows)])
    while any(c.left for c in shares):
        for c in shares:
            c.advance()
    for axis, mask, _ in small_steps:
        small = small + swap(small, axis, mask)
    summed = [c.values for c in shares]
    pieces = [summed] + [[swap(g, "pos", s) for g in summed] for s in range(1, parts)]
    sum_w_qkv = spread(pieces, part, spans)

    vectors = small[: 8 * model].reshape(8, model)
    return (
        layer_home,
        tokens_home,
        vectors[0],
        vectors[1],
        sum_w_qkv,
        vectors[2],
        vectors[3],
        sum_w_out,
        vectors[4],
        vectors[5],
        vectors[6],
        sum_w_up,
        small[8 * model :],
        sum_w_down,
        vectors[7],
    )


def solution(mesh):
    in_specs = (
        P("rows", "pos", None),
        P("rows", "pos"),
        P("rows", None),
        P("rows", None),
        P("rows", None, None),
        P("rows"),
        *([P()] * 13),
        P("rows", "pos", None),
    )
    out_specs = (P("rows", "pos", None), P("rows", "pos", None), *([P()] * 13))
    return jax.shard_map(
        functools.partial(per_device, "rows"),
        mesh=mesh,
        in_specs=in_specs,
        out_specs=out_specs,
        check_vma=False,
    )
```

```python
import functools

import jax
import jax.numpy as jnp
from jax import lax
from jax.experimental import pallas as pl
from jax.experimental.pallas import tpu as pltpu
from jax.sharding import PartitionSpec as P

HEAD_DIM = 64
EPS = 1e-05
NEG = -1e30
GELU_C = 0.7978845608028654
F32 = jnp.float32
BF16 = jnp.bfloat16
VMEM_LIMIT = 60 * 1024 * 1024
FREE = pl.CostEstimate(flops=0, transcendentals=0, bytes_accessed=0)
NT = (((1,), (1,)), ((), ()))
TN = (((0,), (0,)), ((), ()))


def layer_norm(values, gain, shift):
    center = values - jnp.mean(values, axis=-1, keepdims=True)
    spread = jnp.mean(center * center, axis=-1, keepdims=True)
    return center * lax.rsqrt(spread + EPS) * gain + shift


def gelu_tanh(values):
    return 0.5 * values * (1.0 + jnp.tanh(GELU_C * (values + 0.044715 * values * values * values)))


def matmul(left, right, dims=(((1,), (0,)), ((), ()))):
    return lax.dot_general(left, right, dims, preferred_element_type=F32)


def head_pairs(heads):
    return [(h // 2, min(128, heads * HEAD_DIM - (h // 2) * 128)) for h in range(heads)]


def mask_bias(info_ref, key_start, size):
    prefix_start, prefix_end = info_ref[0, 0:1, :], info_ref[0, 1:2, :]
    own_start, query_place = info_ref[0, 2:3, :], info_ref[0, 3:4, :]
    key_place = key_start + lax.broadcasted_iota(jnp.int32, (size, size), 0)
    allowed = ((key_place >= prefix_start) & (key_place < prefix_end)) | (
        (key_place >= own_start) & (key_place <= query_place)
    )
    return jnp.where(allowed, 0.0, NEG).astype(F32)


def fill_padded(source_ref, target_ref, heads):
    for h, (pair, width) in enumerate(head_pairs(heads)):
        rows = source_ref[0, pair * 128 : pair * 128 + width, :]
        if width == 128:
            keep = (lax.broadcasted_iota(jnp.int32, rows.shape, 0) // HEAD_DIM) == (h % 2)
            rows = jnp.where(keep, rows, jnp.zeros_like(rows))
        target_ref[h, 0:width, :] = rows


def forward_kernel(
    heads, blocks, phys_ref, flag_ref, query_t_ref, key_ref, value_t_ref, info_ref,
    mixed_ref, out_t_ref, lse_ref, bias_sc, top_sc, total_sc, acc_sc, query_sc,
):
    size = query_t_ref.shape[2]
    i = pl.program_id(0)
    fill_padded(query_t_ref, query_sc, heads)
    top_sc[...] = jnp.full_like(top_sc, NEG)
    total_sc[...] = jnp.zeros_like(total_sc)
    acc_sc[...] = jnp.zeros_like(acc_sc)

    @pl.loop(0, i + 1)
    def _(j):
        @pl.when(flag_ref[i * blocks + j] > 0)
        def _():
            at = phys_ref[j]
            bias_sc[...] = mask_bias(info_ref, j * size, size)
            for h, (pair, width) in enumerate(head_pairs(heads)):
                rows = slice(h * HEAD_DIM, (h + 1) * HEAD_DIM)
                scores = (
                    matmul(key_ref[at, :, pair * 128 : pair * 128 + width], query_sc[h, 0:width, :])
                    + bias_sc[...]
                )
                old = top_sc[h]
                top = jnp.maximum(old, jnp.max(scores, axis=0, keepdims=True))
                shrink = jnp.exp(old - top)
                weights = jnp.exp(scores - top)
                total_sc[h] = shrink * total_sc[h] + jnp.sum(weights, axis=0, keepdims=True)
                top_sc[h] = top
                acc_sc[rows, :] = shrink * acc_sc[rows, :] + matmul(
                    value_t_ref[at, rows, :], weights.astype(BF16)
                )

    for h in range(heads):
        rows = slice(h * HEAD_DIM, (h + 1) * HEAD_DIM)
        out_t_ref[0, rows, :] = acc_sc[rows, :] / total_sc[h]
        lse_ref[0, h : h + 1, :] = top_sc[h] + jnp.log(total_sc[h])
    mixed_ref[0] = out_t_ref[0].T.astype(BF16)


def attention_forward(phys, flags, query_t, key, value_t, info, heads):
    blocks, width, size = query_t.shape
    lse_rows = -(-heads // 8) * 8
    whole = pl.Buffered(1)
    spec = pltpu.PrefetchScalarGridSpec(
        num_scalar_prefetch=2,
        grid=(blocks,),
        in_specs=[
            pl.BlockSpec((1, width, size), lambda i, p, f: (p[i], 0, 0)),
            pl.BlockSpec((blocks, size, width), lambda i, p, f: (0, 0, 0), pipeline_mode=whole),
            pl.BlockSpec((blocks, width, size), lambda i, p, f: (0, 0, 0), pipeline_mode=whole),
            pl.BlockSpec((1, 8, size), lambda i, p, f: (i, 0, 0)),
        ],
        out_specs=[
            pl.BlockSpec((1, size, width), lambda i, p, f: (p[i], 0, 0)),
            pl.BlockSpec((1, width, size), lambda i, p, f: (p[i], 0, 0)),
            pl.BlockSpec((1, lse_rows, size), lambda i, p, f: (p[i], 0, 0)),
        ],
        scratch_shapes=[
            pltpu.VMEM((size, size), F32),
            pltpu.VMEM((heads, 1, size), F32),
            pltpu.VMEM((heads, 1, size), F32),
            pltpu.VMEM((width, size), F32),
            pltpu.VMEM((heads, 128, size), BF16),
        ],
    )
    pairs = heads * blocks * (blocks + 1) // 2 * size * size
    return pl.pallas_call(
        functools.partial(forward_kernel, heads, blocks),
        grid_spec=spec,
        out_shape=(
            jax.ShapeDtypeStruct((blocks, size, width), BF16),
            jax.ShapeDtypeStruct((blocks, width, size), F32),
            jax.ShapeDtypeStruct((blocks, lse_rows, size), F32),
        ),
        compiler_params=pltpu.CompilerParams(
            dimension_semantics=("arbitrary",), vmem_limit_bytes=VMEM_LIMIT
        ),
        cost_estimate=pl.CostEstimate(
            flops=pairs * 4 * 128, transcendentals=pairs, bytes_accessed=blocks * size * width * 16
        ),
        name="attention_forward",
    )(phys, flags, query_t, key, value_t, info)


def backward_kernel(
    heads, first, blocks, phys_ref, flag_ref, query_t_ref, grad_t_ref, out_t_ref, lse_ref, info_ref,
    key_ref, key_t_ref, value_ref, grads_ref,
    bias_sc, query_grad_sc, key_grad_sc, value_grad_sc, query_sc, grad_sc, delta_sc,
):
    size = query_t_ref.shape[2]
    span = heads * HEAD_DIM
    i = pl.program_id(0)

    @pl.when(i == 0)
    def _():
        key_grad_sc[...] = jnp.zeros_like(key_grad_sc)
        value_grad_sc[...] = jnp.zeros_like(value_grad_sc)

    fill_padded(query_t_ref, query_sc, heads)
    fill_padded(grad_t_ref, grad_sc, heads)
    query_grad_sc[...] = jnp.zeros_like(query_grad_sc)
    for h in range(heads):
        rows = slice(h * HEAD_DIM, (h + 1) * HEAD_DIM)
        delta_sc[h] = jnp.sum(
            grad_t_ref[0, rows, :].astype(F32) * out_t_ref[0, rows, :], axis=0, keepdims=True
        )

    @pl.loop(0, i + 1)
    def _(j):
        @pl.when(flag_ref[i * blocks + j] > 0)
        def _():
            at = phys_ref[j]
            bias_sc[...] = mask_bias(info_ref, j * size, size)
            for h, (pair, width) in enumerate(head_pairs(heads)):
                rows = slice(h * HEAD_DIM, (h + 1) * HEAD_DIM)
                lanes = slice(pair * 128, pair * 128 + width)
                scores = matmul(key_ref[at, :, lanes], query_sc[h, 0:width, :]) + bias_sc[...]
                probs = jnp.exp(scores - lse_ref[0, first + h : first + h + 1, :])
                grad_probs = matmul(value_ref[at, :, lanes], grad_sc[h, 0:width, :])
                grad_scores = (probs * (grad_probs - delta_sc[h])).astype(BF16)
                query_grad_sc[rows, :] += matmul(key_t_ref[at, rows, :], grad_scores)
                value_grad_sc[at, rows, :] += matmul(
                    grad_t_ref[0, rows, :], probs.astype(BF16), NT
                )
                key_grad_sc[at, rows, :] += matmul(query_t_ref[0, rows, :], grad_scores, NT)

    grads_ref[phys_ref[i], :, 0:span] = (query_grad_sc[...] * 0.125).T.astype(BF16)

    @pl.when(i == blocks - 1)
    def _():
        for block in range(blocks):
            grads_ref[block, :, span : 2 * span] = key_grad_sc[block].T.astype(BF16)
            grads_ref[block, :, 2 * span :] = value_grad_sc[block].T.astype(BF16)


def attention_backward(
    phys, flags, query_t, grad_t, out_t, lse, info, key, key_t, value, heads, first
):
    blocks, _, size = query_t.shape
    span = heads * HEAD_DIM
    c = first // heads
    moving_t = pl.BlockSpec((1, span, size), lambda i, p, f: (p[i], c, 0))
    whole = pl.BlockSpec(
        (blocks, size, span), lambda i, p, f: (0, 0, c), pipeline_mode=pl.Buffered(1)
    )
    whole_t = pl.BlockSpec(
        (blocks, span, size), lambda i, p, f: (0, c, 0), pipeline_mode=pl.Buffered(1)
    )
    spec = pltpu.PrefetchScalarGridSpec(
        num_scalar_prefetch=2,
        grid=(blocks,),
        in_specs=[
            moving_t,
            moving_t,
            moving_t,
            pl.BlockSpec((1, lse.shape[1], size), lambda i, p, f: (p[i], 0, 0)),
            pl.BlockSpec((1, 8, size), lambda i, p, f: (i, 0, 0)),
            whole,
            whole_t,
            whole,
        ],
        out_specs=pl.BlockSpec(
            (blocks, size, 3 * span), lambda i, p, f: (0, 0, 0), pipeline_mode=pl.Buffered(1)
        ),
        scratch_shapes=[
            pltpu.VMEM((size, size), F32),
            pltpu.VMEM((span, size), F32),
            pltpu.VMEM((blocks, span, size), F32),
            pltpu.VMEM((blocks, span, size), F32),
            pltpu.VMEM((heads, 128, size), BF16),
            pltpu.VMEM((heads, 128, size), BF16),
            pltpu.VMEM((heads, 1, size), F32),
        ],
    )
    pairs = heads * blocks * (blocks + 1) // 2 * size * size
    return pl.pallas_call(
        functools.partial(backward_kernel, heads, first, blocks),
        grid_spec=spec,
        out_shape=jax.ShapeDtypeStruct((blocks, size, 3 * span), BF16),
        compiler_params=pltpu.CompilerParams(
            dimension_semantics=("arbitrary",), vmem_limit_bytes=VMEM_LIMIT
        ),
        cost_estimate=pl.CostEstimate(
            flops=pairs * 10 * 128, transcendentals=pairs, bytes_accessed=blocks * size * span * 20
        ),
        name="attention_backward",
    )(phys, flags, query_t, grad_t, out_t, lse, info, key, key_t, value)


def project_kernel(
    width, x_ref, gain_ref, shift_ref, w_ref, bias_q_ref, bias_v_ref,
    act_ref, query_t_ref, key_ref, key_t_ref, value_ref, value_t_ref,
):
    act = layer_norm(x_ref[0].astype(F32), gain_ref[...], shift_ref[...]).astype(BF16)
    act_ref[0] = act
    query = (matmul(act, w_ref[:, :width]) + bias_q_ref[...]).astype(BF16).astype(F32) * 0.125
    query_t_ref[0] = query.T.astype(BF16)
    key = matmul(act, w_ref[:, width : 2 * width])
    key_ref[0] = key.astype(BF16)
    key_t_ref[0] = key.T.astype(BF16)
    value = matmul(act, w_ref[:, 2 * width :]) + bias_v_ref[...]
    value_ref[0] = value.astype(BF16)
    value_t_ref[0] = value.T.astype(BF16)


def project(x, gain, shift, weight, bias_q, bias_v):
    blocks, size, model = x.shape
    width = bias_q.shape[1]
    still = lambda i: (0, 0)
    step = lambda i: (i, 0, 0)
    straight, turned = (
        jax.ShapeDtypeStruct((blocks, size, width), BF16),
        jax.ShapeDtypeStruct((blocks, width, size), BF16),
    )
    wide, tall = pl.BlockSpec((1, size, width), step), pl.BlockSpec((1, width, size), step)
    return pl.pallas_call(
        functools.partial(project_kernel, width),
        grid=(blocks,),
        in_specs=[
            pl.BlockSpec((1, size, model), step),
            pl.BlockSpec((1, model), still),
            pl.BlockSpec((1, model), still),
            pl.BlockSpec(weight.shape, still, pipeline_mode=pl.Buffered(1)),
            pl.BlockSpec((1, width), still),
            pl.BlockSpec((1, width), still),
        ],
        out_specs=[pl.BlockSpec((1, size, model), step), tall, wide, tall, wide, tall],
        out_shape=(
            jax.ShapeDtypeStruct((blocks, size, model), BF16),
            turned, straight, turned, straight, turned,
        ),
        compiler_params=pltpu.CompilerParams(
            dimension_semantics=("arbitrary",), vmem_limit_bytes=VMEM_LIMIT
        ),
        cost_estimate=pl.CostEstimate(
            flops=2 * blocks * size * model * 3 * width,
            transcendentals=blocks * size,
            bytes_accessed=blocks * size * (4 * model + 10 * width),
        ),
        name="project",
    )(x, gain, shift, weight, bias_q, bias_v)


def feed_kernel(
    parts, pieces, *refs
):
    mixed_refs, refs = refs[:parts], refs[parts:]
    x_ref, cot_ref, refs = refs[0], refs[1], refs[2:]
    w_out_refs, refs = refs[:parts], refs[parts:]
    (w_up_ref, w_down_ref, out_bias_ref, gain_ref, shift_ref, up_bias_ref, down_bias_ref), refs = (
        refs[:7], refs[7:],
    )
    act_ref, hidden_ref, grad_upper_ref, layer_ref, grad_resid_ref, grad_attn_ref = refs[:6]
    refs = refs[6:]
    grad_mixed_refs, refs = refs[:parts], refs[parts:]
    sums_ref, up_sum_ref, layer_sc, back_sc = refs
    first = pl.program_id(0) == 0

    @pl.when(first)
    def _():
        sums_ref[...] = jnp.zeros_like(sums_ref)
        up_sum_ref[...] = jnp.zeros_like(up_sum_ref)

    attn = out_bias_ref[...]
    for mixed_ref, w_ref in zip(mixed_refs, w_out_refs):
        attn = attn + matmul(mixed_ref[0], w_ref[...])
    resid = x_ref[0].astype(F32) + attn
    center = resid - jnp.mean(resid, axis=-1, keepdims=True)
    root = lax.rsqrt(jnp.mean(center * center, axis=-1, keepdims=True) + EPS)
    normed = center * root
    gain = gain_ref[...]
    act_ref[0] = (normed * gain + shift_ref[...]).astype(BF16)
    layer_sc[...] = resid + down_bias_ref[...]
    back_sc[...] = jnp.zeros_like(back_sc)
    span = w_up_ref.shape[1] // pieces

    for c in range(pieces):
        lanes = slice(c * span, (c + 1) * span)
        upper = matmul(act_ref[0], w_up_ref[:, lanes]) + up_bias_ref[:, lanes]
        square = upper * upper
        bend = jnp.tanh(GELU_C * upper * (1.0 + 0.044715 * square))
        half = 0.5 * (1.0 + bend)
        hidden = (upper * half).astype(BF16)
        hidden_ref[0, :, lanes] = hidden
        slope = half + 0.5 * GELU_C * upper * (1.0 - bend * bend) * (1.0 + 0.134145 * square)
        grad_upper = (matmul(cot_ref[0], w_down_ref[lanes, :], NT) * slope).astype(BF16)
        grad_upper_ref[0, :, lanes] = grad_upper
        up_sum_ref[0:1, lanes] += jnp.sum(grad_upper.astype(F32), axis=0, keepdims=True)
        layer_sc[...] += matmul(hidden, w_down_ref[lanes, :])
        back_sc[...] += matmul(grad_upper, w_up_ref[:, lanes], NT)

    layer_ref[0] = layer_sc[...].astype(BF16)
    back = back_sc[...]
    scaled = back * gain
    grad_out = cot_ref[0].astype(F32)
    grad_resid = grad_out + root * (
        scaled
        - jnp.mean(scaled, axis=-1, keepdims=True)
        - normed * jnp.mean(scaled * normed, axis=-1, keepdims=True)
    )
    grad_resid_ref[0] = grad_resid
    grad_attn = grad_resid.astype(BF16)
    grad_attn_ref[0] = grad_attn
    for w_ref, grad_mixed_ref in zip(w_out_refs, grad_mixed_refs):
        grad_mixed_ref[0] = matmul(grad_attn, w_ref[...], NT).astype(BF16)
    sums_ref[0:1, :] += jnp.sum(grad_attn.astype(F32), axis=0, keepdims=True)
    sums_ref[1:2, :] += jnp.sum(back * normed, axis=0, keepdims=True)
    sums_ref[2:3, :] += jnp.sum(back, axis=0, keepdims=True)
    sums_ref[3:4, :] += jnp.sum(grad_out, axis=0, keepdims=True)


def feed(mixed, x, cotangent, w_out, part, w_up, w_down, vectors, up_bias):
    parts = len(mixed)
    rows, size, model = x.shape
    width = mixed[0].shape[2]
    wide = w_up.shape[1]
    still = lambda i, p: (0, 0)
    step = lambda i, p: (i, 0, 0)
    once = pl.Buffered(1)
    slab = pl.BlockSpec((1, size, model), step)
    head_slab = pl.BlockSpec((1, size, width), step)
    wide_slab = pl.BlockSpec((1, size, wide), step)
    vector = pl.BlockSpec((1, model), still)
    w_out_specs = [
        pl.BlockSpec((width, model), lambda i, p, s=s: (p[0] ^ s, 0), pipeline_mode=once)
        for s in range(parts)
    ]

    def body(p_ref, *refs):
        feed_kernel(parts, wide // model, *refs)

    shape = jax.ShapeDtypeStruct
    out = pl.pallas_call(
        body,
        grid_spec=pltpu.PrefetchScalarGridSpec(
            num_scalar_prefetch=1,
            grid=(rows,),
            in_specs=[head_slab] * parts
            + [slab, slab]
            + w_out_specs
            + [
                pl.BlockSpec(w_up.shape, still, pipeline_mode=once),
                pl.BlockSpec(w_down.shape, still, pipeline_mode=once),
                vector,
                vector,
                vector,
                pl.BlockSpec((1, wide), still),
                vector,
            ],
            out_specs=[slab, wide_slab, wide_slab, slab, slab, slab]
            + [head_slab] * parts
            + [pl.BlockSpec((8, model), still), pl.BlockSpec((8, wide), still)],
            scratch_shapes=[
                pltpu.VMEM((size, model), F32),
                pltpu.VMEM((size, model), F32),
            ],
        ),
        out_shape=[
            shape((rows, size, model), BF16),
            shape((rows, size, wide), BF16),
            shape((rows, size, wide), BF16),
            shape((rows, size, model), BF16),
            shape((rows, size, model), F32),
            shape((rows, size, model), BF16),
        ]
        + [shape((rows, size, width), BF16)] * parts
        + [shape((8, model), F32), shape((8, wide), F32)],
        compiler_params=pltpu.CompilerParams(
            dimension_semantics=("arbitrary",), vmem_limit_bytes=VMEM_LIMIT
        ),
        cost_estimate=pl.CostEstimate(
            flops=2 * rows * size * model * (4 * wide + 2 * model),
            transcendentals=rows * size * wide,
            bytes_accessed=rows * size * (4 * wide + 16 * model),
        ),
        name="feed",
    )(
        part.reshape(1), *mixed, x, cotangent, *([w_out] * parts), w_up, w_down,
        vectors["out_bias"], vectors["gain"], vectors["shift"], up_bias, vectors["down_bias"],
    )
    return out[:6], out[6 : 6 + parts], out[6 + parts], out[7 + parts]


def join_kernel(sources, moves, bit_ref, token_ref, *refs):
    mine_refs, other_refs, out_refs = refs[:sources], refs[sources : 2 * sources], refs[2 * sources :]
    mine = pl.program_id(0) == bit_ref[0]
    for source, begin, out, place, count in moves:
        lanes = slice(begin, begin + count)
        out_refs[out][:, place : place + count] = jnp.where(
            mine, mine_refs[source][:, lanes], other_refs[source][:, lanes]
        ).astype(F32)
    out_refs[-1][0] = token_ref[0]


def join(mine, other, bit, moves, widths, token):
    count = mine[0].shape[0]
    largest = 384 if sum(widths) <= 1024 else 192
    tall = next(t for t in (largest, 192, 96, 48, count) if count % t == 0)
    steps = count // tall

    def mine_map(h, i, b, t):
        return jnp.where(h == b[0], i, jnp.where(h < b[0], 0, steps - 1)), 0

    def other_map(h, i, b, t):
        return jnp.where(h != b[0], i, jnp.where(h < 1 - b[0], 0, steps - 1)), 0

    return pl.pallas_call(
        functools.partial(join_kernel, len(mine), moves),
        grid_spec=pltpu.PrefetchScalarGridSpec(
            num_scalar_prefetch=2,
            grid=(2, steps),
            in_specs=[pl.BlockSpec((tall, m.shape[1]), mine_map) for m in mine]
            + [pl.BlockSpec((tall, m.shape[1]), other_map) for m in mine],
            out_specs=[
                pl.BlockSpec((tall, n), lambda h, i, b, t: (h * steps + i, 0)) for n in widths
            ]
            + [pl.BlockSpec(memory_space=pltpu.SMEM)],
        ),
        out_shape=[jax.ShapeDtypeStruct((2 * count, n), F32) for n in widths]
        + [jax.ShapeDtypeStruct((1,), jnp.int32)],
        compiler_params=pltpu.CompilerParams(
            dimension_semantics=("arbitrary", "arbitrary"), vmem_limit_bytes=VMEM_LIMIT
        ),
        cost_estimate=FREE,
        name="join",
    )(bit.reshape(1), token, *mine, *other)


def project_back_kernel(groups, rows, *refs):
    grad_refs, w_refs, refs = refs[:groups], refs[groups : 2 * groups], refs[2 * groups :]
    own_ref, sent_ref, sums_refs = refs[0], refs[1], refs[2:]
    i = pl.program_id(0)

    def flat(ref):
        return ref[...].reshape(-1, ref.shape[-1])

    total = matmul(flat(grad_refs[0]), w_refs[0][...], NT)
    for grad_ref, w_ref in zip(grad_refs[1:], w_refs[1:]):
        total = total + matmul(flat(grad_ref), w_ref[...], NT)

    @pl.when(i < rows)
    def _():
        own_ref[...] = total.reshape(own_ref.shape)

    @pl.when(i >= rows)
    def _():
        sent_ref[...] = total.astype(BF16).reshape(sent_ref.shape)

    @pl.when(i == 0)
    def _():
        for sums_ref in sums_refs:
            sums_ref[...] = jnp.zeros_like(sums_ref)

    for grad_ref, sums_ref in zip(grad_refs, sums_refs):
        sums_ref[0:1, :] += jnp.sum(flat(grad_ref).astype(F32), axis=0, keepdims=True)


def project_back(grads, weights, rows):
    blocks, size, _ = grads[0].shape
    step = 2 if rows % 2 == 0 else 1
    turn = rows // step
    model = weights[0].shape[0]
    still = lambda i: (0, 0)
    shape = jax.ShapeDtypeStruct
    out = pl.pallas_call(
        functools.partial(project_back_kernel, len(grads), turn),
        grid=(blocks // step,),
        in_specs=[pl.BlockSpec((step, size, g.shape[2]), lambda i: (i, 0, 0)) for g in grads]
        + [pl.BlockSpec(w.shape, still) for w in weights],
        out_specs=[
            pl.BlockSpec((step, size, model), lambda i: (jnp.minimum(i, turn - 1), 0, 0)),
            pl.BlockSpec((step, size, model), lambda i: (jnp.maximum(i - turn, 0), 0, 0)),
        ]
        + [pl.BlockSpec((8, g.shape[2]), still) for g in grads],
        out_shape=[
            shape((rows, size, model), F32),
            shape((blocks - rows, size, model), BF16),
        ]
        + [shape((8, g.shape[2]), F32) for g in grads],
        compiler_params=pltpu.CompilerParams(
            dimension_semantics=("arbitrary",), vmem_limit_bytes=VMEM_LIMIT
        ),
        cost_estimate=FREE,
        name="project_back",
    )(*grads, *weights)
    return out[0], out[1], [sums[0] for sums in out[2:]]


def norm_back_kernel(count, x_ref, own_ref, *refs):
    arrived_refs, (resid_ref, gain_ref, tokens_ref, sums_ref) = refs[:count], refs[count:]

    @pl.when(pl.program_id(0) == 0)
    def _():
        sums_ref[...] = jnp.zeros_like(sums_ref)

    values = x_ref[0].astype(F32)
    center = values - jnp.mean(values, axis=-1, keepdims=True)
    root = lax.rsqrt(jnp.mean(center * center, axis=-1, keepdims=True) + EPS)
    normed = center * root
    back = own_ref[0]
    for arrived_ref in arrived_refs:
        back = back + arrived_ref[0].astype(F32)
    scaled = back * gain_ref[...]
    grad = root * (
        scaled
        - jnp.mean(scaled, axis=-1, keepdims=True)
        - normed * jnp.mean(scaled * normed, axis=-1, keepdims=True)
    )
    tokens_ref[0] = (resid_ref[0] + grad).astype(BF16)
    sums_ref[0:1, :] += jnp.sum(back * normed, axis=0, keepdims=True)
    sums_ref[1:2, :] += jnp.sum(back, axis=0, keepdims=True)


def norm_back(x, own, arrived, grad_resid, gain):
    rows, size, model = x.shape
    slab = pl.BlockSpec((1, size, model), lambda i: (i, 0, 0))
    return pl.pallas_call(
        functools.partial(norm_back_kernel, len(arrived)),
        grid=(rows,),
        in_specs=[slab] * (3 + len(arrived)) + [pl.BlockSpec((1, model), lambda i: (0, 0))],
        out_specs=[slab, pl.BlockSpec((8, model), lambda i: (0, 0))],
        out_shape=[
            jax.ShapeDtypeStruct((rows, size, model), BF16),
            jax.ShapeDtypeStruct((8, model), F32),
        ],
        compiler_params=pltpu.CompilerParams(
            dimension_semantics=("arbitrary",), vmem_limit_bytes=VMEM_LIMIT
        ),
        cost_estimate=FREE,
        name="norm_back",
    )(x, own, *arrived, grad_resid, gain)


def spread_kernel(parts, spans, part_ref, *refs):
    out_ref, refs = refs[-1], refs[:-1]
    part = part_ref[0]
    begin = 0
    for which in range(3):
        for p in range(parts):
            for g, span in enumerate(spans):
                piece = None
                for s in range(parts):
                    here = refs[s * len(spans) + g][:, which * span : (which + 1) * span]
                    piece = here if piece is None else jnp.where((part ^ p) == s, here, piece)
                out_ref[:, begin : begin + span] = piece.astype(F32)
                begin += span


def spread(pieces, part, spans):
    parts = len(pieces)
    count = pieces[0][0].shape[0]
    tall = next(t for t in (192, 96, 48, count) if count % t == 0)
    flat = [p for piece in pieces for p in piece]
    columns = 3 * parts * sum(spans)
    return pl.pallas_call(
        functools.partial(spread_kernel, parts, spans),
        grid_spec=pltpu.PrefetchScalarGridSpec(
            num_scalar_prefetch=1,
            grid=(count // tall,),
            in_specs=[pl.BlockSpec((tall, p.shape[1]), lambda i, b: (i, 0)) for p in flat],
            out_specs=pl.BlockSpec((tall, columns), lambda i, b: (i, 0)),
        ),
        out_shape=jax.ShapeDtypeStruct((count, columns), F32),
        compiler_params=pltpu.CompilerParams(
            dimension_semantics=("arbitrary",), vmem_limit_bytes=VMEM_LIMIT
        ),
        cost_estimate=pl.CostEstimate(
            flops=count * columns, transcendentals=0, bytes_accessed=6 * count * columns
        ),
        name="spread",
    )(part.reshape(1), *flat)


def layout_kernel(owner_ref, sizes_ref, prefixes_ref, lens_ref, padding_ref, info_ref, flags_ref):
    blocks, _, size = info_ref.shape
    groups, slots = lens_ref.shape[1:]
    row = owner_ref[0]
    places = lax.broadcasted_iota(jnp.int32, (blocks, size), 0) * size + lax.broadcasted_iota(
        jnp.int32, (blocks, size), 1
    )
    filled = blocks * size - padding_ref[row]
    prefix_start = jnp.full((blocks, size), filled, jnp.int32)
    prefix_end, own_start = prefix_start, prefix_start
    start = jnp.int32(0)
    for g in range(groups):
        body = start + prefixes_ref[row, g]
        end = jnp.int32(0)
        base = jnp.zeros((blocks, size), jnp.int32)
        for j in range(slots):
            end = end + jnp.where(j < sizes_ref[row, g], lens_ref[row, g, j], 0)
            base = jnp.where(places - body >= end, end, base)
        stop = body + end
        member = (places >= start) & (places < stop) & (places < filled)
        solution = places >= body
        prefix_start = jnp.where(member, start, prefix_start)
        prefix_end = jnp.where(member, jnp.where(solution, body, start), prefix_end)
        own_start = jnp.where(member, jnp.where(solution, body + base, start), own_start)
        start = stop
    info_ref[...] = jnp.zeros_like(info_ref)
    for i, values in enumerate((prefix_start, prefix_end, own_start, places)):
        info_ref[:, i, :] = values
    lane = lax.broadcasted_iota(jnp.int32, flags_ref.shape, 1)
    flags = jnp.zeros(flags_ref.shape, jnp.int32)
    for j in range(blocks):
        low, high = j * size, (j + 1) * size
        need = (jnp.maximum(prefix_start, low) < jnp.minimum(prefix_end, high)) | (
            jnp.maximum(own_start, low) < jnp.minimum(places + 1, high)
        )
        any_need = jnp.max(jnp.where(need, 1, 0), axis=1, keepdims=True)
        flags = jnp.where(lane == j, any_need, flags)
    flags_ref[...] = flags


def row_layout(owner, sizes, prefixes, lens, padding, blocks, size):
    scalars = pl.BlockSpec(memory_space=pltpu.SMEM)
    info, flags = pl.pallas_call(
        layout_kernel,
        in_specs=[scalars] * 5,
        out_shape=(
            jax.ShapeDtypeStruct((blocks, 8, size), jnp.int32),
            jax.ShapeDtypeStruct((blocks, 128), jnp.int32),
        ),
        name="row_layout",
    )(owner.reshape(1).astype(jnp.int32), sizes, prefixes, lens, padding)
    return info, flags[:, :blocks].reshape(-1)


def swap(values, axis, mask):
    count = lax.axis_size(axis)
    return lax.ppermute(values, axis, [(i, i ^ mask) for i in range(count)])


def bits(count):
    return [1 << b for b in range(count.bit_length() - 1)]


def take(values, index):
    return lax.dynamic_index_in_dim(values, index, 0, keepdims=False)


def halve(values, step):
    axis, mask, bit = step
    two = values.reshape(2, values.shape[0] // 2, *values.shape[1:])
    arrived = swap(take(two, 1 - bit), axis, mask)
    return (take(two, bit).astype(F32) + arrived.astype(F32)).astype(values.dtype)


def double(values, step):
    axis, mask, bit = step
    arrived = swap(values, axis, mask)
    return jnp.where(
        bit == 0,
        jnp.concatenate([values, arrived], axis=0),
        jnp.concatenate([arrived, values], axis=0),
    )


class Chain:
    def __init__(self, values, down, up):
        self.values = values
        self.left = [(halve, step) for step in down] + [(double, step) for step in up]

    def advance(self):
        if self.left:
            move, step = self.left.pop(0)
            self.values = move(self.values, step)


def close(chains, *others, early=()):
    order = chains[3:][::-1], chains[2::-1]
    others, small, early, large = lax.optimization_barrier(
        (others, [c.values for c in order[0]], early, [c.values for c in order[1]])
    )
    for chain, values in zip(order[0] + order[1], small + large):
        chain.values = values
    return (*others, *early)


def per_device(
    row_axis,
    tokens,
    segment_ids,
    group_sizes,
    prefix_lens,
    solution_lens,
    padding_counts,
    attn_gain,
    attn_shift,
    w_qkv,
    query_bias,
    value_bias,
    w_out,
    out_bias,
    ffn_gain,
    ffn_shift,
    w_up,
    up_bias,
    w_down,
    down_bias,
    cotangent,
):
    rows, size, model = tokens.shape
    devices = lax.axis_size("pos")
    parts = devices // rows
    blocks = devices
    heads = model // HEAD_DIM // parts
    width = heads * HEAD_DIM
    place = lax.axis_index("pos")
    owner, part = place // parts, place % parts

    def bring(values):
        return jnp.stack(
            [
                swap(take(values, owner ^ m), "pos", m * parts) if m else take(values, owner)
                for m in range(rows)
            ]
        )

    def send_back(values, m):
        return swap(values[m], "pos", m * parts) if m else values[m]

    def arrange(slabs):
        out = jnp.zeros((rows, *slabs[0].shape), slabs[0].dtype)
        for m, slab in enumerate(slabs):
            out = lax.dynamic_update_index_in_dim(out, slab, owner ^ m, 0)
        return out

    info, flags = row_layout(
        owner, group_sizes, prefix_lens, solution_lens, padding_counts, blocks, size
    )
    order = jnp.arange(blocks, dtype=jnp.int32)
    phys = (((order % parts) ^ part) * rows + ((order // parts) ^ owner)).astype(jnp.int32)

    def my_columns(start, first=0, count=None):
        begin = start * model + part * width + first
        return lax.dynamic_slice_in_dim(w_qkv, begin, count or width, 1)

    def as_row(vector):
        return vector.astype(F32).reshape(1, -1)

    groups = [(0, 4), (4, 2)] if heads == 6 else [(0, heads)]
    spans = [count * HEAD_DIM for _, count in groups]
    w_mine = jnp.concatenate([my_columns(n) for n in range(3)], axis=1)
    w_groups = [
        jnp.concatenate([my_columns(n, h * HEAD_DIM, c * HEAD_DIM) for n in range(3)], axis=1)
        for h, c in groups
    ]
    bias_q = lax.dynamic_slice_in_dim(query_bias, part * width, width, 0)
    bias_v = lax.dynamic_slice_in_dim(value_bias, part * width, width, 0)

    mine = bring(tokens)
    row = jnp.concatenate([mine] + [swap(mine, "pos", s) for s in range(1, parts)], axis=0)
    cotangent, row = lax.optimization_barrier((cotangent, row))
    own_cotangent = bring(cotangent)
    act_one, query_t, key, key_t, value, value_t = project(
        row, as_row(attn_gain), as_row(attn_shift), w_mine, as_row(bias_q), as_row(bias_v)
    )
    mixed_all, out_t, lse = attention_forward(
        phys, flags, query_t, key, value_t, info, heads
    )
    mixed_all, own_cotangent = lax.optimization_barrier((mixed_all, own_cotangent))
    mixed_parts = []
    for s in range(parts):
        piece = mixed_all[s * rows : (s + 1) * rows]
        mixed_parts.append(swap(piece, "pos", s) if s else piece)

    (act_two, hidden, grad_upper, layer_out, grad_resid, grad_attn), grad_mixed, sums, up_sum = feed(
        mixed_parts, mine, own_cotangent, w_out, part, w_up, w_down,
        {
            "out_bias": as_row(out_bias),
            "gain": as_row(ffn_gain),
            "shift": as_row(ffn_shift),
            "down_bias": as_row(down_bias),
        },
        as_row(up_bias),
    )
    local = rows * size

    def flat(values):
        return values.reshape(-1, values.shape[-1])

    row_place = lax.axis_index(row_axis)
    row_steps = [(row_axis, m, (row_place // m) % 2) for m in bits(lax.axis_size(row_axis))]
    own_steps = [("pos", m * parts, (owner // m) % 2) for m in bits(rows)]
    part_steps = [("pos", m, (part // m) % 2) for m in bits(parts)]
    turning, last = own_steps + row_steps[:1], row_steps[1:]

    def order(turn):
        turn %= len(turning)
        return turning[turn:] + turning[:turn] + last

    def chain(values, turn, parted=True):
        down = order(turn)
        up = down[::-1] + (part_steps[:0:-1] if parted else [])
        return Chain(values, (part_steps if parted else []) + down, up)

    wide = w_up.shape[1]
    cut = wide * 2 // 3
    near = [m for m in range(1, rows) if m & (m - 1) == 0]
    far = [m for m in range(1, rows) if m & (m - 1)]

    received = [g if s == 0 else swap(g, "pos", s) for s, g in enumerate(grad_mixed)]
    layer_slabs = {m: send_back(layer_out, m) for m in [0] + near}
    down = chain(matmul(flat(hidden), flat(own_cotangent), TN).astype(BF16), 0)
    received, layer_slabs, layer_out, grad_upper = close(
        [down], received, layer_slabs, layer_out, grad_upper
    )
    down.advance()
    layer_slabs.update({m: send_back(layer_out, m) for m in far})
    stacked = jnp.stack(mixed_parts)
    mixed = jnp.concatenate([flat(take(stacked, g ^ part)) for g in range(parts)], axis=1)
    grad_up_flat = flat(grad_upper)
    up_one = chain(matmul(flat(act_two), grad_up_flat[:, :cut], TN).astype(BF16), 1)
    up_two = chain(
        jnp.concatenate(
            [
                matmul(flat(act_two), grad_up_flat[:, cut:], TN).astype(BF16),
                matmul(mixed, flat(grad_attn), TN).astype(BF16),
            ],
            axis=1,
        ),
        2,
    )
    chains = [down, up_one, up_two]
    received, layer_slabs = close(chains, received, layer_slabs)
    up_one.advance()
    up_two.advance()
    for _ in part_steps[1:]:
        for c in chains:
            c.advance()
    grad_t = jnp.concatenate(received, axis=0).transpose(0, 2, 1)
    (grad_t,) = close(chains, grad_t)

    grads, shares = [], []
    for h, count in groups:
        for c in shares[::-1] + chains[::-1]:
            c.advance()
        grad = attention_backward(
            phys, flags, query_t, grad_t, out_t, lse, info, key, key_t, value, count, h
        )
        grad, grad_t = close(chains + shares, grad, grad_t)
        grads.append(grad)
        if len(grads) < len(groups):
            shares.append(chain(matmul(flat(act_one), flat(grad), TN).astype(BF16), 0, False))
            (grad_t,) = close(chains + shares, grad_t)

    def placed(values):
        return lax.dynamic_update_slice_in_dim(jnp.zeros((model,), F32), values, part * width, 0)

    shares.append(chain(matmul(flat(act_one), flat(grads[-1]), TN).astype(BF16), 0, False))
    for c in shares[::-1] + chains[::-1]:
        c.advance()
    own_act, sent_act, sums_grads = project_back(grads, w_groups, rows)
    arrived_act = [
        swap(sent_act[(s - 1) * rows : s * rows], "pos", s) for s in range(1, parts)
    ]

    def column_sums(which):
        return jnp.concatenate(
            [g[which * n : (which + 1) * n] for g, n in zip(sums_grads, spans)]
        )

    sums_q, sums_v = placed(column_sums(0)), placed(column_sums(2))
    own_act, arrived_act, sums_q, sums_v = close(
        chains + shares, own_act, arrived_act, sums_q, sums_v
    )

    for c in shares[::-1] + chains[::-1]:
        c.advance()
    tokens_grad, norm_sums = norm_back(mine, own_act, arrived_act, grad_resid, as_row(attn_gain))
    small = jnp.concatenate(
        [
            norm_sums[0],
            norm_sums[1],
            sums_q,
            sums_v,
            sums[:4].reshape(-1),
            up_sum[0],
        ]
    )
    tokens_grad, small = close(chains + shares, tokens_grad, small)

    small_steps = part_steps + own_steps + row_steps
    token_slabs = {0: tokens_grad[0]}
    layer_home = arrange([layer_slabs[m] for m in range(rows)])
    waves = [[], near + far]
    while any(c.left for c in chains):
        if small_steps:
            axis, mask, _ = small_steps.pop(0)
            small = small + swap(small, axis, mask)
        for c in shares[::-1] + chains[::-1]:
            c.advance()
        wave = waves.pop(0) if waves else []
        token_slabs.update({m: send_back(tokens_grad, m) for m in wave})
        small, tokens_grad, layer_home, *arrived = close(
            chains + shares, small, tokens_grad, layer_home,
            early=tuple(token_slabs[m] for m in wave),
        )
        token_slabs.update(zip(wave, arrived))

    axis, mask, bit = part_steps[0]
    others = [swap(c.values, axis, mask) for c in chains[::-1]][::-1]
    token = own_steps[0][2].astype(jnp.int32).reshape(1)
    sum_w_down, token = join(
        [down.values], others[:1], bit, ((0, 0, 0, 0, model),), (model,), token
    )
    sum_w_up, sum_w_out, token = join(
        [up_one.values, up_two.values],
        others[1:],
        bit,
        ((0, 0, 0, 0, cut), (1, 0, 0, cut, wide - cut), (1, wide - cut, 1, 0, model)),
        (wide, model),
        token,
    )
    for c in shares:
        if c.left:
            move, (axis_last, mask_last, _) = c.left[-1]
            c.left[-1] = (move, (axis_last, mask_last, token[0]))
    tokens_home = arrange([token_slabs[m] for m in range(rows)])
    while any(c.left for c in shares):
        for c in shares:
            c.advance()
    for axis, mask, _ in small_steps:
        small = small + swap(small, axis, mask)
    summed = [c.values for c in shares]
    pieces = [summed] + [[swap(g, "pos", s) for g in summed] for s in range(1, parts)]
    sum_w_qkv = spread(pieces, part, spans)

    vectors = small[: 8 * model].reshape(8, model)
    return (
        layer_home,
        tokens_home,
        vectors[0],
        vectors[1],
        sum_w_qkv,
        vectors[2],
        vectors[3],
        sum_w_out,
        vectors[4],
        vectors[5],
        vectors[6],
        sum_w_up,
        small[8 * model :],
        sum_w_down,
        vectors[7],
    )


def solution(mesh):
    in_specs = (
        P("rows", "pos", None),
        P("rows", "pos"),
        P("rows", None),
        P("rows", None),
        P("rows", None, None),
        P("rows"),
        *([P()] * 13),
        P("rows", "pos", None),
    )
    out_specs = (P("rows", "pos", None), P("rows", "pos", None), *([P()] * 13))
    return jax.shard_map(
        functools.partial(per_device, "rows"),
        mesh=mesh,
        in_specs=in_specs,
        out_specs=out_specs,
        check_vma=False,
    )
```
